32 devices in a mesh: dp: 2 (over x), row: 4 (over y, core), col: 4 (over z).
Axes of the slice: x: 2, y: 2, z: 4, core: 2. Of those that a mesh axis runs over, the one named last changes fastest.
Arguments:
- tokens: bfloat16 [16384, 2048], P(('dp', 'col'), 'row'), may hold values from -6 to 6
- cotangent: bfloat16 [16384, 2048], P(('dp', 'col'), 'row'), may hold values from -6 to 6
- qkv_weight: bfloat16 [3, 2048, 2048], P(None, 'row', 'col')
- attn_weight: bfloat16 [2048, 2048], P('col', 'row')
- expand_weight: bfloat16 [2, 2048, 8192], P(None, 'row', 'col'), may hold values from -0.125 to 0.125
- reduce_weight: bfloat16 [8192, 2048], P('col', 'row')
- headnorm_gain: float32 [2, 2048], P(None, 'col'), may hold values from 0.6 to 1.8
- post_gain: float32 [2, 2048], P(None, 'row'), may hold values from 0.5 to 1.5
- qkv_lowrank: bfloat16 [3, 8, 2048, 16], P(None, None, 'row'), may hold values from -0.125 to 0.125
- qkv_uprank: bfloat16 [3, 8, 16, 2048], P(None, None, None, 'col'), may hold values from -1.5 to 1.5
- attn_lowrank: bfloat16 [8, 2048, 16], P(None, 'col'), may hold values from -0.125 to 0.125
- attn_uprank: bfloat16 [8, 16, 2048], P(None, None, 'row'), may hold values from -1.5 to 1.5
- expand_lowrank: bfloat16 [2, 8, 2048, 16], P(None, None, 'row'), may hold values from -0.125 to 0.125
- expand_uprank: bfloat16 [2, 8, 16, 8192], P(None, None, None, 'col'), may hold values from -1.5 to 1.5
- reduce_lowrank: bfloat16 [8, 8192, 16], P(None, 'col'), may hold values from -0.0625 to 0.0625
- reduce_uprank: bfloat16 [8, 16, 2048], P(None, None, 'row'), may hold values from -1.5 to 1.5
- prefix_length: int32 [8], replicated, may hold values from 204 to 1024, as said below
- adapter_set: int32 [8], replicated, may hold values from 0 to 7
Outputs:
- layer_out: bfloat16 [16384, 2048], P(('dp', 'col'), 'row')
- input_grad: float32 [16384, 2048], P(('dp', 'col'), 'row')
- qkv_lowgrad: float32 [3, 8, 2048, 16], P(None, None, 'row')
- qkv_upgrad: float32 [3, 8, 16, 2048], P(None, None, None, 'col')
- attn_lowgrad: float32 [8, 2048, 16], P(None, 'col')
- attn_upgrad: float32 [8, 16, 2048], P(None, None, 'row')
- expand_lowgrad: float32 [2, 8, 2048, 16], P(None, None, 'row')
- expand_upgrad: float32 [2, 8, 16, 8192], P(None, None, None, 'col')
- reduce_lowgrad: float32 [8, 8192, 16], P(None, 'col')
- reduce_upgrad: float32 [8, 16, 2048], P(None, None, 'row')
The draws below stay inside these ranges and needn't reach their ends.
Inputs may be any that keep to these rules, and one draw needn't show every extreme that they name: The first prefix_length tokens of a sequence see one another; later tokens see the prefix and every earlier token.
All inputs are finite; a program needn't handle non-finite values.
Results may differ from the reference program's by a relative error of at most 0.02.
Values may be sent and summed in bfloat16 or wider, within the bound.
A program may use at most 384 MiB of HBM per device.

```python
import jax
import jax.numpy as jnp
from jax import lax

D = 2048
HEADS = 16
HEAD = 128
FF = 8192
ADAPTER_RANK = 16
SETS = 8
SEQUENCE_LENGTH = 2048
SEQS = 8
TOKENS = 16384


def ramped_matrix(key, shape, fan_in, uniform_law):
    columns = shape[-1]
    ramp = jnp.arange(columns, dtype=jnp.float32) / max(columns - 1, 1)
    if uniform_law:
        base = jax.random.uniform(key, shape, jnp.float32, -1.7320508, 1.7320508)
        factor = 2.0 ** (1.0 - ramp)
    else:
        base = jax.random.normal(key, shape, jnp.float32)
        factor = 3.0 ** (0.5 * ramp)
    return (base * factor * fan_in ** (-0.5)).astype(jnp.bfloat16)


def draw_qkv_weight(key, part):
    return ramped_matrix(jax.random.fold_in(key, 11), (3, D, D), D, False)


def draw_attn_weight(key, part):
    return ramped_matrix(jax.random.fold_in(key, 12), (D, D), D, False)


def draw_reduce_weight(key, part):
    return ramped_matrix(jax.random.fold_in(key, 13), (FF, D), FF, False)


def draw_prefix_length(key, part):
    low_end = SEQUENCE_LENGTH // 10
    high_end = SEQUENCE_LENGTH // 2
    values = jax.random.randint(jax.random.fold_in(key, 21), (SEQS,), low_end, high_end + 1, dtype=jnp.int32)
    order = jax.random.permutation(jax.random.fold_in(key, 22), SEQS)
    values = jnp.where(order == 0, high_end, jnp.where(order == 1, low_end, values))
    return values.astype(jnp.int32)


def draw_adapter_set(key, part):
    order = jax.random.permutation(jax.random.fold_in(key, 31), SEQS).astype(jnp.int32)
    offset = jax.random.randint(jax.random.fold_in(key, 32), (), 0, SETS, dtype=jnp.int32)
    return ((order + offset) % SETS).astype(jnp.int32)


def steps_of(key, shape, split, least, high):
    loudness, own = 1.0, jax.random.fold_in(key, 6)
    for dim, parts in split:
        draws = jnp.exp(jax.random.uniform(jax.random.fold_in(own, dim), (parts,), jnp.float32, least / len(split), high / len(split)))
        loudness = loudness * jnp.repeat(draws, shape[dim] // parts).reshape([-1 if axis == dim else 1 for axis in range(len(shape))])
    return loudness


def noise(stream_key, shape, scale, bound, shards=(), held_as=jnp.bfloat16):
    gain = steps_of(stream_key, shape, shards, -0.22, 0.18) if shards else 1.0
    entries = jax.random.normal(stream_key, shape, jnp.float32) * scale * gain
    return jnp.minimum(jnp.maximum(entries, -bound), bound).astype(held_as)


def setup_inputs(seed: int = 0) -> dict:
    splits = jax.random.split(jax.random.key(seed), 19)
    tokens = noise(splits[0], (TOKENS, D), 1.0, 6.0, ((0, 8), (1, 4)))
    cotangent = noise(splits[1], (TOKENS, D), 1.0, 6.0, ((0, 8), (1, 4)))
    qkv_weight = draw_qkv_weight(jax.random.fold_in(splits[18], 71), 0)
    attn_weight = draw_attn_weight(jax.random.fold_in(splits[18], 71), 0)
    expand_weight = noise(splits[4], (2, D, FF), D ** -0.5, 0.125, ((1, 4), (2, 4)))
    reduce_weight = draw_reduce_weight(jax.random.fold_in(splits[18], 71), 0)
    headnorm_gain = jnp.clip(0.6 + 1.1999999 * jax.random.uniform(splits[6], (2, D), jnp.float32) ** steps_of(splits[6], (2, D), ((1, 4),), -0.2, 0.2), 0.6, 1.8)
    post_gain = jnp.clip(0.5 + 1.0 * jax.random.uniform(splits[7], (2, D), jnp.float32) ** steps_of(splits[7], (2, D), ((1, 4),), -0.2, 0.2), 0.5, 1.5)
    qkv_lowrank = noise(splits[8], (3, SETS, D, ADAPTER_RANK), D ** -0.5, 0.125, ((2, 4),))
    qkv_uprank = noise(splits[9], (3, SETS, ADAPTER_RANK, D), ADAPTER_RANK ** -0.5, 1.5, ((3, 4),))
    attn_lowrank = noise(splits[10], (SETS, D, ADAPTER_RANK), D ** -0.5, 0.125, ((1, 4),))
    attn_uprank = noise(splits[11], (SETS, ADAPTER_RANK, D), ADAPTER_RANK ** -0.5, 1.5, ((2, 4),))
    expand_lowrank = noise(splits[12], (2, SETS, D, ADAPTER_RANK), D ** -0.5, 0.125, ((2, 4),))
    expand_uprank = noise(splits[13], (2, SETS, ADAPTER_RANK, FF), ADAPTER_RANK ** -0.5, 1.5, ((3, 4),))
    reduce_lowrank = noise(splits[14], (SETS, FF, ADAPTER_RANK), FF ** -0.5, 0.0625, ((1, 4),))
    reduce_uprank = noise(splits[15], (SETS, ADAPTER_RANK, D), ADAPTER_RANK ** -0.5, 1.5, ((2, 4),))
    prefix_length = draw_prefix_length(jax.random.fold_in(splits[18], 71), 0)
    adapter_set = draw_adapter_set(jax.random.fold_in(splits[18], 71), 0)
    return dict(tokens=tokens, cotangent=cotangent, qkv_weight=qkv_weight, attn_weight=attn_weight, expand_weight=expand_weight, reduce_weight=reduce_weight, headnorm_gain=headnorm_gain, post_gain=post_gain, qkv_lowrank=qkv_lowrank, qkv_uprank=qkv_uprank, attn_lowrank=attn_lowrank, attn_uprank=attn_uprank, expand_lowrank=expand_lowrank, expand_uprank=expand_uprank, reduce_lowrank=reduce_lowrank, reduce_uprank=reduce_uprank, prefix_length=prefix_length, adapter_set=adapter_set)


@jax.custom_vjp
def low(v):
    return lax.optimization_barrier(v.astype(jnp.bfloat16)).astype(jnp.float32)

@jax.custom_vjp
def lowrank_backward(v):
    return v

def low_keep(v):
    return (low(v), None)

def low_pass(kept, grad):
    return (grad,)

def back_keep(v):
    return (v, None)

def back_low(kept, grad):
    return (low(grad),)
low.defvjp(low_keep, low_pass)
lowrank_backward.defvjp(back_keep, back_low)
EPS = 1e-06
THETA = 500000.0
ADAPTER_FACTOR = 0.5
NEG = -1e+30

def matrix_product(left, right):
    return jnp.dot(left, right, precision=lax.Precision.HIGHEST)

def project(input_rows, weight_matrix, lowrank, upward_rank):
    inner_value = low(lowrank_backward(matrix_product(input_rows, lowrank)))
    return lowrank_backward(matrix_product(input_rows, weight_matrix) + ADAPTER_FACTOR * matrix_product(inner_value, upward_rank))

def rms_scale(values):
    return values * lax.rsqrt(lax.optimization_barrier(jnp.mean(values * values, axis=-1, keepdims=True)) + EPS)

def rotate(values):
    length = values.shape[0]
    heads = values.reshape(length, HEADS, HEAD)
    half = HEAD // 2
    freq = THETA ** (-2.0 * jnp.arange(half, dtype=jnp.float32) / HEAD)
    angle = jnp.arange(length, dtype=jnp.float32)[:, None] * freq[None, :]
    cosine = jnp.cos(angle)[:, None, :]
    sine = jnp.sin(angle)[:, None, :]
    first = heads[..., :half]
    second = heads[..., half:]
    turned = jnp.concatenate([first * cosine - second * sine, second * cosine + first * sine], axis=-1)
    return turned.reshape(length, D)

def split_heads(values):
    return values.reshape(values.shape[0], HEADS, HEAD).transpose(1, 0, 2)

def attend(queries, keys, values, prefix):
    length = queries.shape[0]
    block = min(512, length)
    item_count = length // block
    query_heads = split_heads(queries)
    key_heads = split_heads(keys)
    value_heads = split_heads(values)
    query_blocks = query_heads.reshape(HEADS, item_count, block, HEAD).transpose(1, 0, 2, 3)
    positions = jnp.arange(length, dtype=jnp.int32)

    def one_block(item):
        query_blk, start = item
        scores = jnp.einsum('hqd,hkd->hqk', query_blk, key_heads, precision=lax.Precision.HIGHEST) * HEAD ** (-0.5)
        scores = lowrank_backward(scores)
        rows = start + jnp.arange(block, dtype=jnp.int32)
        allowed = (positions[None, :] <= rows[:, None]) | (positions[None, :] < prefix)
        scores = jnp.where(allowed[None], scores, NEG)
        weights = jax.nn.softmax(scores, axis=-1)
        return jnp.einsum('hqk,hkd->hqd', low(weights), value_heads, precision=lax.Precision.HIGHEST)
    starts = jnp.arange(item_count, dtype=jnp.int32) * block
    outputs = lax.map(jax.checkpoint(one_block), (query_blocks, starts))
    return outputs.transpose(0, 2, 1, 3).reshape(length, D)

def layer(input_rows, adapt, weights, prefix, chosen):
    qkv_weight, attn_weight, expand_weight, reduce_weight, headnorm_gain, post_gain = weights
    qkv_low = jnp.take(adapt[0], chosen, axis=1)
    qkv_up = jnp.take(adapt[1], chosen, axis=1)
    attn_low = jnp.take(adapt[2], chosen, axis=0)
    attn_up = jnp.take(adapt[3], chosen, axis=0)
    expand_low = jnp.take(adapt[4], chosen, axis=1)
    expand_up = jnp.take(adapt[5], chosen, axis=1)
    reduce_low = jnp.take(adapt[6], chosen, axis=0)
    reduce_up = jnp.take(adapt[7], chosen, axis=0)
    queries = project(input_rows, qkv_weight[0], qkv_low[0], qkv_up[0])
    keys = project(input_rows, qkv_weight[1], qkv_low[1], qkv_up[1])
    values = project(input_rows, qkv_weight[2], qkv_low[2], qkv_up[2])
    queries = rotate(rms_scale(queries) * headnorm_gain[0])
    keys = rotate(rms_scale(keys) * headnorm_gain[1])
    mixed = attend(low(queries), low(keys), low(values), prefix)
    mixed = low(lowrank_backward(mixed))
    branch = project(mixed, attn_weight, attn_low, attn_up)
    hidden = input_rows + post_gain[0] * rms_scale(branch)
    hidden_b = low(hidden)
    gate = project(hidden_b, expand_weight[0], expand_low[0], expand_up[0])
    upper = project(hidden_b, expand_weight[1], expand_low[1], expand_up[1])
    inner_value = low(jax.nn.silu(gate) * upper)
    result = project(inner_value, reduce_weight, reduce_low, reduce_up)
    return hidden + post_gain[1] * rms_scale(result)

def reference(tokens, cotangent, qkv_weight, attn_weight, expand_weight, reduce_weight, headnorm_gain, post_gain, qkv_lowrank, qkv_uprank, attn_lowrank, attn_uprank, expand_lowrank, expand_uprank, reduce_lowrank, reduce_uprank, prefix_length, adapter_set):
    weights = (qkv_weight.astype(jnp.float32), attn_weight.astype(jnp.float32), expand_weight.astype(jnp.float32), reduce_weight.astype(jnp.float32), headnorm_gain.astype(jnp.float32), post_gain.astype(jnp.float32))
    adapters = (qkv_lowrank.astype(jnp.float32), qkv_uprank.astype(jnp.float32), attn_lowrank.astype(jnp.float32), attn_uprank.astype(jnp.float32), expand_lowrank.astype(jnp.float32), expand_uprank.astype(jnp.float32), reduce_lowrank.astype(jnp.float32), reduce_uprank.astype(jnp.float32))
    token_seqs = tokens.astype(jnp.float32).reshape(SEQS, SEQUENCE_LENGTH, D)
    grad_seqs = cotangent.astype(jnp.float32).reshape(SEQS, SEQUENCE_LENGTH, D)

    def step(totals, item):
        seq_tokens, seq_grad, prefix, chosen = item

        def forward(input_rows, adapt):
            return layer(input_rows, adapt, weights, prefix, chosen)
        output, pullback = jax.vjp(forward, seq_tokens, adapters)
        grad_in, grad_adapt = pullback(seq_grad)
        totals = jax.tree.map(lambda first, second: first + second, totals, grad_adapt)
        return (totals, (output, grad_in))
    zeros = jax.tree.map(jnp.zeros_like, adapters)
    totals, stacked = lax.scan(step, zeros, (token_seqs, grad_seqs, prefix_length.astype(jnp.int32), adapter_set.astype(jnp.int32)))
    outputs, gradient_list = stacked
    return (outputs.reshape(TOKENS, D).astype(jnp.bfloat16), gradient_list.reshape(TOKENS, D), totals[0], totals[1], totals[2], totals[3], totals[4], totals[5], totals[6], totals[7])
```

```python
import functools

import jax
import jax.numpy as jnp
from jax import lax
from jax.experimental import pallas as pl
from jax.experimental.pallas import tpu as pltpu
from jax.sharding import PartitionSpec as P

D = 2048
HEAD = 128
ADAPTER_RANK = 16
SETS = 8
SEQUENCE_LENGTH = 2048


EPS = 1e-06
THETA = 500000.0
ADAPTER_FACTOR = 0.5
NEG = -1e30


def via_col_row(input_rows, weight_matrix, adapt_mat, compute, seq_pick):
    gathered = lax.all_gather(input_rows, "col", axis=0, tiled=True)
    main, inner_value = compute(gathered, weight_matrix, adapt_mat, seq_pick, False)
    return (
        lax.psum_scatter(main, "row", scatter_dimension=0, tiled=True),
        lax.psum_scatter(inner_value, "row", scatter_dimension=0, tiled=True),
    )


def via_row_col(input_rows, weight_matrix, adapt_mat, compute, seq_pick):
    gathered = lax.all_gather(input_rows, "row", axis=0, tiled=True)
    main, inner_value = compute(gathered, weight_matrix, adapt_mat, seq_pick, False)
    return (
        lax.psum_scatter(main, "col", scatter_dimension=0, tiled=True),
        lax.psum_scatter(inner_value, "col", scatter_dimension=0, tiled=True),
    )


def row_total(values):
    return lax.psum(jnp.sum(values, axis=-1), "row")


def head_totals(first, second):
    return lax.psum((jnp.sum(first, axis=-1), jnp.sum(second, axis=-1)), "col")


def sum_col_tokens(values):
    return lax.psum(values.astype(jnp.bfloat16), ("dp", "col")).astype(jnp.float32)


def sum_row_tokens(values):
    return lax.psum(values.astype(jnp.bfloat16), ("dp", "row")).astype(jnp.float32)


def set_rows(group_sets, first_row, item_count):
    sequence = (first_row + jnp.arange(item_count, dtype=jnp.int32)) // SEQUENCE_LENGTH
    member = sequence[:, None] == jnp.arange(group_sets.shape[0], dtype=jnp.int32)[None, :]
    chosen = jnp.sum(jnp.where(member, group_sets[None, :], 0), axis=1)
    return (chosen[:, None] == jnp.arange(SETS, dtype=jnp.int32)[None, :]).astype(jnp.bfloat16)


def widen(inner_value, onehot, part_list):
    rows = inner_value.shape[0]
    spread = onehot[:, None, :, None] * inner_value.reshape(rows, part_list, 1, ADAPTER_RANK)
    return spread.reshape(rows, part_list, SETS * ADAPTER_RANK)


def adapter_in(gathered, pick, lowrank):
    part_list = lowrank.shape[0]
    width_in = lowrank.shape[2]
    item_count = pick.shape[0]
    chosen = jnp.einsum("sk,pkdr->sdpr", pick, lowrank, preferred_element_type=jnp.float32).astype(
        jnp.bfloat16
    )
    chosen = chosen.reshape(item_count, width_in, part_list * ADAPTER_RANK)
    product_value = jnp.einsum(
        "ehm,emx->ehx",
        gathered.reshape(item_count, SEQUENCE_LENGTH, width_in),
        chosen,
        preferred_element_type=jnp.float32,
    )
    return product_value.reshape(item_count * SEQUENCE_LENGTH, part_list * ADAPTER_RANK)


def adapter_back(gathered, pick, upward_rank):
    part_list = upward_rank.shape[0]
    width_out = upward_rank.shape[-1]
    item_count = pick.shape[0]
    chosen = jnp.einsum(
        "sk,pkre->sper", pick, upward_rank, preferred_element_type=jnp.float32
    ).astype(jnp.bfloat16)
    product_value = jnp.einsum(
        "slpe,sper->slpr",
        gathered.reshape(item_count, SEQUENCE_LENGTH, part_list, width_out),
        chosen,
        preferred_element_type=jnp.float32,
    )
    return ADAPTER_FACTOR * product_value.reshape(
        item_count * SEQUENCE_LENGTH, part_list * ADAPTER_RANK
    )


def adapter_out(wide_output, upward_rank):
    part_list = upward_rank.shape[0]
    flat_up = upward_rank.reshape(part_list, SETS * ADAPTER_RANK, upward_rank.shape[-1])
    return ADAPTER_FACTOR * jnp.einsum(
        "tpk,pke->tpe", wide_output, flat_up, preferred_element_type=jnp.float32
    )


def adapter_grad_in(wide_output, lowrank):
    part_list = lowrank.shape[0]
    width_in = lowrank.shape[2]
    flat_low = lowrank.transpose(0, 1, 3, 2).reshape(part_list, SETS * ADAPTER_RANK, width_in)
    return jnp.einsum("tpk,pkd->td", wide_output, flat_low, preferred_element_type=jnp.float32)


def up_grad(wide_output, gradient_list):
    part_list = gradient_list.shape[1]
    total_sum = ADAPTER_FACTOR * jnp.einsum(
        "jox,joq->oxq", wide_output, gradient_list, preferred_element_type=jnp.float32
    )
    return total_sum.reshape(part_list, SETS, ADAPTER_RANK, gradient_list.shape[2])


def low_grad(input_rows, wide_output):
    part_list = wide_output.shape[1]
    total_sum = jnp.einsum(
        "td,tpk->pkd", input_rows, wide_output, preferred_element_type=jnp.float32
    )
    return total_sum.reshape(part_list, SETS, ADAPTER_RANK, input_rows.shape[1]).transpose(
        0, 1, 3, 2
    )


def swiglu(gate, upper):
    return jax.nn.silu(gate) * upper


def norm_back(grad, values, scale, gain):
    weighted = gain * grad
    inner_sum = row_total(weighted * values)
    return scale[:, None] * weighted - values * (scale**3 * inner_sum / D)[:, None]


def qkv_forward(gathered, weight_matrix, low_flat, pick, per_row):
    input_rows = gathered[:, 0]
    main = jnp.einsum("td,pde->tpe", input_rows, weight_matrix, preferred_element_type=jnp.float32)
    lowrank = low_flat.reshape(3, SETS, low_flat.shape[1], ADAPTER_RANK)
    return (main, adapter_in(input_rows, pick, lowrank))


def expand_forward(gathered, weight_matrix, low_flat, pick, per_row):
    input_rows = gathered[:, 0]
    main = jnp.einsum("td,pdf->tpf", input_rows, weight_matrix, preferred_element_type=jnp.float32)
    lowrank = low_flat.reshape(2, SETS, low_flat.shape[1], ADAPTER_RANK)
    return (main, adapter_in(input_rows, pick, lowrank))


def single_forward(gathered, weight_matrix, low_four, pick, per_row):
    input_rows = gathered[:, 0]
    main = jnp.dot(input_rows, weight_matrix[0, 0], preferred_element_type=jnp.float32)
    return (main, adapter_in(input_rows, pick, low_four))


def single_backward(gathered, weight_matrix, up_flat, pick, per_row):
    main = jnp.einsum(
        "te,fe->tf", gathered[:, 0], weight_matrix, preferred_element_type=jnp.float32
    )
    upward_rank = up_flat.reshape(1, SETS, ADAPTER_RANK, up_flat.shape[1])
    return (main, adapter_back(gathered, pick, upward_rank))


def multi_backward(gathered, weight_matrix, up_flat, pick, per_row):
    part_list = weight_matrix.shape[0]
    main = jnp.einsum("tpf,pdf->td", gathered, weight_matrix, preferred_element_type=jnp.float32)
    upward_rank = up_flat.reshape(part_list, SETS, ADAPTER_RANK, up_flat.shape[2])
    return (main, adapter_back(gathered, pick, upward_rank))


def general_shards(
    tokens,
    cotangent,
    qkv_weight,
    attn_weight,
    expand_weight,
    reduce_weight,
    headnorm_gain,
    post_gain,
    qkv_lowrank,
    qkv_uprank,
    attn_lowrank,
    attn_uprank,
    expand_lowrank,
    expand_uprank,
    reduce_lowrank,
    reduce_uprank,
    prefix_length,
    adapter_set,
):
    rows_a = tokens.shape[0]
    group_rows = rows_a * lax.axis_size("col")
    rows_b = group_rows // lax.axis_size("row")
    group_seqs = group_rows // SEQUENCE_LENGTH
    group_first = lax.axis_index("dp") * group_seqs
    group_sets = lax.dynamic_slice_in_dim(adapter_set, group_first, group_seqs)
    group_prefix = lax.dynamic_slice_in_dim(prefix_length, group_first, group_seqs)
    seq_pick = (group_sets[:, None] == jnp.arange(SETS, dtype=jnp.int32)[None, :]).astype(
        jnp.bfloat16
    )
    pick_a = set_rows(group_sets, lax.axis_index("col") * rows_a, rows_a)
    pick_b = set_rows(group_sets, lax.axis_index("row") * rows_b, rows_b)
    width_row = qkv_weight.shape[1]
    width_col = qkv_weight.shape[2]
    ff_col = expand_weight.shape[2]
    qkv_low_flat = qkv_lowrank.reshape(3 * SETS, width_row, ADAPTER_RANK)
    projected, inner_value = via_col_row(
        tokens[:, None], qkv_weight, qkv_low_flat, qkv_forward, seq_pick
    )
    qkv_wide = widen(inner_value.astype(jnp.bfloat16), pick_b, 3)
    projected = projected + adapter_out(qkv_wide, qkv_uprank)
    queries = projected[:, 0]
    keys = projected[:, 1]
    values = projected[:, 2]
    query_sq, key_sq = head_totals(queries * queries, keys * keys)
    query_scale = lax.rsqrt(query_sq / D + EPS)
    key_scale = lax.rsqrt(key_sq / D + EPS)
    query_norm = queries * query_scale[:, None] * headnorm_gain[0]
    key_norm = keys * key_scale[:, None] * headnorm_gain[1]
    local_heads = queries.shape[1] // HEAD
    half = HEAD // 2
    freq = THETA ** (-2.0 * jnp.arange(half, dtype=jnp.float32) / HEAD)
    position = (jnp.arange(rows_b, dtype=jnp.int32) % SEQUENCE_LENGTH).astype(jnp.float32)
    angle = position[:, None] * freq[None, :]
    cosine = jnp.cos(angle)[:, None, :]
    sine = jnp.sin(angle)[:, None, :]

    def rotate(source):
        heads = source.reshape(rows_b, local_heads, HEAD)
        first = heads[..., :half]
        second = heads[..., half:]
        return jnp.concatenate(
            [first * cosine - second * sine, second * cosine + first * sine], axis=-1
        )

    def unrotate(gradient_list):
        first = gradient_list[..., :half]
        second = gradient_list[..., half:]
        return jnp.concatenate(
            [first * cosine + second * sine, second * cosine - first * sine], axis=-1
        ).reshape(rows_b, local_heads * HEAD)

    query_b = rotate(query_norm).astype(jnp.bfloat16)
    key_b = rotate(key_norm).astype(jnp.bfloat16)
    value_b = values.astype(jnp.bfloat16).reshape(rows_b, local_heads, HEAD)
    block = min(512, SEQUENCE_LENGTH)
    blocks = rows_b // block
    key_pos = jnp.arange(SEQUENCE_LENGTH, dtype=jnp.int32)
    local_first = lax.axis_index("row") * (rows_b // SEQUENCE_LENGTH)
    scale = HEAD ** (-0.5)

    def scores_of(index):
        start = index * block
        seq_start = start // SEQUENCE_LENGTH * SEQUENCE_LENGTH
        which = local_first + start // SEQUENCE_LENGTH
        prefix = jnp.sum(
            jnp.where(jnp.arange(group_seqs, dtype=jnp.int32) == which, group_prefix, 0)
        )
        rows = start - seq_start + jnp.arange(block, dtype=jnp.int32)
        allowed = (key_pos[None, :] <= rows[:, None]) | (key_pos[None, :] < prefix)
        query_blk = lax.dynamic_slice_in_dim(query_b, start, block, 0)
        raw = (
            jnp.einsum("qhd,khd->hqk", query_blk, key_b, preferred_element_type=jnp.float32) * scale
        )
        return (jnp.where(allowed[None], raw, NEG), start, seq_start)

    def attend_block(index):
        scores, start, seq_start = scores_of(index)
        top = jnp.max(scores, axis=-1, keepdims=True)
        powers = jnp.exp(scores - top)
        total_sum = jnp.sum(powers, axis=-1, keepdims=True)
        weights = (powers / total_sum).astype(jnp.bfloat16)
        output = jnp.einsum("hqk,khd->qhd", weights, value_b, preferred_element_type=jnp.float32)
        return (output, (top + jnp.log(total_sum))[..., 0])

    attended, logsum = lax.map(attend_block, jnp.arange(blocks, dtype=jnp.int32))
    mixed_b = attended.reshape(rows_b, local_heads * HEAD).astype(jnp.bfloat16)
    attn_weight_four = attn_weight.reshape(1, 1, width_col, width_row)
    attn_low_four = attn_lowrank.reshape(1, SETS, width_col, ADAPTER_RANK)
    branch, inner_value = via_row_col(
        mixed_b[:, None], attn_weight_four, attn_low_four, single_forward, seq_pick
    )
    attn_wide = widen(inner_value.astype(jnp.bfloat16), pick_a, 1)
    branch = branch + adapter_out(attn_wide, attn_uprank[None])[:, 0]
    branch_scale = lax.rsqrt(row_total(branch * branch) / D + EPS)
    hidden = tokens.astype(jnp.float32) + post_gain[0] * branch * branch_scale[:, None]
    hidden_b = hidden.astype(jnp.bfloat16)
    expand_low_flat = expand_lowrank.reshape(2 * SETS, width_row, ADAPTER_RANK)
    gate_up, inner_value = via_col_row(
        hidden_b[:, None], expand_weight, expand_low_flat, expand_forward, seq_pick
    )
    expand_wide = widen(inner_value.astype(jnp.bfloat16), pick_b, 2)
    gate_up = gate_up + adapter_out(expand_wide, expand_uprank)
    gate = gate_up[:, 0]
    upper = gate_up[:, 1]
    act_b = swiglu(gate, upper).astype(jnp.bfloat16)
    reduce_weight_four = reduce_weight.reshape(1, 1, ff_col, width_row)
    reduce_low_four = reduce_lowrank.reshape(1, SETS, ff_col, ADAPTER_RANK)
    result, inner_value = via_row_col(
        act_b[:, None], reduce_weight_four, reduce_low_four, single_forward, seq_pick
    )
    reduce_wide = widen(inner_value.astype(jnp.bfloat16), pick_a, 1)
    result = result + adapter_out(reduce_wide, reduce_uprank[None])[:, 0]
    result_scale = lax.rsqrt(row_total(result * result) / D + EPS)
    layer_out = (hidden + post_gain[1] * result * result_scale[:, None]).astype(jnp.bfloat16)
    incoming = cotangent.astype(jnp.float32)
    d_result = norm_back(incoming, result, result_scale, post_gain[1]).astype(jnp.bfloat16)
    grad_reduce_up = up_grad(reduce_wide, d_result[:, None])[0]
    grad_reduce_up = sum_col_tokens(grad_reduce_up)
    reduce_up_flat = reduce_uprank.reshape(SETS * ADAPTER_RANK, width_row)
    d_act, inner_value = via_col_row(
        d_result[:, None], reduce_weight, reduce_up_flat, single_backward, seq_pick
    )
    act_wide = widen(inner_value.astype(jnp.bfloat16), pick_b, 1)
    d_act = d_act + adapter_grad_in(act_wide, reduce_lowrank[None])
    grad_reduce_low = low_grad(act_b, act_wide)[0]
    grad_reduce_low = sum_row_tokens(grad_reduce_low)
    unused, pullback = jax.vjp(swiglu, gate, upper)
    d_gate, d_upper = pullback(d_act)
    d_gate_up = jnp.stack([d_gate, d_upper], axis=1).astype(jnp.bfloat16)
    grad_expand_up = up_grad(expand_wide, d_gate_up)
    grad_expand_up = sum_row_tokens(grad_expand_up)
    expand_up_flat = expand_uprank.reshape(2 * SETS, ADAPTER_RANK, ff_col)
    d_hidden_in, inner_value = via_row_col(
        d_gate_up, expand_weight, expand_up_flat, multi_backward, seq_pick
    )
    hidden_wide = widen(inner_value.astype(jnp.bfloat16), pick_a, 2)
    d_hidden = incoming + d_hidden_in + adapter_grad_in(hidden_wide, expand_lowrank)
    grad_expand_low = low_grad(hidden_b, hidden_wide)
    grad_expand_low = sum_col_tokens(grad_expand_low)
    d_branch = norm_back(d_hidden, branch, branch_scale, post_gain[0]).astype(jnp.bfloat16)
    grad_attn_up = up_grad(attn_wide, d_branch[:, None])[0]
    grad_attn_up = sum_col_tokens(grad_attn_up)
    attn_up_flat = attn_uprank.reshape(SETS * ADAPTER_RANK, width_row)
    d_mixed, inner_value = via_col_row(
        d_branch[:, None], attn_weight, attn_up_flat, single_backward, seq_pick
    )
    mixed_wide = widen(inner_value.astype(jnp.bfloat16), pick_b, 1)
    d_mixed = (d_mixed + adapter_grad_in(mixed_wide, attn_lowrank[None])).astype(jnp.bfloat16)
    grad_attn_low = low_grad(mixed_b, mixed_wide)[0]
    grad_attn_low = sum_row_tokens(grad_attn_low)
    d_mixed_heads = d_mixed.reshape(rows_b, local_heads, HEAD)

    def back_block(index, carry):
        d_query, d_key, d_value = carry
        scores, start, seq_start = scores_of(index)
        probs = jnp.exp(
            scores - lax.dynamic_index_in_dim(logsum, index, 0, keepdims=False)[..., None]
        )
        grad_blk = lax.dynamic_slice_in_dim(d_mixed_heads, start, block, 0)
        query_blk = lax.dynamic_slice_in_dim(query_b, start, block, 0)
        d_probs = jnp.einsum("qhd,khd->hqk", grad_blk, value_b, preferred_element_type=jnp.float32)
        delta = jnp.sum(probs * d_probs, axis=-1, keepdims=True)
        d_scores = (probs * (d_probs - delta)).astype(jnp.bfloat16)
        query_part = scale * jnp.einsum(
            "hqk,khd->qhd", d_scores, key_b, preferred_element_type=jnp.float32
        )
        key_part = scale * jnp.einsum(
            "hqk,qhd->khd", d_scores, query_blk, preferred_element_type=jnp.float32
        )
        value_part = jnp.einsum(
            "hqk,qhd->khd", probs.astype(jnp.bfloat16), grad_blk, preferred_element_type=jnp.float32
        )
        d_query = lax.dynamic_update_slice_in_dim(d_query, query_part, start, 0)
        d_key = d_key + key_part
        d_value = d_value + value_part
        return (d_query, d_key, d_value)

    zeros = jnp.zeros((rows_b, local_heads, HEAD), jnp.float32)
    d_query, d_key, d_value = lax.fori_loop(0, blocks, back_block, (zeros, zeros, zeros))
    query_weighted = headnorm_gain[0] * unrotate(d_query)
    key_weighted = headnorm_gain[1] * unrotate(d_key)
    query_sum, key_sum = head_totals(query_weighted * queries, key_weighted * keys)
    d_queries = (
        query_scale[:, None] * query_weighted - queries * (query_scale**3 * query_sum / D)[:, None]
    )
    d_keys = key_scale[:, None] * key_weighted - keys * (key_scale**3 * key_sum / D)[:, None]
    d_qkv = jnp.stack(
        [d_queries, d_keys, d_value.reshape(rows_b, local_heads * HEAD)], axis=1
    ).astype(jnp.bfloat16)
    grad_qkv_up = up_grad(qkv_wide, d_qkv)
    grad_qkv_up = sum_row_tokens(grad_qkv_up)
    qkv_up_flat = qkv_uprank.reshape(3 * SETS, ADAPTER_RANK, width_col)
    d_tokens_in, inner_value = via_row_col(d_qkv, qkv_weight, qkv_up_flat, multi_backward, seq_pick)
    tokens_wide = widen(inner_value.astype(jnp.bfloat16), pick_a, 3)
    input_grad = d_hidden + d_tokens_in + adapter_grad_in(tokens_wide, qkv_lowrank)
    grad_qkv_low = low_grad(tokens, tokens_wide)
    grad_qkv_low = sum_col_tokens(grad_qkv_low)
    return (
        layer_out,
        input_grad,
        grad_qkv_low,
        grad_qkv_up,
        grad_attn_low,
        grad_attn_up,
        grad_expand_low,
        grad_expand_up,
        grad_reduce_low,
        grad_reduce_up,
    )


LOG2E = 1.4426950408889634
CHUNKS = 2
Q_BLOCK = 512
K_BLOCK = 512
BF = jnp.bfloat16
F32 = jnp.float32


def dot_of(left, right, left_dim, right_dim, out=F32):
    return lax.dot_general(
        left, right, (((left_dim,), (right_dim,)), ((), ())), preferred_element_type=out
    )


def attend_kernel(prefix_ref, q_ref, k_ref, v_ref, out_ref, log_ref, *, first):
    rows = q_ref.shape[0]
    start = first + pl.program_id(1) * rows
    prefix = prefix_ref[0]
    blocks = lax.div(jnp.maximum(start + rows, prefix) + K_BLOCK - 1, K_BLOCK)
    query = q_ref[...]
    limit = jnp.maximum(lax.broadcasted_iota(jnp.int32, (1, rows), 1) + start, prefix - 1)
    key_pos = lax.broadcasted_iota(jnp.int32, (K_BLOCK, rows), 0)

    def body(index, carry):
        top, total, mixed = carry
        at = pl.multiple_of(index * K_BLOCK, K_BLOCK)
        scores = dot_of(k_ref[pl.ds(at, K_BLOCK), :], query, 1, 1) * (HEAD**-0.5 * LOG2E)
        scores = jnp.where(key_pos <= limit - at, scores, NEG)
        top_now = jnp.maximum(top, jnp.max(scores, axis=0, keepdims=True))
        fade = jnp.exp2(top - top_now)
        powers = jnp.exp2(scores - top_now)
        total = fade * total + jnp.sum(powers, axis=0, keepdims=True)
        mixed = mixed * fade + dot_of(v_ref[pl.ds(at, K_BLOCK), :], powers.astype(BF), 0, 0)
        return top_now, total, mixed

    top, total, mixed = lax.fori_loop(
        0,
        blocks,
        body,
        (
            jnp.full((1, rows), NEG, F32),
            jnp.zeros((1, rows), F32),
            jnp.zeros((HEAD, rows), F32),
        ),
    )
    out_ref[...] = (mixed / total).T.astype(BF)
    log_ref[0] = top + jnp.log2(total)


def attend(prefix, query, key, value, first):
    rows, length, heads = query.shape[0], key.shape[0], query.shape[1] // HEAD
    q_spec = pl.BlockSpec((Q_BLOCK, HEAD), lambda h, i, p: (i, h))
    k_spec = pl.BlockSpec((length, HEAD), lambda h, i, p: (0, h))
    return pl.pallas_call(
        functools.partial(attend_kernel, first=first),
        out_shape=(
            jax.ShapeDtypeStruct(query.shape, BF),
            jax.ShapeDtypeStruct((heads, 1, rows), F32),
        ),
        grid_spec=pltpu.PrefetchScalarGridSpec(
            num_scalar_prefetch=1,
            grid=(heads, rows // Q_BLOCK),
            in_specs=[q_spec, k_spec, k_spec],
            out_specs=[q_spec, pl.BlockSpec((1, 1, Q_BLOCK), lambda h, i, p: (h, 0, i))],
        ),
        cost_estimate=pl.CostEstimate(
            flops=3 * rows * length * heads * HEAD,
            bytes_accessed=8 * rows * heads * HEAD,
            transcendentals=rows * length * heads,
        ),
        name="attend",
    )(prefix, query, key, value)


def attend_back_kernel(
    prefix_ref, q_ref, grad_ref, out_ref, log_ref, k_ref, v_ref, dq_ref, dk_ref, dv_ref
):
    rows = q_ref.shape[0]
    start = pl.program_id(1) * rows
    prefix = prefix_ref[0]
    blocks = lax.div(jnp.maximum(start + rows, prefix) + K_BLOCK - 1, K_BLOCK)

    @pl.when(pl.program_id(1) == 0)
    def _():
        dk_ref[...] = jnp.zeros_like(dk_ref)
        dv_ref[...] = jnp.zeros_like(dv_ref)

    query = q_ref[...]
    grad = grad_ref[...]
    limit = jnp.maximum(lax.broadcasted_iota(jnp.int32, (1, rows), 1) + start, prefix - 1)
    key_pos = lax.broadcasted_iota(jnp.int32, (K_BLOCK, rows), 0)
    log_total = log_ref[0]
    delta = lax.dot_general(
        jnp.ones((8, HEAD), F32),
        grad.astype(F32) * out_ref[...].astype(F32),
        (((1,), (1,)), ((), ())),
        precision=lax.Precision.HIGHEST,
        preferred_element_type=F32,
    )[0:1]

    def body(index, d_query):
        at = pl.multiple_of(index * K_BLOCK, K_BLOCK)
        span = pl.ds(at, K_BLOCK)
        key = k_ref[span, :]
        scores = dot_of(key, query, 1, 1) * (HEAD**-0.5 * LOG2E)
        probs = jnp.where(key_pos <= limit - at, jnp.exp2(scores - log_total), 0.0)
        d_probs = dot_of(v_ref[span, :], grad, 1, 1)
        d_scores = (probs * (d_probs - delta)).astype(BF)
        dv_ref[span, :] += dot_of(probs.astype(BF), grad, 1, 0)
        dk_ref[span, :] += dot_of(d_scores, query, 1, 0)
        return d_query + dot_of(d_scores, key, 0, 0)

    dq_ref[...] = lax.fori_loop(0, blocks, body, jnp.zeros((rows, HEAD), F32)) * HEAD**-0.5

    @pl.when(pl.program_id(1) == pl.num_programs(1) - 1)
    def _():
        dk_ref[...] = dk_ref[...] * HEAD**-0.5


def attend_back(prefix, query, grad, mixed, log_total, key, value):
    rows, length, heads = query.shape[0], key.shape[0], query.shape[1] // HEAD
    q_spec = pl.BlockSpec((Q_BLOCK, HEAD), lambda h, i, p: (i, h))
    k_spec = pl.BlockSpec((length, HEAD), lambda h, i, p: (0, h))
    return pl.pallas_call(
        attend_back_kernel,
        out_shape=(
            jax.ShapeDtypeStruct(query.shape, F32),
            jax.ShapeDtypeStruct(key.shape, F32),
            jax.ShapeDtypeStruct(key.shape, F32),
        ),
        grid_spec=pltpu.PrefetchScalarGridSpec(
            num_scalar_prefetch=1,
            grid=(heads, rows // Q_BLOCK),
            in_specs=[
                q_spec,
                q_spec,
                q_spec,
                pl.BlockSpec((1, 1, Q_BLOCK), lambda h, i, p: (h, 0, i)),
                k_spec,
                k_spec,
            ],
            out_specs=[q_spec, k_spec, k_spec],
        ),
        cost_estimate=pl.CostEstimate(
            flops=7 * rows * length * heads * HEAD,
            bytes_accessed=24 * rows * heads * HEAD,
            transcendentals=rows * length * heads,
        ),
        name="attend_back",
    )(prefix, query, grad, mixed, log_total, key, value)


def rotate_kernel(raw_ref, scale_ref, gain_ref, cos_ref, sin_ref, q_ref, k_ref, v_ref):
    width = q_ref.shape[1]
    cosine = cos_ref[...]
    sine = sin_ref[...]
    for part, out in ((0, q_ref), (1, k_ref)):
        scale = scale_ref[:, part : part + 1]
        for at in range(0, width, HEAD):
            normed = raw_ref[:, part * width + at : part * width + at + HEAD] * scale
            normed = normed * gain_ref[part : part + 1, at : at + HEAD]
            turned = normed * cosine + pltpu.roll(normed, HEAD // 2, 1) * sine
            out[:, at : at + HEAD] = turned.astype(BF)
    v_ref[...] = raw_ref[:, 2 * width :].astype(BF)


def rotate_rows(raw, scales, gains, cosine, sine):
    rows, width = raw.shape[0], raw.shape[1] // 3
    step = min(512, rows)
    out_spec = pl.BlockSpec((step, width), lambda i: (i, 0))
    table = pl.BlockSpec((step, HEAD), lambda i: (i, 0))
    return pl.pallas_call(
        rotate_kernel,
        out_shape=(jax.ShapeDtypeStruct((rows, width), BF),) * 3,
        grid=(rows // step,),
        in_specs=[
            pl.BlockSpec((step, 3 * width), lambda i: (i, 0)),
            pl.BlockSpec((step, 2), lambda i: (i, 0)),
            pl.BlockSpec((2, width), lambda i: (0, 0)),
            table,
            table,
        ],
        out_specs=[out_spec] * 3,
        name="rotate_rows",
    )(raw, scales, gains, cosine, sine)


def unrotate_kernel(
    raw_ref, dq_ref, dk_ref, dv_ref, scale_ref, back_ref, gain_ref, cos_ref, sin_ref, out_ref
):
    width = dq_ref.shape[1]
    cosine = cos_ref[...]
    sine = sin_ref[...]
    for part, grad in ((0, dq_ref), (1, dk_ref)):
        scale = scale_ref[:, part : part + 1]
        back = back_ref[:, part : part + 1]
        for at in range(0, width, HEAD):
            turned = grad[:, at : at + HEAD]
            turned = turned * cosine - pltpu.roll(turned, HEAD // 2, 1) * sine
            turned = turned * gain_ref[part : part + 1, at : at + HEAD] * scale
            lane = part * width + at
            out_ref[:, lane : lane + HEAD] = (
                turned - raw_ref[:, lane : lane + HEAD] * back
            ).astype(BF)
    out_ref[:, 2 * width :] = dv_ref[...].astype(BF)


def unrotate_rows(raw, d_query, d_key, d_value, scales, backs, gains, cosine, sine):
    rows, width = d_query.shape
    step = min(512, rows)
    part = pl.BlockSpec((step, width), lambda i: (i, 0))
    table = pl.BlockSpec((step, HEAD), lambda i: (i, 0))
    pair = pl.BlockSpec((step, 2), lambda i: (i, 0))
    wide = pl.BlockSpec((step, 3 * width), lambda i: (i, 0))
    return pl.pallas_call(
        unrotate_kernel,
        out_shape=jax.ShapeDtypeStruct((rows, 3 * width), BF),
        grid=(rows // step,),
        in_specs=[
            wide,
            part,
            part,
            part,
            pair,
            pair,
            pl.BlockSpec((2, width), lambda i: (0, 0)),
            table,
            table,
        ],
        out_specs=wide,
        name="unrotate_rows",
    )(raw, d_query, d_key, d_value, scales, backs, gains, cosine, sine)


def across(values, step):
    return lax.ppermute(values, "row", [(i, i ^ step) for i in range(4)])


def gather_row(own):
    core = across(own, 1)
    side = across(own, 2)
    return [own, core, side, across(side, 1)]


def sum_row(values):
    values = values + across(values, 1)
    return values + across(values, 2)


def scatter_row(parts):
    near = parts[0].astype(F32) + across(parts[1], 1).astype(F32)
    far = parts[2].astype(F32) + across(parts[3], 1).astype(F32)
    return near + across(far.astype(BF), 2).astype(F32)


def deal_row(pieces, me):
    out = []
    for step in range(4):
        piece = lax.dynamic_index_in_dim(pieces, me ^ step, 0, keepdims=False)
        out.append(piece if step == 0 else across(piece, step))
    return out


def gather_col(values):
    return lax.all_gather(values, "col", axis=0, tiled=False)


def swap_pair(values):
    return lax.ppermute(values, "dp", [(0, 1), (1, 0)])


def group_shards(
    tokens,
    cotangent,
    qkv_weight,
    attn_weight,
    expand_weight,
    reduce_weight,
    headnorm_gain,
    post_gain,
    qkv_lowrank,
    qkv_uprank,
    attn_lowrank,
    attn_uprank,
    expand_lowrank,
    expand_uprank,
    reduce_lowrank,
    reduce_uprank,
    prefix_length,
    adapter_set,
):
    cols = lax.axis_size("col")
    pair = lax.axis_index("dp")
    me = lax.axis_index("row")
    col = lax.axis_index("col")
    rows, width = tokens.shape
    sub = qkv_weight.shape[2] // 4
    ff = expand_weight.shape[2]
    ff_sub = ff // 4
    ff_half = ff_sub // 2
    local = cols * sub
    ff_local = cols * ff_sub
    out_half = width // 2
    sequence = pair * cols + col
    mine = lax.dynamic_index_in_dim(adapter_set, sequence, 0, keepdims=False)
    prefix = lax.dynamic_slice_in_dim(prefix_length, sequence, 1)
    cols_sets = lax.dynamic_slice_in_dim(adapter_set, pair * cols, cols)

    def own_set(array, axis):
        return lax.dynamic_index_in_dim(array, mine, axis, keepdims=False)

    row_pack = jnp.concatenate(
        [
            own_set(qkv_lowrank, 1).transpose(0, 2, 1).reshape(3 * ADAPTER_RANK, width),
            own_set(attn_uprank, 0),
            own_set(expand_lowrank, 1).transpose(0, 2, 1).reshape(2 * ADAPTER_RANK, width),
            own_set(reduce_uprank, 0),
        ],
        axis=0,
    )
    row_all = jnp.concatenate(gather_row(row_pack), axis=1)
    qkv_low = row_all[:48]
    attn_up = row_all[48:64]
    expand_low = row_all[64:96]
    reduce_up = row_all[96:112]

    def col_pack_of(which):
        one = lambda array, axis: lax.dynamic_index_in_dim(array, which, axis, keepdims=False)
        cut = lambda array, axis, size: lax.dynamic_slice_in_dim(array, me * size, size, axis)
        up_qkv = cut(one(qkv_uprank, 1), 2, sub)
        up_exp = cut(one(expand_uprank, 1), 2, ff_sub)
        return jnp.concatenate(
            [
                up_qkv[0],
                up_qkv[1],
                up_qkv[2],
                cut(one(attn_lowrank, 0), 0, sub).T,
                up_exp[0],
                up_exp[1],
                cut(one(reduce_lowrank, 0), 0, ff_sub).T,
            ],
            axis=1,
        )

    col_pack = jnp.stack([col_pack_of(cols_sets[i]) for i in range(cols)])
    col_all = lax.all_to_all(col_pack, "col", split_axis=0, concat_axis=0, tiled=True)
    heads_of = lambda at: col_all[:, :, at : at + sub].transpose(1, 0, 2).reshape(16, local)

    def swap_halves(array):
        return jnp.where(pair == 0, array, array[:, ::-1])

    def ff_of(at):
        part = col_all[:, :, at : at + ff_sub].reshape(cols, 16, 2, ff_half)
        part = part.transpose(1, 2, 0, 3)
        return swap_halves(part).reshape(16, ff_local)

    qkv_up = [heads_of(i * sub) for i in range(3)]
    attn_low = heads_of(3 * sub)
    expand_up = [ff_of(4 * sub), ff_of(4 * sub + ff_sub)]
    reduce_low = ff_of(4 * sub + 2 * ff_sub)
    gains = lax.dynamic_slice_in_dim(headnorm_gain, me * sub, sub, 1)
    gains = gather_col(gains).transpose(1, 0, 2).reshape(2, local)

    def merged(base, low, up):
        return (base.astype(F32) + ADAPTER_FACTOR * dot_of(low, up, 0, 0)).astype(BF)

    pieces = qkv_weight.reshape(3, width, 4, sub).transpose(2, 0, 1, 3)
    qkv_all = gather_col(jnp.stack(deal_row(pieces, me)))
    qkv_all = qkv_all.transpose(2, 1, 3, 0, 4).reshape(3, 4 * width, local)
    qkv_w = jnp.concatenate(
        [merged(qkv_all[i], qkv_low[16 * i : 16 * i + 16], qkv_up[i]) for i in range(3)], axis=1
    )

    pieces = attn_weight.reshape(4, sub, 2, out_half)
    pieces = lax.dynamic_index_in_dim(pieces, pair, 2, keepdims=False)
    own = gather_col(jnp.stack(deal_row(pieces, me)))
    other = swap_pair(own)
    both = jnp.where(pair == 0, jnp.stack([own, other]), jnp.stack([other, own]))
    attn_all = both.transpose(1, 3, 2, 0, 4).reshape(local, 4 * width)
    attn_w = merged(attn_all, attn_low, attn_up)

    expand_w = []
    for part in range(2):
        pieces = expand_weight[part].reshape(width, 4, 2, ff_half)
        pieces = lax.dynamic_index_in_dim(pieces, pair, 2, keepdims=False).transpose(1, 0, 2)
        own = gather_col(jnp.stack(deal_row(pieces, me)))
        both = jnp.stack([own, swap_pair(own)])
        whole = both.transpose(2, 3, 0, 1, 4).reshape(4 * width, ff_local)
        expand_w.append(merged(whole, expand_low[16 * part : 16 * part + 16], expand_up[part]))

    pieces = reduce_weight.reshape(4, 2, ff_half, width)
    pieces = lax.dynamic_index_in_dim(pieces, pair, 1, keepdims=False)
    own = gather_col(jnp.stack(deal_row(pieces, me)))
    both = jnp.stack([own, swap_pair(own)])
    whole = both.transpose(0, 1, 3, 2, 4).reshape(ff_local, 4 * width)
    reduce_w = merged(whole, reduce_low, reduce_up)

    def in_parts(left, matrix):
        return [
            dot_of(left, matrix[:, i * width : (i + 1) * width], 1, 0, BF if i in (1, 3) else F32)
            for i in range(4)
        ]

    half = HEAD // 2
    freq = THETA ** (-2.0 * jnp.arange(half, dtype=F32) / HEAD)
    angle = jnp.arange(rows, dtype=jnp.int32).astype(F32)[:, None] * freq[None, :]
    cosine = jnp.concatenate([jnp.cos(angle)] * 2, axis=1)
    sine = jnp.sin(angle)
    sine = jnp.concatenate([-sine, sine], axis=1)
    step = rows // CHUNKS
    spans = [slice(i * step, (i + 1) * step) for i in range(CHUNKS)]
    raws, scales, turned, qkv_inner = [], [], [], []
    for span in spans:
        full = jnp.concatenate(gather_row(tokens[span]), axis=1)
        qkv_inner.append(dot_of(qkv_low, full, 1, 1).astype(BF))
        raw = dot_of(full, qkv_w, 1, 0)
        squares = jnp.stack(
            [jnp.sum(raw[:, i * local : (i + 1) * local] ** 2, axis=1) for i in range(2)]
        )
        scale = lax.rsqrt(sum_row(squares) / D + EPS).T
        raws.append(raw)
        scales.append(scale)
        turned.append(rotate_rows(raw, scale, gains, cosine[span], sine[span]))
    key = jnp.concatenate([part[1] for part in turned])
    value = jnp.concatenate([part[2] for part in turned])

    layer_parts, d_hiddens, mixeds, logs, d_mixeds = [], [], [], [], []
    grads = []
    for index, span in enumerate(spans):
        query = turned[index][0]
        mixed, log_total = attend(prefix, query, key, value, index * step)
        mixeds.append(mixed)
        logs.append(log_total)
        attn_inner = sum_row(dot_of(attn_low, mixed, 0 + 1, 1)).astype(BF)
        branch = scatter_row(in_parts(mixed, attn_w))
        branch_scale = lax.rsqrt(sum_row(jnp.sum(branch * branch, axis=1)) / D + EPS)[:, None]
        hidden = tokens[span].astype(F32) + post_gain[0] * branch * branch_scale
        hidden_b = hidden.astype(BF)
        full = jnp.concatenate(gather_row(hidden_b), axis=1)
        expand_inner = dot_of(expand_low, full, 1, 1).astype(BF)
        gate = dot_of(full, expand_w[0], 1, 0)
        upper = dot_of(full, expand_w[1], 1, 0)
        act = (jax.nn.silu(gate) * upper).astype(BF)
        gate_b = gate.astype(BF)
        upper_b = upper.astype(BF)
        reduce_inner = sum_row(dot_of(reduce_low, act, 1, 1)).astype(BF)
        result = scatter_row(in_parts(act, reduce_w))
        incoming = cotangent[span].astype(F32)
        weighted = post_gain[1] * incoming
        sums = sum_row(
            jnp.stack([jnp.sum(result * result, axis=1), jnp.sum(weighted * result, axis=1)])
        )
        result_scale = lax.rsqrt(sums[0] / D + EPS)[:, None]
        layer_parts.append((hidden + post_gain[1] * result * result_scale).astype(BF))
        d_result = (
            result_scale * weighted - result * (result_scale**3 * sums[1][:, None] / D)
        ).astype(BF)
        full = jnp.concatenate(gather_row(d_result), axis=1)
        g_reduce_up = ADAPTER_FACTOR * dot_of(reduce_inner, d_result, 1, 0)
        d_inner = (ADAPTER_FACTOR * dot_of(reduce_up, full, 1, 1)).astype(BF)
        g_reduce_low = dot_of(d_inner, act, 1, 0)
        d_act = dot_of(full, reduce_w, 1, 1)
        gate = gate_b.astype(F32)
        upper = upper_b.astype(F32)
        sigma = jax.nn.sigmoid(gate)
        d_gate = (d_act * upper * sigma * (1 + gate * (1 - sigma))).astype(BF)
        d_upper = (d_act * gate * sigma).astype(BF)
        g_expand_up = [
            ADAPTER_FACTOR * dot_of(expand_inner[:16], d_gate, 1, 0),
            ADAPTER_FACTOR * dot_of(expand_inner[16:], d_upper, 1, 0),
        ]
        d_inner = sum_row(
            ADAPTER_FACTOR
            * jnp.concatenate(
                [dot_of(expand_up[0], d_gate, 1, 1), dot_of(expand_up[1], d_upper, 1, 1)]
            )
        ).astype(BF)
        g_expand_low = dot_of(d_inner, hidden_b, 1, 0)
        parts = []
        for i in range(4):
            cut = slice(i * width, (i + 1) * width)
            part = dot_of(d_gate, expand_w[0][cut], 1, 1) + dot_of(d_upper, expand_w[1][cut], 1, 1)
            parts.append(part.astype(BF) if i in (1, 3) else part)
        d_hidden = incoming + scatter_row(parts)
        weighted = post_gain[0] * d_hidden
        inner_sum = sum_row(jnp.sum(weighted * branch, axis=1))[:, None]
        d_branch = (
            branch_scale * weighted - branch * (branch_scale**3 * inner_sum / D)
        ).astype(BF)
        d_hiddens.append(d_hidden)
        full = jnp.concatenate(gather_row(d_branch), axis=1)
        g_attn_up = ADAPTER_FACTOR * dot_of(attn_inner, d_branch, 1, 0)
        d_inner = (ADAPTER_FACTOR * dot_of(attn_up, full, 1, 1)).astype(BF)
        g_attn_low = dot_of(d_inner, mixed, 1, 0)
        d_mixeds.append(dot_of(full, attn_w, 1, 1, BF))
        grads.append(
            (g_attn_up, g_expand_low, g_reduce_up, g_attn_low, *g_expand_up, g_reduce_low)
        )

    d_query, d_key, d_value = attend_back(
        prefix,
        jnp.concatenate([part[0] for part in turned]),
        jnp.concatenate(d_mixeds),
        jnp.concatenate(mixeds),
        jnp.concatenate(logs, axis=2),
        key,
        value,
    )
    grads = [functools.reduce(jnp.add, parts) for parts in zip(*grads)]
    input_parts, g_low, g_up = [], [], []
    for index, span in enumerate(spans):
        scale = scales[index]
        inner = sum_row(
            jnp.stack(
                [
                    jnp.sum(d_query[span] * turned[index][0].astype(F32), axis=1),
                    jnp.sum(d_key[span] * turned[index][1].astype(F32), axis=1),
                ]
            )
        ).T
        d_qkv = unrotate_rows(
            raws[index],
            d_query[span],
            d_key[span],
            d_value[span],
            scale,
            scale * scale * inner / D,
            gains,
            cosine[span],
            sine[span],
        )
        part = [d_qkv[:, i * local : (i + 1) * local] for i in range(3)]
        g_up.append(
            [
                ADAPTER_FACTOR * dot_of(qkv_inner[index][16 * i : 16 * i + 16], part[i], 1, 0)
                for i in range(3)
            ]
        )
        d_inner = sum_row(
            ADAPTER_FACTOR
            * jnp.concatenate([dot_of(qkv_up[i], part[i], 1, 1) for i in range(3)])
        ).astype(BF)
        g_low.append(dot_of(d_inner, tokens[span], 1, 0))
        parts = [
            dot_of(d_qkv, qkv_w[i * width : (i + 1) * width], 1, 1, BF if i in (1, 3) else F32)
            for i in range(4)
        ]
        input_parts.append(d_hiddens[index] + scatter_row(parts))
    g_qkv_low = functools.reduce(jnp.add, g_low)
    g_qkv_up = [functools.reduce(jnp.add, parts) for parts in zip(*g_up)]
    g_attn_up, g_expand_low, g_reduce_up, g_attn_low, g_gate_up, g_upper_up, g_reduce_low = grads

    member = (adapter_set[None, :] == jnp.arange(SETS, dtype=jnp.int32)[:, None]).astype(F32)

    def to_sets(by_sequence):
        return jnp.einsum(
            "ks,sab->kab", member, by_sequence.astype(F32), precision=lax.Precision.HIGHEST
        )

    def sum_groups(pack):
        return to_sets(lax.all_gather(pack.astype(BF), ("dp", "col"), axis=0, tiled=False))

    early = sum_groups(jnp.concatenate([g_attn_up, g_expand_low, g_reduce_up], axis=0))
    late = sum_groups(g_qkv_low)

    def heads_back(grad):
        return grad.reshape(16, cols, sub).transpose(1, 0, 2)

    def ff_back(grad):
        part = swap_halves(grad.reshape(16, 2, cols, ff_half))
        return part.transpose(2, 0, 1, 3).reshape(cols, 16, ff_sub)

    def sum_tokens(pack):
        dealt = lax.all_to_all(pack.astype(BF), "col", split_axis=0, concat_axis=0, tiled=True)
        every = lax.all_gather(dealt, "row", axis=0, tiled=False)
        every = lax.all_gather(every, "dp", axis=0, tiled=False)
        every = every.transpose(0, 2, 3, 1, 4)
        return to_sets(every.reshape(2 * cols, 16, -1)).reshape(SETS, 16, 4, -1)

    early_col = sum_tokens(
        jnp.concatenate(
            [heads_back(g_attn_low), ff_back(g_gate_up), ff_back(g_upper_up), ff_back(g_reduce_low)],
            axis=2,
        )
    )
    late_col = sum_tokens(jnp.concatenate([heads_back(grad) for grad in g_qkv_up], axis=2))

    def low_of(array):
        return array.transpose(0, 2, 1)

    def piece_of(array, at, size):
        return array[:, :, :, at : at + size].reshape(SETS, 16, 4 * size)

    return (
        jnp.concatenate(layer_parts),
        jnp.concatenate(input_parts),
        jnp.stack([low_of(late[:, 16 * i : 16 * i + 16]) for i in range(3)]),
        jnp.stack([piece_of(late_col, i * sub, sub) for i in range(3)]),
        low_of(piece_of(early_col, 0, sub)),
        early[:, :16],
        jnp.stack([low_of(early[:, 16 + 16 * i : 32 + 16 * i]) for i in range(2)]),
        jnp.stack([piece_of(early_col, sub + i * ff_sub, ff_sub) for i in range(2)]),
        low_of(piece_of(early_col, sub + 2 * ff_sub, ff_sub)),
        early[:, 48:64],
    )


def shards(*arrays):
    whole = (
        lax.axis_size("dp") == 2
        and lax.axis_size("row") == 4
        and arrays[0].shape[0] == SEQUENCE_LENGTH
    )
    return group_shards(*arrays) if whole else general_shards(*arrays)


def solution(mesh):
    placed = (
        P(("dp", "col"), "row"),
        P(("dp", "col"), "row"),
        P(None, "row", "col"),
        P("col", "row"),
        P(None, "row", "col"),
        P("col", "row"),
        P(None, "col"),
        P(None, "row"),
        P(None, None, "row", None),
        P(None, None, None, "col"),
        P(None, "col", None),
        P(None, None, "row"),
        P(None, None, "row", None),
        P(None, None, None, "col"),
        P(None, "col", None),
        P(None, None, "row"),
        P(),
        P(),
    )
    return jax.shard_map(
        shards,
        mesh=mesh,
        in_specs=placed,
        out_specs=(
            P(("dp", "col"), "row"),
            P(("dp", "col"), "row"),
            P(None, None, "row", None),
            P(None, None, None, "col"),
            P(None, "col", None),
            P(None, None, "row"),
            P(None, None, "row", None),
            P(None, None, None, "col"),
            P(None, "col", None),
            P(None, None, "row"),
        ),
        check_vma=False,
    )
```

```python
import functools

import jax
import jax.numpy as jnp
from jax import lax
from jax.experimental import pallas as pl
from jax.experimental.pallas import tpu as pltpu
from jax.sharding import PartitionSpec as P

D = 2048
HEAD = 128
ADAPTER_RANK = 16
SETS = 8
SEQUENCE_LENGTH = 2048


EPS = 1e-06
THETA = 500000.0
ADAPTER_FACTOR = 0.5
NEG = -1e30


def via_col_row(input_rows, weight_matrix, adapt_mat, compute, seq_pick):
    gathered = lax.all_gather(input_rows, "col", axis=0, tiled=True)
    main, inner_value = compute(gathered, weight_matrix, adapt_mat, seq_pick, False)
    return (
        lax.psum_scatter(main, "row", scatter_dimension=0, tiled=True),
        lax.psum_scatter(inner_value, "row", scatter_dimension=0, tiled=True),
    )


def via_row_col(input_rows, weight_matrix, adapt_mat, compute, seq_pick):
    gathered = lax.all_gather(input_rows, "row", axis=0, tiled=True)
    main, inner_value = compute(gathered, weight_matrix, adapt_mat, seq_pick, False)
    return (
        lax.psum_scatter(main, "col", scatter_dimension=0, tiled=True),
        lax.psum_scatter(inner_value, "col", scatter_dimension=0, tiled=True),
    )


def row_total(values):
    return lax.psum(jnp.sum(values, axis=-1), "row")


def head_totals(first, second):
    return lax.psum((jnp.sum(first, axis=-1), jnp.sum(second, axis=-1)), "col")


def sum_col_tokens(values):
    return lax.psum(values.astype(jnp.bfloat16), ("dp", "col")).astype(jnp.float32)


def sum_row_tokens(values):
    return lax.psum(values.astype(jnp.bfloat16), ("dp", "row")).astype(jnp.float32)


def set_rows(group_sets, first_row, item_count):
    sequence = (first_row + jnp.arange(item_count, dtype=jnp.int32)) // SEQUENCE_LENGTH
    member = sequence[:, None] == jnp.arange(group_sets.shape[0], dtype=jnp.int32)[None, :]
    chosen = jnp.sum(jnp.where(member, group_sets[None, :], 0), axis=1)
    return (chosen[:, None] == jnp.arange(SETS, dtype=jnp.int32)[None, :]).astype(jnp.bfloat16)


def widen(inner_value, onehot, part_list):
    rows = inner_value.shape[0]
    spread = onehot[:, None, :, None] * inner_value.reshape(rows, part_list, 1, ADAPTER_RANK)
    return spread.reshape(rows, part_list, SETS * ADAPTER_RANK)


def adapter_in(gathered, pick, lowrank):
    part_list = lowrank.shape[0]
    width_in = lowrank.shape[2]
    item_count = pick.shape[0]
    chosen = jnp.einsum("sk,pkdr->sdpr", pick, lowrank, preferred_element_type=jnp.float32).astype(
        jnp.bfloat16
    )
    chosen = chosen.reshape(item_count, width_in, part_list * ADAPTER_RANK)
    product_value = jnp.einsum(
        "ehm,emx->ehx",
        gathered.reshape(item_count, SEQUENCE_LENGTH, width_in),
        chosen,
        preferred_element_type=jnp.float32,
    )
    return product_value.reshape(item_count * SEQUENCE_LENGTH, part_list * ADAPTER_RANK)


def adapter_back(gathered, pick, upward_rank):
    part_list = upward_rank.shape[0]
    width_out = upward_rank.shape[-1]
    item_count = pick.shape[0]
    chosen = jnp.einsum(
        "sk,pkre->sper", pick, upward_rank, preferred_element_type=jnp.float32
    ).astype(jnp.bfloat16)
    product_value = jnp.einsum(
        "slpe,sper->slpr",
        gathered.reshape(item_count, SEQUENCE_LENGTH, part_list, width_out),
        chosen,
        preferred_element_type=jnp.float32,
    )
    return ADAPTER_FACTOR * product_value.reshape(
        item_count * SEQUENCE_LENGTH, part_list * ADAPTER_RANK
    )


def adapter_out(wide_output, upward_rank):
    part_list = upward_rank.shape[0]
    flat_up = upward_rank.reshape(part_list, SETS * ADAPTER_RANK, upward_rank.shape[-1])
    return ADAPTER_FACTOR * jnp.einsum(
        "tpk,pke->tpe", wide_output, flat_up, preferred_element_type=jnp.float32
    )


def adapter_grad_in(wide_output, lowrank):
    part_list = lowrank.shape[0]
    width_in = lowrank.shape[2]
    flat_low = lowrank.transpose(0, 1, 3, 2).reshape(part_list, SETS * ADAPTER_RANK, width_in)
    return jnp.einsum("tpk,pkd->td", wide_output, flat_low, preferred_element_type=jnp.float32)


def up_grad(wide_output, gradient_list):
    part_list = gradient_list.shape[1]
    total_sum = ADAPTER_FACTOR * jnp.einsum(
        "jox,joq->oxq", wide_output, gradient_list, preferred_element_type=jnp.float32
    )
    return total_sum.reshape(part_list, SETS, ADAPTER_RANK, gradient_list.shape[2])


def low_grad(input_rows, wide_output):
    part_list = wide_output.shape[1]
    total_sum = jnp.einsum(
        "td,tpk->pkd", input_rows, wide_output, preferred_element_type=jnp.float32
    )
    return total_sum.reshape(part_list, SETS, ADAPTER_RANK, input_rows.shape[1]).transpose(
        0, 1, 3, 2
    )


def swiglu(gate, upper):
    return jax.nn.silu(gate) * upper


def norm_back(grad, values, scale, gain):
    weighted = gain * grad
    inner_sum = row_total(weighted * values)
    return scale[:, None] * weighted - values * (scale**3 * inner_sum / D)[:, None]


def qkv_forward(gathered, weight_matrix, low_flat, pick, per_row):
    input_rows = gathered[:, 0]
    main = jnp.einsum("td,pde->tpe", input_rows, weight_matrix, preferred_element_type=jnp.float32)
    lowrank = low_flat.reshape(3, SETS, low_flat.shape[1], ADAPTER_RANK)
    return (main, adapter_in(input_rows, pick, lowrank))


def expand_forward(gathered, weight_matrix, low_flat, pick, per_row):
    input_rows = gathered[:, 0]
    main = jnp.einsum("td,pdf->tpf", input_rows, weight_matrix, preferred_element_type=jnp.float32)
    lowrank = low_flat.reshape(2, SETS, low_flat.shape[1], ADAPTER_RANK)
    return (main, adapter_in(input_rows, pick, lowrank))


def single_forward(gathered, weight_matrix, low_four, pick, per_row):
    input_rows = gathered[:, 0]
    main = jnp.dot(input_rows, weight_matrix[0, 0], preferred_element_type=jnp.float32)
    return (main, adapter_in(input_rows, pick, low_four))


def single_backward(gathered, weight_matrix, up_flat, pick, per_row):
    main = jnp.einsum(
        "te,fe->tf", gathered[:, 0], weight_matrix, preferred_element_type=jnp.float32
    )
    upward_rank = up_flat.reshape(1, SETS, ADAPTER_RANK, up_flat.shape[1])
    return (main, adapter_back(gathered, pick, upward_rank))


def multi_backward(gathered, weight_matrix, up_flat, pick, per_row):
    part_list = weight_matrix.shape[0]
    main = jnp.einsum("tpf,pdf->td", gathered, weight_matrix, preferred_element_type=jnp.float32)
    upward_rank = up_flat.reshape(part_list, SETS, ADAPTER_RANK, up_flat.shape[2])
    return (main, adapter_back(gathered, pick, upward_rank))


def general_shards(
    tokens,
    cotangent,
    qkv_weight,
    attn_weight,
    expand_weight,
    reduce_weight,
    headnorm_gain,
    post_gain,
    qkv_lowrank,
    qkv_uprank,
    attn_lowrank,
    attn_uprank,
    expand_lowrank,
    expand_uprank,
    reduce_lowrank,
    reduce_uprank,
    prefix_length,
    adapter_set,
):
    rows_a = tokens.shape[0]
    group_rows = rows_a * lax.axis_size("col")
    rows_b = group_rows // lax.axis_size("row")
    group_seqs = group_rows // SEQUENCE_LENGTH
    group_first = lax.axis_index("dp") * group_seqs
    group_sets = lax.dynamic_slice_in_dim(adapter_set, group_first, group_seqs)
    group_prefix = lax.dynamic_slice_in_dim(prefix_length, group_first, group_seqs)
    seq_pick = (group_sets[:, None] == jnp.arange(SETS, dtype=jnp.int32)[None, :]).astype(
        jnp.bfloat16
    )
    pick_a = set_rows(group_sets, lax.axis_index("col") * rows_a, rows_a)
    pick_b = set_rows(group_sets, lax.axis_index("row") * rows_b, rows_b)
    width_row = qkv_weight.shape[1]
    width_col = qkv_weight.shape[2]
    ff_col = expand_weight.shape[2]
    qkv_low_flat = qkv_lowrank.reshape(3 * SETS, width_row, ADAPTER_RANK)
    projected, inner_value = via_col_row(
        tokens[:, None], qkv_weight, qkv_low_flat, qkv_forward, seq_pick
    )
    qkv_wide = widen(inner_value.astype(jnp.bfloat16), pick_b, 3)
    projected = projected + adapter_out(qkv_wide, qkv_uprank)
    queries = projected[:, 0]
    keys = projected[:, 1]
    values = projected[:, 2]
    query_sq, key_sq = head_totals(queries * queries, keys * keys)
    query_scale = lax.rsqrt(query_sq / D + EPS)
    key_scale = lax.rsqrt(key_sq / D + EPS)
    query_norm = queries * query_scale[:, None] * headnorm_gain[0]
    key_norm = keys * key_scale[:, None] * headnorm_gain[1]
    local_heads = queries.shape[1] // HEAD
    half = HEAD // 2
    freq = THETA ** (-2.0 * jnp.arange(half, dtype=jnp.float32) / HEAD)
    position = (jnp.arange(rows_b, dtype=jnp.int32) % SEQUENCE_LENGTH).astype(jnp.float32)
    angle = position[:, None] * freq[None, :]
    cosine = jnp.cos(angle)[:, None, :]
    sine = jnp.sin(angle)[:, None, :]

    def rotate(source):
        heads = source.reshape(rows_b, local_heads, HEAD)
        first = heads[..., :half]
        second = heads[..., half:]
        return jnp.concatenate(
            [first * cosine - second * sine, second * cosine + first * sine], axis=-1
        )

    def unrotate(gradient_list):
        first = gradient_list[..., :half]
        second = gradient_list[..., half:]
        return jnp.concatenate(
            [first * cosine + second * sine, second * cosine - first * sine], axis=-1
        ).reshape(rows_b, local_heads * HEAD)

    query_b = rotate(query_norm).astype(jnp.bfloat16)
    key_b = rotate(key_norm).astype(jnp.bfloat16)
    value_b = values.astype(jnp.bfloat16).reshape(rows_b, local_heads, HEAD)
    block = min(512, SEQUENCE_LENGTH)
    blocks = rows_b // block
    key_pos = jnp.arange(SEQUENCE_LENGTH, dtype=jnp.int32)
    local_first = lax.axis_index("row") * (rows_b // SEQUENCE_LENGTH)
    scale = HEAD ** (-0.5)

    def scores_of(index):
        start = index * block
        seq_start = start // SEQUENCE_LENGTH * SEQUENCE_LENGTH
        which = local_first + start // SEQUENCE_LENGTH
        prefix = jnp.sum(
            jnp.where(jnp.arange(group_seqs, dtype=jnp.int32) == which, group_prefix, 0)
        )
        rows = start - seq_start + jnp.arange(block, dtype=jnp.int32)
        allowed = (key_pos[None, :] <= rows[:, None]) | (key_pos[None, :] < prefix)
        query_blk = lax.dynamic_slice_in_dim(query_b, start, block, 0)
        raw = (
            jnp.einsum("qhd,khd->hqk", query_blk, key_b, preferred_element_type=jnp.float32) * scale
        )
        return (jnp.where(allowed[None], raw, NEG), start, seq_start)

    def attend_block(index):
        scores, start, seq_start = scores_of(index)
        top = jnp.max(scores, axis=-1, keepdims=True)
        powers = jnp.exp(scores - top)
        total_sum = jnp.sum(powers, axis=-1, keepdims=True)
        weights = (powers / total_sum).astype(jnp.bfloat16)
        output = jnp.einsum("hqk,khd->qhd", weights, value_b, preferred_element_type=jnp.float32)
        return (output, (top + jnp.log(total_sum))[..., 0])

    attended, logsum = lax.map(attend_block, jnp.arange(blocks, dtype=jnp.int32))
    mixed_b = attended.reshape(rows_b, local_heads * HEAD).astype(jnp.bfloat16)
    attn_weight_four = attn_weight.reshape(1, 1, width_col, width_row)
    attn_low_four = attn_lowrank.reshape(1, SETS, width_col, ADAPTER_RANK)
    branch, inner_value = via_row_col(
        mixed_b[:, None], attn_weight_four, attn_low_four, single_forward, seq_pick
    )
    attn_wide = widen(inner_value.astype(jnp.bfloat16), pick_a, 1)
    branch = branch + adapter_out(attn_wide, attn_uprank[None])[:, 0]
    branch_scale = lax.rsqrt(row_total(branch * branch) / D + EPS)
    hidden = tokens.astype(jnp.float32) + post_gain[0] * branch * branch_scale[:, None]
    hidden_b = hidden.astype(jnp.bfloat16)
    expand_low_flat = expand_lowrank.reshape(2 * SETS, width_row, ADAPTER_RANK)
    gate_up, inner_value = via_col_row(
        hidden_b[:, None], expand_weight, expand_low_flat, expand_forward, seq_pick
    )
    expand_wide = widen(inner_value.astype(jnp.bfloat16), pick_b, 2)
    gate_up = gate_up + adapter_out(expand_wide, expand_uprank)
    gate = gate_up[:, 0]
    upper = gate_up[:, 1]
    act_b = swiglu(gate, upper).astype(jnp.bfloat16)
    reduce_weight_four = reduce_weight.reshape(1, 1, ff_col, width_row)
    reduce_low_four = reduce_lowrank.reshape(1, SETS, ff_col, ADAPTER_RANK)
    result, inner_value = via_row_col(
        act_b[:, None], reduce_weight_four, reduce_low_four, single_forward, seq_pick
    )
    reduce_wide = widen(inner_value.astype(jnp.bfloat16), pick_a, 1)
    result = result + adapter_out(reduce_wide, reduce_uprank[None])[:, 0]
    result_scale = lax.rsqrt(row_total(result * result) / D + EPS)
    layer_out = (hidden + post_gain[1] * result * result_scale[:, None]).astype(jnp.bfloat16)
    incoming = cotangent.astype(jnp.float32)
    d_result = norm_back(incoming, result, result_scale, post_gain[1]).astype(jnp.bfloat16)
    grad_reduce_up = up_grad(reduce_wide, d_result[:, None])[0]
    grad_reduce_up = sum_col_tokens(grad_reduce_up)
    reduce_up_flat = reduce_uprank.reshape(SETS * ADAPTER_RANK, width_row)
    d_act, inner_value = via_col_row(
        d_result[:, None], reduce_weight, reduce_up_flat, single_backward, seq_pick
    )
    act_wide = widen(inner_value.astype(jnp.bfloat16), pick_b, 1)
    d_act = d_act + adapter_grad_in(act_wide, reduce_lowrank[None])
    grad_reduce_low = low_grad(act_b, act_wide)[0]
    grad_reduce_low = sum_row_tokens(grad_reduce_low)
    unused, pullback = jax.vjp(swiglu, gate, upper)
    d_gate, d_upper = pullback(d_act)
    d_gate_up = jnp.stack([d_gate, d_upper], axis=1).astype(jnp.bfloat16)
    grad_expand_up = up_grad(expand_wide, d_gate_up)
    grad_expand_up = sum_row_tokens(grad_expand_up)
    expand_up_flat = expand_uprank.reshape(2 * SETS, ADAPTER_RANK, ff_col)
    d_hidden_in, inner_value = via_row_col(
        d_gate_up, expand_weight, expand_up_flat, multi_backward, seq_pick
    )
    hidden_wide = widen(inner_value.astype(jnp.bfloat16), pick_a, 2)
    d_hidden = incoming + d_hidden_in + adapter_grad_in(hidden_wide, expand_lowrank)
    grad_expand_low = low_grad(hidden_b, hidden_wide)
    grad_expand_low = sum_col_tokens(grad_expand_low)
    d_branch = norm_back(d_hidden, branch, branch_scale, post_gain[0]).astype(jnp.bfloat16)
    grad_attn_up = up_grad(attn_wide, d_branch[:, None])[0]
    grad_attn_up = sum_col_tokens(grad_attn_up)
    attn_up_flat = attn_uprank.reshape(SETS * ADAPTER_RANK, width_row)
    d_mixed, inner_value = via_col_row(
        d_branch[:, None], attn_weight, attn_up_flat, single_backward, seq_pick
    )
    mixed_wide = widen(inner_value.astype(jnp.bfloat16), pick_b, 1)
    d_mixed = (d_mixed + adapter_grad_in(mixed_wide, attn_lowrank[None])).astype(jnp.bfloat16)
    grad_attn_low = low_grad(mixed_b, mixed_wide)[0]
    grad_attn_low = sum_row_tokens(grad_attn_low)
    d_mixed_heads = d_mixed.reshape(rows_b, local_heads, HEAD)

    def back_block(index, carry):
        d_query, d_key, d_value = carry
        scores, start, seq_start = scores_of(index)
        probs = jnp.exp(
            scores - lax.dynamic_index_in_dim(logsum, index, 0, keepdims=False)[..., None]
        )
        grad_blk = lax.dynamic_slice_in_dim(d_mixed_heads, start, block, 0)
        query_blk = lax.dynamic_slice_in_dim(query_b, start, block, 0)
        d_probs = jnp.einsum("qhd,khd->hqk", grad_blk, value_b, preferred_element_type=jnp.float32)
        delta = jnp.sum(probs * d_probs, axis=-1, keepdims=True)
        d_scores = (probs * (d_probs - delta)).astype(jnp.bfloat16)
        query_part = scale * jnp.einsum(
            "hqk,khd->qhd", d_scores, key_b, preferred_element_type=jnp.float32
        )
        key_part = scale * jnp.einsum(
            "hqk,qhd->khd", d_scores, query_blk, preferred_element_type=jnp.float32
        )
        value_part = jnp.einsum(
            "hqk,qhd->khd", probs.astype(jnp.bfloat16), grad_blk, preferred_element_type=jnp.float32
        )
        d_query = lax.dynamic_update_slice_in_dim(d_query, query_part, start, 0)
        d_key = d_key + key_part
        d_value = d_value + value_part
        return (d_query, d_key, d_value)

    zeros = jnp.zeros((rows_b, local_heads, HEAD), jnp.float32)
    d_query, d_key, d_value = lax.fori_loop(0, blocks, back_block, (zeros, zeros, zeros))
    query_weighted = headnorm_gain[0] * unrotate(d_query)
    key_weighted = headnorm_gain[1] * unrotate(d_key)
    query_sum, key_sum = head_totals(query_weighted * queries, key_weighted * keys)
    d_queries = (
        query_scale[:, None] * query_weighted - queries * (query_scale**3 * query_sum / D)[:, None]
    )
    d_keys = key_scale[:, None] * key_weighted - keys * (key_scale**3 * key_sum / D)[:, None]
    d_qkv = jnp.stack(
        [d_queries, d_keys, d_value.reshape(rows_b, local_heads * HEAD)], axis=1
    ).astype(jnp.bfloat16)
    grad_qkv_up = up_grad(qkv_wide, d_qkv)
    grad_qkv_up = sum_row_tokens(grad_qkv_up)
    qkv_up_flat = qkv_uprank.reshape(3 * SETS, ADAPTER_RANK, width_col)
    d_tokens_in, inner_value = via_row_col(d_qkv, qkv_weight, qkv_up_flat, multi_backward, seq_pick)
    tokens_wide = widen(inner_value.astype(jnp.bfloat16), pick_a, 3)
    input_grad = d_hidden + d_tokens_in + adapter_grad_in(tokens_wide, qkv_lowrank)
    grad_qkv_low = low_grad(tokens, tokens_wide)
    grad_qkv_low = sum_col_tokens(grad_qkv_low)
    return (
        layer_out,
        input_grad,
        grad_qkv_low,
        grad_qkv_up,
        grad_attn_low,
        grad_attn_up,
        grad_expand_low,
        grad_expand_up,
        grad_reduce_low,
        grad_reduce_up,
    )


LOG2E = 1.4426950408889634
CHUNKS = 1
Q_BLOCK = 512
K_BLOCK = 512
BF = jnp.bfloat16
F32 = jnp.float32


def dot_of(left, right, left_dim, right_dim, out=F32):
    return lax.dot_general(
        left, right, (((left_dim,), (right_dim,)), ((), ())), preferred_element_type=out
    )


def attend_kernel(prefix_ref, q_ref, k_ref, v_ref, out_ref, log_ref, *, first):
    rows = q_ref.shape[0]
    start = first + pl.program_id(1) * rows
    prefix = prefix_ref[0]
    blocks = lax.div(jnp.maximum(start + rows, prefix) + K_BLOCK - 1, K_BLOCK)
    query = q_ref[...]
    limit = jnp.maximum(lax.broadcasted_iota(jnp.int32, (1, rows), 1) + start, prefix - 1)
    key_pos = lax.broadcasted_iota(jnp.int32, (K_BLOCK, rows), 0)

    def body(index, carry):
        top, total, mixed = carry
        at = pl.multiple_of(index * K_BLOCK, K_BLOCK)
        scores = dot_of(k_ref[pl.ds(at, K_BLOCK), :], query, 1, 1) * (HEAD**-0.5 * LOG2E)
        scores = jnp.where(key_pos <= limit - at, scores, NEG)
        top_now = jnp.maximum(top, jnp.max(scores, axis=0, keepdims=True))
        fade = jnp.exp2(top - top_now)
        powers = jnp.exp2(scores - top_now)
        total = fade * total + jnp.sum(powers, axis=0, keepdims=True)
        mixed = mixed * fade + dot_of(v_ref[pl.ds(at, K_BLOCK), :], powers.astype(BF), 0, 0)
        return top_now, total, mixed

    top, total, mixed = lax.fori_loop(
        0,
        blocks,
        body,
        (
            jnp.full((1, rows), NEG, F32),
            jnp.zeros((1, rows), F32),
            jnp.zeros((HEAD, rows), F32),
        ),
    )
    out_ref[...] = (mixed / total).T.astype(BF)
    log_ref[0] = top + jnp.log2(total)


def attend(prefix, query, key, value, first):
    rows, length, heads = query.shape[0], key.shape[0], query.shape[1] // HEAD
    q_spec = pl.BlockSpec((Q_BLOCK, HEAD), lambda h, i, p: (i, h))
    k_spec = pl.BlockSpec((length, HEAD), lambda h, i, p: (0, h))
    return pl.pallas_call(
        functools.partial(attend_kernel, first=first),
        out_shape=(
            jax.ShapeDtypeStruct(query.shape, BF),
            jax.ShapeDtypeStruct((heads, 1, rows), F32),
        ),
        grid_spec=pltpu.PrefetchScalarGridSpec(
            num_scalar_prefetch=1,
            grid=(heads, rows // Q_BLOCK),
            in_specs=[q_spec, k_spec, k_spec],
            out_specs=[q_spec, pl.BlockSpec((1, 1, Q_BLOCK), lambda h, i, p: (h, 0, i))],
        ),
        cost_estimate=pl.CostEstimate(
            flops=3 * rows * length * heads * HEAD,
            bytes_accessed=8 * rows * heads * HEAD,
            transcendentals=rows * length * heads,
        ),
        name="attend",
    )(prefix, query, key, value)


def row_sums(values):
    return lax.dot_general(
        jnp.ones((8, values.shape[1]), F32),
        values,
        (((1,), (1,)), ((), ())),
        precision=lax.Precision.HIGHEST,
        preferred_element_type=F32,
    )[0:1]


def attend_back_kernel(
    prefix_ref,
    q_ref,
    grad_ref,
    out_ref,
    log_ref,
    k_ref,
    v_ref,
    dq_ref,
    dk_ref,
    dv_ref,
    q_sum_ref,
    k_sum_ref,
):
    rows = q_ref.shape[0]
    start = pl.program_id(1) * rows
    prefix = prefix_ref[0]
    blocks = lax.div(jnp.maximum(start + rows, prefix) + K_BLOCK - 1, K_BLOCK)

    @pl.when(pl.program_id(1) == 0)
    def _():
        dk_ref[...] = jnp.zeros_like(dk_ref)
        dv_ref[...] = jnp.zeros_like(dv_ref)

    query = q_ref[...]
    grad = grad_ref[...]
    limit = jnp.maximum(lax.broadcasted_iota(jnp.int32, (1, rows), 1) + start, prefix - 1)
    key_pos = lax.broadcasted_iota(jnp.int32, (K_BLOCK, rows), 0)
    log_total = log_ref[0]
    delta = row_sums(grad.astype(F32) * out_ref[...].astype(F32))

    def body(index, d_query):
        at = pl.multiple_of(index * K_BLOCK, K_BLOCK)
        span = pl.ds(at, K_BLOCK)
        key = k_ref[span, :]
        scores = dot_of(key, query, 1, 1) * (HEAD**-0.5 * LOG2E)
        probs = jnp.where(key_pos <= limit - at, jnp.exp2(scores - log_total), 0.0)
        d_probs = dot_of(v_ref[span, :], grad, 1, 1)
        d_scores = (probs * (d_probs - delta)).astype(BF)
        dv_ref[span, :] += dot_of(probs.astype(BF), grad, 1, 0)
        dk_ref[span, :] += dot_of(d_scores, query, 1, 0)
        return d_query + dot_of(d_scores, key, 0, 0)

    d_query = lax.fori_loop(0, blocks, body, jnp.zeros((rows, HEAD), F32)) * HEAD**-0.5
    dq_ref[...] = d_query
    q_sum_ref[0] = row_sums(d_query * query.astype(F32))

    @pl.when(pl.program_id(1) == pl.num_programs(1) - 1)
    def _():
        d_key = dk_ref[...] * HEAD**-0.5
        dk_ref[...] = d_key
        k_sum_ref[0] = row_sums(d_key * k_ref[...].astype(F32))


def attend_back(prefix, query, grad, mixed, log_total, key, value):
    rows, length, heads = query.shape[0], key.shape[0], query.shape[1] // HEAD
    q_spec = pl.BlockSpec((Q_BLOCK, HEAD), lambda h, i, p: (i, h))
    k_spec = pl.BlockSpec((length, HEAD), lambda h, i, p: (0, h))
    return pl.pallas_call(
        attend_back_kernel,
        out_shape=(
            jax.ShapeDtypeStruct(query.shape, F32),
            jax.ShapeDtypeStruct(key.shape, F32),
            jax.ShapeDtypeStruct(key.shape, F32),
            jax.ShapeDtypeStruct((heads, 1, rows), F32),
            jax.ShapeDtypeStruct((heads, 1, length), F32),
        ),
        grid_spec=pltpu.PrefetchScalarGridSpec(
            num_scalar_prefetch=1,
            grid=(heads, rows // Q_BLOCK),
            in_specs=[
                q_spec,
                q_spec,
                q_spec,
                pl.BlockSpec((1, 1, Q_BLOCK), lambda h, i, p: (h, 0, i)),
                k_spec,
                k_spec,
            ],
            out_specs=[
                q_spec,
                k_spec,
                k_spec,
                pl.BlockSpec((1, 1, Q_BLOCK), lambda h, i, p: (h, 0, i)),
                pl.BlockSpec((1, 1, length), lambda h, i, p: (h, 0, 0)),
            ],
        ),
        cost_estimate=pl.CostEstimate(
            flops=7 * rows * length * heads * HEAD,
            bytes_accessed=24 * rows * heads * HEAD,
            transcendentals=rows * length * heads,
        ),
        name="attend_back",
    )(prefix, query, grad, mixed, log_total, key, value)


def rotate_kernel(raw_ref, scale_ref, gain_ref, cos_ref, sin_ref, q_ref, k_ref, v_ref):
    width = q_ref.shape[1]
    cosine = cos_ref[...]
    sine = sin_ref[...]
    for part, out in ((0, q_ref), (1, k_ref)):
        scale = scale_ref[:, part : part + 1]
        for at in range(0, width, HEAD):
            normed = raw_ref[:, part * width + at : part * width + at + HEAD] * scale
            normed = normed * gain_ref[part : part + 1, at : at + HEAD]
            turned = normed * cosine + pltpu.roll(normed, HEAD // 2, 1) * sine
            out[:, at : at + HEAD] = turned.astype(BF)
    v_ref[...] = raw_ref[:, 2 * width :].astype(BF)


def rotate_rows(raw, scales, gains, cosine, sine):
    rows, width = raw.shape[0], raw.shape[1] // 3
    step = min(512, rows)
    out_spec = pl.BlockSpec((step, width), lambda i: (i, 0))
    table = pl.BlockSpec((step, HEAD), lambda i: (i, 0))
    return pl.pallas_call(
        rotate_kernel,
        out_shape=(jax.ShapeDtypeStruct((rows, width), BF),) * 3,
        grid=(rows // step,),
        in_specs=[
            pl.BlockSpec((step, 3 * width), lambda i: (i, 0)),
            pl.BlockSpec((step, 2), lambda i: (i, 0)),
            pl.BlockSpec((2, width), lambda i: (0, 0)),
            table,
            table,
        ],
        out_specs=[out_spec] * 3,
        name="rotate_rows",
    )(raw, scales, gains, cosine, sine)


def unrotate_kernel(
    raw_ref, dq_ref, dk_ref, dv_ref, scale_ref, back_ref, gain_ref, cos_ref, sin_ref, out_ref
):
    width = dq_ref.shape[1]
    cosine = cos_ref[...]
    sine = sin_ref[...]
    for part, grad in ((0, dq_ref), (1, dk_ref)):
        scale = scale_ref[:, part : part + 1]
        back = back_ref[:, part : part + 1]
        for at in range(0, width, HEAD):
            turned = grad[:, at : at + HEAD]
            turned = turned * cosine - pltpu.roll(turned, HEAD // 2, 1) * sine
            turned = turned * gain_ref[part : part + 1, at : at + HEAD] * scale
            lane = part * width + at
            out_ref[:, lane : lane + HEAD] = (
                turned - raw_ref[:, lane : lane + HEAD] * back
            ).astype(BF)
    out_ref[:, 2 * width :] = dv_ref[...].astype(BF)


def unrotate_rows(raw, d_query, d_key, d_value, scales, backs, gains, cosine, sine, first):
    rows, width = raw.shape[0], d_query.shape[1]
    step = min(512, rows)
    part = pl.BlockSpec((step, width), lambda i: (i + first // step, 0))
    table = pl.BlockSpec((step, HEAD), lambda i: (i, 0))
    pair = pl.BlockSpec((step, 2), lambda i: (i, 0))
    wide = pl.BlockSpec((step, 3 * width), lambda i: (i, 0))
    return pl.pallas_call(
        unrotate_kernel,
        out_shape=jax.ShapeDtypeStruct((rows, 3 * width), BF),
        grid=(rows // step,),
        in_specs=[
            wide,
            part,
            part,
            part,
            pair,
            pair,
            pl.BlockSpec((2, width), lambda i: (0, 0)),
            table,
            table,
        ],
        out_specs=wide,
        name="unrotate_rows",
    )(raw, d_query, d_key, d_value, scales, backs, gains, cosine, sine)


def flip(values):
    rank = values.shape[1]
    row = lax.broadcasted_iota(jnp.int32, (rank, rank), 0)
    unit = (row == lax.broadcasted_iota(jnp.int32, (rank, rank), 1)).astype(BF)
    return dot_of(unit, values, 1, 1).astype(BF)


def row_pack_kernel(set_ref, qkv_ref, attn_ref, expand_ref, reduce_ref, out_ref):
    for part in range(3):
        out_ref[16 * part : 16 * part + 16, :] = flip(qkv_ref[part, 0])
    out_ref[48:64, :] = attn_ref[0]
    for part in range(2):
        out_ref[64 + 16 * part : 80 + 16 * part, :] = flip(expand_ref[part, 0])
    out_ref[96:112, :] = reduce_ref[0]


def row_pack_of(which, qkv_low, attn_up, expand_low, reduce_up):
    width = attn_up.shape[2]
    up = pl.BlockSpec((1, 16, width), lambda i, c: (c[0], 0, 0))

    def low(parts):
        return pl.BlockSpec((parts, 1, width, 16), lambda i, c: (0, c[0], 0, 0))

    return pl.pallas_call(
        row_pack_kernel,
        out_shape=jax.ShapeDtypeStruct((112, width), BF),
        grid_spec=pltpu.PrefetchScalarGridSpec(
            num_scalar_prefetch=1,
            grid=(1,),
            in_specs=[low(3), up, low(2), up],
            out_specs=pl.BlockSpec((112, width), lambda i, c: (0, 0)),
        ),
        name="row_pack",
    )(which, qkv_low, attn_up, expand_low, reduce_up)


def col_pack_kernel(set_ref, qkv_ref, attn_ref, expand_ref, reduce_ref, out_ref):
    sub, ff_sub = qkv_ref.shape[3], expand_ref.shape[3]
    for part in range(3):
        out_ref[0, :, part * sub : (part + 1) * sub] = qkv_ref[part, 0]
    at = 4 * sub
    out_ref[0, :, 3 * sub : at] = flip(attn_ref[0])
    for part in range(2):
        out_ref[0, :, at : at + ff_sub] = expand_ref[part, 0]
        at += ff_sub
    out_ref[0, :, at:] = flip(reduce_ref[0])


def col_pack_of(which, qkv_up, attn_low, expand_up, reduce_low):
    cols = which.shape[0] - 1
    sub, ff_sub = qkv_up.shape[3] // 4, expand_up.shape[3] // 4

    def up(parts, size):
        return pl.BlockSpec((parts, 1, 16, size), lambda i, c: (0, c[i], 0, c[cols]))

    def low(size):
        return pl.BlockSpec((1, size, 16), lambda i, c: (c[i], c[cols], 0))

    total = 4 * sub + 3 * ff_sub
    return pl.pallas_call(
        col_pack_kernel,
        out_shape=jax.ShapeDtypeStruct((cols, 16, total), BF),
        grid_spec=pltpu.PrefetchScalarGridSpec(
            num_scalar_prefetch=1,
            grid=(cols,),
            in_specs=[up(3, sub), low(sub), up(2, ff_sub), low(ff_sub)],
            out_specs=pl.BlockSpec((1, 16, total), lambda i, c: (i, 0, 0)),
        ),
        name="col_pack",
    )(which, qkv_up, attn_low, expand_up, reduce_low)


def cost_of(flops, bytes_accessed):
    return pl.CostEstimate(flops=int(flops), bytes_accessed=int(bytes_accessed), transcendentals=0)


def row_tile(rows):
    return min(512, rows)


def merge_rows_kernel(pair_ref, own_ref, other_ref, low_ref, up_ref, out_ref):
    def put(piece):
        for block in range(4):
            base = piece[(0, block) + (0,) * (len(piece.shape) - 4)].astype(F32)
            extra = dot_of(low_ref[block, 0], up_ref[...], 0, 0)
            out_ref[block, 0] = (base + ADAPTER_FACTOR * extra).astype(BF)

    mine = pl.program_id(0) == pair_ref[0]
    pl.when(mine)(functools.partial(put, own_ref))
    pl.when(jnp.logical_not(mine))(functools.partial(put, other_ref))


def merge_columns_kernel(pair_ref, *refs):
    *pieces, low_ref, up_ref, out_ref = refs
    width = out_ref.shape[1] // 4

    def put(piece):
        for block in range(4):
            span = slice(block * width, (block + 1) * width)
            extra = dot_of(low_ref[0], up_ref[:, span], 0, 0)
            out_ref[:, span] = (piece[0, block].astype(F32) + ADAPTER_FACTOR * extra).astype(BF)

    if len(pieces) == 1:
        put(pieces[0])
        return
    mine = pl.program_id(0) == pair_ref[0]
    pl.when(mine)(functools.partial(put, pieces[0]))
    pl.when(jnp.logical_not(mine))(functools.partial(put, pieces[1]))


def merge_qkv(pair, own, other, low, up):
    cols, _, parts, cut, sub = own.shape
    last = cols * parts - 1

    def piece(half, relative):
        def place(h, p, c, pair_ref):
            at = p * cols + c
            at = jnp.where(h == half(pair_ref[0]), at, jnp.where(h == 0, 0, last))
            which = lax.rem(at, cols)
            if relative:
                which = lax.rem(which - pair_ref[1] + cols, cols)
            return (which, 0, lax.div(at, cols), 0, 0)

        return pl.BlockSpec((1, 4, 1, cut, sub), place)

    whole = pl.pallas_call(
        merge_rows_kernel,
        out_shape=jax.ShapeDtypeStruct((4, 2, cut, parts * cols * sub), BF),
        grid_spec=pltpu.PrefetchScalarGridSpec(
            num_scalar_prefetch=1,
            grid=(2, parts, cols),
            in_specs=[
                piece(lambda one: one, False),
                piece(lambda one: 1 - one, True),
                pl.BlockSpec((4, 1, 16, cut), lambda h, p, c, one: (0, h, p, 0)),
                pl.BlockSpec((16, sub), lambda h, p, c, one: (p, c)),
            ],
            out_specs=pl.BlockSpec(
                (4, 1, cut, sub), lambda h, p, c, one: (0, h, 0, p * cols + c)
            ),
        ),
        cost_estimate=cost_of(0, 8 * own.size),
        name="merge_qkv",
    )(pair, own, other, low.reshape(16 * parts, 4, 2, cut).transpose(1, 2, 0, 3), up)
    return whole.reshape(8 * cut, parts * cols * sub)


def half_specs(block, cols):
    def piece(half, relative):
        def place(h, c, pair_ref):
            at = jnp.where(h == half(pair_ref[0]), c, jnp.where(h == 0, 0, cols - 1))
            if relative:
                at = lax.rem(at - pair_ref[1] + cols, cols)
            return (at,) + (0,) * (len(block) - 1)

        return pl.BlockSpec(block, place)

    return [piece(lambda one: one, False), piece(lambda one: 1 - one, True)]


def merge_expand(pair, own, other, low, up):
    cols, _, width, cut = own.shape
    whole = pl.pallas_call(
        merge_rows_kernel,
        out_shape=jax.ShapeDtypeStruct((4, 1, width, 2 * cols * cut), BF),
        grid_spec=pltpu.PrefetchScalarGridSpec(
            num_scalar_prefetch=1,
            grid=(2, cols),
            in_specs=half_specs((1, 4, width, cut), cols)
            + [
                pl.BlockSpec((4, 1, 16, width), lambda h, c, one: (0, 0, 0, 0)),
                pl.BlockSpec((16, cut), lambda h, c, one: (0, 2 * c + h)),
            ],
            out_specs=pl.BlockSpec((4, 1, width, cut), lambda h, c, one: (0, 0, 0, 2 * c + h)),
        ),
        cost_estimate=cost_of(0, 8 * own.size),
        name="merge_expand",
    )(pair, own, other, low.reshape(16, 4, 1, width).transpose(1, 2, 0, 3), up)
    return whole.reshape(4 * width, 2 * cols * cut)


def merge_out(pair, pieces, low, up):
    cols, _, rows, width = pieces[0].shape
    takes = len(pieces)
    block = (1, 4, rows, width)
    specs = half_specs(block, cols)
    if takes == 1:
        specs = [pl.BlockSpec(block, lambda h, c, one: (c, 0, 0, 0))]
    return pl.pallas_call(
        merge_columns_kernel,
        out_shape=jax.ShapeDtypeStruct((takes * cols * rows, 4 * width), BF),
        grid_spec=pltpu.PrefetchScalarGridSpec(
            num_scalar_prefetch=1,
            grid=(takes, cols),
            in_specs=specs
            + [
                pl.BlockSpec((1, 16, rows), lambda h, c, one: (takes * c + h, 0, 0)),
                pl.BlockSpec((16, 4 * width), lambda h, c, one: (0, 0)),
            ],
            out_specs=pl.BlockSpec((rows, 4 * width), lambda h, c, one: (takes * c + h, 0)),
        ),
        cost_estimate=cost_of(0, 4 * takes * pieces[0].size),
        name="merge_out",
    )(pair, *pieces, low.reshape(16, takes * cols, rows).transpose(1, 0, 2), up)


def project_kernel(*refs, right_dim):
    *lefts, matrix, out = refs
    left = jnp.concatenate([ref[...] for ref in lefts], axis=1)
    out[...] = dot_of(left, matrix[...], 1, right_dim).astype(out.dtype)


def project(lefts, matrix, right_dim, out_type):
    rows, depth = lefts[0].shape[0], matrix.shape[right_dim]
    wide = matrix.shape[1 - right_dim]
    tile, cut = row_tile(rows), min(512, wide)
    shape = (depth, cut) if right_dim == 0 else (cut, depth)
    place = (lambda n, m: (0, n)) if right_dim == 0 else (lambda n, m: (n, 0))
    return pl.pallas_call(
        functools.partial(project_kernel, right_dim=right_dim),
        out_shape=jax.ShapeDtypeStruct((rows, wide), out_type),
        grid=(wide // cut, rows // tile),
        in_specs=[pl.BlockSpec((tile, left.shape[1]), lambda n, m: (m, 0)) for left in lefts]
        + [pl.BlockSpec(shape, place)],
        out_specs=pl.BlockSpec((tile, cut), lambda n, m: (m, n)),
        cost_estimate=cost_of(2 * rows * depth * wide, 2 * (rows * depth + depth * wide)),
        name="project",
    )(*lefts, matrix)


BLOCK = 256
RING = 5


def peer(step):
    return {"row": lax.axis_index("row") ^ step}


def send(source, target, sems, index, step):
    return pltpu.make_async_remote_copy(
        src_ref=source,
        dst_ref=target,
        send_sem=sems.at[0, index],
        recv_sem=sems.at[1, index],
        device_id=peer(step),
        device_id_type=pl.DeviceIdType.MESH,
    )


def greet():
    barrier = pltpu.get_barrier_semaphore()
    for step in (1, 2, 3):
        pl.semaphore_signal(
            barrier, inc=1, device_id=peer(step), device_id_type=pl.DeviceIdType.MESH
        )
    pl.semaphore_wait(barrier, 3)


def exchange_scratch(count, width, gathers):
    sem = pltpu.SemaphoreType.DMA((2, count))
    shapes = [
        pltpu.VMEM((2, 2, BLOCK, width), BF),
        pltpu.VMEM((count, 2, BLOCK, width), BF),
        pltpu.VMEM((2, BLOCK, width), F32),
        pltpu.VMEM((2, BLOCK, width), BF),
        pltpu.VMEM((count, BLOCK, width), BF),
        pltpu.VMEM((RING, BLOCK, width), F32),
        sem,
        sem,
    ]
    if gathers:
        shapes += [
            pltpu.VMEM((count, 8, BLOCK), F32),
            pltpu.VMEM((3, count, 8, BLOCK), F32),
        ] + [sem] * 6
    return shapes


def run_blocks(count, bufs, compute, stats, finish, own_ref=None, arrived=None):
    pair_out, pair_in, far, side_out, side_in, near, pair_sem, side_sem, *rest = bufs
    gathers = own_ref is not None
    if gathers:
        stat_own, stat_in, stat_1, stat_2, stat_3, core_sem, far_sem, relay_sem = rest
        stat_sems = (stat_1, stat_2, stat_3)

    def rows_of(c):
        return pl.ds(pl.multiple_of(c * BLOCK, BLOCK), BLOCK)

    def to_core(c):
        return send(pair_out.at[lax.rem(c, 2)], pair_in.at[c], pair_sem, c, 1)

    def to_side(c):
        return send(side_out.at[lax.rem(c, 2)], side_in.at[c], side_sem, c, 2)

    def to_stat(c, step):
        return send(stat_own.at[c], stat_in.at[step - 1, c], stat_sems[step - 1], c, step)

    def gather_core(c):
        return send(own_ref.at[rows_of(c)], arrived[0].at[rows_of(c)], core_sem, c, 1)

    def gather_side(c):
        return send(own_ref.at[rows_of(c)], arrived[1].at[rows_of(c)], far_sem, c, 2)

    def relay(c):
        return send(arrived[1].at[rows_of(c)], arrived[2].at[rows_of(c)], relay_sem, c, 1)

    def stage(c, body):
        pl.when(jnp.logical_and(c >= 0, c < count))(functools.partial(body, c))

    def multiply(c):
        @pl.when(c >= 2)
        def _():
            to_core(c - 2).wait_send()

        slot = lax.rem(c, 2)

        def put(block, value):
            if block == 0:
                near[lax.rem(c, RING)] = value
            elif block == 2:
                far[slot] = value
            else:
                pair_out[slot, block // 2] = value.astype(BF)
            if block == 3:
                to_core(c).start()

        compute(c, put)

    def sum_core(c):
        @pl.when(c >= 2)
        def _():
            to_side(c - 2).wait_send()

        to_core(c).wait_recv()
        slot = lax.rem(c, 2)
        side_out[slot] = (far[slot] + pair_in[c, 1].astype(F32)).astype(BF)
        to_side(c).start()
        at = lax.rem(c, RING)
        near[at] = near[at] + pair_in[c, 0].astype(F32)

    def sum_side(c):
        to_side(c).wait_recv()
        at = lax.rem(c, RING)
        total = near[at] + side_in[c].astype(F32)
        if not gathers:
            finish(c, rows_of(c), total)
            return
        near[at] = total
        stat_own[c] = stats(c, rows_of(c), total)
        for step in (1, 2, 3):
            to_stat(c, step).start()

    def normalise(c):
        total = stat_own[c]
        for step in (1, 2, 3):
            to_stat(c, step).wait_recv()
            total = total + stat_in[step - 1, c]
        own_ref[rows_of(c), :] = finish(c, rows_of(c), near[lax.rem(c, RING)], total)
        gather_side(c).start()
        gather_core(c).start()

    def pass_on(c):
        gather_side(c).wait_recv()
        relay(c).start()

    def body(t, carry):
        stage(t - 1, sum_core)
        stage(t, multiply)
        stage(t - 2, sum_side)
        if gathers:
            stage(t - 3, normalise)
            stage(t - 4, pass_on)
        return carry

    lax.fori_loop(0, count + (4 if gathers else 2), body, 0)

    def close(c, carry):
        if gathers:
            for step in (1, 2, 3):
                to_stat(c, step).wait_send()
            gather_core(c).wait()
            gather_side(c).wait_send()
            relay(c).wait()
        return carry

    if gathers:
        lax.fori_loop(0, count, close, 0)
    for c in range(max(count - 2, 0), count):
        to_core(c).wait_send()
        to_side(c).wait_send()


def sums_of(*values):
    out = None
    for index, value in enumerate(values):
        pick = lax.broadcasted_iota(jnp.int32, (8, value.shape[1]), 0) == index
        term = lax.dot_general(
            pick.astype(F32),
            value,
            (((1,), (1,)), ((), ())),
            precision=lax.Precision.HIGHEST,
            preferred_element_type=F32,
        )
        out = term if out is None else out + term
    return out


def column_of(stats, index):
    pick = lax.broadcasted_iota(jnp.int32, (8, HEAD), 0) == index
    wide = lax.dot_general(
        stats,
        pick.astype(F32),
        (((0,), (0,)), ((), ())),
        precision=lax.Precision.HIGHEST,
        preferred_element_type=F32,
    )
    return wide[:, :1]


def branch_kernel(
    mixed_ref, matrix_ref, tokens_ref, gain_ref, branch_ref, hidden_ref, stat_ref, own_ref, *rest
):
    arrived, bufs = rest[:3], rest[3:]
    width = own_ref.shape[1]
    count = own_ref.shape[0] // BLOCK
    greet()

    def compute(c, put):
        left = mixed_ref[pl.ds(pl.multiple_of(c * BLOCK, BLOCK), BLOCK), :]
        for block in (1, 3, 2, 0):
            put(block, dot_of(left, matrix_ref[:, block * width : (block + 1) * width], 1, 0))

    def stats(c, rows, branch):
        branch_ref[rows, :] = branch
        return sums_of(branch * branch)

    def finish(c, rows, branch, total):
        stat_ref[c] = total
        scale = lax.rsqrt(column_of(total, 0) / D + EPS)
        hidden = tokens_ref[rows, :].astype(F32) + gain_ref[0:1, :] * branch * scale
        hidden_ref[rows, :] = hidden
        return hidden.astype(BF)

    run_blocks(count, bufs, compute, stats, finish, own_ref, arrived)


VMEM_SPEC = pl.BlockSpec(memory_space=pltpu.VMEM)
ANY_SPEC = pl.BlockSpec(memory_space=pl.ANY)


def talk_params(number):
    return pltpu.CompilerParams(
        collective_id=number, has_side_effects=True, vmem_limit_bytes=63 * 2**20
    )


def branch_call(mixed, matrix, tokens, gain):
    rows, width = tokens.shape
    count = rows // BLOCK
    part = jax.ShapeDtypeStruct((rows, width), BF)
    whole = jax.ShapeDtypeStruct((rows, width), F32)
    return pl.pallas_call(
        branch_kernel,
        out_shape=[whole, whole, jax.ShapeDtypeStruct((count, 8, BLOCK), F32)] + [part] * 4,
        in_specs=[VMEM_SPEC] * 4,
        out_specs=[VMEM_SPEC] * 4 + [ANY_SPEC] * 3,
        scratch_shapes=exchange_scratch(count, width, True),
        compiler_params=talk_params(0),
        cost_estimate=cost_of(8 * rows * width * matrix.shape[0], 2**27),
        name="branch",
    )(mixed, matrix, tokens, gain)


def load_lefts(lefts, buffer, sems, count):
    width = buffer.shape[2] // 4

    def copies(c):
        slot = lax.rem(c, 2)
        rows = pl.ds(pl.multiple_of(c * BLOCK, BLOCK), BLOCK)
        return [
            pltpu.make_async_copy(
                left.at[rows], buffer.at[slot, :, index * width : (index + 1) * width], sems.at[slot, index]
            )
            for index, left in enumerate(lefts)
        ]

    def start(c):
        @pl.when(c < count)
        def _():
            for copy in copies(c):
                copy.start()

    def wait(c):
        for copy in copies(c):
            copy.wait()

    return start, wait


def move_rows(outer, buffer, sems, index, inward):
    def copy(c):
        slot = lax.rem(c, 2)
        rows = pl.ds(pl.multiple_of(c * BLOCK, BLOCK), BLOCK)
        ends = (outer.at[rows], buffer.at[slot])
        if not inward:
            ends = ends[::-1]
        return pltpu.make_async_copy(*ends, sems.at[index, slot])

    return copy


def forward_kernel(x0, x1, x2, x3, gate_hbm, upper_hbm, reduce_hbm, hidden_ref, cot_ref, gain_ref, *rest):
    act_out, gate_out, upper_out, layer_ref, own_ref, *rest = rest
    arrived, rest = rest[:3], rest[3:]
    gate_w, upper_w, reduce_w, lefts, act_buf, gate_buf, upper_buf, w_sem, x_sem, o_sem, *bufs = rest
    width = own_ref.shape[1]
    count = own_ref.shape[0] // BLOCK
    ff = gate_w.shape[1]
    tile = 512
    loads = [
        pltpu.make_async_copy(source, target, w_sem.at[index])
        for index, (source, target) in enumerate(
            ((gate_hbm, gate_w), (upper_hbm, upper_w), (reduce_hbm, reduce_w))
        )
    ]
    start_left, wait_left = load_lefts((x0, x1, x2, x3), lefts, x_sem, count)
    start_left(0)
    for load in loads:
        load.start()
    greet()
    outs = [
        move_rows(outer, buffer, o_sem, index, False)
        for index, (outer, buffer) in enumerate(
            ((act_out, act_buf), (gate_out, gate_buf), (upper_out, upper_buf))
        )
    ]

    def compute(c, put):
        slot = lax.rem(c, 2)
        wait_left(c)
        start_left(c + 1)

        @pl.when(c == 0)
        def _():
            for load in loads:
                load.wait()

        @pl.when(c >= 2)
        def _():
            for out in outs:
                out(c - 2).wait()

        def tiles(n, carry):
            at = pl.ds(pl.multiple_of(n * tile, tile), tile)
            left = lefts[slot]
            gate = dot_of(left, gate_w[:, at], 1, 0)
            upper = dot_of(left, upper_w[:, at], 1, 0)
            act_buf[slot, :, at] = (gate * jax.nn.sigmoid(gate) * upper).astype(BF)
            gate_buf[slot, :, at] = gate.astype(BF)
            upper_buf[slot, :, at] = upper.astype(BF)
            return carry

        lax.fori_loop(0, ff // tile, tiles, 0)
        for out in outs:
            out(c).start()
        for block in (1, 3, 2, 0):
            span = slice(block * width, (block + 1) * width)
            put(block, dot_of(act_buf[slot], reduce_w[:, span], 1, 0))

    def stats(c, rows, result):
        weighted = gain_ref[1:2, :] * cot_ref[rows, :].astype(F32)
        return sums_of(result * result, weighted * result)

    def finish(c, rows, result, total):
        scale = lax.rsqrt(column_of(total, 0) / D + EPS)
        gain = gain_ref[1:2, :]
        layer_ref[rows, :] = (hidden_ref[rows, :] + gain * result * scale).astype(BF)
        weighted = gain * cot_ref[rows, :].astype(F32)
        inner = column_of(total, 1)
        return (scale * weighted - result * (scale * scale * scale * inner / D)).astype(BF)

    run_blocks(count, bufs, compute, stats, finish, own_ref, arrived)
    for c in range(max(count - 2, 0), count):
        for out in outs:
            out(c).wait()


def forward_call(lefts, gate_w, upper_w, reduce_w, hidden, cotangent, gain):
    rows, width = hidden.shape
    count = rows // BLOCK
    ff = gate_w.shape[1]
    part = jax.ShapeDtypeStruct((rows, width), BF)
    wide = jax.ShapeDtypeStruct((rows, ff), BF)
    return pl.pallas_call(
        forward_kernel,
        out_shape=[wide] * 3 + [part] * 5,
        in_specs=[ANY_SPEC] * 7 + [VMEM_SPEC] * 3,
        out_specs=[ANY_SPEC] * 3 + [VMEM_SPEC] * 2 + [ANY_SPEC] * 3,
        scratch_shapes=[
            pltpu.VMEM(gate_w.shape, BF),
            pltpu.VMEM(upper_w.shape, BF),
            pltpu.VMEM(reduce_w.shape, BF),
            pltpu.VMEM((2, BLOCK, 4 * width), BF),
            pltpu.VMEM((2, BLOCK, ff), BF),
            pltpu.VMEM((2, BLOCK, ff), BF),
            pltpu.VMEM((2, BLOCK, ff), BF),
            pltpu.SemaphoreType.DMA((3,)),
            pltpu.SemaphoreType.DMA((2, 4)),
            pltpu.SemaphoreType.DMA((3, 2)),
        ]
        + exchange_scratch(count, width, True),
        compiler_params=talk_params(1),
        cost_estimate=cost_of(24 * rows * width * ff, 2**27),
        name="forward",
    )(*lefts, gate_w, upper_w, reduce_w, hidden, cotangent, gain)


def backward_kernel(
    x0, x1, x2, x3, gate_hbm, upper_hbm, reduce_hbm, gate_in, upper_in, cot_ref, branch_ref, stat_ref, gain_ref, *rest
):
    d_gate_out, d_upper_out, d_hidden_ref, own_ref, *rest = rest
    arrived, rest = rest[:3], rest[3:]
    gate_w, upper_w, reduce_w, lefts, gate_buf, upper_buf, d_gate_buf, d_upper_buf, *rest = rest
    w_sem, x_sem, i_sem, o_sem, *bufs = rest
    width = own_ref.shape[1]
    count = own_ref.shape[0] // BLOCK
    ff = gate_w.shape[1]
    tile = 512
    loads = [
        pltpu.make_async_copy(source, target, w_sem.at[index])
        for index, (source, target) in enumerate(
            ((reduce_hbm, reduce_w), (gate_hbm, gate_w), (upper_hbm, upper_w))
        )
    ]
    start_left, wait_left = load_lefts((x0, x1, x2, x3), lefts, x_sem, count)
    ins = [
        move_rows(outer, buffer, i_sem, index, True)
        for index, (outer, buffer) in enumerate(((gate_in, gate_buf), (upper_in, upper_buf)))
    ]
    outs = [
        move_rows(outer, buffer, o_sem, index, False)
        for index, (outer, buffer) in enumerate(
            ((d_gate_out, d_gate_buf), (d_upper_out, d_upper_buf))
        )
    ]
    start_left(0)
    for one in ins:
        one(0).start()
    for load in loads:
        load.start()
    greet()

    def compute(c, put):
        slot = lax.rem(c, 2)
        wait_left(c)
        start_left(c + 1)
        for one in ins:
            one(c).wait()

        @pl.when(c + 1 < count)
        def _():
            for one in ins:
                one(c + 1).start()

        @pl.when(c == 0)
        def _():
            for load in loads:
                load.wait()

        @pl.when(c >= 2)
        def _():
            for out in outs:
                out(c - 2).wait()

        def tiles(n, carry):
            at = pl.ds(pl.multiple_of(n * tile, tile), tile)
            d_act = dot_of(lefts[slot], reduce_w[at, :], 1, 1)
            gate = gate_buf[slot, :, at].astype(F32)
            sigma = jax.nn.sigmoid(gate)
            d_gate = d_act * upper_buf[slot, :, at].astype(F32) * (sigma * (1 + gate * (1 - sigma)))
            d_gate_buf[slot, :, at] = d_gate.astype(BF)
            d_upper_buf[slot, :, at] = (d_act * (gate * sigma)).astype(BF)
            return carry

        lax.fori_loop(0, ff // tile, tiles, 0)
        for out in outs:
            out(c).start()
        for block in (1, 3, 2, 0):
            span = slice(block * width, (block + 1) * width)
            put(
                block,
                dot_of(d_gate_buf[slot], gate_w[span, :], 1, 1)
                + dot_of(d_upper_buf[slot], upper_w[span, :], 1, 1),
            )

    def stats(c, rows, total):
        d_hidden = cot_ref[rows, :].astype(F32) + total
        d_hidden_ref[rows, :] = d_hidden
        return sums_of(gain_ref[0:1, :] * d_hidden * branch_ref[rows, :])

    def finish(c, rows, total, sums):
        scale = lax.rsqrt(column_of(stat_ref[c], 0) / D + EPS)
        weighted = gain_ref[0:1, :] * d_hidden_ref[rows, :]
        inner = column_of(sums, 0)
        back = scale * scale * scale * inner / D
        return (scale * weighted - branch_ref[rows, :] * back).astype(BF)

    run_blocks(count, bufs, compute, stats, finish, own_ref, arrived)
    for c in range(max(count - 2, 0), count):
        for out in outs:
            out(c).wait()


def backward_call(lefts, gate_w, upper_w, reduce_w, gate, upper, cotangent, branch, stats, gain):
    rows, width = branch.shape
    count = rows // BLOCK
    ff = gate_w.shape[1]
    part = jax.ShapeDtypeStruct((rows, width), BF)
    wide = jax.ShapeDtypeStruct((rows, ff), BF)
    return pl.pallas_call(
        backward_kernel,
        out_shape=[wide] * 2 + [jax.ShapeDtypeStruct((rows, width), F32)] + [part] * 4,
        in_specs=[ANY_SPEC] * 9 + [VMEM_SPEC] * 4,
        out_specs=[ANY_SPEC] * 2 + [VMEM_SPEC] * 2 + [ANY_SPEC] * 3,
        scratch_shapes=[
            pltpu.VMEM(gate_w.shape, BF),
            pltpu.VMEM(upper_w.shape, BF),
            pltpu.VMEM(reduce_w.shape, BF),
            pltpu.VMEM((2, BLOCK, 4 * width), BF),
            pltpu.VMEM((2, BLOCK, ff), BF),
            pltpu.VMEM((2, BLOCK, ff), BF),
            pltpu.VMEM((2, BLOCK, ff), BF),
            pltpu.VMEM((2, BLOCK, ff), BF),
            pltpu.SemaphoreType.DMA((3,)),
            pltpu.SemaphoreType.DMA((2, 4)),
            pltpu.SemaphoreType.DMA((2, 2)),
            pltpu.SemaphoreType.DMA((2, 2)),
        ]
        + exchange_scratch(count, width, True),
        compiler_params=talk_params(2),
        cost_estimate=cost_of(24 * rows * width * ff, 2**27),
        name="backward",
    )(*lefts, gate_w, upper_w, reduce_w, gate, upper, cotangent, branch, stats, gain)


def input_kernel(d_qkv_ref, matrix_ref, d_hidden_ref, out_ref, *bufs):
    width = out_ref.shape[1]
    count = out_ref.shape[0] // BLOCK
    greet()

    def compute(c, put):
        left = d_qkv_ref[pl.ds(pl.multiple_of(c * BLOCK, BLOCK), BLOCK), :]
        for block in (1, 3, 2, 0):
            put(block, dot_of(left, matrix_ref[block * width : (block + 1) * width, :], 1, 1))

    def finish(c, rows, total):
        out_ref[rows, :] = d_hidden_ref[rows, :] + total

    run_blocks(count, bufs, compute, None, finish)


def input_call(d_qkv, matrix, d_hidden):
    rows, width = d_hidden.shape
    return pl.pallas_call(
        input_kernel,
        out_shape=jax.ShapeDtypeStruct((rows, width), F32),
        in_specs=[VMEM_SPEC] * 3,
        out_specs=VMEM_SPEC,
        scratch_shapes=exchange_scratch(rows // BLOCK, width, False),
        compiler_params=talk_params(3),
        cost_estimate=cost_of(8 * rows * width * d_qkv.shape[1], 2**26),
        name="input_grad",
    )(d_qkv, matrix, d_hidden)


def across(values, step):
    return lax.ppermute(values, "row", [(i, i ^ step) for i in range(4)])


def gather_row(own):
    core = across(own, 1)
    side = across(own, 2)
    return [own, core, side, across(side, 1)]


def sum_row(values):
    values = values + across(values, 1)
    return values + across(values, 2)


def deal_row(piece_for, me):
    out = []
    for step in range(4):
        piece = piece_for(me ^ step)
        out.append(piece if step == 0 else across(piece, step))
    return jnp.stack(out)


def gather_col(values):
    return lax.all_gather(values, "col", axis=0, tiled=False)


def swap_pair(values):
    return lax.ppermute(values, "dp", [(0, 1), (1, 0)])


def round_col(values, cols):
    shift = lambda k: [(i, (i + k) % cols) for i in range(cols)]
    return [values] + [lax.ppermute(values, "col", shift(k)) for k in range(1, cols)]


def after(values, earlier):
    return lax.optimization_barrier((values, earlier))[0]


def join(parts, axis=0):
    return parts[0] if len(parts) == 1 else jnp.concatenate(parts, axis=axis)


def group_shards(
    tokens,
    cotangent,
    qkv_weight,
    attn_weight,
    expand_weight,
    reduce_weight,
    headnorm_gain,
    post_gain,
    qkv_lowrank,
    qkv_uprank,
    attn_lowrank,
    attn_uprank,
    expand_lowrank,
    expand_uprank,
    reduce_lowrank,
    reduce_uprank,
    prefix_length,
    adapter_set,
):
    cols = lax.axis_size("col")
    pair = lax.axis_index("dp")
    me = lax.axis_index("row")
    col = lax.axis_index("col")
    rows, width = tokens.shape
    sub = qkv_weight.shape[2] // 4
    ff = expand_weight.shape[2]
    ff_sub = ff // 4
    ff_half = ff_sub // 2
    local = cols * sub
    ff_local = cols * ff_sub
    sequence = pair * cols + col
    mine = lax.dynamic_index_in_dim(adapter_set, sequence, 0, keepdims=False)
    prefix = lax.dynamic_slice_in_dim(prefix_length, sequence, 1)
    cols_sets = lax.dynamic_slice_in_dim(adapter_set, pair * cols, cols)

    row_pack = row_pack_of(mine.reshape(1), qkv_lowrank, attn_uprank, expand_lowrank, reduce_uprank)
    row_all = jnp.concatenate(gather_row(row_pack), axis=1)
    qkv_low = row_all[:48]
    attn_up = row_all[48:64]
    expand_low = row_all[64:96]
    reduce_up = row_all[96:112]
    col_pack = col_pack_of(
        jnp.concatenate([cols_sets, me.reshape(1)]),
        qkv_uprank,
        attn_lowrank,
        expand_uprank,
        reduce_lowrank,
    )
    col_all = lax.all_to_all(col_pack, "col", split_axis=0, concat_axis=0, tiled=True)

    def own_columns(at, size):
        return col_all[:, :, at : at + size].transpose(1, 0, 2).reshape(16, cols * size)

    qkv_up = [own_columns(i * sub, sub) for i in range(3)]
    attn_low = own_columns(3 * sub, sub)
    expand_up = [own_columns(4 * sub + i * ff_sub, ff_sub) for i in range(2)]
    reduce_low = own_columns(4 * sub + 2 * ff_sub, ff_sub)
    gains = lax.dynamic_slice_in_dim(headnorm_gain, me * sub, sub, 1)
    gains = jnp.stack(round_col(gains, cols))
    gains = jnp.concatenate(
        [
            lax.dynamic_index_in_dim(gains, lax.rem(col - i + cols, cols), 0, keepdims=False)
            for i in range(cols)
        ],
        axis=1,
    )

    place = jnp.stack([pair, col])
    in_half = width // 2
    head_half = sub // 2

    def exchanged(own, other_piece):
        sent = jnp.stack(
            [
                lax.dynamic_index_in_dim(own, lax.rem(col + k, cols), 0, keepdims=False)
                for k in range(1, cols)
            ]
        )
        return jnp.concatenate([other_piece[None], swap_pair(sent)])

    def qkv_piece(half):
        return lambda row: lax.dynamic_slice(
            qkv_weight, (0, half * in_half, row * sub), (3, in_half, sub)
        )

    def attn_piece(half, earlier):
        return lambda row: after(
            lax.dynamic_slice_in_dim(attn_weight, row * sub + half * head_half, head_half, 0),
            earlier,
        )

    def expand_piece(part, half, earlier):
        return lambda row: after(
            lax.dynamic_slice(
                expand_weight[part], (0, row * ff_sub + half * ff_half), (width, ff_half)
            ),
            earlier,
        )

    step = rows // CHUNKS
    spans = [slice(i * step, (i + 1) * step) for i in range(CHUNKS)]
    qkv_own = deal_row(qkv_piece(pair), me)
    attn_own = deal_row(attn_piece(pair, qkv_own), me)
    gate_own = deal_row(expand_piece(0, pair, attn_own), me)
    qkv_rest = deal_row(lambda row: after(qkv_piece(1 - pair)(row), gate_own), me)
    token_parts = []
    for span in spans:
        token_parts.append(gather_row(after(tokens[span], qkv_rest)))
    last = token_parts[-1][3]
    up_own = deal_row(expand_piece(1, pair, last), me)
    attn_rest = deal_row(attn_piece(1 - pair, up_own), me)
    gate_rest = deal_row(expand_piece(0, 1 - pair, attn_rest), me)
    reduce_own = deal_row(
        lambda row: after(
            lax.dynamic_slice_in_dim(reduce_weight, row * ff_sub, ff_sub, 0), gate_rest
        ),
        me,
    )
    up_rest = deal_row(expand_piece(1, 1 - pair, reduce_own), me)
    qkv_all = gather_col(qkv_own)
    attn_all = gather_col(attn_own)
    gate_all = gather_col(gate_own)
    up_all = gather_col(up_own)
    reduce_all = gather_col(reduce_own)
    qkv_w = merge_qkv(
        place, qkv_all, exchanged(qkv_all, qkv_rest), qkv_low, jnp.concatenate(qkv_up)
    )
    attn_w = merge_out(place, [attn_all, exchanged(attn_all, attn_rest)], attn_low, attn_up)
    expand_w = [
        merge_expand(
            place, whole, exchanged(whole, rest), expand_low[16 * i : 16 * i + 16], expand_up[i]
        )
        for i, (whole, rest) in enumerate(((gate_all, gate_rest), (up_all, up_rest)))
    ]
    reduce_w = merge_out(place, [reduce_all], reduce_low, reduce_up)

    half = HEAD // 2
    freq = THETA ** (-2.0 * jnp.arange(half, dtype=F32) / HEAD)
    angle = jnp.arange(rows, dtype=jnp.int32).astype(F32)[:, None] * freq[None, :]
    cosine = jnp.concatenate([jnp.cos(angle)] * 2, axis=1)
    sine = jnp.sin(angle)
    sine = jnp.concatenate([-sine, sine], axis=1)
    raws, scales, turned, qkv_inner = [], [], [], []

    def low_of_parts(low, parts):
        return functools.reduce(
            jnp.add,
            [dot_of(low[:, i * width : (i + 1) * width], parts[i], 1, 1) for i in range(4)],
        )

    for span, parts in zip(spans, token_parts):
        qkv_inner.append(low_of_parts(qkv_low, parts).astype(BF))
        raw = project(parts, qkv_w, 0, F32)
        squares = jnp.stack(
            [jnp.sum(raw[:, i * local : (i + 1) * local] ** 2, axis=1) for i in range(2)]
        )
        scale = lax.rsqrt(sum_row(squares) / D + EPS).T
        raws.append(raw)
        scales.append(scale)
        turned.append(rotate_rows(after(raw, gate_all), scale, gains, cosine[span], sine[span]))
    key = join([part[1] for part in turned])
    value = join([part[2] for part in turned])

    query = join([part[0] for part in turned])
    mixed, log_total = attend(prefix, query, key, value, 0)
    mixed = after(mixed, up_all)
    branch, hidden, branch_stats, *hidden_parts = branch_call(mixed, attn_w, tokens, post_gain)
    act, gate, upper, layer_out, *result_parts = forward_call(
        hidden_parts, *expand_w, reduce_w, hidden, cotangent, post_gain
    )
    d_gate, d_upper, d_hidden, *branch_parts = backward_call(
        result_parts, *expand_w, reduce_w, gate, upper, cotangent, branch, branch_stats, post_gain
    )
    d_mixed = project(branch_parts, attn_w, 1, BF)
    d_query, d_key, d_value, q_sums, k_sums = attend_back(
        prefix, query, d_mixed, mixed, log_total, key, value
    )
    attn_inner = sum_row(dot_of(attn_low, mixed, 1, 1)).astype(BF)
    expand_inner = low_of_parts(expand_low, hidden_parts).astype(BF)
    reduce_inner = sum_row(dot_of(reduce_low, act, 1, 1)).astype(BF)
    g_reduce_up = ADAPTER_FACTOR * dot_of(reduce_inner, result_parts[0], 1, 0)
    d_inner = (ADAPTER_FACTOR * low_of_parts(reduce_up, result_parts)).astype(BF)
    g_reduce_low = dot_of(d_inner, act, 1, 0)
    g_gate_up = ADAPTER_FACTOR * dot_of(expand_inner[:16], d_gate, 1, 0)
    g_upper_up = ADAPTER_FACTOR * dot_of(expand_inner[16:], d_upper, 1, 0)
    d_inner = sum_row(
        ADAPTER_FACTOR
        * jnp.concatenate(
            [dot_of(expand_up[0], d_gate, 1, 1), dot_of(expand_up[1], d_upper, 1, 1)]
        )
    ).astype(BF)
    g_expand_low = dot_of(d_inner, hidden_parts[0], 1, 0)
    g_attn_up = ADAPTER_FACTOR * dot_of(attn_inner, branch_parts[0], 1, 0)
    d_inner = (ADAPTER_FACTOR * low_of_parts(attn_up, branch_parts)).astype(BF)
    g_attn_low = dot_of(d_inner, mixed, 1, 0)

    all_sums = sum_row(jnp.stack([jnp.sum(part[:, 0], axis=0) for part in (q_sums, k_sums)]))
    d_parts, g_low, g_up = [], [], []
    for index, span in enumerate(spans):
        scale = scales[index]
        d_qkv = unrotate_rows(
            raws[index],
            d_query,
            d_key,
            d_value,
            scale,
            scale * scale * all_sums[:, span].T / D,
            gains,
            cosine[span],
            sine[span],
            index * step,
        )
        d_parts.append(d_qkv)
    d_qkv = join(d_parts)
    input_grad = input_call(d_qkv, qkv_w, d_hidden)
    part = [d_qkv[:, i * local : (i + 1) * local] for i in range(3)]
    qkv_inner = join(qkv_inner, 1)
    g_qkv_up = [
        ADAPTER_FACTOR * dot_of(qkv_inner[16 * i : 16 * i + 16], part[i], 1, 0) for i in range(3)
    ]
    d_inner = sum_row(
        ADAPTER_FACTOR * jnp.concatenate([dot_of(qkv_up[i], part[i], 1, 1) for i in range(3)])
    ).astype(BF)
    g_qkv_low = dot_of(d_inner, tokens, 1, 0)

    def set_of(other, back):
        sequence = (pair ^ other) * cols + lax.rem(col - back + cols, cols)
        which = lax.dynamic_index_in_dim(adapter_set, sequence, 0, keepdims=False)
        return (jnp.arange(SETS, dtype=jnp.int32) == which).astype(F32)

    def to_sets(terms):
        shape = (SETS,) + (1,) * terms[0][1].ndim
        return functools.reduce(
            jnp.add, [hot.reshape(shape) * term.astype(F32)[None] for hot, term in terms]
        )

    def sum_groups(pack):
        pack = pack.astype(BF)
        both = jnp.stack([pack, swap_pair(pack)])
        terms = []
        for back, arrived in enumerate(round_col(both, cols)):
            terms += [(set_of(other, back), arrived[other]) for other in range(2)]
        return to_sets(terms)

    early = sum_groups(jnp.concatenate([g_attn_up, g_expand_low, g_reduce_up], axis=0))
    late = sum_groups(g_qkv_low)

    def by_col(grad):
        return grad.reshape(16, cols, -1).transpose(1, 0, 2)

    def sum_tokens(pack):
        dealt = lax.all_to_all(pack.astype(BF), "col", split_axis=0, concat_axis=0, tiled=True)
        every = jnp.stack(gather_row(dealt))
        other = swap_pair(every)
        terms = []
        for which in range(2):
            for index in range(cols):
                sequence = (pair ^ which) * cols + index
                chosen = lax.dynamic_index_in_dim(adapter_set, sequence, 0, keepdims=False)
                hot = (jnp.arange(SETS, dtype=jnp.int32) == chosen).astype(F32)
                terms.append((hot, (every, other)[which][:, index]))
        total = to_sets(terms)
        total = jnp.stack(
            [lax.dynamic_index_in_dim(total, me ^ row, 1, keepdims=False) for row in range(4)],
            axis=2,
        )
        return total

    early_col = sum_tokens(
        jnp.concatenate(
            [by_col(grad) for grad in (g_attn_low, g_gate_up, g_upper_up, g_reduce_low)],
            axis=2,
        )
    )
    late_col = sum_tokens(jnp.concatenate([by_col(grad) for grad in g_qkv_up], axis=2))

    def low_of(array):
        return array.transpose(0, 2, 1)

    def piece_of(array, at, size):
        return array[:, :, :, at : at + size].reshape(SETS, 16, 4 * size)

    return (
        layer_out,
        input_grad,
        jnp.stack([low_of(late[:, 16 * i : 16 * i + 16]) for i in range(3)]),
        jnp.stack([piece_of(late_col, i * sub, sub) for i in range(3)]),
        low_of(piece_of(early_col, 0, sub)),
        early[:, :16],
        jnp.stack([low_of(early[:, 16 + 16 * i : 32 + 16 * i]) for i in range(2)]),
        jnp.stack([piece_of(early_col, sub + i * ff_sub, ff_sub) for i in range(2)]),
        low_of(piece_of(early_col, sub + 2 * ff_sub, ff_sub)),
        early[:, 48:64],
    )


def shards(*arrays):
    whole = (
        lax.axis_size("dp") == 2
        and lax.axis_size("row") == 4
        and arrays[0].shape[0] == SEQUENCE_LENGTH
    )
    return group_shards(*arrays) if whole else general_shards(*arrays)


def solution(mesh):
    placed = (
        P(("dp", "col"), "row"),
        P(("dp", "col"), "row"),
        P(None, "row", "col"),
        P("col", "row"),
        P(None, "row", "col"),
        P("col", "row"),
        P(None, "col"),
        P(None, "row"),
        P(None, None, "row", None),
        P(None, None, None, "col"),
        P(None, "col", None),
        P(None, None, "row"),
        P(None, None, "row", None),
        P(None, None, None, "col"),
        P(None, "col", None),
        P(None, None, "row"),
        P(),
        P(),
    )
    return jax.shard_map(
        shards,
        mesh=mesh,
        in_specs=placed,
        out_specs=(
            P(("dp", "col"), "row"),
            P(("dp", "col"), "row"),
            P(None, None, "row", None),
            P(None, None, None, "col"),
            P(None, "col", None),
            P(None, None, "row"),
            P(None, None, "row", None),
            P(None, None, None, "col"),
            P(None, "col", None),
            P(None, None, "row"),
        ),
        check_vma=False,
    )
```

```python
import functools

import jax
import jax.numpy as jnp
from jax import lax
from jax.experimental import pallas as pl
from jax.experimental.pallas import tpu as pltpu
from jax.sharding import PartitionSpec as P

D = 2048
HEAD = 128
ADAPTER_RANK = 16
SETS = 8
SEQUENCE_LENGTH = 2048


EPS = 1e-06
THETA = 500000.0
ADAPTER_FACTOR = 0.5
NEG = -1e30


def via_col_row(input_rows, weight_matrix, adapt_mat, compute, seq_pick):
    gathered = lax.all_gather(input_rows, "col", axis=0, tiled=True)
    main, inner_value = compute(gathered, weight_matrix, adapt_mat, seq_pick, False)
    return (
        lax.psum_scatter(main, "row", scatter_dimension=0, tiled=True),
        lax.psum_scatter(inner_value, "row", scatter_dimension=0, tiled=True),
    )


def via_row_col(input_rows, weight_matrix, adapt_mat, compute, seq_pick):
    gathered = lax.all_gather(input_rows, "row", axis=0, tiled=True)
    main, inner_value = compute(gathered, weight_matrix, adapt_mat, seq_pick, False)
    return (
        lax.psum_scatter(main, "col", scatter_dimension=0, tiled=True),
        lax.psum_scatter(inner_value, "col", scatter_dimension=0, tiled=True),
    )


def row_total(values):
    return lax.psum(jnp.sum(values, axis=-1), "row")


def head_totals(first, second):
    return lax.psum((jnp.sum(first, axis=-1), jnp.sum(second, axis=-1)), "col")


def sum_col_tokens(values):
    return lax.psum(values.astype(jnp.bfloat16), ("dp", "col")).astype(jnp.float32)


def sum_row_tokens(values):
    return lax.psum(values.astype(jnp.bfloat16), ("dp", "row")).astype(jnp.float32)


def set_rows(group_sets, first_row, item_count):
    sequence = (first_row + jnp.arange(item_count, dtype=jnp.int32)) // SEQUENCE_LENGTH
    member = sequence[:, None] == jnp.arange(group_sets.shape[0], dtype=jnp.int32)[None, :]
    chosen = jnp.sum(jnp.where(member, group_sets[None, :], 0), axis=1)
    return (chosen[:, None] == jnp.arange(SETS, dtype=jnp.int32)[None, :]).astype(jnp.bfloat16)


def widen(inner_value, onehot, part_list):
    rows = inner_value.shape[0]
    spread = onehot[:, None, :, None] * inner_value.reshape(rows, part_list, 1, ADAPTER_RANK)
    return spread.reshape(rows, part_list, SETS * ADAPTER_RANK)


def adapter_in(gathered, pick, lowrank):
    part_list = lowrank.shape[0]
    width_in = lowrank.shape[2]
    item_count = pick.shape[0]
    chosen = jnp.einsum("sk,pkdr->sdpr", pick, lowrank, preferred_element_type=jnp.float32).astype(
        jnp.bfloat16
    )
    chosen = chosen.reshape(item_count, width_in, part_list * ADAPTER_RANK)
    product_value = jnp.einsum(
        "ehm,emx->ehx",
        gathered.reshape(item_count, SEQUENCE_LENGTH, width_in),
        chosen,
        preferred_element_type=jnp.float32,
    )
    return product_value.reshape(item_count * SEQUENCE_LENGTH, part_list * ADAPTER_RANK)


def adapter_back(gathered, pick, upward_rank):
    part_list = upward_rank.shape[0]
    width_out = upward_rank.shape[-1]
    item_count = pick.shape[0]
    chosen = jnp.einsum(
        "sk,pkre->sper", pick, upward_rank, preferred_element_type=jnp.float32
    ).astype(jnp.bfloat16)
    product_value = jnp.einsum(
        "slpe,sper->slpr",
        gathered.reshape(item_count, SEQUENCE_LENGTH, part_list, width_out),
        chosen,
        preferred_element_type=jnp.float32,
    )
    return ADAPTER_FACTOR * product_value.reshape(
        item_count * SEQUENCE_LENGTH, part_list * ADAPTER_RANK
    )


def adapter_out(wide_output, upward_rank):
    part_list = upward_rank.shape[0]
    flat_up = upward_rank.reshape(part_list, SETS * ADAPTER_RANK, upward_rank.shape[-1])
    return ADAPTER_FACTOR * jnp.einsum(
        "tpk,pke->tpe", wide_output, flat_up, preferred_element_type=jnp.float32
    )


def adapter_grad_in(wide_output, lowrank):
    part_list = lowrank.shape[0]
    width_in = lowrank.shape[2]
    flat_low = lowrank.transpose(0, 1, 3, 2).reshape(part_list, SETS * ADAPTER_RANK, width_in)
    return jnp.einsum("tpk,pkd->td", wide_output, flat_low, preferred_element_type=jnp.float32)


def up_grad(wide_output, gradient_list):
    part_list = gradient_list.shape[1]
    total_sum = ADAPTER_FACTOR * jnp.einsum(
        "jox,joq->oxq", wide_output, gradient_list, preferred_element_type=jnp.float32
    )
    return total_sum.reshape(part_list, SETS, ADAPTER_RANK, gradient_list.shape[2])


def low_grad(input_rows, wide_output):
    part_list = wide_output.shape[1]
    total_sum = jnp.einsum(
        "td,tpk->pkd", input_rows, wide_output, preferred_element_type=jnp.float32
    )
    return total_sum.reshape(part_list, SETS, ADAPTER_RANK, input_rows.shape[1]).transpose(
        0, 1, 3, 2
    )


def swiglu(gate, upper):
    return jax.nn.silu(gate) * upper


def norm_back(grad, values, scale, gain):
    weighted = gain * grad
    inner_sum = row_total(weighted * values)
    return scale[:, None] * weighted - values * (scale**3 * inner_sum / D)[:, None]


def qkv_forward(gathered, weight_matrix, low_flat, pick, per_row):
    input_rows = gathered[:, 0]
    main = jnp.einsum("td,pde->tpe", input_rows, weight_matrix, preferred_element_type=jnp.float32)
    lowrank = low_flat.reshape(3, SETS, low_flat.shape[1], ADAPTER_RANK)
    return (main, adapter_in(input_rows, pick, lowrank))


def expand_forward(gathered, weight_matrix, low_flat, pick, per_row):
    input_rows = gathered[:, 0]
    main = jnp.einsum("td,pdf->tpf", input_rows, weight_matrix, preferred_element_type=jnp.float32)
    lowrank = low_flat.reshape(2, SETS, low_flat.shape[1], ADAPTER_RANK)
    return (main, adapter_in(input_rows, pick, lowrank))


def single_forward(gathered, weight_matrix, low_four, pick, per_row):
    input_rows = gathered[:, 0]
    main = jnp.dot(input_rows, weight_matrix[0, 0], preferred_element_type=jnp.float32)
    return (main, adapter_in(input_rows, pick, low_four))


def single_backward(gathered, weight_matrix, up_flat, pick, per_row):
    main = jnp.einsum(
        "te,fe->tf", gathered[:, 0], weight_matrix, preferred_element_type=jnp.float32
    )
    upward_rank = up_flat.reshape(1, SETS, ADAPTER_RANK, up_flat.shape[1])
    return (main, adapter_back(gathered, pick, upward_rank))


def multi_backward(gathered, weight_matrix, up_flat, pick, per_row):
    part_list = weight_matrix.shape[0]
    main = jnp.einsum("tpf,pdf->td", gathered, weight_matrix, preferred_element_type=jnp.float32)
    upward_rank = up_flat.reshape(part_list, SETS, ADAPTER_RANK, up_flat.shape[2])
    return (main, adapter_back(gathered, pick, upward_rank))


def general_shards(
    tokens,
    cotangent,
    qkv_weight,
    attn_weight,
    expand_weight,
    reduce_weight,
    headnorm_gain,
    post_gain,
    qkv_lowrank,
    qkv_uprank,
    attn_lowrank,
    attn_uprank,
    expand_lowrank,
    expand_uprank,
    reduce_lowrank,
    reduce_uprank,
    prefix_length,
    adapter_set,
):
    rows_a = tokens.shape[0]
    group_rows = rows_a * lax.axis_size("col")
    rows_b = group_rows // lax.axis_size("row")
    group_seqs = group_rows // SEQUENCE_LENGTH
    group_first = lax.axis_index("dp") * group_seqs
    group_sets = lax.dynamic_slice_in_dim(adapter_set, group_first, group_seqs)
    group_prefix = lax.dynamic_slice_in_dim(prefix_length, group_first, group_seqs)
    seq_pick = (group_sets[:, None] == jnp.arange(SETS, dtype=jnp.int32)[None, :]).astype(
        jnp.bfloat16
    )
    pick_a = set_rows(group_sets, lax.axis_index("col") * rows_a, rows_a)
    pick_b = set_rows(group_sets, lax.axis_index("row") * rows_b, rows_b)
    width_row = qkv_weight.shape[1]
    width_col = qkv_weight.shape[2]
    ff_col = expand_weight.shape[2]
    qkv_low_flat = qkv_lowrank.reshape(3 * SETS, width_row, ADAPTER_RANK)
    projected, inner_value = via_col_row(
        tokens[:, None], qkv_weight, qkv_low_flat, qkv_forward, seq_pick
    )
    qkv_wide = widen(inner_value.astype(jnp.bfloat16), pick_b, 3)
    projected = projected + adapter_out(qkv_wide, qkv_uprank)
    queries = projected[:, 0]
    keys = projected[:, 1]
    values = projected[:, 2]
    query_sq, key_sq = head_totals(queries * queries, keys * keys)
    query_scale = lax.rsqrt(query_sq / D + EPS)
    key_scale = lax.rsqrt(key_sq / D + EPS)
    query_norm = queries * query_scale[:, None] * headnorm_gain[0]
    key_norm = keys * key_scale[:, None] * headnorm_gain[1]
    local_heads = queries.shape[1] // HEAD
    half = HEAD // 2
    freq = THETA ** (-2.0 * jnp.arange(half, dtype=jnp.float32) / HEAD)
    position = (jnp.arange(rows_b, dtype=jnp.int32) % SEQUENCE_LENGTH).astype(jnp.float32)
    angle = position[:, None] * freq[None, :]
    cosine = jnp.cos(angle)[:, None, :]
    sine = jnp.sin(angle)[:, None, :]

    def rotate(source):
        heads = source.reshape(rows_b, local_heads, HEAD)
        first = heads[..., :half]
        second = heads[..., half:]
        return jnp.concatenate(
            [first * cosine - second * sine, second * cosine + first * sine], axis=-1
        )

    def unrotate(gradient_list):
        first = gradient_list[..., :half]
        second = gradient_list[..., half:]
        return jnp.concatenate(
            [first * cosine + second * sine, second * cosine - first * sine], axis=-1
        ).reshape(rows_b, local_heads * HEAD)

    query_b = rotate(query_norm).astype(jnp.bfloat16)
    key_b = rotate(key_norm).astype(jnp.bfloat16)
    value_b = values.astype(jnp.bfloat16).reshape(rows_b, local_heads, HEAD)
    block = min(512, SEQUENCE_LENGTH)
    blocks = rows_b // block
    key_pos = jnp.arange(SEQUENCE_LENGTH, dtype=jnp.int32)
    local_first = lax.axis_index("row") * (rows_b // SEQUENCE_LENGTH)
    scale = HEAD ** (-0.5)

    def scores_of(index):
        start = index * block
        seq_start = start // SEQUENCE_LENGTH * SEQUENCE_LENGTH
        which = local_first + start // SEQUENCE_LENGTH
        prefix = jnp.sum(
            jnp.where(jnp.arange(group_seqs, dtype=jnp.int32) == which, group_prefix, 0)
        )
        rows = start - seq_start + jnp.arange(block, dtype=jnp.int32)
        allowed = (key_pos[None, :] <= rows[:, None]) | (key_pos[None, :] < prefix)
        query_blk = lax.dynamic_slice_in_dim(query_b, start, block, 0)
        raw = (
            jnp.einsum("qhd,khd->hqk", query_blk, key_b, preferred_element_type=jnp.float32) * scale
        )
        return (jnp.where(allowed[None], raw, NEG), start, seq_start)

    def attend_block(index):
        scores, start, seq_start = scores_of(index)
        top = jnp.max(scores, axis=-1, keepdims=True)
        powers = jnp.exp(scores - top)
        total_sum = jnp.sum(powers, axis=-1, keepdims=True)
        weights = (powers / total_sum).astype(jnp.bfloat16)
        output = jnp.einsum("hqk,khd->qhd", weights, value_b, preferred_element_type=jnp.float32)
        return (output, (top + jnp.log(total_sum))[..., 0])

    attended, logsum = lax.map(attend_block, jnp.arange(blocks, dtype=jnp.int32))
    mixed_b = attended.reshape(rows_b, local_heads * HEAD).astype(jnp.bfloat16)
    attn_weight_four = attn_weight.reshape(1, 1, width_col, width_row)
    attn_low_four = attn_lowrank.reshape(1, SETS, width_col, ADAPTER_RANK)
    branch, inner_value = via_row_col(
        mixed_b[:, None], attn_weight_four, attn_low_four, single_forward, seq_pick
    )
    attn_wide = widen(inner_value.astype(jnp.bfloat16), pick_a, 1)
    branch = branch + adapter_out(attn_wide, attn_uprank[None])[:, 0]
    branch_scale = lax.rsqrt(row_total(branch * branch) / D + EPS)
    hidden = tokens.astype(jnp.float32) + post_gain[0] * branch * branch_scale[:, None]
    hidden_b = hidden.astype(jnp.bfloat16)
    expand_low_flat = expand_lowrank.reshape(2 * SETS, width_row, ADAPTER_RANK)
    gate_up, inner_value = via_col_row(
        hidden_b[:, None], expand_weight, expand_low_flat, expand_forward, seq_pick
    )
    expand_wide = widen(inner_value.astype(jnp.bfloat16), pick_b, 2)
    gate_up = gate_up + adapter_out(expand_wide, expand_uprank)
    gate = gate_up[:, 0]
    upper = gate_up[:, 1]
    act_b = swiglu(gate, upper).astype(jnp.bfloat16)
    reduce_weight_four = reduce_weight.reshape(1, 1, ff_col, width_row)
    reduce_low_four = reduce_lowrank.reshape(1, SETS, ff_col, ADAPTER_RANK)
    result, inner_value = via_row_col(
        act_b[:, None], reduce_weight_four, reduce_low_four, single_forward, seq_pick
    )
    reduce_wide = widen(inner_value.astype(jnp.bfloat16), pick_a, 1)
    result = result + adapter_out(reduce_wide, reduce_uprank[None])[:, 0]
    result_scale = lax.rsqrt(row_total(result * result) / D + EPS)
    layer_out = (hidden + post_gain[1] * result * result_scale[:, None]).astype(jnp.bfloat16)
    incoming = cotangent.astype(jnp.float32)
    d_result = norm_back(incoming, result, result_scale, post_gain[1]).astype(jnp.bfloat16)
    grad_reduce_up = up_grad(reduce_wide, d_result[:, None])[0]
    grad_reduce_up = sum_col_tokens(grad_reduce_up)
    reduce_up_flat = reduce_uprank.reshape(SETS * ADAPTER_RANK, width_row)
    d_act, inner_value = via_col_row(
        d_result[:, None], reduce_weight, reduce_up_flat, single_backward, seq_pick
    )
    act_wide = widen(inner_value.astype(jnp.bfloat16), pick_b, 1)
    d_act = d_act + adapter_grad_in(act_wide, reduce_lowrank[None])
    grad_reduce_low = low_grad(act_b, act_wide)[0]
    grad_reduce_low = sum_row_tokens(grad_reduce_low)
    unused, pullback = jax.vjp(swiglu, gate, upper)
    d_gate, d_upper = pullback(d_act)
    d_gate_up = jnp.stack([d_gate, d_upper], axis=1).astype(jnp.bfloat16)
    grad_expand_up = up_grad(expand_wide, d_gate_up)
    grad_expand_up = sum_row_tokens(grad_expand_up)
    expand_up_flat = expand_uprank.reshape(2 * SETS, ADAPTER_RANK, ff_col)
    d_hidden_in, inner_value = via_row_col(
        d_gate_up, expand_weight, expand_up_flat, multi_backward, seq_pick
    )
    hidden_wide = widen(inner_value.astype(jnp.bfloat16), pick_a, 2)
    d_hidden = incoming + d_hidden_in + adapter_grad_in(hidden_wide, expand_lowrank)
    grad_expand_low = low_grad(hidden_b, hidden_wide)
    grad_expand_low = sum_col_tokens(grad_expand_low)
    d_branch = norm_back(d_hidden, branch, branch_scale, post_gain[0]).astype(jnp.bfloat16)
    grad_attn_up = up_grad(attn_wide, d_branch[:, None])[0]
    grad_attn_up = sum_col_tokens(grad_attn_up)
    attn_up_flat = attn_uprank.reshape(SETS * ADAPTER_RANK, width_row)
    d_mixed, inner_value = via_col_row(
        d_branch[:, None], attn_weight, attn_up_flat, single_backward, seq_pick
    )
    mixed_wide = widen(inner_value.astype(jnp.bfloat16), pick_b, 1)
    d_mixed = (d_mixed + adapter_grad_in(mixed_wide, attn_lowrank[None])).astype(jnp.bfloat16)
    grad_attn_low = low_grad(mixed_b, mixed_wide)[0]
    grad_attn_low = sum_row_tokens(grad_attn_low)
    d_mixed_heads = d_mixed.reshape(rows_b, local_heads, HEAD)

    def back_block(index, carry):
        d_query, d_key, d_value = carry
        scores, start, seq_start = scores_of(index)
        probs = jnp.exp(
            scores - lax.dynamic_index_in_dim(logsum, index, 0, keepdims=False)[..., None]
        )
        grad_blk = lax.dynamic_slice_in_dim(d_mixed_heads, start, block, 0)
        query_blk = lax.dynamic_slice_in_dim(query_b, start, block, 0)
        d_probs = jnp.einsum("qhd,khd->hqk", grad_blk, value_b, preferred_element_type=jnp.float32)
        delta = jnp.sum(probs * d_probs, axis=-1, keepdims=True)
        d_scores = (probs * (d_probs - delta)).astype(jnp.bfloat16)
        query_part = scale * jnp.einsum(
            "hqk,khd->qhd", d_scores, key_b, preferred_element_type=jnp.float32
        )
        key_part = scale * jnp.einsum(
            "hqk,qhd->khd", d_scores, query_blk, preferred_element_type=jnp.float32
        )
        value_part = jnp.einsum(
            "hqk,qhd->khd", probs.astype(jnp.bfloat16), grad_blk, preferred_element_type=jnp.float32
        )
        d_query = lax.dynamic_update_slice_in_dim(d_query, query_part, start, 0)
        d_key = d_key + key_part
        d_value = d_value + value_part
        return (d_query, d_key, d_value)

    zeros = jnp.zeros((rows_b, local_heads, HEAD), jnp.float32)
    d_query, d_key, d_value = lax.fori_loop(0, blocks, back_block, (zeros, zeros, zeros))
    query_weighted = headnorm_gain[0] * unrotate(d_query)
    key_weighted = headnorm_gain[1] * unrotate(d_key)
    query_sum, key_sum = head_totals(query_weighted * queries, key_weighted * keys)
    d_queries = (
        query_scale[:, None] * query_weighted - queries * (query_scale**3 * query_sum / D)[:, None]
    )
    d_keys = key_scale[:, None] * key_weighted - keys * (key_scale**3 * key_sum / D)[:, None]
    d_qkv = jnp.stack(
        [d_queries, d_keys, d_value.reshape(rows_b, local_heads * HEAD)], axis=1
    ).astype(jnp.bfloat16)
    grad_qkv_up = up_grad(qkv_wide, d_qkv)
    grad_qkv_up = sum_row_tokens(grad_qkv_up)
    qkv_up_flat = qkv_uprank.reshape(3 * SETS, ADAPTER_RANK, width_col)
    d_tokens_in, inner_value = via_row_col(d_qkv, qkv_weight, qkv_up_flat, multi_backward, seq_pick)
    tokens_wide = widen(inner_value.astype(jnp.bfloat16), pick_a, 3)
    input_grad = d_hidden + d_tokens_in + adapter_grad_in(tokens_wide, qkv_lowrank)
    grad_qkv_low = low_grad(tokens, tokens_wide)
    grad_qkv_low = sum_col_tokens(grad_qkv_low)
    return (
        layer_out,
        input_grad,
        grad_qkv_low,
        grad_qkv_up,
        grad_attn_low,
        grad_attn_up,
        grad_expand_low,
        grad_expand_up,
        grad_reduce_low,
        grad_reduce_up,
    )


LOG2E = 1.4426950408889634
Q_BLOCK = 512
K_BLOCK = 512
BF = jnp.bfloat16
F32 = jnp.float32


def dot_of(left, right, left_dim, right_dim, out=F32):
    return lax.dot_general(
        left, right, (((left_dim,), (right_dim,)), ((), ())), preferred_element_type=out
    )


def attend_kernel(prefix_ref, q_ref, k_ref, v_ref, out_ref, log_ref, *, first):
    rows = q_ref.shape[0]
    start = first + pl.program_id(1) * rows
    prefix = prefix_ref[0]
    blocks = lax.div(jnp.maximum(start + rows, prefix) + K_BLOCK - 1, K_BLOCK)
    query = q_ref[...]
    limit = jnp.maximum(lax.broadcasted_iota(jnp.int32, (1, rows), 1) + start, prefix - 1)
    key_pos = lax.broadcasted_iota(jnp.int32, (K_BLOCK, rows), 0)

    def body(index, carry):
        top, total, mixed = carry
        at = pl.multiple_of(index * K_BLOCK, K_BLOCK)
        scores = dot_of(k_ref[pl.ds(at, K_BLOCK), :], query, 1, 1) * (HEAD**-0.5 * LOG2E)
        scores = jnp.where(key_pos <= limit - at, scores, NEG)
        top_now = jnp.maximum(top, jnp.max(scores, axis=0, keepdims=True))
        fade = jnp.exp2(top - top_now)
        powers = jnp.exp2(scores - top_now)
        total = fade * total + jnp.sum(powers, axis=0, keepdims=True)
        mixed = mixed * fade + dot_of(v_ref[pl.ds(at, K_BLOCK), :], powers.astype(BF), 0, 0)
        return top_now, total, mixed

    top, total, mixed = lax.fori_loop(
        0,
        blocks,
        body,
        (
            jnp.full((1, rows), NEG, F32),
            jnp.zeros((1, rows), F32),
            jnp.zeros((HEAD, rows), F32),
        ),
    )
    out_ref[...] = (mixed / total).T.astype(BF)
    log_ref[0] = top + jnp.log2(total)


def attend(prefix, query, key, value, first):
    rows, length, heads = query.shape[0], key.shape[0], query.shape[1] // HEAD
    q_spec = pl.BlockSpec((Q_BLOCK, HEAD), lambda h, i, p: (i, h))
    k_spec = pl.BlockSpec((length, HEAD), lambda h, i, p: (0, h))
    return pl.pallas_call(
        functools.partial(attend_kernel, first=first),
        out_shape=(
            jax.ShapeDtypeStruct(query.shape, BF),
            jax.ShapeDtypeStruct((heads, 1, rows), F32),
        ),
        grid_spec=pltpu.PrefetchScalarGridSpec(
            num_scalar_prefetch=1,
            grid=(heads, rows // Q_BLOCK),
            in_specs=[q_spec, k_spec, k_spec],
            out_specs=[q_spec, pl.BlockSpec((1, 1, Q_BLOCK), lambda h, i, p: (h, 0, i))],
        ),
        cost_estimate=pl.CostEstimate(
            flops=3 * rows * length * heads * HEAD,
            bytes_accessed=8 * rows * heads * HEAD,
            transcendentals=rows * length * heads,
        ),
        name="attend",
    )(prefix, query, key, value)


def row_sums(values):
    return lax.dot_general(
        jnp.ones((8, values.shape[1]), F32),
        values,
        (((1,), (1,)), ((), ())),
        precision=lax.Precision.HIGHEST,
        preferred_element_type=F32,
    )[0:1]


def attend_back_kernel(
    prefix_ref,
    q_ref,
    grad_ref,
    out_ref,
    log_ref,
    k_ref,
    v_ref,
    dq_ref,
    dk_ref,
    dv_ref,
    q_sum_ref,
    k_sum_ref,
):
    rows = q_ref.shape[0]
    start = pl.program_id(1) * rows
    prefix = prefix_ref[0]
    blocks = lax.div(jnp.maximum(start + rows, prefix) + K_BLOCK - 1, K_BLOCK)

    @pl.when(pl.program_id(1) == 0)
    def _():
        dk_ref[...] = jnp.zeros_like(dk_ref)
        dv_ref[...] = jnp.zeros_like(dv_ref)

    query = q_ref[...]
    grad = grad_ref[...]
    limit = jnp.maximum(lax.broadcasted_iota(jnp.int32, (1, rows), 1) + start, prefix - 1)
    key_pos = lax.broadcasted_iota(jnp.int32, (K_BLOCK, rows), 0)
    log_total = log_ref[0]
    delta = row_sums(grad.astype(F32) * out_ref[...].astype(F32))

    def body(index, d_query):
        at = pl.multiple_of(index * K_BLOCK, K_BLOCK)
        span = pl.ds(at, K_BLOCK)
        key = k_ref[span, :]
        scores = dot_of(key, query, 1, 1) * (HEAD**-0.5 * LOG2E)
        probs = jnp.where(key_pos <= limit - at, jnp.exp2(scores - log_total), 0.0)
        d_probs = dot_of(v_ref[span, :], grad, 1, 1)
        d_scores = (probs * (d_probs - delta)).astype(BF)
        dv_ref[span, :] += dot_of(probs.astype(BF), grad, 1, 0)
        dk_ref[span, :] += dot_of(d_scores, query, 1, 0)
        return d_query + dot_of(d_scores, key, 0, 0)

    d_query = lax.fori_loop(0, blocks, body, jnp.zeros((rows, HEAD), F32)) * HEAD**-0.5
    dq_ref[...] = d_query
    q_sum_ref[0] = row_sums(d_query * query.astype(F32))

    @pl.when(pl.program_id(1) == pl.num_programs(1) - 1)
    def _():
        d_key = dk_ref[...] * HEAD**-0.5
        dk_ref[...] = d_key
        k_sum_ref[0] = row_sums(d_key * k_ref[...].astype(F32))


def attend_back(prefix, query, grad, mixed, log_total, key, value):
    rows, length, heads = query.shape[0], key.shape[0], query.shape[1] // HEAD
    q_spec = pl.BlockSpec((Q_BLOCK, HEAD), lambda h, i, p: (i, h))
    k_spec = pl.BlockSpec((length, HEAD), lambda h, i, p: (0, h))
    return pl.pallas_call(
        attend_back_kernel,
        out_shape=(
            jax.ShapeDtypeStruct(query.shape, F32),
            jax.ShapeDtypeStruct(key.shape, F32),
            jax.ShapeDtypeStruct(key.shape, F32),
            jax.ShapeDtypeStruct((heads, 1, rows), F32),
            jax.ShapeDtypeStruct((heads, 1, length), F32),
        ),
        grid_spec=pltpu.PrefetchScalarGridSpec(
            num_scalar_prefetch=1,
            grid=(heads, rows // Q_BLOCK),
            in_specs=[
                q_spec,
                q_spec,
                q_spec,
                pl.BlockSpec((1, 1, Q_BLOCK), lambda h, i, p: (h, 0, i)),
                k_spec,
                k_spec,
            ],
            out_specs=[
                q_spec,
                k_spec,
                k_spec,
                pl.BlockSpec((1, 1, Q_BLOCK), lambda h, i, p: (h, 0, i)),
                pl.BlockSpec((1, 1, length), lambda h, i, p: (h, 0, 0)),
            ],
        ),
        cost_estimate=pl.CostEstimate(
            flops=7 * rows * length * heads * HEAD,
            bytes_accessed=24 * rows * heads * HEAD,
            transcendentals=rows * length * heads,
        ),
        name="attend_back",
    )(prefix, query, grad, mixed, log_total, key, value)


def rotate_kernel(raw_ref, scale_ref, gain_ref, cos_ref, sin_ref, q_ref, k_ref, v_ref):
    width = q_ref.shape[1]
    cosine = cos_ref[...]
    sine = sin_ref[...]
    for part, out in ((0, q_ref), (1, k_ref)):
        scale = scale_ref[:, part : part + 1]
        for at in range(0, width, HEAD):
            normed = raw_ref[:, part * width + at : part * width + at + HEAD] * scale
            normed = normed * gain_ref[part : part + 1, at : at + HEAD]
            turned = normed * cosine + pltpu.roll(normed, HEAD // 2, 1) * sine
            out[:, at : at + HEAD] = turned.astype(BF)
    v_ref[...] = raw_ref[:, 2 * width :].astype(BF)


def rotate_rows(raw, scales, gains, cosine, sine):
    rows, width = raw.shape[0], raw.shape[1] // 3
    step = min(512, rows)
    out_spec = pl.BlockSpec((step, width), lambda i: (i, 0))
    table = pl.BlockSpec((step, HEAD), lambda i: (i, 0))
    return pl.pallas_call(
        rotate_kernel,
        out_shape=(jax.ShapeDtypeStruct((rows, width), BF),) * 3,
        grid=(rows // step,),
        in_specs=[
            pl.BlockSpec((step, 3 * width), lambda i: (i, 0)),
            pl.BlockSpec((step, 2), lambda i: (i, 0)),
            pl.BlockSpec((2, width), lambda i: (0, 0)),
            table,
            table,
        ],
        out_specs=[out_spec] * 3,
        name="rotate_rows",
    )(raw, scales, gains, cosine, sine)


def row_pack_kernel(set_ref, qkv_ref, attn_ref, expand_ref, reduce_ref, out_ref):
    for part in range(3):
        out_ref[16 * part : 16 * part + 16, :] = qkv_ref[part, 0]
    out_ref[48:64, :] = attn_ref[0]
    for part in range(2):
        out_ref[64 + 16 * part : 80 + 16 * part, :] = expand_ref[part, 0]
    out_ref[96:112, :] = reduce_ref[0]


def row_pack_of(which, qkv_low, attn_up, expand_low, reduce_up):
    width = attn_up.shape[2]
    one = pl.BlockSpec((1, 16, width), lambda i, c: (c[0], 0, 0))

    def many(parts):
        return pl.BlockSpec((parts, 1, 16, width), lambda i, c: (0, c[0], 0, 0))

    return pl.pallas_call(
        row_pack_kernel,
        out_shape=jax.ShapeDtypeStruct((112, width), BF),
        grid_spec=pltpu.PrefetchScalarGridSpec(
            num_scalar_prefetch=1,
            grid=(1,),
            in_specs=[many(3), one, many(2), one],
            out_specs=pl.BlockSpec((112, width), lambda i, c: (0, 0)),
        ),
        name="row_pack",
    )(which, qkv_low, attn_up, expand_low, reduce_up)


def col_pack_kernel(set_ref, qkv_ref, attn_ref, expand_ref, reduce_ref, out_ref):
    sub, ff_sub = qkv_ref.shape[3], expand_ref.shape[3]
    for part in range(3):
        out_ref[0, :, part * sub : (part + 1) * sub] = qkv_ref[part, 0]
    at = 4 * sub
    out_ref[0, :, 3 * sub : at] = attn_ref[0]
    for part in range(2):
        out_ref[0, :, at : at + ff_sub] = expand_ref[part, 0]
        at += ff_sub
    out_ref[0, :, at:] = reduce_ref[0]


def col_pack_of(which, qkv_up, attn_low, expand_up, reduce_low):
    cols = which.shape[0] - 1
    sub, ff_sub = qkv_up.shape[3] // 4, expand_up.shape[3] // 4

    def many(parts, size):
        return pl.BlockSpec((parts, 1, 16, size), lambda i, c: (0, c[i], 0, c[cols]))

    def one(size):
        return pl.BlockSpec((1, 16, size), lambda i, c: (c[i], 0, c[cols]))

    total = 4 * sub + 3 * ff_sub
    return pl.pallas_call(
        col_pack_kernel,
        out_shape=jax.ShapeDtypeStruct((cols, 16, total), BF),
        grid_spec=pltpu.PrefetchScalarGridSpec(
            num_scalar_prefetch=1,
            grid=(cols,),
            in_specs=[many(3, sub), one(sub), many(2, ff_sub), one(ff_sub)],
            out_specs=pl.BlockSpec((1, 16, total), lambda i, c: (i, 0, 0)),
        ),
        name="col_pack",
    )(which, qkv_up, attn_low, expand_up, reduce_low)


def finish_kernel(ids_ref, rows_ref, cols_ref, *outs):
    qkv_low, qkv_up, attn_low, attn_up, expand_low, expand_up, reduce_low, reduce_up = outs
    cols = cols_ref.shape[2]
    groups = 2 * cols
    here = pl.program_id(0)
    me = ids_ref[2 * groups]

    def weight(index):
        return (ids_ref[index] == here).astype(F32)

    total = jnp.zeros(rows_ref.shape[2:], F32)
    for k in range(cols):
        for other in range(2):
            total = total + weight(2 * k + other) * rows_ref[k, other].astype(F32)
    for part in range(3):
        qkv_low[part, 0] = total[16 * part : 16 * part + 16]
    attn_up[0] = total[48:64]
    for part in range(2):
        expand_low[part, 0] = total[64 + 16 * part : 80 + 16 * part]
    reduce_up[0] = total[96:112]
    sub = qkv_up.shape[3] // 4
    ff_sub = expand_up.shape[3] // 4
    for row in range(4):
        block = me ^ row
        total = jnp.zeros(cols_ref.shape[3:], F32)
        for other in range(2):
            for index in range(cols):
                one = cols_ref[block, other, index].astype(F32)
                total = total + weight(groups + other * cols + index) * one
        near = slice(row * sub, (row + 1) * sub)
        wide = slice(row * ff_sub, (row + 1) * ff_sub)
        for part in range(3):
            qkv_up[part, 0, :, near] = total[:, part * sub : (part + 1) * sub]
        attn_low[0, :, near] = total[:, 3 * sub : 4 * sub]
        for part in range(2):
            at = 4 * sub + part * ff_sub
            expand_up[part, 0, :, wide] = total[:, at : at + ff_sub]
        reduce_low[0, :, wide] = total[:, 4 * sub + 2 * ff_sub :]


def finish_call(ids, rows, cols, sub, ff_sub):
    width = rows.shape[3]
    shapes = [
        (3, width),
        (3, 4 * sub),
        (0, 4 * sub),
        (0, width),
        (2, width),
        (2, 4 * ff_sub),
        (0, 4 * ff_sub),
        (0, width),
    ]
    out_shape, out_specs = [], []
    for parts, size in shapes:
        if parts:
            out_shape.append(jax.ShapeDtypeStruct((parts, SETS, 16, size), F32))
            out_specs.append(pl.BlockSpec((parts, 1, 16, size), lambda k, c: (0, k, 0, 0)))
        else:
            out_shape.append(jax.ShapeDtypeStruct((SETS, 16, size), F32))
            out_specs.append(pl.BlockSpec((1, 16, size), lambda k, c: (k, 0, 0)))

    def whole(array):
        return pl.BlockSpec(array.shape, lambda k, c: (0,) * array.ndim)

    return pl.pallas_call(
        finish_kernel,
        out_shape=out_shape,
        grid_spec=pltpu.PrefetchScalarGridSpec(
            num_scalar_prefetch=1,
            grid=(SETS,),
            in_specs=[whole(rows), whole(cols)],
            out_specs=out_specs,
        ),
        name="finish",
    )(ids, rows, cols)


def cost_of(flops, bytes_accessed):
    return pl.CostEstimate(flops=int(flops), bytes_accessed=int(bytes_accessed), transcendentals=0)


def row_tile(rows):
    return min(512, rows)


def merge_rows_kernel(pair_ref, own_ref, other_ref, low_ref, up_ref, out_ref):
    def put(piece):
        for block in range(4):
            base = piece[0, block].astype(F32)
            extra = dot_of(low_ref[block, 0], up_ref[...], 0, 0)
            out_ref[block, 0] = (base + ADAPTER_FACTOR * extra).astype(BF)

    mine = pl.program_id(0) == pair_ref[0]
    pl.when(mine)(functools.partial(put, own_ref))
    pl.when(jnp.logical_not(mine))(functools.partial(put, other_ref))


def merge_qkv_kernel(pair_ref, own_ref, other_ref, low_ref, up_ref, out_ref):
    cols, sub = own_ref.shape[0], own_ref.shape[4]

    def put(piece, back):
        for block in range(4):
            extra = dot_of(low_ref[block, 0], up_ref[...], 0, 0)
            for index in range(cols):
                at = lax.rem(index - back + cols, cols)
                lanes = slice(index * sub, (index + 1) * sub)
                base = piece[at, block, 0].astype(F32)
                out_ref[block, 0, :, lanes] = (base + ADAPTER_FACTOR * extra[:, lanes]).astype(BF)

    mine = pl.program_id(0) == pair_ref[0]
    pl.when(mine)(functools.partial(put, own_ref, 0))
    pl.when(jnp.logical_not(mine))(functools.partial(put, other_ref, pair_ref[1]))


def merge_columns_kernel(pair_ref, *refs):
    *pieces, low_ref, up_ref, out_ref = refs
    width = out_ref.shape[1] // 4

    def put(piece):
        for block in range(4):
            span = slice(block * width, (block + 1) * width)
            extra = dot_of(low_ref[0], up_ref[:, span], 0, 0)
            out_ref[:, span] = (piece[0, block].astype(F32) + ADAPTER_FACTOR * extra).astype(BF)

    if len(pieces) == 1:
        put(pieces[0])
        return
    mine = pl.program_id(0) == pair_ref[0]
    pl.when(mine)(functools.partial(put, pieces[0]))
    pl.when(jnp.logical_not(mine))(functools.partial(put, pieces[1]))


def merge_qkv(pair, own, other, low, up):
    cols, _, parts, cut, sub = own.shape

    def piece(half):
        def place(h, p, pair_ref):
            mine = h == half(pair_ref[0])
            return (0, 0, jnp.where(mine, p, jnp.where(h == 0, 0, parts - 1)), 0, 0)

        return pl.BlockSpec((cols, 4, 1, cut, sub), place)

    whole = pl.pallas_call(
        merge_qkv_kernel,
        out_shape=jax.ShapeDtypeStruct((4, 2, cut, parts * cols * sub), BF),
        grid_spec=pltpu.PrefetchScalarGridSpec(
            num_scalar_prefetch=1,
            grid=(2, parts),
            in_specs=[
                piece(lambda one: one),
                piece(lambda one: 1 - one),
                pl.BlockSpec((4, 1, 16, cut), lambda h, p, one: (0, h, p, 0)),
                pl.BlockSpec((16, cols * sub), lambda h, p, one: (p, 0)),
            ],
            out_specs=pl.BlockSpec((4, 1, cut, cols * sub), lambda h, p, one: (0, h, 0, p)),
        ),
        cost_estimate=cost_of(0, 8 * own.size),
        name="merge_qkv",
    )(pair, own, other, low.reshape(16 * parts, 4, 2, cut).transpose(1, 2, 0, 3), up)
    return whole.reshape(8 * cut, parts * cols * sub)


def half_specs(block, cols):
    def piece(half, relative):
        def place(h, c, pair_ref):
            at = jnp.where(h == half(pair_ref[0]), c, jnp.where(h == 0, 0, cols - 1))
            if relative:
                at = lax.rem(at - pair_ref[1] + cols, cols)
            return (at,) + (0,) * (len(block) - 1)

        return pl.BlockSpec(block, place)

    return [piece(lambda one: one, False), piece(lambda one: 1 - one, True)]


def merge_expand(pair, own, other, low, up):
    cols, _, width, cut = own.shape
    whole = pl.pallas_call(
        merge_rows_kernel,
        out_shape=jax.ShapeDtypeStruct((4, 1, width, 2 * cols * cut), BF),
        grid_spec=pltpu.PrefetchScalarGridSpec(
            num_scalar_prefetch=1,
            grid=(2, cols),
            in_specs=half_specs((1, 4, width, cut), cols)
            + [
                pl.BlockSpec((4, 1, 16, width), lambda h, c, one: (0, 0, 0, 0)),
                pl.BlockSpec((16, cut), lambda h, c, one: (0, 2 * c + h)),
            ],
            out_specs=pl.BlockSpec((4, 1, width, cut), lambda h, c, one: (0, 0, 0, 2 * c + h)),
        ),
        cost_estimate=cost_of(0, 8 * own.size),
        name="merge_expand",
    )(pair, own, other, low.reshape(16, 4, 1, width).transpose(1, 2, 0, 3), up)
    return whole.reshape(4 * width, 2 * cols * cut)


def merge_out(pair, pieces, low, up):
    cols, _, rows, width = pieces[0].shape
    takes = len(pieces)
    block = (1, 4, rows, width)
    specs = half_specs(block, cols)
    if takes == 1:
        specs = [pl.BlockSpec(block, lambda h, c, one: (c, 0, 0, 0))]
    return pl.pallas_call(
        merge_columns_kernel,
        out_shape=jax.ShapeDtypeStruct((takes * cols * rows, 4 * width), BF),
        grid_spec=pltpu.PrefetchScalarGridSpec(
            num_scalar_prefetch=1,
            grid=(takes, cols),
            in_specs=specs
            + [
                pl.BlockSpec((1, 16, rows), lambda h, c, one: (takes * c + h, 0, 0)),
                pl.BlockSpec((16, 4 * width), lambda h, c, one: (0, 0)),
            ],
            out_specs=pl.BlockSpec((rows, 4 * width), lambda h, c, one: (takes * c + h, 0)),
        ),
        cost_estimate=cost_of(0, 4 * takes * pieces[0].size),
        name="merge_out",
    )(pair, *pieces, low.reshape(16, takes * cols, rows).transpose(1, 0, 2), up)


def project_kernel(*refs, right_dim):
    *lefts, matrix, out = refs
    left = jnp.concatenate([ref[...] for ref in lefts], axis=1)
    out[...] = dot_of(left, matrix[...], 1, right_dim).astype(out.dtype)


def project(lefts, matrix, right_dim, out_type):
    rows, depth = lefts[0].shape[0], matrix.shape[right_dim]
    wide = matrix.shape[1 - right_dim]
    tile, cut = row_tile(rows), min(512, wide)
    shape = (depth, cut) if right_dim == 0 else (cut, depth)
    place = (lambda n, m: (0, n)) if right_dim == 0 else (lambda n, m: (n, 0))
    return pl.pallas_call(
        functools.partial(project_kernel, right_dim=right_dim),
        out_shape=jax.ShapeDtypeStruct((rows, wide), out_type),
        grid=(wide // cut, rows // tile),
        in_specs=[pl.BlockSpec((tile, left.shape[1]), lambda n, m: (m, 0)) for left in lefts]
        + [pl.BlockSpec(shape, place)],
        out_specs=pl.BlockSpec((tile, cut), lambda n, m: (m, n)),
        cost_estimate=cost_of(2 * rows * depth * wide, 2 * (rows * depth + depth * wide)),
        name="project",
    )(*lefts, matrix)


BLOCK = 256
RING = 5


def peer(step):
    return {"row": lax.axis_index("row") ^ step}


def send(source, target, sems, index, step):
    return pltpu.make_async_remote_copy(
        src_ref=source,
        dst_ref=target,
        send_sem=sems.at[0, index],
        recv_sem=sems.at[1, index],
        device_id=peer(step),
        device_id_type=pl.DeviceIdType.MESH,
    )


def greet():
    barrier = pltpu.get_barrier_semaphore()
    for step in (1, 2, 3):
        pl.semaphore_signal(
            barrier, inc=1, device_id=peer(step), device_id_type=pl.DeviceIdType.MESH
        )
    pl.semaphore_wait(barrier, 3)


def exchange_scratch(count, width, gathers):
    sem = pltpu.SemaphoreType.DMA((2, count))
    shapes = [
        pltpu.VMEM((2, 2, BLOCK, width), BF),
        pltpu.VMEM((count, 2, BLOCK, width), BF),
        pltpu.VMEM((2, BLOCK, width), F32),
        pltpu.VMEM((2, BLOCK, width), BF),
        pltpu.VMEM((count, BLOCK, width), BF),
        pltpu.VMEM((RING, BLOCK, width), F32),
        sem,
        sem,
    ]
    if gathers:
        shapes += [
            pltpu.VMEM((count, 8, BLOCK), F32),
            pltpu.VMEM((3, count, 8, BLOCK), F32),
        ] + [sem] * 6
    return shapes


def run_blocks(count, bufs, compute, stats, finish, own_ref=None, arrived=None, extra=None):
    pair_out, pair_in, far, side_out, side_in, near, pair_sem, side_sem, *rest = bufs
    gathers = own_ref is not None
    if gathers:
        stat_own, stat_in, stat_1, stat_2, stat_3, core_sem, far_sem, relay_sem = rest
        stat_sems = (stat_1, stat_2, stat_3)

    def rows_of(c):
        return pl.ds(pl.multiple_of(c * BLOCK, BLOCK), BLOCK)

    def to_core(c):
        return send(pair_out.at[lax.rem(c, 2)], pair_in.at[c], pair_sem, c, 1)

    def to_side(c):
        return send(side_out.at[lax.rem(c, 2)], side_in.at[c], side_sem, c, 2)

    def to_stat(c, step):
        return send(stat_own.at[c], stat_in.at[step - 1, c], stat_sems[step - 1], c, step)

    def gather_core(c):
        return send(own_ref.at[rows_of(c)], arrived[0].at[rows_of(c)], core_sem, c, 1)

    def gather_side(c):
        return send(own_ref.at[rows_of(c)], arrived[1].at[rows_of(c)], far_sem, c, 2)

    def relay(c):
        return send(arrived[1].at[rows_of(c)], arrived[2].at[rows_of(c)], relay_sem, c, 1)

    def stage(c, body):
        pl.when(jnp.logical_and(c >= 0, c < count))(functools.partial(body, c))

    def multiply(c):
        @pl.when(c >= 2)
        def _():
            to_core(c - 2).wait_send()

        slot = lax.rem(c, 2)

        def put(block, value):
            if block == 0:
                near[lax.rem(c, RING)] = value
            elif block == 2:
                far[slot] = value
            else:
                pair_out[slot, block // 2] = value.astype(BF)
            if block == 3:
                to_core(c).start()

        compute(c, put)

    def sum_core(c):
        @pl.when(c >= 2)
        def _():
            to_side(c - 2).wait_send()

        to_core(c).wait_recv()
        slot = lax.rem(c, 2)
        side_out[slot] = (far[slot] + pair_in[c, 1].astype(F32)).astype(BF)
        to_side(c).start()
        at = lax.rem(c, RING)
        near[at] = near[at] + pair_in[c, 0].astype(F32)
        if extra is not None:
            extra[0](c)

    def sum_side(c):
        if extra is not None:
            extra[1](c)
        to_side(c).wait_recv()
        at = lax.rem(c, RING)
        total = near[at] + side_in[c].astype(F32)
        if not gathers:
            finish(c, rows_of(c), total)
            return
        near[at] = total
        stat_own[c] = stats(c, rows_of(c), total)
        for step in (1, 2, 3):
            to_stat(c, step).start()

    def normalise(c):
        total = stat_own[c]
        for step in (1, 2, 3):
            to_stat(c, step).wait_recv()
            total = total + stat_in[step - 1, c]
        own_ref[rows_of(c), :] = finish(c, rows_of(c), near[lax.rem(c, RING)], total)
        gather_side(c).start()
        gather_core(c).start()

    def pass_on(c):
        gather_side(c).wait_recv()
        relay(c).start()

    def body(t, carry):
        stage(t - 1, sum_core)
        stage(t, multiply)
        stage(t - 2, sum_side)
        if gathers:
            stage(t - 3, normalise)
            stage(t - 4, pass_on)
        return carry

    lax.fori_loop(0, count + (4 if gathers else 2), body, 0)

    def close(c, carry):
        if gathers:
            for step in (1, 2, 3):
                to_stat(c, step).wait_send()
            gather_core(c).wait()
            gather_side(c).wait_send()
            relay(c).wait()
        return carry

    if gathers:
        lax.fori_loop(0, count, close, 0)
    for c in range(max(count - 2, 0), count):
        to_core(c).wait_send()
        to_side(c).wait_send()


def sums_of(*values):
    out = None
    for index, value in enumerate(values):
        pick = lax.broadcasted_iota(jnp.int32, (8, value.shape[1]), 0) == index
        term = lax.dot_general(
            pick.astype(F32),
            value,
            (((1,), (1,)), ((), ())),
            precision=lax.Precision.HIGHEST,
            preferred_element_type=F32,
        )
        out = term if out is None else out + term
    return out


def column_of(stats, index):
    pick = lax.broadcasted_iota(jnp.int32, (8, HEAD), 0) == index
    wide = lax.dot_general(
        stats,
        pick.astype(F32),
        (((0,), (0,)), ((), ())),
        precision=lax.Precision.HIGHEST,
        preferred_element_type=F32,
    )
    return wide[:, :1]


def branch_kernel(
    mixed_ref,
    matrix_ref,
    tokens_ref,
    gain_ref,
    gate_all,
    gate_rest,
    upper_all,
    upper_rest,
    branch_ref,
    hidden_ref,
    stat_ref,
    own_ref,
    *rest,
):
    arrived, halves, rest = rest[:3], rest[3:5], rest[5:]
    swap_sems, local_sem, *bufs = rest
    width = own_ref.shape[1]
    count = own_ref.shape[0] // BLOCK
    greet_all([peer(step) for step in (1, 2, 3)] + [other_of_pair()])
    swaps = []
    for index, (whole, rest_half) in enumerate(((gate_all, gate_rest), (upper_all, upper_rest))):
        swaps += exchange_halves(
            whole, rest_half, halves[index], swap_sems.at[index], local_sem.at[index]
        )
    for copy in swaps:
        copy.start()

    def compute(c, put):
        left = mixed_ref[pl.ds(pl.multiple_of(c * BLOCK, BLOCK), BLOCK), :]
        for block in (1, 3, 2, 0):
            put(block, dot_of(left, matrix_ref[:, block * width : (block + 1) * width], 1, 0))

    def stats(c, rows, branch):
        branch_ref[rows, :] = branch
        return sums_of(branch * branch)

    def finish(c, rows, branch, total):
        stat_ref[c] = total
        scale = lax.rsqrt(column_of(total, 0) / D + EPS)
        hidden = tokens_ref[rows, :].astype(F32) + gain_ref[0:1, :] * branch * scale
        hidden_ref[rows, :] = hidden
        return hidden.astype(BF)

    run_blocks(count, bufs, compute, stats, finish, own_ref, arrived)
    wait_all(swaps)


VMEM_SPEC = pl.BlockSpec(memory_space=pltpu.VMEM)
ANY_SPEC = pl.BlockSpec(memory_space=pl.ANY)


def talk_params(number):
    return pltpu.CompilerParams(
        collective_id=number, has_side_effects=True, vmem_limit_bytes=63 * 2**20
    )


def branch_call(mixed, matrix, tokens, gain, halves):
    rows, width = tokens.shape
    count = rows // BLOCK
    cols = halves[0].shape[0]
    part = jax.ShapeDtypeStruct((rows, width), BF)
    whole = jax.ShapeDtypeStruct((rows, width), F32)
    half = jax.ShapeDtypeStruct(halves[0].shape, BF)
    return pl.pallas_call(
        branch_kernel,
        out_shape=[whole, whole, jax.ShapeDtypeStruct((count, 8, BLOCK), F32)]
        + [part] * 4
        + [half] * 2,
        in_specs=[VMEM_SPEC] * 4 + [ANY_SPEC] * 4,
        out_specs=[VMEM_SPEC] * 4 + [ANY_SPEC] * 5,
        scratch_shapes=[
            pltpu.SemaphoreType.DMA((2, 2, cols - 1)),
            pltpu.SemaphoreType.DMA((2,)),
        ]
        + exchange_scratch(count, width, True),
        compiler_params=talk_params(0),
        cost_estimate=cost_of(8 * rows * width * matrix.shape[0], 2**27),
        name="branch",
    )(mixed, matrix, tokens, gain, *halves)


def load_lefts(lefts, buffer, sems, count):
    width = buffer.shape[2] // 4

    def copies(c):
        slot = lax.rem(c, 2)
        rows = pl.ds(pl.multiple_of(c * BLOCK, BLOCK), BLOCK)
        return [
            pltpu.make_async_copy(
                left.at[rows], buffer.at[slot, :, index * width : (index + 1) * width], sems.at[slot, index]
            )
            for index, left in enumerate(lefts)
        ]

    def start(c):
        @pl.when(c < count)
        def _():
            for copy in copies(c):
                copy.start()

    def wait(c):
        for copy in copies(c):
            copy.wait()

    return start, wait


def move_rows(outer, buffer, sems, index, inward):
    def copy(c):
        slot = lax.rem(c, 2)
        rows = pl.ds(pl.multiple_of(c * BLOCK, BLOCK), BLOCK)
        ends = (outer.at[rows], buffer.at[slot])
        if not inward:
            ends = ends[::-1]
        return pltpu.make_async_copy(*ends, sems.at[index, slot])

    return copy


def forward_kernel(x0, x1, x2, x3, gate_hbm, upper_hbm, reduce_hbm, hidden_ref, cot_ref, gain_ref, *rest):
    act_out, gate_out, upper_out, layer_ref, own_ref, *rest = rest
    arrived, rest = rest[:3], rest[3:]
    gate_w, upper_w, reduce_w, lefts, act_buf, gate_buf, upper_buf, w_sem, x_sem, o_sem, *bufs = rest
    width = own_ref.shape[1]
    count = own_ref.shape[0] // BLOCK
    ff = gate_w.shape[1]
    tile = 512
    loads = [
        pltpu.make_async_copy(source, target, w_sem.at[index])
        for index, (source, target) in enumerate(
            ((gate_hbm, gate_w), (upper_hbm, upper_w), (reduce_hbm, reduce_w))
        )
    ]
    start_left, wait_left = load_lefts((x0, x1, x2, x3), lefts, x_sem, count)
    start_left(0)
    for load in loads:
        load.start()
    greet()
    outs = [
        move_rows(outer, buffer, o_sem, index, False)
        for index, (outer, buffer) in enumerate(
            ((act_out, act_buf), (gate_out, gate_buf), (upper_out, upper_buf))
        )
    ]

    def compute(c, put):
        slot = lax.rem(c, 2)
        wait_left(c)
        start_left(c + 1)

        @pl.when(c == 0)
        def _():
            for load in loads:
                load.wait()

        @pl.when(c >= 2)
        def _():
            for out in outs:
                out(c - 2).wait()

        def tiles(n, carry):
            at = pl.ds(pl.multiple_of(n * tile, tile), tile)
            left = lefts[slot]
            gate = dot_of(left, gate_w[:, at], 1, 0)
            upper = dot_of(left, upper_w[:, at], 1, 0)
            act_buf[slot, :, at] = (gate * jax.nn.sigmoid(gate) * upper).astype(BF)
            gate_buf[slot, :, at] = gate.astype(BF)
            upper_buf[slot, :, at] = upper.astype(BF)
            return carry

        lax.fori_loop(0, ff // tile, tiles, 0)
        for out in outs:
            out(c).start()
        for block in (1, 3, 2, 0):
            span = slice(block * width, (block + 1) * width)
            put(block, dot_of(act_buf[slot], reduce_w[:, span], 1, 0))

    def stats(c, rows, result):
        weighted = gain_ref[1:2, :] * cot_ref[rows, :].astype(F32)
        return sums_of(result * result, weighted * result)

    def finish(c, rows, result, total):
        scale = lax.rsqrt(column_of(total, 0) / D + EPS)
        gain = gain_ref[1:2, :]
        layer_ref[rows, :] = (hidden_ref[rows, :] + gain * result * scale).astype(BF)
        weighted = gain * cot_ref[rows, :].astype(F32)
        inner = column_of(total, 1)
        return (scale * weighted - result * (scale * scale * scale * inner / D)).astype(BF)

    run_blocks(count, bufs, compute, stats, finish, own_ref, arrived)
    for c in range(max(count - 2, 0), count):
        for out in outs:
            out(c).wait()


def forward_call(lefts, gate_w, upper_w, reduce_w, hidden, cotangent, gain):
    rows, width = hidden.shape
    count = rows // BLOCK
    ff = gate_w.shape[1]
    part = jax.ShapeDtypeStruct((rows, width), BF)
    wide = jax.ShapeDtypeStruct((rows, ff), BF)
    return pl.pallas_call(
        forward_kernel,
        out_shape=[wide] * 3 + [part] * 5,
        in_specs=[ANY_SPEC] * 7 + [VMEM_SPEC] * 3,
        out_specs=[ANY_SPEC] * 3 + [VMEM_SPEC] * 2 + [ANY_SPEC] * 3,
        scratch_shapes=[
            pltpu.VMEM(gate_w.shape, BF),
            pltpu.VMEM(upper_w.shape, BF),
            pltpu.VMEM(reduce_w.shape, BF),
            pltpu.VMEM((2, BLOCK, 4 * width), BF),
            pltpu.VMEM((2, BLOCK, ff), BF),
            pltpu.VMEM((2, BLOCK, ff), BF),
            pltpu.VMEM((2, BLOCK, ff), BF),
            pltpu.SemaphoreType.DMA((3,)),
            pltpu.SemaphoreType.DMA((2, 4)),
            pltpu.SemaphoreType.DMA((3, 2)),
        ]
        + exchange_scratch(count, width, True),
        compiler_params=talk_params(1),
        cost_estimate=cost_of(24 * rows * width * ff, 2**27),
        name="forward",
    )(*lefts, gate_w, upper_w, reduce_w, hidden, cotangent, gain)


def backward_kernel(
    x0, x1, x2, x3, gate_hbm, upper_hbm, reduce_hbm, gate_in, upper_in, cot_ref, branch_ref, stat_ref, gain_ref, *rest
):
    d_gate_out, d_upper_out, d_hidden_ref, own_ref, *rest = rest
    arrived, rest = rest[:3], rest[3:]
    gate_w, upper_w, reduce_w, lefts, gate_buf, upper_buf, d_gate_buf, d_upper_buf, *rest = rest
    w_sem, x_sem, i_sem, o_sem, *bufs = rest
    width = own_ref.shape[1]
    count = own_ref.shape[0] // BLOCK
    ff = gate_w.shape[1]
    tile = 512
    loads = [
        pltpu.make_async_copy(source, target, w_sem.at[index])
        for index, (source, target) in enumerate(
            ((reduce_hbm, reduce_w), (gate_hbm, gate_w), (upper_hbm, upper_w))
        )
    ]
    start_left, wait_left = load_lefts((x0, x1, x2, x3), lefts, x_sem, count)
    ins = [
        move_rows(outer, buffer, i_sem, index, True)
        for index, (outer, buffer) in enumerate(((gate_in, gate_buf), (upper_in, upper_buf)))
    ]
    outs = [
        move_rows(outer, buffer, o_sem, index, False)
        for index, (outer, buffer) in enumerate(
            ((d_gate_out, d_gate_buf), (d_upper_out, d_upper_buf))
        )
    ]
    start_left(0)
    for one in ins:
        one(0).start()
    for load in loads:
        load.start()
    greet()

    def compute(c, put):
        slot = lax.rem(c, 2)
        wait_left(c)
        start_left(c + 1)
        for one in ins:
            one(c).wait()

        @pl.when(c + 1 < count)
        def _():
            for one in ins:
                one(c + 1).start()

        @pl.when(c == 0)
        def _():
            for load in loads:
                load.wait()

        @pl.when(c >= 2)
        def _():
            for out in outs:
                out(c - 2).wait()

        def tiles(n, carry):
            at = pl.ds(pl.multiple_of(n * tile, tile), tile)
            d_act = dot_of(lefts[slot], reduce_w[at, :], 1, 1)
            gate = gate_buf[slot, :, at].astype(F32)
            sigma = jax.nn.sigmoid(gate)
            d_gate = d_act * upper_buf[slot, :, at].astype(F32) * (sigma * (1 + gate * (1 - sigma)))
            d_gate_buf[slot, :, at] = d_gate.astype(BF)
            d_upper_buf[slot, :, at] = (d_act * (gate * sigma)).astype(BF)
            return carry

        lax.fori_loop(0, ff // tile, tiles, 0)
        for out in outs:
            out(c).start()
        for block in (1, 3, 2, 0):
            span = slice(block * width, (block + 1) * width)
            put(
                block,
                dot_of(d_gate_buf[slot], gate_w[span, :], 1, 1)
                + dot_of(d_upper_buf[slot], upper_w[span, :], 1, 1),
            )

    def stats(c, rows, total):
        d_hidden = cot_ref[rows, :].astype(F32) + total
        d_hidden_ref[rows, :] = d_hidden
        return sums_of(gain_ref[0:1, :] * d_hidden * branch_ref[rows, :])

    def finish(c, rows, total, sums):
        scale = lax.rsqrt(column_of(stat_ref[c], 0) / D + EPS)
        weighted = gain_ref[0:1, :] * d_hidden_ref[rows, :]
        inner = column_of(sums, 0)
        back = scale * scale * scale * inner / D
        return (scale * weighted - branch_ref[rows, :] * back).astype(BF)

    run_blocks(count, bufs, compute, stats, finish, own_ref, arrived)
    for c in range(max(count - 2, 0), count):
        for out in outs:
            out(c).wait()


def backward_call(lefts, gate_w, upper_w, reduce_w, gate, upper, cotangent, branch, stats, gain):
    rows, width = branch.shape
    count = rows // BLOCK
    ff = gate_w.shape[1]
    part = jax.ShapeDtypeStruct((rows, width), BF)
    wide = jax.ShapeDtypeStruct((rows, ff), BF)
    return pl.pallas_call(
        backward_kernel,
        out_shape=[wide] * 2 + [jax.ShapeDtypeStruct((rows, width), F32)] + [part] * 4,
        in_specs=[ANY_SPEC] * 9 + [VMEM_SPEC] * 4,
        out_specs=[ANY_SPEC] * 2 + [VMEM_SPEC] * 2 + [ANY_SPEC] * 3,
        scratch_shapes=[
            pltpu.VMEM(gate_w.shape, BF),
            pltpu.VMEM(upper_w.shape, BF),
            pltpu.VMEM(reduce_w.shape, BF),
            pltpu.VMEM((2, BLOCK, 4 * width), BF),
            pltpu.VMEM((2, BLOCK, ff), BF),
            pltpu.VMEM((2, BLOCK, ff), BF),
            pltpu.VMEM((2, BLOCK, ff), BF),
            pltpu.VMEM((2, BLOCK, ff), BF),
            pltpu.SemaphoreType.DMA((3,)),
            pltpu.SemaphoreType.DMA((2, 4)),
            pltpu.SemaphoreType.DMA((2, 2)),
            pltpu.SemaphoreType.DMA((2, 2)),
        ]
        + exchange_scratch(count, width, True),
        compiler_params=talk_params(2),
        cost_estimate=cost_of(24 * rows * width * ff, 2**27),
        name="backward",
    )(*lefts, gate_w, upper_w, reduce_w, gate, upper, cotangent, branch, stats, gain)


def input_kernel(
    raw_hbm,
    dq_hbm,
    dk_hbm,
    dv_hbm,
    matrix_ref,
    d_hidden_ref,
    scale_ref,
    back_ref,
    gain_ref,
    cos_ref,
    sin_ref,
    tokens_ref,
    inner_ref,
    up_ref,
    out_ref,
    low_grad_ref,
    up_grad_ref,
    raw_buf,
    dq_buf,
    dk_buf,
    dv_buf,
    left_ref,
    inner_out,
    inner_in,
    inner_mid,
    inner_far,
    in_sem,
    core_sem,
    far_sem,
    *bufs,
):
    width = out_ref.shape[1]
    local = dq_buf.shape[2]
    count = out_ref.shape[0] // BLOCK
    ins = [
        move_rows(outer, buffer, in_sem, index, True)
        for index, (outer, buffer) in enumerate(
            ((raw_hbm, raw_buf), (dq_hbm, dq_buf), (dk_hbm, dk_buf), (dv_hbm, dv_buf))
        )
    ]
    for one in ins:
        one(0).start()
    low_grad_ref[...] = jnp.zeros_like(low_grad_ref)
    up_grad_ref[...] = jnp.zeros_like(up_grad_ref)
    greet()

    def inner_core(c):
        return send(inner_out.at[lax.rem(c, 2)], inner_in.at[c], core_sem, c, 1)

    def inner_side(c):
        return send(inner_mid.at[lax.rem(c, 2)], inner_far.at[c], far_sem, c, 2)

    def after_core(c):
        @pl.when(c >= 2)
        def _():
            inner_side(c - 2).wait_send()

        inner_core(c).wait_recv()
        slot = lax.rem(c, 2)
        inner_mid[slot] = inner_out[slot] + inner_in[c]
        inner_side(c).start()

    def after_side(c):
        inner_side(c).wait_recv()
        total = (inner_mid[lax.rem(c, 2)] + inner_far[c]).astype(BF)
        low_grad_ref[...] += dot_of(total, tokens_ref[span_of(c, BLOCK), :], 1, 0)

    def compute(c, put):
        slot = lax.rem(c, 2)
        for one in ins:
            one(c).wait()

        @pl.when(c + 1 < count)
        def _():
            for one in ins:
                one(c + 1).start()

        @pl.when(c >= 2)
        def _():
            inner_core(c - 2).wait_send()

        rows = span_of(c, BLOCK)
        cosine = cos_ref[rows, :]
        sine = sin_ref[rows, :]
        for part, grad in ((0, dq_buf), (1, dk_buf)):
            scale = scale_ref[rows, part : part + 1]
            back = back_ref[rows, part : part + 1]
            for at in range(0, local, HEAD):
                turned = grad[slot, :, at : at + HEAD]
                turned = turned * cosine - pltpu.roll(turned, HEAD // 2, 1) * sine
                turned = turned * gain_ref[part : part + 1, at : at + HEAD] * scale
                lane = part * local + at
                left_ref[:, lane : lane + HEAD] = (
                    turned - raw_buf[slot, :, lane : lane + HEAD] * back
                ).astype(BF)
        left_ref[:, 2 * local :] = dv_buf[slot].astype(BF)
        for part in range(3):
            own = slice(16 * part, 16 * part + 16)
            grad = left_ref[:, part * local : (part + 1) * local]
            inner_out[slot, own, :] = ADAPTER_FACTOR * dot_of(up_ref[own, :], grad, 1, 1)
            up_grad_ref[own, :] += ADAPTER_FACTOR * dot_of(inner_ref[own, rows], grad, 1, 0)
        inner_core(c).start()
        left = left_ref[...]
        for block in (1, 3, 2, 0):
            put(block, dot_of(left, matrix_ref[block * width : (block + 1) * width, :], 1, 1))

    def finish(c, rows, total):
        out_ref[rows, :] = d_hidden_ref[rows, :] + total

    run_blocks(count, bufs, compute, None, finish, extra=(after_core, after_side))
    for c in range(max(count - 2, 0), count):
        inner_core(c).wait_send()
        inner_side(c).wait_send()


def input_call(
    raw, d_query, d_key, d_value, matrix, d_hidden, scales, backs, gains, cosine, sine, *adapters
):
    rows, width = d_hidden.shape
    local = d_query.shape[1]
    count = rows // BLOCK
    part = pltpu.VMEM((2, BLOCK, local), F32)
    sem = pltpu.SemaphoreType.DMA((2, count))
    return pl.pallas_call(
        input_kernel,
        out_shape=[
            jax.ShapeDtypeStruct((rows, width), F32),
            jax.ShapeDtypeStruct((48, width), F32),
            jax.ShapeDtypeStruct((48, local), F32),
        ],
        in_specs=[ANY_SPEC] * 4 + [VMEM_SPEC] * 10,
        out_specs=[VMEM_SPEC] * 3,
        scratch_shapes=[
            pltpu.VMEM((2, BLOCK, 3 * local), F32),
            part,
            part,
            part,
            pltpu.VMEM((BLOCK, 3 * local), BF),
            pltpu.VMEM((2, 48, BLOCK), F32),
            pltpu.VMEM((count, 48, BLOCK), F32),
            pltpu.VMEM((2, 48, BLOCK), F32),
            pltpu.VMEM((count, 48, BLOCK), F32),
            pltpu.SemaphoreType.DMA((4, 2)),
            sem,
            sem,
        ]
        + exchange_scratch(count, width, False),
        compiler_params=talk_params(3),
        cost_estimate=cost_of(24 * rows * width * local, 2**26),
        name="input_grad",
    )(raw, d_query, d_key, d_value, matrix, d_hidden, scales, backs, gains, cosine, sine, *adapters)


def deal(items, outs, sems):
    me = lax.axis_index("row")
    copies = []
    for index, (view, out) in enumerate(zip(items, outs)):
        mine = [pltpu.make_async_copy(view(me), out.at[0], sems.at[0, index, 0])]
        for step in (1, 2, 3):
            mine.append(
                pltpu.make_async_remote_copy(
                    src_ref=view(me ^ step),
                    dst_ref=out.at[step],
                    send_sem=sems.at[0, index, step],
                    recv_sem=sems.at[1, index, step],
                    device_id=peer(step),
                    device_id_type=pl.DeviceIdType.MESH,
                )
            )
        copies.append(mine)
    return copies


def start_all(copies):
    for step in (2, 3, 1, 0):
        copies[step].start()


def wait_all(copies):
    for copy in copies:
        copy.wait()


def span_of(at, size):
    return pl.ds(pl.multiple_of(at * size, size), size)


def qkv_view(ref, half):
    _, rows, columns = ref.shape
    return lambda row: ref.at[:, span_of(half, rows // 2), span_of(row, columns // 4)]


def attn_view(ref, half):
    cut = ref.shape[0] // 8
    return lambda row: ref.at[span_of(2 * row + half, cut)]


def expand_view(ref, part, half):
    cut = ref.shape[2] // 8
    return lambda row: ref.at[part, :, span_of(2 * row + half, cut)]


def reduce_view(ref):
    cut = ref.shape[0] // 4
    return lambda row: ref.at[span_of(row, cut)]


def like_views(shapes):
    return [jax.ShapeDtypeStruct((4, *shape), BF) for shape in shapes]


def first_deal_kernel(qkv_ref, attn_ref, qkv_out, attn_out, sems):
    half = lax.axis_index("dp")
    greet()
    copies = deal([qkv_view(qkv_ref, half), attn_view(attn_ref, half)], [qkv_out, attn_out], sems)
    for one in copies:
        start_all(one)
    for one in copies:
        wait_all(one)


def first_deal(qkv_weight, attn_weight):
    parts, rows, columns = qkv_weight.shape
    return pl.pallas_call(
        first_deal_kernel,
        out_shape=like_views(
            [(parts, rows // 2, columns // 4), (attn_weight.shape[0] // 8, attn_weight.shape[1])]
        ),
        in_specs=[ANY_SPEC] * 2,
        out_specs=[ANY_SPEC] * 2,
        scratch_shapes=[pltpu.SemaphoreType.DMA((2, 2, 4))],
        compiler_params=talk_params(4),
        cost_estimate=cost_of(0, 2**26),
        name="first_deal",
    )(qkv_weight, attn_weight)


def second_deal_kernel(qkv_ref, attn_ref, expand_ref, tokens_ref, pack_ref, *rest):
    *outs, t1, t2, t3, p1, p2, p3, sems, token_sem, pack_sem = rest
    half = lax.axis_index("dp")
    greet()
    gate, rest_qkv, rest_attn, upper = deal(
        [
            expand_view(expand_ref, 0, half),
            qkv_view(qkv_ref, 1 - half),
            attn_view(attn_ref, 1 - half),
            expand_view(expand_ref, 1, half),
        ],
        outs,
        sems,
    )
    gathers = []
    for source, targets, one_sem in ((pack_ref, (p1, p2, p3), pack_sem), (tokens_ref, (t1, t2, t3), token_sem)):
        gathers.append(
            (
                send(source, targets[1], one_sem, 1, 2),
                send(source, targets[0], one_sem, 0, 1),
                send(targets[1], targets[2], one_sem, 2, 1),
            )
        )
    start_all(gate)
    start_all(rest_qkv)
    start_all(rest_attn)
    for side, core, _ in gathers:
        side.start()
        core.start()
    start_all(upper)
    for side, core, relay in gathers:
        side.wait_recv()
        relay.start()
    for one in (gate, rest_qkv, rest_attn, upper):
        wait_all(one)
    for side, core, relay in gathers:
        side.wait_send()
        core.wait()
        relay.wait()


def second_deal(qkv_weight, attn_weight, expand_weight, tokens, pack):
    parts, rows, columns = qkv_weight.shape
    cut = expand_weight.shape[2] // 8
    wide = (expand_weight.shape[1], cut)
    sem = pltpu.SemaphoreType.DMA((2, 3))
    return pl.pallas_call(
        second_deal_kernel,
        out_shape=like_views(
            [
                wide,
                (parts, rows // 2, columns // 4),
                (attn_weight.shape[0] // 8, attn_weight.shape[1]),
                wide,
            ]
        )
        + [jax.ShapeDtypeStruct(tokens.shape, BF)] * 3
        + [jax.ShapeDtypeStruct(pack.shape, BF)] * 3,
        in_specs=[ANY_SPEC] * 5,
        out_specs=[ANY_SPEC] * 10,
        scratch_shapes=[pltpu.SemaphoreType.DMA((2, 4, 4)), sem, sem],
        compiler_params=talk_params(5),
        cost_estimate=cost_of(0, 2**27),
        name="second_deal",
    )(qkv_weight, attn_weight, expand_weight, tokens, pack)


def greet_all(peers):
    barrier = pltpu.get_barrier_semaphore()
    for device in peers:
        pl.semaphore_signal(barrier, inc=1, device_id=device, device_id_type=pl.DeviceIdType.MESH)
    pl.semaphore_wait(barrier, len(peers))


def copy_to(source, target, sems, index, device):
    return pltpu.make_async_remote_copy(
        src_ref=source,
        dst_ref=target,
        send_sem=sems.at[0, index],
        recv_sem=sems.at[1, index],
        device_id=device,
        device_id_type=pl.DeviceIdType.MESH,
    )


def other_of_pair():
    return {"dp": 1 - lax.axis_index("dp")}


def exchange_halves(whole, rest, out, sems, local_sem):
    cols = whole.shape[0]
    col = lax.axis_index("col")
    copies = [pltpu.make_async_copy(rest, out.at[0], local_sem)]
    for k in range(1, cols):
        place = lax.rem(col + k, cols)
        copies.append(copy_to(whole.at[place], out.at[k], sems, k - 1, other_of_pair()))
    return copies


def send_round(view, out, sems, local_sem):
    cols = out.shape[0]
    col = lax.axis_index("col")
    local = pltpu.make_async_copy(view(col), out.at[col], local_sem)
    sends = []
    arrivals = []
    for k in range(1, cols):
        place = lax.rem(col + k, cols)
        came = lax.rem(col - k + cols, cols)
        sends.append(copy_to(view(place), out.at[col], sems, k - 1, {"col": place}))
        arrivals.append(copy_to(view(place), out.at[came], sems, k - 1, {"col": place}))

    def wait():
        local.wait()
        for one in arrivals:
            one.wait_recv()
        for one in sends:
            one.wait_send()

    return [local, *sends], wait


def row_and_col_peers():
    cols = lax.axis_size("col")
    col = lax.axis_index("col")
    return [peer(step) for step in (1, 2, 3)] + [
        {"col": lax.rem(col + k, cols)} for k in range(1, cols)
    ]


def third_deal_kernel(
    expand_ref, reduce_ref, qkv_all, qkv_rest, attn_all, attn_rest, pack_ref, gain_ref, *rest
):
    *outs, qkv_out, attn_out, pack_out, gain_out = rest[:7]
    deal_sem, qkv_sem, attn_sem, pack_sem, gain_sem, local_sem = rest[7:]
    other = 1 - lax.axis_index("dp")
    me = lax.axis_index("row")
    greet_all(row_and_col_peers() + [other_of_pair()])
    sub = gain_out.shape[2]
    swaps = exchange_halves(qkv_all, qkv_rest, qkv_out, qkv_sem, local_sem.at[0])
    swaps += exchange_halves(attn_all, attn_rest, attn_out, attn_sem, local_sem.at[1])
    packs, wait_packs = send_round(lambda place: pack_ref.at[place], pack_out, pack_sem, local_sem.at[2])
    gains, wait_gains = send_round(
        lambda place: gain_ref.at[:, span_of(me, sub)], gain_out, gain_sem, local_sem.at[3]
    )
    for copy in packs + gains + swaps:
        copy.start()
    copies = deal(
        [
            reduce_view(reduce_ref),
            expand_view(expand_ref, 0, other),
            expand_view(expand_ref, 1, other),
        ],
        outs,
        deal_sem,
    )
    for one in copies:
        start_all(one)
    wait_packs()
    wait_gains()
    for one in copies:
        wait_all(one)
    wait_all(swaps)


def third_deal(expand_weight, reduce_weight, qkv_all, qkv_rest, attn_all, attn_rest, pack, gain):
    wide = (expand_weight.shape[1], expand_weight.shape[2] // 8)
    cols = qkv_all.shape[0]
    round_sem = pltpu.SemaphoreType.DMA((2, cols - 1))
    return pl.pallas_call(
        third_deal_kernel,
        out_shape=like_views([(reduce_weight.shape[0] // 4, reduce_weight.shape[1]), wide, wide])
        + [
            jax.ShapeDtypeStruct(qkv_all.shape, BF),
            jax.ShapeDtypeStruct(attn_all.shape, BF),
            jax.ShapeDtypeStruct(pack.shape, BF),
            jax.ShapeDtypeStruct((cols, gain.shape[0], gain.shape[1] // 4), F32),
        ],
        in_specs=[ANY_SPEC] * 8,
        out_specs=[ANY_SPEC] * 7,
        scratch_shapes=[
            pltpu.SemaphoreType.DMA((2, 3, 4)),
            round_sem,
            round_sem,
            round_sem,
            round_sem,
            pltpu.SemaphoreType.DMA((4,)),
        ],
        compiler_params=talk_params(6),
        cost_estimate=cost_of(0, 2**27),
        name="third_deal",
    )(expand_weight, reduce_weight, qkv_all, qkv_rest, attn_all, attn_rest, pack, gain)


def groups_kernel(row_ref, col_ref, rows_out, cols_out, local_sem, pair_sem, round_sem, deal_sem, row_sem):
    cols = col_ref.shape[0]
    col = lax.axis_index("col")
    places = [lax.rem(col + k, cols) for k in range(cols)]
    to = copy_to
    greet_all(row_and_col_peers() + [other_of_pair()])
    swap_rows = to(row_ref, rows_out.at[0, 1], pair_sem, 0, other_of_pair())
    swap_rows.start()
    dealt = [
        to(col_ref.at[places[k]], cols_out.at[0, 0, col], deal_sem, k - 1, {"col": places[k]})
        for k in range(1, cols)
    ]
    for copy in dealt:
        copy.start()
    keep_rows = pltpu.make_async_copy(row_ref, rows_out.at[0, 0], local_sem.at[0])
    keep_cols = pltpu.make_async_copy(col_ref.at[col], cols_out.at[0, 0, col], local_sem.at[1])
    keep_rows.start()
    keep_cols.start()
    for k in range(1, cols):
        came = lax.rem(col - k + cols, cols)
        to(col_ref.at[came], cols_out.at[0, 0, came], deal_sem, k - 1, {"col": places[k]}).wait_recv()
    keep_cols.wait()
    swap_cols = to(cols_out.at[0, 0], cols_out.at[0, 1], pair_sem, 1, other_of_pair())
    swap_cols.start()
    keep_rows.wait()
    swap_rows.wait_recv()
    rounds = [
        to(rows_out.at[0], rows_out.at[k], round_sem, k - 1, {"col": places[k]})
        for k in range(1, cols)
    ]
    for copy in rounds:
        copy.start()
    swap_cols.wait_recv()
    side = to(cols_out.at[0], cols_out.at[2], row_sem, 1, peer(2))
    core = to(cols_out.at[0], cols_out.at[1], row_sem, 0, peer(1))
    relay = to(cols_out.at[2], cols_out.at[3], row_sem, 2, peer(1))
    side.start()
    core.start()
    side.wait_recv()
    relay.start()
    core.wait()
    relay.wait()
    side.wait_send()
    for copy in rounds:
        copy.wait()
    for copy in dealt:
        copy.wait_send()
    swap_rows.wait_send()
    swap_cols.wait_send()


def groups_call(row_pack, col_pack):
    cols = col_pack.shape[0]
    return pl.pallas_call(
        groups_kernel,
        out_shape=[
            jax.ShapeDtypeStruct((cols, 2, *row_pack.shape), BF),
            jax.ShapeDtypeStruct((4, 2, *col_pack.shape), BF),
        ],
        in_specs=[ANY_SPEC] * 2,
        out_specs=[ANY_SPEC] * 2,
        scratch_shapes=[
            pltpu.SemaphoreType.DMA((2,)),
            pltpu.SemaphoreType.DMA((2, 2)),
            pltpu.SemaphoreType.DMA((2, cols - 1)),
            pltpu.SemaphoreType.DMA((2, cols - 1)),
            pltpu.SemaphoreType.DMA((2, 3)),
        ],
        compiler_params=talk_params(7),
        cost_estimate=cost_of(0, 2**26),
        name="groups",
    )(row_pack, col_pack)


def across(values, step):
    return lax.ppermute(values, "row", [(i, i ^ step) for i in range(4)])


def sum_row(values):
    values = values + across(values, 1)
    return values + across(values, 2)


def gather_col(values):
    return lax.all_gather(values, "col", axis=0, tiled=False)


def swap_pair(values):
    return lax.ppermute(values, "dp", [(0, 1), (1, 0)])


def round_col(values, cols):
    shift = lambda k: [(i, (i + k) % cols) for i in range(cols)]
    return [values] + [lax.ppermute(values, "col", shift(k)) for k in range(1, cols)]


def after(values, earlier):
    return lax.optimization_barrier((values, earlier))[0]


def group_shards(
    tokens,
    cotangent,
    qkv_weight,
    attn_weight,
    expand_weight,
    reduce_weight,
    headnorm_gain,
    post_gain,
    qkv_lowrank,
    qkv_uprank,
    attn_lowrank,
    attn_uprank,
    expand_lowrank,
    expand_uprank,
    reduce_lowrank,
    reduce_uprank,
    prefix_length,
    adapter_set,
):
    cols = lax.axis_size("col")
    pair = lax.axis_index("dp")
    me = lax.axis_index("row")
    col = lax.axis_index("col")
    rows, width = tokens.shape
    sub = qkv_weight.shape[2] // 4
    ff = expand_weight.shape[2]
    ff_sub = ff // 4
    ff_half = ff_sub // 2
    local = cols * sub
    ff_local = cols * ff_sub
    sequence = pair * cols + col
    mine = lax.dynamic_index_in_dim(adapter_set, sequence, 0, keepdims=False)
    prefix = lax.dynamic_slice_in_dim(prefix_length, sequence, 1)
    cols_sets = lax.dynamic_slice_in_dim(adapter_set, pair * cols, cols)

    row_pack = row_pack_of(
        mine.reshape(1),
        qkv_lowrank.transpose(0, 1, 3, 2),
        attn_uprank,
        expand_lowrank.transpose(0, 1, 3, 2),
        reduce_uprank,
    )
    col_pack = col_pack_of(
        jnp.concatenate([cols_sets, me.reshape(1)]),
        qkv_uprank,
        attn_lowrank.transpose(0, 2, 1),
        expand_uprank,
        reduce_lowrank.transpose(0, 2, 1),
    )

    place = jnp.stack([pair, col])

    qkv_own, attn_own = first_deal(qkv_weight, attn_weight)
    col_pack = after(col_pack, qkv_own)
    gate_own, qkv_rest, attn_rest, up_own, *others = second_deal(
        qkv_weight, attn_weight, expand_weight, tokens, after(row_pack, qkv_own)
    )
    token_parts = [tokens, *others[:3]]
    row_all = jnp.concatenate([row_pack, *others[3:]], axis=1)
    qkv_low = row_all[:48]
    attn_up = row_all[48:64]
    expand_low = row_all[64:96]
    reduce_up = row_all[96:112]
    qkv_all = gather_col(qkv_own)
    attn_all = gather_col(attn_own)
    gate_all = gather_col(gate_own)
    up_all = gather_col(up_own)
    reduce_own, gate_rest, up_rest, qkv_other, attn_other, col_all, gains = third_deal(
        expand_weight,
        after(reduce_weight, others[0]),
        qkv_all,
        qkv_rest,
        attn_all,
        attn_rest,
        col_pack,
        headnorm_gain,
    )
    reduce_all = gather_col(reduce_own)
    gains = gains.transpose(1, 0, 2).reshape(2, local)

    def own_columns(at, size):
        return col_all[:, :, at : at + size].transpose(1, 0, 2).reshape(16, cols * size)

    qkv_up = [own_columns(i * sub, sub) for i in range(3)]
    attn_low = own_columns(3 * sub, sub)
    expand_up = [own_columns(4 * sub + i * ff_sub, ff_sub) for i in range(2)]
    reduce_low = own_columns(4 * sub + 2 * ff_sub, ff_sub)

    qkv_up = jnp.concatenate(qkv_up)
    qkv_w = merge_qkv(place, qkv_all, qkv_other, qkv_low, qkv_up)
    attn_w = merge_out(place, [attn_all, attn_other], attn_low, attn_up)

    half = HEAD // 2
    freq = THETA ** (-2.0 * jnp.arange(half, dtype=F32) / HEAD)
    angle = jnp.arange(rows, dtype=jnp.int32).astype(F32)[:, None] * freq[None, :]
    cosine = jnp.concatenate([jnp.cos(angle)] * 2, axis=1)
    sine = jnp.sin(angle)
    sine = jnp.concatenate([-sine, sine], axis=1)

    def low_of_parts(low, parts):
        return functools.reduce(
            jnp.add,
            [dot_of(low[:, i * width : (i + 1) * width], parts[i], 1, 1) for i in range(4)],
        )

    raw = project(token_parts, qkv_w, 0, F32)
    squares = jnp.stack(
        [jnp.sum(raw[:, i * local : (i + 1) * local] ** 2, axis=1) for i in range(2)]
    )
    scale = lax.rsqrt(sum_row(squares) / D + EPS)
    query, key, value = rotate_rows(raw, scale.T, gains, cosine, sine)
    mixed, log_total = attend(prefix, query, key, value, 0)
    branch, hidden, branch_stats, *hidden_parts, gate_other, up_other = branch_call(
        mixed, attn_w, tokens, post_gain, (gate_all, gate_rest, up_all, up_rest)
    )
    expand_w = [
        merge_expand(
            place, whole, other, expand_low[16 * i : 16 * i + 16], expand_up[i]
        )
        for i, (whole, other) in enumerate(((gate_all, gate_other), (up_all, up_other)))
    ]
    reduce_w = merge_out(place, [reduce_all], reduce_low, reduce_up)
    act, gate, upper, layer_out, *result_parts = forward_call(
        hidden_parts, *expand_w, reduce_w, hidden, cotangent, post_gain
    )
    d_gate, d_upper, d_hidden, *branch_parts = backward_call(
        result_parts, *expand_w, reduce_w, gate, upper, cotangent, branch, branch_stats, post_gain
    )
    d_mixed = project(branch_parts, attn_w, 1, BF)
    d_query, d_key, d_value, q_sums, k_sums = attend_back(
        prefix, query, d_mixed, mixed, log_total, key, value
    )
    attn_inner = sum_row(dot_of(attn_low, mixed, 1, 1)).astype(BF)
    expand_inner = low_of_parts(expand_low, hidden_parts).astype(BF)
    reduce_inner = sum_row(dot_of(reduce_low, act, 1, 1)).astype(BF)
    g_reduce_up = ADAPTER_FACTOR * dot_of(reduce_inner, result_parts[0], 1, 0)
    d_inner = (ADAPTER_FACTOR * low_of_parts(reduce_up, result_parts)).astype(BF)
    g_reduce_low = dot_of(d_inner, act, 1, 0)
    g_gate_up = ADAPTER_FACTOR * dot_of(expand_inner[:16], d_gate, 1, 0)
    g_upper_up = ADAPTER_FACTOR * dot_of(expand_inner[16:], d_upper, 1, 0)
    d_inner = sum_row(
        ADAPTER_FACTOR
        * jnp.concatenate(
            [dot_of(expand_up[0], d_gate, 1, 1), dot_of(expand_up[1], d_upper, 1, 1)]
        )
    ).astype(BF)
    g_expand_low = dot_of(d_inner, hidden_parts[0], 1, 0)
    g_attn_up = ADAPTER_FACTOR * dot_of(attn_inner, branch_parts[0], 1, 0)
    d_inner = (ADAPTER_FACTOR * low_of_parts(attn_up, branch_parts)).astype(BF)
    g_attn_low = dot_of(d_inner, mixed, 1, 0)

    all_sums = sum_row(jnp.stack([jnp.sum(part[:, 0], axis=0) for part in (q_sums, k_sums)]))
    qkv_inner = low_of_parts(qkv_low, token_parts).astype(BF)
    input_grad, g_qkv_low, g_qkv_up = input_call(
        raw,
        d_query,
        d_key,
        d_value,
        qkv_w,
        d_hidden,
        scale.T,
        (scale * scale * all_sums / D).T,
        gains,
        cosine,
        sine,
        tokens,
        qkv_inner,
        qkv_up,
    )

    def by_col(grad):
        return grad.reshape(16, cols, -1).transpose(1, 0, 2)

    row_pack = jnp.concatenate([g_qkv_low, g_attn_up, g_expand_low, g_reduce_up], axis=0)
    col_pack = jnp.concatenate(
        [
            by_col(grad)
            for grad in (g_qkv_up[:16], g_qkv_up[16:32], g_qkv_up[32:], g_attn_low, g_gate_up, g_upper_up, g_reduce_low)
        ],
        axis=2,
    )
    every_row, every_col = groups_call(row_pack.astype(BF), col_pack.astype(BF))
    row_ids = [
        adapter_set[(pair ^ other) * cols + lax.rem(col - k + cols, cols)]
        for k in range(cols)
        for other in range(2)
    ]
    col_ids = [adapter_set[(pair ^ other) * cols + index] for other in range(2) for index in range(cols)]
    ids = jnp.stack(row_ids + col_ids + [me])
    qkv_low, qkv_up, attn_low, attn_up, expand_low, expand_up, reduce_low, reduce_up = finish_call(
        ids, every_row, every_col, sub, ff_sub
    )
    return (
        layer_out,
        input_grad,
        qkv_low.transpose(0, 1, 3, 2),
        qkv_up,
        attn_low.transpose(0, 2, 1),
        attn_up,
        expand_low.transpose(0, 1, 3, 2),
        expand_up,
        reduce_low.transpose(0, 2, 1),
        reduce_up,
    )


def shards(*arrays):
    whole = (
        lax.axis_size("dp") == 2
        and lax.axis_size("row") == 4
        and arrays[0].shape[0] == SEQUENCE_LENGTH
    )
    return group_shards(*arrays) if whole else general_shards(*arrays)


def solution(mesh):
    placed = (
        P(("dp", "col"), "row"),
        P(("dp", "col"), "row"),
        P(None, "row", "col"),
        P("col", "row"),
        P(None, "row", "col"),
        P("col", "row"),
        P(None, "col"),
        P(None, "row"),
        P(None, None, "row", None),
        P(None, None, None, "col"),
        P(None, "col", None),
        P(None, None, "row"),
        P(None, None, "row", None),
        P(None, None, None, "col"),
        P(None, "col", None),
        P(None, None, "row"),
        P(),
        P(),
    )
    return jax.shard_map(
        shards,
        mesh=mesh,
        in_specs=placed,
        out_specs=(
            P(("dp", "col"), "row"),
            P(("dp", "col"), "row"),
            P(None, None, "row", None),
            P(None, None, None, "col"),
            P(None, "col", None),
            P(None, None, "row"),
            P(None, None, "row", None),
            P(None, None, None, "col"),
            P(None, "col", None),
            P(None, None, "row"),
        ),
        check_vma=False,
    )
```

```python
import functools

import jax
import jax.numpy as jnp
from jax import lax
from jax.experimental import pallas as pl
from jax.experimental.pallas import tpu as pltpu
from jax.sharding import PartitionSpec as P

D = 2048
HEAD = 128
ADAPTER_RANK = 16
SETS = 8
SEQUENCE_LENGTH = 2048


EPS = 1e-06
THETA = 500000.0
ADAPTER_FACTOR = 0.5
NEG = -1e30


def via_col_row(input_rows, weight_matrix, adapt_mat, compute, seq_pick):
    gathered = lax.all_gather(input_rows, "col", axis=0, tiled=True)
    main, inner_value = compute(gathered, weight_matrix, adapt_mat, seq_pick, False)
    return (
        lax.psum_scatter(main, "row", scatter_dimension=0, tiled=True),
        lax.psum_scatter(inner_value, "row", scatter_dimension=0, tiled=True),
    )


def via_row_col(input_rows, weight_matrix, adapt_mat, compute, seq_pick):
    gathered = lax.all_gather(input_rows, "row", axis=0, tiled=True)
    main, inner_value = compute(gathered, weight_matrix, adapt_mat, seq_pick, False)
    return (
        lax.psum_scatter(main, "col", scatter_dimension=0, tiled=True),
        lax.psum_scatter(inner_value, "col", scatter_dimension=0, tiled=True),
    )


def row_total(values):
    return lax.psum(jnp.sum(values, axis=-1), "row")


def head_totals(first, second):
    return lax.psum((jnp.sum(first, axis=-1), jnp.sum(second, axis=-1)), "col")


def sum_col_tokens(values):
    return lax.psum(values.astype(jnp.bfloat16), ("dp", "col")).astype(jnp.float32)


def sum_row_tokens(values):
    return lax.psum(values.astype(jnp.bfloat16), ("dp", "row")).astype(jnp.float32)


def set_rows(group_sets, first_row, item_count):
    sequence = (first_row + jnp.arange(item_count, dtype=jnp.int32)) // SEQUENCE_LENGTH
    member = sequence[:, None] == jnp.arange(group_sets.shape[0], dtype=jnp.int32)[None, :]
    chosen = jnp.sum(jnp.where(member, group_sets[None, :], 0), axis=1)
    return (chosen[:, None] == jnp.arange(SETS, dtype=jnp.int32)[None, :]).astype(jnp.bfloat16)


def widen(inner_value, onehot, part_list):
    rows = inner_value.shape[0]
    spread = onehot[:, None, :, None] * inner_value.reshape(rows, part_list, 1, ADAPTER_RANK)
    return spread.reshape(rows, part_list, SETS * ADAPTER_RANK)


def adapter_in(gathered, pick, lowrank):
    part_list = lowrank.shape[0]
    width_in = lowrank.shape[2]
    item_count = pick.shape[0]
    chosen = jnp.einsum("sk,pkdr->sdpr", pick, lowrank, preferred_element_type=jnp.float32).astype(
        jnp.bfloat16
    )
    chosen = chosen.reshape(item_count, width_in, part_list * ADAPTER_RANK)
    product_value = jnp.einsum(
        "ehm,emx->ehx",
        gathered.reshape(item_count, SEQUENCE_LENGTH, width_in),
        chosen,
        preferred_element_type=jnp.float32,
    )
    return product_value.reshape(item_count * SEQUENCE_LENGTH, part_list * ADAPTER_RANK)


def adapter_back(gathered, pick, upward_rank):
    part_list = upward_rank.shape[0]
    width_out = upward_rank.shape[-1]
    item_count = pick.shape[0]
    chosen = jnp.einsum(
        "sk,pkre->sper", pick, upward_rank, preferred_element_type=jnp.float32
    ).astype(jnp.bfloat16)
    product_value = jnp.einsum(
        "slpe,sper->slpr",
        gathered.reshape(item_count, SEQUENCE_LENGTH, part_list, width_out),
        chosen,
        preferred_element_type=jnp.float32,
    )
    return ADAPTER_FACTOR * product_value.reshape(
        item_count * SEQUENCE_LENGTH, part_list * ADAPTER_RANK
    )


def adapter_out(wide_output, upward_rank):
    part_list = upward_rank.shape[0]
    flat_up = upward_rank.reshape(part_list, SETS * ADAPTER_RANK, upward_rank.shape[-1])
    return ADAPTER_FACTOR * jnp.einsum(
        "tpk,pke->tpe", wide_output, flat_up, preferred_element_type=jnp.float32
    )


def adapter_grad_in(wide_output, lowrank):
    part_list = lowrank.shape[0]
    width_in = lowrank.shape[2]
    flat_low = lowrank.transpose(0, 1, 3, 2).reshape(part_list, SETS * ADAPTER_RANK, width_in)
    return jnp.einsum("tpk,pkd->td", wide_output, flat_low, preferred_element_type=jnp.float32)


def up_grad(wide_output, gradient_list):
    part_list = gradient_list.shape[1]
    total_sum = ADAPTER_FACTOR * jnp.einsum(
        "jox,joq->oxq", wide_output, gradient_list, preferred_element_type=jnp.float32
    )
    return total_sum.reshape(part_list, SETS, ADAPTER_RANK, gradient_list.shape[2])


def low_grad(input_rows, wide_output):
    part_list = wide_output.shape[1]
    total_sum = jnp.einsum(
        "td,tpk->pkd", input_rows, wide_output, preferred_element_type=jnp.float32
    )
    return total_sum.reshape(part_list, SETS, ADAPTER_RANK, input_rows.shape[1]).transpose(
        0, 1, 3, 2
    )


def swiglu(gate, upper):
    return jax.nn.silu(gate) * upper


def norm_back(grad, values, scale, gain):
    weighted = gain * grad
    inner_sum = row_total(weighted * values)
    return scale[:, None] * weighted - values * (scale**3 * inner_sum / D)[:, None]


def qkv_forward(gathered, weight_matrix, low_flat, pick, per_row):
    input_rows = gathered[:, 0]
    main = jnp.einsum("td,pde->tpe", input_rows, weight_matrix, preferred_element_type=jnp.float32)
    lowrank = low_flat.reshape(3, SETS, low_flat.shape[1], ADAPTER_RANK)
    return (main, adapter_in(input_rows, pick, lowrank))


def expand_forward(gathered, weight_matrix, low_flat, pick, per_row):
    input_rows = gathered[:, 0]
    main = jnp.einsum("td,pdf->tpf", input_rows, weight_matrix, preferred_element_type=jnp.float32)
    lowrank = low_flat.reshape(2, SETS, low_flat.shape[1], ADAPTER_RANK)
    return (main, adapter_in(input_rows, pick, lowrank))


def single_forward(gathered, weight_matrix, low_four, pick, per_row):
    input_rows = gathered[:, 0]
    main = jnp.dot(input_rows, weight_matrix[0, 0], preferred_element_type=jnp.float32)
    return (main, adapter_in(input_rows, pick, low_four))


def single_backward(gathered, weight_matrix, up_flat, pick, per_row):
    main = jnp.einsum(
        "te,fe->tf", gathered[:, 0], weight_matrix, preferred_element_type=jnp.float32
    )
    upward_rank = up_flat.reshape(1, SETS, ADAPTER_RANK, up_flat.shape[1])
    return (main, adapter_back(gathered, pick, upward_rank))


def multi_backward(gathered, weight_matrix, up_flat, pick, per_row):
    part_list = weight_matrix.shape[0]
    main = jnp.einsum("tpf,pdf->td", gathered, weight_matrix, preferred_element_type=jnp.float32)
    upward_rank = up_flat.reshape(part_list, SETS, ADAPTER_RANK, up_flat.shape[2])
    return (main, adapter_back(gathered, pick, upward_rank))


def general_shards(
    tokens,
    cotangent,
    qkv_weight,
    attn_weight,
    expand_weight,
    reduce_weight,
    headnorm_gain,
    post_gain,
    qkv_lowrank,
    qkv_uprank,
    attn_lowrank,
    attn_uprank,
    expand_lowrank,
    expand_uprank,
    reduce_lowrank,
    reduce_uprank,
    prefix_length,
    adapter_set,
):
    rows_a = tokens.shape[0]
    group_rows = rows_a * lax.axis_size("col")
    rows_b = group_rows // lax.axis_size("row")
    group_seqs = group_rows // SEQUENCE_LENGTH
    group_first = lax.axis_index("dp") * group_seqs
    group_sets = lax.dynamic_slice_in_dim(adapter_set, group_first, group_seqs)
    group_prefix = lax.dynamic_slice_in_dim(prefix_length, group_first, group_seqs)
    seq_pick = (group_sets[:, None] == jnp.arange(SETS, dtype=jnp.int32)[None, :]).astype(
        jnp.bfloat16
    )
    pick_a = set_rows(group_sets, lax.axis_index("col") * rows_a, rows_a)
    pick_b = set_rows(group_sets, lax.axis_index("row") * rows_b, rows_b)
    width_row = qkv_weight.shape[1]
    width_col = qkv_weight.shape[2]
    ff_col = expand_weight.shape[2]
    qkv_low_flat = qkv_lowrank.reshape(3 * SETS, width_row, ADAPTER_RANK)
    projected, inner_value = via_col_row(
        tokens[:, None], qkv_weight, qkv_low_flat, qkv_forward, seq_pick
    )
    qkv_wide = widen(inner_value.astype(jnp.bfloat16), pick_b, 3)
    projected = projected + adapter_out(qkv_wide, qkv_uprank)
    queries = projected[:, 0]
    keys = projected[:, 1]
    values = projected[:, 2]
    query_sq, key_sq = head_totals(queries * queries, keys * keys)
    query_scale = lax.rsqrt(query_sq / D + EPS)
    key_scale = lax.rsqrt(key_sq / D + EPS)
    query_norm = queries * query_scale[:, None] * headnorm_gain[0]
    key_norm = keys * key_scale[:, None] * headnorm_gain[1]
    local_heads = queries.shape[1] // HEAD
    half = HEAD // 2
    freq = THETA ** (-2.0 * jnp.arange(half, dtype=jnp.float32) / HEAD)
    position = (jnp.arange(rows_b, dtype=jnp.int32) % SEQUENCE_LENGTH).astype(jnp.float32)
    angle = position[:, None] * freq[None, :]
    cosine = jnp.cos(angle)[:, None, :]
    sine = jnp.sin(angle)[:, None, :]

    def rotate(source):
        heads = source.reshape(rows_b, local_heads, HEAD)
        first = heads[..., :half]
        second = heads[..., half:]
        return jnp.concatenate(
            [first * cosine - second * sine, second * cosine + first * sine], axis=-1
        )

    def unrotate(gradient_list):
        first = gradient_list[..., :half]
        second = gradient_list[..., half:]
        return jnp.concatenate(
            [first * cosine + second * sine, second * cosine - first * sine], axis=-1
        ).reshape(rows_b, local_heads * HEAD)

    query_b = rotate(query_norm).astype(jnp.bfloat16)
    key_b = rotate(key_norm).astype(jnp.bfloat16)
    value_b = values.astype(jnp.bfloat16).reshape(rows_b, local_heads, HEAD)
    block = min(512, SEQUENCE_LENGTH)
    blocks = rows_b // block
    key_pos = jnp.arange(SEQUENCE_LENGTH, dtype=jnp.int32)
    local_first = lax.axis_index("row") * (rows_b // SEQUENCE_LENGTH)
    scale = HEAD ** (-0.5)

    def scores_of(index):
        start = index * block
        seq_start = start // SEQUENCE_LENGTH * SEQUENCE_LENGTH
        which = local_first + start // SEQUENCE_LENGTH
        prefix = jnp.sum(
            jnp.where(jnp.arange(group_seqs, dtype=jnp.int32) == which, group_prefix, 0)
        )
        rows = start - seq_start + jnp.arange(block, dtype=jnp.int32)
        allowed = (key_pos[None, :] <= rows[:, None]) | (key_pos[None, :] < prefix)
        query_blk = lax.dynamic_slice_in_dim(query_b, start, block, 0)
        raw = (
            jnp.einsum("qhd,khd->hqk", query_blk, key_b, preferred_element_type=jnp.float32) * scale
        )
        return (jnp.where(allowed[None], raw, NEG), start, seq_start)

    def attend_block(index):
        scores, start, seq_start = scores_of(index)
        top = jnp.max(scores, axis=-1, keepdims=True)
        powers = jnp.exp(scores - top)
        total_sum = jnp.sum(powers, axis=-1, keepdims=True)
        weights = (powers / total_sum).astype(jnp.bfloat16)
        output = jnp.einsum("hqk,khd->qhd", weights, value_b, preferred_element_type=jnp.float32)
        return (output, (top + jnp.log(total_sum))[..., 0])

    attended, logsum = lax.map(attend_block, jnp.arange(blocks, dtype=jnp.int32))
    mixed_b = attended.reshape(rows_b, local_heads * HEAD).astype(jnp.bfloat16)
    attn_weight_four = attn_weight.reshape(1, 1, width_col, width_row)
    attn_low_four = attn_lowrank.reshape(1, SETS, width_col, ADAPTER_RANK)
    branch, inner_value = via_row_col(
        mixed_b[:, None], attn_weight_four, attn_low_four, single_forward, seq_pick
    )
    attn_wide = widen(inner_value.astype(jnp.bfloat16), pick_a, 1)
    branch = branch + adapter_out(attn_wide, attn_uprank[None])[:, 0]
    branch_scale = lax.rsqrt(row_total(branch * branch) / D + EPS)
    hidden = tokens.astype(jnp.float32) + post_gain[0] * branch * branch_scale[:, None]
    hidden_b = hidden.astype(jnp.bfloat16)
    expand_low_flat = expand_lowrank.reshape(2 * SETS, width_row, ADAPTER_RANK)
    gate_up, inner_value = via_col_row(
        hidden_b[:, None], expand_weight, expand_low_flat, expand_forward, seq_pick
    )
    expand_wide = widen(inner_value.astype(jnp.bfloat16), pick_b, 2)
    gate_up = gate_up + adapter_out(expand_wide, expand_uprank)
    gate = gate_up[:, 0]
    upper = gate_up[:, 1]
    act_b = swiglu(gate, upper).astype(jnp.bfloat16)
    reduce_weight_four = reduce_weight.reshape(1, 1, ff_col, width_row)
    reduce_low_four = reduce_lowrank.reshape(1, SETS, ff_col, ADAPTER_RANK)
    result, inner_value = via_row_col(
        act_b[:, None], reduce_weight_four, reduce_low_four, single_forward, seq_pick
    )
    reduce_wide = widen(inner_value.astype(jnp.bfloat16), pick_a, 1)
    result = result + adapter_out(reduce_wide, reduce_uprank[None])[:, 0]
    result_scale = lax.rsqrt(row_total(result * result) / D + EPS)
    layer_out = (hidden + post_gain[1] * result * result_scale[:, None]).astype(jnp.bfloat16)
    incoming = cotangent.astype(jnp.float32)
    d_result = norm_back(incoming, result, result_scale, post_gain[1]).astype(jnp.bfloat16)
    grad_reduce_up = up_grad(reduce_wide, d_result[:, None])[0]
    grad_reduce_up = sum_col_tokens(grad_reduce_up)
    reduce_up_flat = reduce_uprank.reshape(SETS * ADAPTER_RANK, width_row)
    d_act, inner_value = via_col_row(
        d_result[:, None], reduce_weight, reduce_up_flat, single_backward, seq_pick
    )
    act_wide = widen(inner_value.astype(jnp.bfloat16), pick_b, 1)
    d_act = d_act + adapter_grad_in(act_wide, reduce_lowrank[None])
    grad_reduce_low = low_grad(act_b, act_wide)[0]
    grad_reduce_low = sum_row_tokens(grad_reduce_low)
    unused, pullback = jax.vjp(swiglu, gate, upper)
    d_gate, d_upper = pullback(d_act)
    d_gate_up = jnp.stack([d_gate, d_upper], axis=1).astype(jnp.bfloat16)
    grad_expand_up = up_grad(expand_wide, d_gate_up)
    grad_expand_up = sum_row_tokens(grad_expand_up)
    expand_up_flat = expand_uprank.reshape(2 * SETS, ADAPTER_RANK, ff_col)
    d_hidden_in, inner_value = via_row_col(
        d_gate_up, expand_weight, expand_up_flat, multi_backward, seq_pick
    )
    hidden_wide = widen(inner_value.astype(jnp.bfloat16), pick_a, 2)
    d_hidden = incoming + d_hidden_in + adapter_grad_in(hidden_wide, expand_lowrank)
    grad_expand_low = low_grad(hidden_b, hidden_wide)
    grad_expand_low = sum_col_tokens(grad_expand_low)
    d_branch = norm_back(d_hidden, branch, branch_scale, post_gain[0]).astype(jnp.bfloat16)
    grad_attn_up = up_grad(attn_wide, d_branch[:, None])[0]
    grad_attn_up = sum_col_tokens(grad_attn_up)
    attn_up_flat = attn_uprank.reshape(SETS * ADAPTER_RANK, width_row)
    d_mixed, inner_value = via_col_row(
        d_branch[:, None], attn_weight, attn_up_flat, single_backward, seq_pick
    )
    mixed_wide = widen(inner_value.astype(jnp.bfloat16), pick_b, 1)
    d_mixed = (d_mixed + adapter_grad_in(mixed_wide, attn_lowrank[None])).astype(jnp.bfloat16)
    grad_attn_low = low_grad(mixed_b, mixed_wide)[0]
    grad_attn_low = sum_row_tokens(grad_attn_low)
    d_mixed_heads = d_mixed.reshape(rows_b, local_heads, HEAD)

    def back_block(index, carry):
        d_query, d_key, d_value = carry
        scores, start, seq_start = scores_of(index)
        probs = jnp.exp(
            scores - lax.dynamic_index_in_dim(logsum, index, 0, keepdims=False)[..., None]
        )
        grad_blk = lax.dynamic_slice_in_dim(d_mixed_heads, start, block, 0)
        query_blk = lax.dynamic_slice_in_dim(query_b, start, block, 0)
        d_probs = jnp.einsum("qhd,khd->hqk", grad_blk, value_b, preferred_element_type=jnp.float32)
        delta = jnp.sum(probs * d_probs, axis=-1, keepdims=True)
        d_scores = (probs * (d_probs - delta)).astype(jnp.bfloat16)
        query_part = scale * jnp.einsum(
            "hqk,khd->qhd", d_scores, key_b, preferred_element_type=jnp.float32
        )
        key_part = scale * jnp.einsum(
            "hqk,qhd->khd", d_scores, query_blk, preferred_element_type=jnp.float32
        )
        value_part = jnp.einsum(
            "hqk,qhd->khd", probs.astype(jnp.bfloat16), grad_blk, preferred_element_type=jnp.float32
        )
        d_query = lax.dynamic_update_slice_in_dim(d_query, query_part, start, 0)
        d_key = d_key + key_part
        d_value = d_value + value_part
        return (d_query, d_key, d_value)

    zeros = jnp.zeros((rows_b, local_heads, HEAD), jnp.float32)
    d_query, d_key, d_value = lax.fori_loop(0, blocks, back_block, (zeros, zeros, zeros))
    query_weighted = headnorm_gain[0] * unrotate(d_query)
    key_weighted = headnorm_gain[1] * unrotate(d_key)
    query_sum, key_sum = head_totals(query_weighted * queries, key_weighted * keys)
    d_queries = (
        query_scale[:, None] * query_weighted - queries * (query_scale**3 * query_sum / D)[:, None]
    )
    d_keys = key_scale[:, None] * key_weighted - keys * (key_scale**3 * key_sum / D)[:, None]
    d_qkv = jnp.stack(
        [d_queries, d_keys, d_value.reshape(rows_b, local_heads * HEAD)], axis=1
    ).astype(jnp.bfloat16)
    grad_qkv_up = up_grad(qkv_wide, d_qkv)
    grad_qkv_up = sum_row_tokens(grad_qkv_up)
    qkv_up_flat = qkv_uprank.reshape(3 * SETS, ADAPTER_RANK, width_col)
    d_tokens_in, inner_value = via_row_col(d_qkv, qkv_weight, qkv_up_flat, multi_backward, seq_pick)
    tokens_wide = widen(inner_value.astype(jnp.bfloat16), pick_a, 3)
    input_grad = d_hidden + d_tokens_in + adapter_grad_in(tokens_wide, qkv_lowrank)
    grad_qkv_low = low_grad(tokens, tokens_wide)
    grad_qkv_low = sum_col_tokens(grad_qkv_low)
    return (
        layer_out,
        input_grad,
        grad_qkv_low,
        grad_qkv_up,
        grad_attn_low,
        grad_attn_up,
        grad_expand_low,
        grad_expand_up,
        grad_reduce_low,
        grad_reduce_up,
    )


LOG2E = 1.4426950408889634
Q_BLOCK = 512
K_BLOCK = 512
HEADS_AT_ONCE = 2
BF = jnp.bfloat16
F32 = jnp.float32


def dot_of(left, right, left_dim, right_dim, out=F32):
    return lax.dot_general(
        left, right, (((left_dim,), (right_dim,)), ((), ())), preferred_element_type=out
    )


def attend_rows(query, limit, key_of, value_of, blocks):
    rows = query.shape[0]
    key_pos = lax.broadcasted_iota(jnp.int32, (K_BLOCK, rows), 0)

    def body(index, carry):
        top, total, mixed = carry
        at = pl.multiple_of(index * K_BLOCK, K_BLOCK)
        scores = dot_of(key_of(at), query, 1, 1) * (HEAD**-0.5 * LOG2E)
        scores = jnp.where(key_pos <= limit - at, scores, NEG)
        top_now = jnp.maximum(top, jnp.max(scores, axis=0, keepdims=True))
        fade = jnp.exp2(top - top_now)
        powers = jnp.exp2(scores - top_now)
        total = fade * total + jnp.sum(powers, axis=0, keepdims=True)
        mixed = mixed * fade + dot_of(value_of(at), powers.astype(BF), 0, 0)
        return top_now, total, mixed

    top, total, mixed = lax.fori_loop(
        0,
        blocks,
        body,
        (
            jnp.full((1, rows), NEG, F32),
            jnp.zeros((1, rows), F32),
            jnp.zeros((HEAD, rows), F32),
        ),
    )
    return mixed / total, top + jnp.log2(total)


def row_sums(values):
    return lax.dot_general(
        jnp.ones((8, values.shape[1]), F32),
        values,
        (((1,), (1,)), ((), ())),
        precision=lax.Precision.HIGHEST,
        preferred_element_type=F32,
    )[0:1]


def attend_back_kernel(
    prefix_ref,
    q_ref,
    grad_ref,
    out_ref,
    log_ref,
    k_ref,
    v_ref,
    dq_ref,
    dk_ref,
    dv_ref,
    q_sum_ref,
    k_sum_ref,
):
    rows = q_ref.shape[0]
    start = pl.program_id(1) * rows
    prefix = prefix_ref[0]
    blocks = lax.div(jnp.maximum(start + rows, prefix) + K_BLOCK - 1, K_BLOCK)

    @pl.when(pl.program_id(1) == 0)
    def _():
        dk_ref[...] = jnp.zeros_like(dk_ref)
        dv_ref[...] = jnp.zeros_like(dv_ref)

    limit = jnp.maximum(lax.broadcasted_iota(jnp.int32, (1, rows), 1) + start, prefix - 1)
    key_pos = lax.broadcasted_iota(jnp.int32, (K_BLOCK, rows), 0)
    heads = [slice(h * HEAD, (h + 1) * HEAD) for h in range(HEADS_AT_ONCE)]
    deltas = [
        row_sums(grad_ref[:, lanes].astype(F32) * out_ref[:, lanes].astype(F32)) for lanes in heads
    ]

    def body(index, carry):
        at = pl.multiple_of(index * K_BLOCK, K_BLOCK)
        span = pl.ds(at, K_BLOCK)
        seen = key_pos <= limit - at
        sums = []
        for h, lanes in enumerate(heads):
            query, grad, key = q_ref[:, lanes], grad_ref[:, lanes], k_ref[span, lanes]
            scores = dot_of(key, query, 1, 1) * (HEAD**-0.5 * LOG2E)
            probs = jnp.where(seen, jnp.exp2(scores - log_ref[h]), 0.0)
            d_probs = dot_of(v_ref[span, lanes], grad, 1, 1)
            d_scores = (probs * (d_probs - deltas[h])).astype(BF)
            dv_ref[span, lanes] += dot_of(probs.astype(BF), grad, 1, 0)
            dk_ref[span, lanes] += dot_of(d_scores, query, 1, 0)
            sums.append(carry[h] + dot_of(d_scores, key, 0, 0))
        return tuple(sums)

    d_queries = lax.fori_loop(0, blocks, body, (jnp.zeros((rows, HEAD), F32),) * len(heads))
    for h, lanes in enumerate(heads):
        d_query = d_queries[h] * HEAD**-0.5
        dq_ref[:, lanes] = d_query
        q_sum_ref[h] = row_sums(d_query * q_ref[:, lanes].astype(F32))

    @pl.when(pl.program_id(1) == pl.num_programs(1) - 1)
    def _():
        for h, lanes in enumerate(heads):
            d_key = dk_ref[:, lanes] * HEAD**-0.5
            dk_ref[:, lanes] = d_key
            k_sum_ref[h] = row_sums(d_key * k_ref[:, lanes].astype(F32))


def attend_back(prefix, query, grad, mixed, log_total, key, value):
    rows, length, heads = query.shape[0], key.shape[0], query.shape[1] // HEAD
    wide = HEADS_AT_ONCE * HEAD
    q_spec = pl.BlockSpec((Q_BLOCK, wide), lambda h, i, p: (i, h))
    k_spec = pl.BlockSpec((length, wide), lambda h, i, p: (0, h))
    row_spec = pl.BlockSpec((HEADS_AT_ONCE, 1, Q_BLOCK), lambda h, i, p: (h, 0, i))
    return pl.pallas_call(
        attend_back_kernel,
        out_shape=(
            jax.ShapeDtypeStruct(query.shape, F32),
            jax.ShapeDtypeStruct(key.shape, F32),
            jax.ShapeDtypeStruct(key.shape, F32),
            jax.ShapeDtypeStruct((heads, 1, rows), F32),
            jax.ShapeDtypeStruct((heads, 1, length), F32),
        ),
        grid_spec=pltpu.PrefetchScalarGridSpec(
            num_scalar_prefetch=1,
            grid=(heads // HEADS_AT_ONCE, rows // Q_BLOCK),
            in_specs=[q_spec, q_spec, q_spec, row_spec, k_spec, k_spec],
            out_specs=[
                q_spec,
                k_spec,
                k_spec,
                row_spec,
                pl.BlockSpec((HEADS_AT_ONCE, 1, length), lambda h, i, p: (h, 0, 0)),
            ],
        ),
        cost_estimate=pl.CostEstimate(
            flops=7 * rows * length * heads * HEAD,
            bytes_accessed=24 * rows * heads * HEAD,
            transcendentals=rows * length * heads,
        ),
        name="attend_back",
    )(prefix, query, grad, mixed, log_total, key, value)


def rotate_kernel(raw_ref, scale_ref, gain_ref, cos_ref, sin_ref, q_ref, k_ref, v_ref):
    width = q_ref.shape[1]
    cosine = cos_ref[...]
    sine = sin_ref[...]
    scales = scale_ref[...]
    for part, out in ((0, q_ref), (1, k_ref)):
        scale = column_of(scales, part)
        for at in range(0, width, HEAD):
            normed = raw_ref[:, part * width + at : part * width + at + HEAD] * scale
            normed = normed * gain_ref[part : part + 1, at : at + HEAD]
            turned = normed * cosine + pltpu.roll(normed, HEAD // 2, 1) * sine
            out[:, at : at + HEAD] = turned.astype(BF)
    v_ref[...] = raw_ref[:, 2 * width :].astype(BF)


def rotate_rows(raw, scales, gains, cosine, sine):
    rows, width = raw.shape[0], raw.shape[1] // 3
    step = min(512, rows)
    out_spec = pl.BlockSpec((step, width), lambda i: (i, 0))
    table = pl.BlockSpec((step, HEAD), lambda i: (i, 0))
    return pl.pallas_call(
        rotate_kernel,
        out_shape=(jax.ShapeDtypeStruct((rows, width), BF),) * 3,
        grid=(rows // step,),
        in_specs=[
            pl.BlockSpec((step, 3 * width), lambda i: (i, 0)),
            pl.BlockSpec((8, step), lambda i: (0, i)),
            pl.BlockSpec((2, width), lambda i: (0, 0)),
            table,
            table,
        ],
        out_specs=[out_spec] * 3,
        name="rotate_rows",
    )(raw, scales, gains, cosine, sine)


def row_pack_kernel(set_ref, qkv_ref, attn_ref, expand_ref, reduce_ref, out_ref):
    for part in range(3):
        out_ref[16 * part : 16 * part + 16, :] = qkv_ref[part, 0]
    out_ref[48:64, :] = attn_ref[0]
    for part in range(2):
        out_ref[64 + 16 * part : 80 + 16 * part, :] = expand_ref[part, 0]
    out_ref[96:112, :] = reduce_ref[0]


def row_pack_of(which, qkv_low, attn_up, expand_low, reduce_up):
    width = attn_up.shape[2]
    one = pl.BlockSpec((1, 16, width), lambda i, c: (c[0], 0, 0))

    def many(parts):
        return pl.BlockSpec((parts, 1, 16, width), lambda i, c: (0, c[0], 0, 0))

    return pl.pallas_call(
        row_pack_kernel,
        out_shape=jax.ShapeDtypeStruct((112, width), BF),
        grid_spec=pltpu.PrefetchScalarGridSpec(
            num_scalar_prefetch=1,
            grid=(1,),
            in_specs=[many(3), one, many(2), one],
            out_specs=pl.BlockSpec((112, width), lambda i, c: (0, 0)),
        ),
        name="row_pack",
    )(which, qkv_low, attn_up, expand_low, reduce_up)


def col_pack_kernel(set_ref, qkv_ref, attn_ref, expand_ref, reduce_ref, out_ref):
    sub, ff_sub = qkv_ref.shape[3], expand_ref.shape[3]
    for part in range(3):
        out_ref[0, :, part * sub : (part + 1) * sub] = qkv_ref[part, 0]
    at = 4 * sub
    out_ref[0, :, 3 * sub : at] = attn_ref[0]
    for part in range(2):
        out_ref[0, :, at : at + ff_sub] = expand_ref[part, 0]
        at += ff_sub
    out_ref[0, :, at:] = reduce_ref[0]


def col_pack_of(which, qkv_up, attn_low, expand_up, reduce_low):
    cols = which.shape[0] - 1
    sub, ff_sub = qkv_up.shape[3] // 4, expand_up.shape[3] // 4

    def many(parts, size):
        return pl.BlockSpec((parts, 1, 16, size), lambda i, c: (0, c[i], 0, c[cols]))

    def one(size):
        return pl.BlockSpec((1, 16, size), lambda i, c: (c[i], 0, c[cols]))

    total = 4 * sub + 3 * ff_sub
    return pl.pallas_call(
        col_pack_kernel,
        out_shape=jax.ShapeDtypeStruct((cols, 16, total), BF),
        grid_spec=pltpu.PrefetchScalarGridSpec(
            num_scalar_prefetch=1,
            grid=(cols,),
            in_specs=[many(3, sub), one(sub), many(2, ff_sub), one(ff_sub)],
            out_specs=pl.BlockSpec((1, 16, total), lambda i, c: (i, 0, 0)),
        ),
        name="col_pack",
    )(which, qkv_up, attn_low, expand_up, reduce_low)


def finish_kernel(ids_ref, rows_ref, cols_ref, *outs):
    qkv_low, qkv_up, attn_low, attn_up, expand_low, expand_up, reduce_low, reduce_up = outs
    cols = cols_ref.shape[2]
    groups = 2 * cols
    here = pl.program_id(0)
    me = ids_ref[2 * groups]

    def weight(index):
        return (ids_ref[index] == here).astype(F32)

    total = jnp.zeros(rows_ref.shape[2:], F32)
    for k in range(cols):
        for other in range(2):
            total = total + weight(2 * k + other) * rows_ref[k, other].astype(F32)
    for part in range(3):
        qkv_low[part, 0] = total[16 * part : 16 * part + 16]
    attn_up[0] = total[48:64]
    for part in range(2):
        expand_low[part, 0] = total[64 + 16 * part : 80 + 16 * part]
    reduce_up[0] = total[96:112]
    sub = qkv_up.shape[3] // 4
    ff_sub = expand_up.shape[3] // 4
    for row in range(4):
        block = me ^ row
        total = jnp.zeros(cols_ref.shape[3:], F32)
        for other in range(2):
            for index in range(cols):
                one = cols_ref[block, other, index].astype(F32)
                total = total + weight(groups + other * cols + index) * one
        near = slice(row * sub, (row + 1) * sub)
        wide = slice(row * ff_sub, (row + 1) * ff_sub)
        for part in range(3):
            qkv_up[part, 0, :, near] = total[:, part * sub : (part + 1) * sub]
        attn_low[0, :, near] = total[:, 3 * sub : 4 * sub]
        for part in range(2):
            at = 4 * sub + part * ff_sub
            expand_up[part, 0, :, wide] = total[:, at : at + ff_sub]
        reduce_low[0, :, wide] = total[:, 4 * sub + 2 * ff_sub :]


def finish_call(ids, rows, cols, sub, ff_sub):
    width = rows.shape[3]
    shapes = [
        (3, width),
        (3, 4 * sub),
        (0, 4 * sub),
        (0, width),
        (2, width),
        (2, 4 * ff_sub),
        (0, 4 * ff_sub),
        (0, width),
    ]
    out_shape, out_specs = [], []
    for parts, size in shapes:
        if parts:
            out_shape.append(jax.ShapeDtypeStruct((parts, SETS, 16, size), F32))
            out_specs.append(pl.BlockSpec((parts, 1, 16, size), lambda k, c: (0, k, 0, 0)))
        else:
            out_shape.append(jax.ShapeDtypeStruct((SETS, 16, size), F32))
            out_specs.append(pl.BlockSpec((1, 16, size), lambda k, c: (k, 0, 0)))

    def whole(array):
        return pl.BlockSpec(array.shape, lambda k, c: (0,) * array.ndim)

    return pl.pallas_call(
        finish_kernel,
        out_shape=out_shape,
        grid_spec=pltpu.PrefetchScalarGridSpec(
            num_scalar_prefetch=1,
            grid=(SETS,),
            in_specs=[whole(rows), whole(cols)],
            out_specs=out_specs,
        ),
        name="finish",
    )(ids, rows, cols)


def cost_of(flops, bytes_accessed):
    return pl.CostEstimate(flops=int(flops), bytes_accessed=int(bytes_accessed), transcendentals=0)


def row_tile(rows):
    return min(512, rows)


def merge_rows_kernel(pair_ref, own_ref, other_ref, low_ref, up_ref, out_ref):
    def put(piece):
        for block in range(4):
            base = piece[0, block].astype(F32)
            extra = dot_of(low_ref[block, 0], up_ref[...], 0, 0)
            out_ref[block, 0] = (base + ADAPTER_FACTOR * extra).astype(BF)

    mine = pl.program_id(0) == pair_ref[0]
    pl.when(mine)(functools.partial(put, own_ref))
    pl.when(jnp.logical_not(mine))(functools.partial(put, other_ref))


def merge_qkv_kernel(pair_ref, own_ref, other_ref, low_ref, up_ref, out_ref):
    cols, sub = own_ref.shape[0], own_ref.shape[4]

    def put(piece, back):
        for block in range(4):
            extra = dot_of(low_ref[block, 0], up_ref[...], 0, 0)
            for index in range(cols):
                at = lax.rem(index - back + cols, cols)
                lanes = slice(index * sub, (index + 1) * sub)
                base = piece[at, block, 0].astype(F32)
                out_ref[block, 0, :, lanes] = (base + ADAPTER_FACTOR * extra[:, lanes]).astype(BF)

    mine = pl.program_id(0) == pair_ref[0]
    pl.when(mine)(functools.partial(put, own_ref, 0))
    pl.when(jnp.logical_not(mine))(functools.partial(put, other_ref, pair_ref[1]))


def merge_columns_kernel(pair_ref, *refs):
    *pieces, low_ref, up_ref, out_ref = refs
    width = out_ref.shape[1] // 4

    def put(piece):
        for block in range(4):
            span = slice(block * width, (block + 1) * width)
            extra = dot_of(low_ref[0], up_ref[:, span], 0, 0)
            out_ref[:, span] = (piece[0, block].astype(F32) + ADAPTER_FACTOR * extra).astype(BF)

    if len(pieces) == 1:
        put(pieces[0])
        return
    mine = pl.program_id(0) == pair_ref[0]
    pl.when(mine)(functools.partial(put, pieces[0]))
    pl.when(jnp.logical_not(mine))(functools.partial(put, pieces[1]))


def merge_qkv(pair, own, other, low, up):
    cols, _, parts, cut, sub = own.shape

    def piece(half):
        def place(h, p, pair_ref):
            mine = h == half(pair_ref[0])
            return (0, 0, jnp.where(mine, p, jnp.where(h == 0, 0, parts - 1)), 0, 0)

        return pl.BlockSpec((cols, 4, 1, cut, sub), place)

    whole = pl.pallas_call(
        merge_qkv_kernel,
        out_shape=jax.ShapeDtypeStruct((4, 2, cut, parts * cols * sub), BF),
        grid_spec=pltpu.PrefetchScalarGridSpec(
            num_scalar_prefetch=1,
            grid=(2, parts),
            in_specs=[
                piece(lambda one: one),
                piece(lambda one: 1 - one),
                pl.BlockSpec((4, 1, 16, cut), lambda h, p, one: (0, h, p, 0)),
                pl.BlockSpec((16, cols * sub), lambda h, p, one: (p, 0)),
            ],
            out_specs=pl.BlockSpec((4, 1, cut, cols * sub), lambda h, p, one: (0, h, 0, p)),
        ),
        cost_estimate=cost_of(0, 8 * own.size),
        name="merge_qkv",
    )(pair, own, other, low.reshape(16 * parts, 4, 2, cut).transpose(1, 2, 0, 3), up)
    return whole.reshape(8 * cut, parts * cols * sub)


def half_specs(block, cols):
    def piece(half, relative):
        def place(h, c, pair_ref):
            at = jnp.where(h == half(pair_ref[0]), c, jnp.where(h == 0, 0, cols - 1))
            if relative:
                at = lax.rem(at - pair_ref[1] + cols, cols)
            return (at,) + (0,) * (len(block) - 1)

        return pl.BlockSpec(block, place)

    return [piece(lambda one: one, False), piece(lambda one: 1 - one, True)]


def merge_expand(pair, own, other, low, up):
    cols, _, width, cut = own.shape
    whole = pl.pallas_call(
        merge_rows_kernel,
        out_shape=jax.ShapeDtypeStruct((4, 1, width, 2 * cols * cut), BF),
        grid_spec=pltpu.PrefetchScalarGridSpec(
            num_scalar_prefetch=1,
            grid=(2, cols),
            in_specs=half_specs((1, 4, width, cut), cols)
            + [
                pl.BlockSpec((4, 1, 16, width), lambda h, c, one: (0, 0, 0, 0)),
                pl.BlockSpec((16, cut), lambda h, c, one: (0, 2 * c + h)),
            ],
            out_specs=pl.BlockSpec((4, 1, width, cut), lambda h, c, one: (0, 0, 0, 2 * c + h)),
        ),
        cost_estimate=cost_of(0, 8 * own.size),
        name="merge_expand",
    )(pair, own, other, low.reshape(16, 4, 1, width).transpose(1, 2, 0, 3), up)
    return whole.reshape(4 * width, 2 * cols * cut)


def merge_out(pair, pieces, low, up):
    cols, _, rows, width = pieces[0].shape
    takes = len(pieces)
    block = (1, 4, rows, width)
    specs = half_specs(block, cols)
    if takes == 1:
        specs = [pl.BlockSpec(block, lambda h, c, one: (c, 0, 0, 0))]
    return pl.pallas_call(
        merge_columns_kernel,
        out_shape=jax.ShapeDtypeStruct((takes * cols * rows, 4 * width), BF),
        grid_spec=pltpu.PrefetchScalarGridSpec(
            num_scalar_prefetch=1,
            grid=(takes, cols),
            in_specs=specs
            + [
                pl.BlockSpec((1, 16, rows), lambda h, c, one: (takes * c + h, 0, 0)),
                pl.BlockSpec((16, 4 * width), lambda h, c, one: (0, 0)),
            ],
            out_specs=pl.BlockSpec((rows, 4 * width), lambda h, c, one: (takes * c + h, 0)),
        ),
        cost_estimate=cost_of(0, 4 * takes * pieces[0].size),
        name="merge_out",
    )(pair, *pieces, low.reshape(16, takes * cols, rows).transpose(1, 0, 2), up)


def mixed_back_kernel(x0, x1, x2, x3, matrix_ref, up_ref, out_ref, inner_ref):
    left = jnp.concatenate([x0[...], x1[...], x2[...], x3[...]], axis=1)
    out_ref[...] = dot_of(left, matrix_ref[...], 1, 1).astype(BF)
    inner_ref[...] = (ADAPTER_FACTOR * dot_of(up_ref[...], left, 1, 1)).astype(BF)


def mixed_back(lefts, matrix, up):
    rows, width = lefts[0].shape
    local = matrix.shape[0]
    tile = row_tile(rows)

    def whole(array):
        return pl.BlockSpec(array.shape, lambda m: (0, 0))

    return pl.pallas_call(
        mixed_back_kernel,
        out_shape=[
            jax.ShapeDtypeStruct((rows, local), BF),
            jax.ShapeDtypeStruct((16, rows), BF),
        ],
        grid=(rows // tile,),
        in_specs=[pl.BlockSpec((tile, width), lambda m: (m, 0))] * 4 + [whole(matrix), whole(up)],
        out_specs=[
            pl.BlockSpec((tile, local), lambda m: (m, 0)),
            pl.BlockSpec((16, tile), lambda m: (0, m)),
        ],
        cost_estimate=cost_of(8 * rows * width * local, 8 * width * (rows + local)),
        name="mixed_back",
    )(*lefts, matrix, up)


BLOCK = 256
RING = 5


def peer(step):
    return {"row": lax.axis_index("row") ^ step}


def send(source, target, sems, index, step):
    return pltpu.make_async_remote_copy(
        src_ref=source,
        dst_ref=target,
        send_sem=sems.at[0, index],
        recv_sem=sems.at[1, index],
        device_id=peer(step),
        device_id_type=pl.DeviceIdType.MESH,
    )


def greet():
    barrier = pltpu.get_barrier_semaphore()
    for step in (1, 2, 3):
        pl.semaphore_signal(
            barrier, inc=1, device_id=peer(step), device_id_type=pl.DeviceIdType.MESH
        )
    pl.semaphore_wait(barrier, 3)


def exchange_scratch(count, width, gathers):
    sem = pltpu.SemaphoreType.DMA((2, count))
    shapes = [
        pltpu.VMEM((2, 2, BLOCK, width), BF),
        pltpu.VMEM((count, 2, BLOCK, width), BF),
        pltpu.VMEM((2, BLOCK, width), F32),
        pltpu.VMEM((2, BLOCK, width), BF),
        pltpu.VMEM((count, BLOCK, width), BF),
        pltpu.VMEM((RING, BLOCK, width), F32),
        sem,
        sem,
    ]
    if gathers:
        shapes += [
            pltpu.VMEM((count, 8, BLOCK), F32),
            pltpu.VMEM((3, count, 8, BLOCK), F32),
        ] + [sem] * 6
    return shapes


def run_blocks(count, bufs, compute, stats, finish, own_ref=None, arrived=None, extra=None):
    pair_out, pair_in, far, side_out, side_in, near, pair_sem, side_sem, *rest = bufs
    gathers = own_ref is not None
    if gathers:
        stat_own, stat_in, stat_1, stat_2, stat_3, core_sem, far_sem, relay_sem = rest
        stat_sems = (stat_1, stat_2, stat_3)

    def rows_of(c):
        return pl.ds(pl.multiple_of(c * BLOCK, BLOCK), BLOCK)

    def to_core(c):
        return send(pair_out.at[lax.rem(c, 2)], pair_in.at[c], pair_sem, c, 1)

    def to_side(c):
        return send(side_out.at[lax.rem(c, 2)], side_in.at[c], side_sem, c, 2)

    def to_stat(c, step):
        return send(stat_own.at[c], stat_in.at[step - 1, c], stat_sems[step - 1], c, step)

    def gather_core(c):
        return send(own_ref.at[rows_of(c)], arrived[0].at[rows_of(c)], core_sem, c, 1)

    def gather_side(c):
        return send(own_ref.at[rows_of(c)], arrived[1].at[rows_of(c)], far_sem, c, 2)

    def relay(c):
        return send(arrived[1].at[rows_of(c)], arrived[2].at[rows_of(c)], relay_sem, c, 1)

    def stage(c, body):
        pl.when(jnp.logical_and(c >= 0, c < count))(functools.partial(body, c))

    def multiply(c):
        @pl.when(c >= 2)
        def _():
            to_core(c - 2).wait_send()

        slot = lax.rem(c, 2)

        def put(block, value):
            if block == 0:
                near[lax.rem(c, RING)] = value
            elif block == 2:
                far[slot] = value
            else:
                pair_out[slot, block // 2] = value.astype(BF)
            if block == 3:
                to_core(c).start()

        compute(c, put)

    def sum_core(c):
        @pl.when(c >= 2)
        def _():
            to_side(c - 2).wait_send()

        to_core(c).wait_recv()
        slot = lax.rem(c, 2)
        side_out[slot] = (far[slot] + pair_in[c, 1].astype(F32)).astype(BF)
        to_side(c).start()
        at = lax.rem(c, RING)
        near[at] = near[at] + pair_in[c, 0].astype(F32)
        if extra is not None:
            extra[0](c)

    def sum_side(c):
        if extra is not None:
            extra[1](c)
        to_side(c).wait_recv()
        at = lax.rem(c, RING)
        total = near[at] + side_in[c].astype(F32)
        if not gathers:
            finish(c, rows_of(c), total)
            return
        near[at] = total
        stat_own[c] = stats(c, rows_of(c), total)
        for step in (1, 2, 3):
            to_stat(c, step).start()

    def normalise(c):
        total = stat_own[c]
        for step in (1, 2, 3):
            to_stat(c, step).wait_recv()
            total = total + stat_in[step - 1, c]
        own_ref[rows_of(c), :] = finish(c, rows_of(c), near[lax.rem(c, RING)], total)
        gather_side(c).start()
        gather_core(c).start()

    def pass_on(c):
        gather_side(c).wait_recv()
        relay(c).start()

    def body(t, carry):
        stage(t - 1, sum_core)
        stage(t, multiply)
        stage(t - 2, sum_side)
        if gathers:
            stage(t - 3, normalise)
            stage(t - 4, pass_on)
        return carry

    lax.fori_loop(0, count + (4 if gathers else 2), body, 0)

    def close(c, carry):
        if gathers:
            for step in (1, 2, 3):
                to_stat(c, step).wait_send()
            gather_core(c).wait()
            gather_side(c).wait_send()
            relay(c).wait()
        return carry

    if gathers:
        lax.fori_loop(0, count, close, 0)
    for c in range(max(count - 2, 0), count):
        to_core(c).wait_send()
        to_side(c).wait_send()


def sums_of(*values):
    out = None
    for index, value in enumerate(values):
        pick = lax.broadcasted_iota(jnp.int32, (8, value.shape[1]), 0) == index
        term = lax.dot_general(
            pick.astype(F32),
            value,
            (((1,), (1,)), ((), ())),
            precision=lax.Precision.HIGHEST,
            preferred_element_type=F32,
        )
        out = term if out is None else out + term
    return out


def column_of(stats, index):
    pick = lax.broadcasted_iota(jnp.int32, (8, HEAD), 0) == index
    wide = lax.dot_general(
        stats,
        pick.astype(F32),
        (((0,), (0,)), ((), ())),
        precision=lax.Precision.HIGHEST,
        preferred_element_type=F32,
    )
    return wide[:, :1]


def branch_kernel(
    q_ref,
    k_ref,
    v_ref,
    limit_ref,
    matrix_ref,
    tokens_ref,
    gain_ref,
    gate_all,
    gate_part,
    upper_all,
    upper_rest,
    mixed_ref,
    log_ref,
    branch_ref,
    hidden_ref,
    stat_ref,
    own_ref,
    *rest,
):
    arrived, halves, rest = rest[:3], rest[3:5], rest[5:]
    swap_sems, local_sem, *bufs = rest
    width = own_ref.shape[1]
    count = own_ref.shape[0] // BLOCK
    greet_all([peer(step) for step in (1, 2, 3)] + [other_of_pair()])
    later = range(2, gate_all.shape[0])
    swaps = exchange_halves(
        gate_all, None, halves[0], swap_sems.at[0], local_sem.at[0], later
    )
    swaps += exchange_halves(upper_all, upper_rest, halves[1], swap_sems.at[1], local_sem.at[1])
    for copy in swaps:
        copy.start()

    heads = log_ref.shape[0]

    def attend(group):
        rows = span_of(group, Q_BLOCK)
        reach = jnp.maximum((group + 1) * Q_BLOCK, SEQUENCE_LENGTH // 2)

        def head(h, carry):
            lanes = span_of(h, HEAD)
            mixed, logs = attend_rows(
                q_ref[rows, lanes],
                limit_ref[:, rows],
                lambda at: k_ref[pl.ds(at, K_BLOCK), lanes],
                lambda at: v_ref[pl.ds(at, K_BLOCK), lanes],
                reach // K_BLOCK,
            )
            mixed_ref[rows, lanes] = mixed.T.astype(BF)
            log_ref[h, :, rows] = logs
            return carry

        lax.fori_loop(0, heads, head, 0)

    def compute(c, put):
        ratio = Q_BLOCK // BLOCK
        pl.when(lax.rem(c, ratio) == 0)(lambda: attend(c // ratio))
        left = mixed_ref[pl.ds(pl.multiple_of(c * BLOCK, BLOCK), BLOCK), :]
        for block in (1, 3, 2, 0):
            put(block, dot_of(left, matrix_ref[:, block * width : (block + 1) * width], 1, 0))

    def stats(c, rows, branch):
        branch_ref[rows, :] = branch
        return sums_of(branch * branch)

    def finish(c, rows, branch, total):
        stat_ref[c] = total
        scale = lax.rsqrt(column_of(total, 0) / D + EPS)
        hidden = tokens_ref[rows, :].astype(F32) + gain_ref[0:1, :] * branch * scale
        hidden_ref[rows, :] = hidden
        return hidden.astype(BF)

    run_blocks(count, bufs, compute, stats, finish, own_ref, arrived)
    wait_all(swaps)


VMEM_SPEC = pl.BlockSpec(memory_space=pltpu.VMEM)
ANY_SPEC = pl.BlockSpec(memory_space=pl.ANY)


def talk_params(number):
    return pltpu.CompilerParams(
        collective_id=number, has_side_effects=True, vmem_limit_bytes=63 * 2**20
    )


def branch_call(query, key, value, limit, matrix, tokens, gain, halves):
    rows, width = tokens.shape
    local = query.shape[1]
    count = rows // BLOCK
    cols = halves[0].shape[0]
    part = jax.ShapeDtypeStruct((rows, width), BF)
    whole = jax.ShapeDtypeStruct((rows, width), F32)
    half = jax.ShapeDtypeStruct(halves[0].shape, BF)
    return pl.pallas_call(
        branch_kernel,
        out_shape=[
            jax.ShapeDtypeStruct((rows, local), BF),
            jax.ShapeDtypeStruct((local // HEAD, 1, rows), F32),
            whole,
            whole,
            jax.ShapeDtypeStruct((count, 8, BLOCK), F32),
        ]
        + [part] * 4
        + [half] * 2,
        in_specs=[VMEM_SPEC] * 7 + [ANY_SPEC] * 4,
        out_specs=[VMEM_SPEC] * 6 + [ANY_SPEC] * 5,
        scratch_shapes=[
            pltpu.SemaphoreType.DMA((2, 2, cols - 1)),
            pltpu.SemaphoreType.DMA((2,)),
        ]
        + exchange_scratch(count, width, True),
        input_output_aliases={8: 9},
        compiler_params=talk_params(0),
        cost_estimate=cost_of(8 * rows * width * matrix.shape[0], 2**27),
        name="branch",
    )(query, key, value, limit, matrix, tokens, gain, *halves)


def load_lefts(lefts, buffer, sems, count):
    width = buffer.shape[2] // 4

    def copies(c):
        slot = lax.rem(c, 2)
        rows = pl.ds(pl.multiple_of(c * BLOCK, BLOCK), BLOCK)
        return [
            pltpu.make_async_copy(
                left.at[rows], buffer.at[slot, :, index * width : (index + 1) * width], sems.at[slot, index]
            )
            for index, left in enumerate(lefts)
        ]

    def start(c):
        @pl.when(c < count)
        def _():
            for copy in copies(c):
                copy.start()

    def wait(c):
        for copy in copies(c):
            copy.wait()

    return start, wait


def move_rows(outer, buffer, sems, index, inward):
    def copy(c):
        slot = lax.rem(c, 2)
        rows = pl.ds(pl.multiple_of(c * BLOCK, BLOCK), BLOCK)
        ends = (outer.at[rows], buffer.at[slot])
        if not inward:
            ends = ends[::-1]
        return pltpu.make_async_copy(*ends, sems.at[index, slot])

    return copy


def forward_kernel(
    x0,
    x1,
    x2,
    x3,
    gate_hbm,
    upper_hbm,
    reduce_hbm,
    hidden_ref,
    cot_ref,
    gain_ref,
    expand_low_ref,
    reduce_low_ref,
    act_out,
    gate_out,
    upper_out,
    layer_ref,
    expand_inner_ref,
    reduce_inner_ref,
    own_ref,
    *rest,
):
    arrived, rest = rest[:3], rest[3:]
    gate_w, upper_w, reduce_w, lefts, act_buf, gate_buf, upper_buf, w_sem, x_sem, o_sem, *bufs = rest
    width = own_ref.shape[1]
    count = own_ref.shape[0] // BLOCK
    ff = gate_w.shape[1]
    tile = min(1024, ff)
    loads = [
        pltpu.make_async_copy(source, target, w_sem.at[index])
        for index, (source, target) in enumerate(
            ((gate_hbm, gate_w), (upper_hbm, upper_w), (reduce_hbm, reduce_w))
        )
    ]
    start_left, wait_left = load_lefts((x0, x1, x2, x3), lefts, x_sem, count)
    start_left(0)
    for load in loads:
        load.start()
    greet()
    outs = [
        move_rows(outer, buffer, o_sem, index, False)
        for index, (outer, buffer) in enumerate(
            ((act_out, act_buf), (gate_out, gate_buf), (upper_out, upper_buf))
        )
    ]

    def compute(c, put):
        slot = lax.rem(c, 2)
        wait_left(c)
        start_left(c + 1)

        @pl.when(c == 0)
        def _():
            loads[0].wait()
            loads[1].wait()

        @pl.when(c >= 2)
        def _():
            for out in outs:
                out(c - 2).wait()

        def tiles(n, carry):
            at = pl.ds(pl.multiple_of(n * tile, tile), tile)
            left = lefts[slot]
            gate = dot_of(left, gate_w[:, at], 1, 0)
            upper = dot_of(left, upper_w[:, at], 1, 0)
            act_buf[slot, :, at] = (gate * jax.nn.sigmoid(gate) * upper).astype(BF)
            gate_buf[slot, :, at] = gate.astype(BF)
            upper_buf[slot, :, at] = upper.astype(BF)
            return carry

        lax.fori_loop(0, ff // tile, tiles, 0)
        for out in outs:
            out(c).start()

        @pl.when(c == 0)
        def _():
            loads[2].wait()

        for block in (1, 3, 2, 0):
            span = slice(block * width, (block + 1) * width)
            put(block, dot_of(act_buf[slot], reduce_w[:, span], 1, 0))
        rows = span_of(c, BLOCK)
        expand_inner_ref[:, rows] = dot_of(expand_low_ref[...], lefts[slot], 1, 1).astype(BF)
        reduce_inner_ref[:, rows] = dot_of(reduce_low_ref[...], act_buf[slot], 1, 1)

    def stats(c, rows, result):
        weighted = gain_ref[1:2, :] * cot_ref[rows, :].astype(F32)
        return sums_of(result * result, weighted * result)

    def finish(c, rows, result, total):
        scale = lax.rsqrt(column_of(total, 0) / D + EPS)
        gain = gain_ref[1:2, :]
        layer_ref[rows, :] = (hidden_ref[rows, :] + gain * result * scale).astype(BF)
        weighted = gain * cot_ref[rows, :].astype(F32)
        inner = column_of(total, 1)
        return (scale * weighted - result * (scale * scale * scale * inner / D)).astype(BF)

    run_blocks(count, bufs, compute, stats, finish, own_ref, arrived)
    for c in range(max(count - 2, 0), count):
        for out in outs:
            out(c).wait()


def forward_call(lefts, gate_w, upper_w, reduce_w, hidden, cotangent, gain, low, reduce_low):
    rows, width = hidden.shape
    count = rows // BLOCK
    ff = gate_w.shape[1]
    part = jax.ShapeDtypeStruct((rows, width), BF)
    wide = jax.ShapeDtypeStruct((rows, ff), BF)
    return pl.pallas_call(
        forward_kernel,
        out_shape=[wide] * 3
        + [
            part,
            jax.ShapeDtypeStruct((32, rows), BF),
            jax.ShapeDtypeStruct((16, rows), F32),
        ]
        + [part] * 4,
        in_specs=[ANY_SPEC] * 7 + [VMEM_SPEC] * 5,
        out_specs=[ANY_SPEC] * 3 + [VMEM_SPEC] * 4 + [ANY_SPEC] * 3,
        scratch_shapes=[
            pltpu.VMEM(gate_w.shape, BF),
            pltpu.VMEM(upper_w.shape, BF),
            pltpu.VMEM(reduce_w.shape, BF),
            pltpu.VMEM((2, BLOCK, 4 * width), BF),
            pltpu.VMEM((2, BLOCK, ff), BF),
            pltpu.VMEM((2, BLOCK, ff), BF),
            pltpu.VMEM((2, BLOCK, ff), BF),
            pltpu.SemaphoreType.DMA((3,)),
            pltpu.SemaphoreType.DMA((2, 4)),
            pltpu.SemaphoreType.DMA((3, 2)),
        ]
        + exchange_scratch(count, width, True),
        compiler_params=talk_params(1),
        cost_estimate=cost_of(24 * rows * width * ff, 2**27),
        name="forward",
    )(*lefts, gate_w, upper_w, reduce_w, hidden, cotangent, gain, low, reduce_low)


def backward_kernel(
    x0,
    x1,
    x2,
    x3,
    gate_hbm,
    upper_hbm,
    reduce_hbm,
    gate_in,
    upper_in,
    cot_ref,
    branch_ref,
    stat_ref,
    gain_ref,
    reduce_up_ref,
    expand_up_ref,
    expand_inner_ref,
    d_hidden_ref,
    reduce_inner_ref,
    d_inner_ref,
    up_grad_ref,
    own_ref,
    *rest,
):
    arrived, rest = rest[:3], rest[3:]
    gate_w, upper_w, reduce_w, lefts, gate_buf, upper_buf, d_gate_buf, d_upper_buf, *rest = rest
    w_sem, x_sem, i_sem, *bufs = rest
    width = own_ref.shape[1]
    count = own_ref.shape[0] // BLOCK
    ff = gate_w.shape[1]
    up_grad_ref[...] = jnp.zeros_like(up_grad_ref)
    tile = min(1024, ff)
    loads = [
        pltpu.make_async_copy(source, target, w_sem.at[index])
        for index, (source, target) in enumerate(
            ((reduce_hbm, reduce_w), (gate_hbm, gate_w), (upper_hbm, upper_w))
        )
    ]
    start_left, wait_left = load_lefts((x0, x1, x2, x3), lefts, x_sem, count)
    ins = [
        move_rows(outer, buffer, i_sem, index, True)
        for index, (outer, buffer) in enumerate(((gate_in, gate_buf), (upper_in, upper_buf)))
    ]
    start_left(0)
    for one in ins:
        one(0).start()
    for load in loads:
        load.start()
    greet()

    def compute(c, put):
        slot = lax.rem(c, 2)
        wait_left(c)
        start_left(c + 1)
        for one in ins:
            one(c).wait()

        @pl.when(c + 1 < count)
        def _():
            for one in ins:
                one(c + 1).start()

        @pl.when(c == 0)
        def _():
            loads[0].wait()

        def tiles(n, carry):
            at = pl.ds(pl.multiple_of(n * tile, tile), tile)
            d_act = dot_of(lefts[slot], reduce_w[at, :], 1, 1)
            gate = gate_buf[slot, :, at].astype(F32)
            sigma = jax.nn.sigmoid(gate)
            d_gate = d_act * upper_buf[slot, :, at].astype(F32) * (sigma * (1 + gate * (1 - sigma)))
            d_gate_buf[:, at] = d_gate.astype(BF)
            d_upper_buf[:, at] = (d_act * (gate * sigma)).astype(BF)
            return carry

        lax.fori_loop(0, ff // tile, tiles, 0)
        @pl.when(c == 0)
        def _():
            loads[1].wait()
            loads[2].wait()

        for block in (1, 3, 2, 0):
            span = slice(block * width, (block + 1) * width)
            put(
                block,
                dot_of(d_gate_buf[...], gate_w[span, :], 1, 1)
                + dot_of(d_upper_buf[...], upper_w[span, :], 1, 1),
            )
        rows = span_of(c, BLOCK)
        inner = dot_of(reduce_up_ref[...], lefts[slot], 1, 1)
        reduce_inner_ref[:, rows] = (ADAPTER_FACTOR * inner).astype(BF)
        for part, grad in enumerate((d_gate_buf, d_upper_buf)):
            own = slice(16 * part, 16 * part + 16)
            d_inner_ref[own, rows] = ADAPTER_FACTOR * dot_of(expand_up_ref[own, :], grad[...], 1, 1)
            up_grad_ref[own, :] += ADAPTER_FACTOR * dot_of(
                expand_inner_ref[own, rows], grad[...], 1, 0
            )

    def stats(c, rows, total):
        d_hidden = cot_ref[rows, :].astype(F32) + total
        d_hidden_ref[rows, :] = d_hidden
        return sums_of(gain_ref[0:1, :] * d_hidden * branch_ref[rows, :])

    def finish(c, rows, total, sums):
        scale = lax.rsqrt(column_of(stat_ref[c], 0) / D + EPS)
        weighted = gain_ref[0:1, :] * d_hidden_ref[rows, :]
        inner = column_of(sums, 0)
        back = scale * scale * scale * inner / D
        return (scale * weighted - branch_ref[rows, :] * back).astype(BF)

    run_blocks(count, bufs, compute, stats, finish, own_ref, arrived)


def backward_call(
    lefts, gate_w, upper_w, reduce_w, gate, upper, cotangent, branch, stats, gain, *adapters
):
    rows, width = branch.shape
    count = rows // BLOCK
    ff = gate_w.shape[1]
    part = jax.ShapeDtypeStruct((rows, width), BF)
    return pl.pallas_call(
        backward_kernel,
        out_shape=[
            jax.ShapeDtypeStruct((rows, width), F32),
            jax.ShapeDtypeStruct((16, rows), BF),
            jax.ShapeDtypeStruct((32, rows), F32),
            jax.ShapeDtypeStruct((32, ff), F32),
        ]
        + [part] * 4,
        in_specs=[ANY_SPEC] * 9 + [VMEM_SPEC] * 7,
        out_specs=[VMEM_SPEC] * 5 + [ANY_SPEC] * 3,
        scratch_shapes=[
            pltpu.VMEM(gate_w.shape, BF),
            pltpu.VMEM(upper_w.shape, BF),
            pltpu.VMEM(reduce_w.shape, BF),
            pltpu.VMEM((2, BLOCK, 4 * width), BF),
            pltpu.VMEM((2, BLOCK, ff), BF),
            pltpu.VMEM((2, BLOCK, ff), BF),
            pltpu.VMEM((BLOCK, ff), BF),
            pltpu.VMEM((BLOCK, ff), BF),
            pltpu.SemaphoreType.DMA((3,)),
            pltpu.SemaphoreType.DMA((2, 4)),
            pltpu.SemaphoreType.DMA((2, 2)),
        ]
        + exchange_scratch(count, width, True),
        compiler_params=talk_params(2),
        cost_estimate=cost_of(24 * rows * width * ff, 2**27),
        name="backward",
    )(
        *lefts, gate_w, upper_w, reduce_w, gate, upper, cotangent, branch, stats, gain, *adapters
    )


def input_kernel(
    raw_hbm,
    dq_hbm,
    dk_hbm,
    dv_hbm,
    matrix_ref,
    d_hidden_ref,
    scale_ref,
    q_sum_ref,
    k_sum_ref,
    gain_ref,
    cos_ref,
    sin_ref,
    tokens_ref,
    inner_ref,
    up_ref,
    out_ref,
    low_grad_ref,
    up_grad_ref,
    raw_buf,
    dq_buf,
    dk_buf,
    dv_buf,
    left_ref,
    inner_out,
    inner_in,
    inner_mid,
    inner_far,
    sum_own,
    sum_in,
    back_ref,
    in_sem,
    core_sem,
    far_sem,
    sum_sem,
    *bufs,
):
    width = out_ref.shape[1]
    local = dq_buf.shape[2]
    count = out_ref.shape[0] // BLOCK
    ins = [
        move_rows(outer, buffer, in_sem, index, True)
        for index, (outer, buffer) in enumerate(
            ((raw_hbm, raw_buf), (dq_hbm, dq_buf), (dk_hbm, dk_buf), (dv_hbm, dv_buf))
        )
    ]
    for one in ins:
        one(0).start()
    low_grad_ref[...] = jnp.zeros_like(low_grad_ref)
    up_grad_ref[...] = jnp.zeros_like(up_grad_ref)
    sum_own[...] = jnp.zeros_like(sum_own)
    for row, part in enumerate((q_sum_ref, k_sum_ref)):
        total = part[0]
        for h in range(1, part.shape[0]):
            total = total + part[h]
        sum_own[row : row + 1, :] = total
    greet()
    exchanges = [send(sum_own, sum_in.at[step - 1], sum_sem, step - 1, step) for step in (1, 2, 3)]
    for copy in exchanges:
        copy.start()
    for copy in exchanges:
        copy.wait()
    total = sum_own[...] + sum_in[0] + sum_in[1] + sum_in[2]
    back_ref[...] = scale_ref[...] * scale_ref[...] * total / D

    def inner_core(c):
        return send(inner_out.at[lax.rem(c, 2)], inner_in.at[c], core_sem, c, 1)

    def inner_side(c):
        return send(inner_mid.at[lax.rem(c, 2)], inner_far.at[c], far_sem, c, 2)

    def after_core(c):
        @pl.when(c >= 2)
        def _():
            inner_side(c - 2).wait_send()

        inner_core(c).wait_recv()
        slot = lax.rem(c, 2)
        inner_mid[slot] = inner_out[slot] + inner_in[c]
        inner_side(c).start()

    def after_side(c):
        inner_side(c).wait_recv()
        total = (inner_mid[lax.rem(c, 2)] + inner_far[c]).astype(BF)
        low_grad_ref[...] += dot_of(total, tokens_ref[span_of(c, BLOCK), :], 1, 0)

    def compute(c, put):
        slot = lax.rem(c, 2)
        for one in ins:
            one(c).wait()

        @pl.when(c + 1 < count)
        def _():
            for one in ins:
                one(c + 1).start()

        @pl.when(c >= 2)
        def _():
            inner_core(c - 2).wait_send()

        rows = span_of(c, BLOCK)
        cosine = cos_ref[rows, :]
        sine = sin_ref[rows, :]
        for part, grad in ((0, dq_buf), (1, dk_buf)):
            scale = column_of(scale_ref[:, rows], part)
            back = column_of(back_ref[:, rows], part)
            for at in range(0, local, HEAD):
                turned = grad[slot, :, at : at + HEAD]
                turned = turned * cosine - pltpu.roll(turned, HEAD // 2, 1) * sine
                turned = turned * gain_ref[part : part + 1, at : at + HEAD] * scale
                lane = part * local + at
                left_ref[:, lane : lane + HEAD] = (
                    turned - raw_buf[slot, :, lane : lane + HEAD] * back
                ).astype(BF)
        left_ref[:, 2 * local :] = dv_buf[slot].astype(BF)
        for part in range(3):
            own = slice(16 * part, 16 * part + 16)
            grad = left_ref[:, part * local : (part + 1) * local]
            inner_out[slot, own, :] = ADAPTER_FACTOR * dot_of(up_ref[own, :], grad, 1, 1)
            up_grad_ref[own, :] += ADAPTER_FACTOR * dot_of(inner_ref[own, rows], grad, 1, 0)
        inner_core(c).start()
        left = left_ref[...]
        for block in (1, 3, 2, 0):
            put(block, dot_of(left, matrix_ref[block * width : (block + 1) * width, :], 1, 1))

    def finish(c, rows, total):
        out_ref[rows, :] = d_hidden_ref[rows, :] + total

    run_blocks(count, bufs, compute, None, finish, extra=(after_core, after_side))
    for c in range(max(count - 2, 0), count):
        inner_core(c).wait_send()
        inner_side(c).wait_send()


def input_call(
    raw, d_query, d_key, d_value, matrix, d_hidden, scales, q_sums, k_sums, *others
):
    rows, width = d_hidden.shape
    local = d_query.shape[1]
    count = rows // BLOCK
    part = pltpu.VMEM((2, BLOCK, local), F32)
    sem = pltpu.SemaphoreType.DMA((2, count))
    return pl.pallas_call(
        input_kernel,
        out_shape=[
            jax.ShapeDtypeStruct((rows, width), F32),
            jax.ShapeDtypeStruct((48, width), F32),
            jax.ShapeDtypeStruct((48, local), F32),
        ],
        in_specs=[ANY_SPEC] * 4 + [VMEM_SPEC] * 11,
        out_specs=[VMEM_SPEC] * 3,
        scratch_shapes=[
            pltpu.VMEM((2, BLOCK, 3 * local), F32),
            part,
            part,
            part,
            pltpu.VMEM((BLOCK, 3 * local), BF),
            pltpu.VMEM((2, 48, BLOCK), F32),
            pltpu.VMEM((count, 48, BLOCK), F32),
            pltpu.VMEM((2, 48, BLOCK), F32),
            pltpu.VMEM((count, 48, BLOCK), F32),
            pltpu.VMEM((8, rows), F32),
            pltpu.VMEM((3, 8, rows), F32),
            pltpu.VMEM((8, rows), F32),
            pltpu.SemaphoreType.DMA((4, 2)),
            sem,
            sem,
            pltpu.SemaphoreType.DMA((2, 3)),
        ]
        + exchange_scratch(count, width, False),
        compiler_params=talk_params(3),
        cost_estimate=cost_of(24 * rows * width * local, 2**26),
        name="input_grad",
    )(raw, d_query, d_key, d_value, matrix, d_hidden, scales, q_sums, k_sums, *others)


def deal(items, outs, sems):
    me = lax.axis_index("row")
    copies = []
    for index, (view, out) in enumerate(zip(items, outs)):
        mine = [pltpu.make_async_copy(view(me), out.at[0], sems.at[0, index, 0])]
        for step in (1, 2, 3):
            mine.append(
                pltpu.make_async_remote_copy(
                    src_ref=view(me ^ step),
                    dst_ref=out.at[step],
                    send_sem=sems.at[0, index, step],
                    recv_sem=sems.at[1, index, step],
                    device_id=peer(step),
                    device_id_type=pl.DeviceIdType.MESH,
                )
            )
        copies.append(mine)
    return copies


def start_all(copies):
    for step in (2, 3, 1, 0):
        copies[step].start()


def wait_all(copies):
    for copy in copies:
        copy.wait()


def span_of(at, size):
    return pl.ds(pl.multiple_of(at * size, size), size)


def qkv_view(ref, half):
    _, rows, columns = ref.shape
    return lambda row: ref.at[:, span_of(half, rows // 2), span_of(row, columns // 4)]


def attn_view(ref, half):
    cut = ref.shape[0] // 8
    return lambda row: ref.at[span_of(2 * row + half, cut)]


def expand_view(ref, part, half):
    cut = ref.shape[2] // 8
    return lambda row: ref.at[part, :, span_of(2 * row + half, cut)]


def reduce_view(ref):
    cut = ref.shape[0] // 4
    return lambda row: ref.at[span_of(row, cut)]


def like_views(shapes):
    return [jax.ShapeDtypeStruct((4, *shape), BF) for shape in shapes]


def first_deal_kernel(qkv_ref, attn_ref, qkv_out, attn_out, sems):
    half = lax.axis_index("dp")
    greet()
    copies = deal([qkv_view(qkv_ref, half), attn_view(attn_ref, half)], [qkv_out, attn_out], sems)
    for one in copies:
        start_all(one)
    for one in copies:
        wait_all(one)


def first_deal(qkv_weight, attn_weight):
    parts, rows, columns = qkv_weight.shape
    return pl.pallas_call(
        first_deal_kernel,
        out_shape=like_views(
            [(parts, rows // 2, columns // 4), (attn_weight.shape[0] // 8, attn_weight.shape[1])]
        ),
        in_specs=[ANY_SPEC] * 2,
        out_specs=[ANY_SPEC] * 2,
        scratch_shapes=[pltpu.SemaphoreType.DMA((2, 2, 4))],
        compiler_params=talk_params(4),
        cost_estimate=cost_of(0, 2**26),
        name="first_deal",
    )(qkv_weight, attn_weight)


def second_deal_kernel(qkv_ref, attn_ref, expand_ref, tokens_ref, pack_ref, *rest):
    *outs, t1, t2, t3, p1, p2, p3, sems, token_sem, pack_sem = rest
    half = lax.axis_index("dp")
    greet()
    gate, rest_qkv, rest_attn, upper = deal(
        [
            expand_view(expand_ref, 0, half),
            qkv_view(qkv_ref, 1 - half),
            attn_view(attn_ref, 1 - half),
            expand_view(expand_ref, 1, half),
        ],
        outs,
        sems,
    )
    gathers = []
    for source, targets, one_sem in ((pack_ref, (p1, p2, p3), pack_sem), (tokens_ref, (t1, t2, t3), token_sem)):
        gathers.append(
            (
                send(source, targets[1], one_sem, 1, 2),
                send(source, targets[0], one_sem, 0, 1),
                send(targets[1], targets[2], one_sem, 2, 1),
            )
        )
    start_all(gate)
    start_all(rest_qkv)
    start_all(rest_attn)
    for side, core, _ in gathers:
        side.start()
        core.start()
    start_all(upper)
    for side, core, relay in gathers:
        side.wait_recv()
        relay.start()
    for one in (gate, rest_qkv, rest_attn, upper):
        wait_all(one)
    for side, core, relay in gathers:
        side.wait_send()
        core.wait()
        relay.wait()


def second_deal(qkv_weight, attn_weight, expand_weight, tokens, pack):
    parts, rows, columns = qkv_weight.shape
    cut = expand_weight.shape[2] // 8
    wide = (expand_weight.shape[1], cut)
    sem = pltpu.SemaphoreType.DMA((2, 3))
    return pl.pallas_call(
        second_deal_kernel,
        out_shape=like_views(
            [
                wide,
                (parts, rows // 2, columns // 4),
                (attn_weight.shape[0] // 8, attn_weight.shape[1]),
                wide,
            ]
        )
        + [jax.ShapeDtypeStruct(tokens.shape, BF)] * 3
        + [jax.ShapeDtypeStruct(pack.shape, BF)] * 3,
        in_specs=[ANY_SPEC] * 5,
        out_specs=[ANY_SPEC] * 10,
        scratch_shapes=[pltpu.SemaphoreType.DMA((2, 4, 4)), sem, sem],
        compiler_params=talk_params(5),
        cost_estimate=cost_of(0, 2**27),
        name="second_deal",
    )(qkv_weight, attn_weight, expand_weight, tokens, pack)


def greet_all(peers):
    barrier = pltpu.get_barrier_semaphore()
    for device in peers:
        pl.semaphore_signal(barrier, inc=1, device_id=device, device_id_type=pl.DeviceIdType.MESH)
    pl.semaphore_wait(barrier, len(peers))


def copy_to(source, target, sems, index, device):
    return pltpu.make_async_remote_copy(
        src_ref=source,
        dst_ref=target,
        send_sem=sems.at[0, index],
        recv_sem=sems.at[1, index],
        device_id=device,
        device_id_type=pl.DeviceIdType.MESH,
    )


def other_of_pair():
    return {"dp": 1 - lax.axis_index("dp")}


def exchange_halves(whole, rest, out, sems, local_sem, steps=None):
    cols = whole.shape[0]
    col = lax.axis_index("col")
    copies = []
    for k in range(cols) if steps is None else steps:
        if k == 0:
            copies.append(pltpu.make_async_copy(rest, out.at[0], local_sem))
            continue
        place = lax.rem(col + k, cols)
        copies.append(copy_to(whole.at[place], out.at[k], sems, k - 1, other_of_pair()))
    return copies


def send_round(view, out, sems, local_sem):
    cols = out.shape[0]
    col = lax.axis_index("col")
    local = pltpu.make_async_copy(view(col), out.at[col], local_sem)
    sends = []
    arrivals = []
    for k in range(1, cols):
        place = lax.rem(col + k, cols)
        came = lax.rem(col - k + cols, cols)
        sends.append(copy_to(view(place), out.at[col], sems, k - 1, {"col": place}))
        arrivals.append(copy_to(view(place), out.at[came], sems, k - 1, {"col": place}))

    def wait():
        local.wait()
        for one in arrivals:
            one.wait_recv()
        for one in sends:
            one.wait_send()

    return [local, *sends], wait


def row_and_col_peers():
    cols = lax.axis_size("col")
    col = lax.axis_index("col")
    return [peer(step) for step in (1, 2, 3)] + [
        {"col": lax.rem(col + k, cols)} for k in range(1, cols)
    ]


def third_deal_kernel(
    expand_ref, reduce_ref, qkv_all, qkv_rest, attn_all, attn_rest, pack_ref, gain_ref, *rest
):
    *outs, qkv_out, attn_out, pack_out, gain_out = rest[:7]
    deal_sem, qkv_sem, attn_sem, pack_sem, gain_sem, local_sem = rest[7:]
    other = 1 - lax.axis_index("dp")
    me = lax.axis_index("row")
    greet_all(row_and_col_peers() + [other_of_pair()])
    sub = gain_out.shape[2]
    swaps = exchange_halves(qkv_all, qkv_rest, qkv_out, qkv_sem, local_sem.at[0])
    swaps += exchange_halves(attn_all, attn_rest, attn_out, attn_sem, local_sem.at[1])
    packs, wait_packs = send_round(lambda place: pack_ref.at[place], pack_out, pack_sem, local_sem.at[2])
    gains, wait_gains = send_round(
        lambda place: gain_ref.at[:, span_of(me, sub)], gain_out, gain_sem, local_sem.at[3]
    )
    for copy in packs + gains + swaps:
        copy.start()
    copies = deal(
        [
            reduce_view(reduce_ref),
            expand_view(expand_ref, 0, other),
            expand_view(expand_ref, 1, other),
        ],
        outs,
        deal_sem,
    )
    for one in copies:
        start_all(one)
    wait_packs()
    wait_gains()
    for one in copies:
        wait_all(one)
    wait_all(swaps)


def third_deal(expand_weight, reduce_weight, qkv_all, qkv_rest, attn_all, attn_rest, pack, gain):
    wide = (expand_weight.shape[1], expand_weight.shape[2] // 8)
    cols = qkv_all.shape[0]
    round_sem = pltpu.SemaphoreType.DMA((2, cols - 1))
    return pl.pallas_call(
        third_deal_kernel,
        out_shape=like_views([(reduce_weight.shape[0] // 4, reduce_weight.shape[1]), wide, wide])
        + [
            jax.ShapeDtypeStruct(qkv_all.shape, BF),
            jax.ShapeDtypeStruct(attn_all.shape, BF),
            jax.ShapeDtypeStruct(pack.shape, BF),
            jax.ShapeDtypeStruct((cols, gain.shape[0], gain.shape[1] // 4), F32),
        ],
        in_specs=[ANY_SPEC] * 8,
        out_specs=[ANY_SPEC] * 7,
        scratch_shapes=[
            pltpu.SemaphoreType.DMA((2, 3, 4)),
            round_sem,
            round_sem,
            round_sem,
            round_sem,
            pltpu.SemaphoreType.DMA((4,)),
        ],
        compiler_params=talk_params(6),
        cost_estimate=cost_of(0, 2**27),
        name="third_deal",
    )(expand_weight, reduce_weight, qkv_all, qkv_rest, attn_all, attn_rest, pack, gain)


def front_kernel(
    x0,
    x1,
    x2,
    x3,
    matrix_ref,
    low_ref,
    gate_all,
    gate_rest,
    raw_ref,
    square_ref,
    inner_ref,
    gate_out,
    swap_sem,
    local_sem,
):
    local = raw_ref.shape[1] // 3
    first = exchange_halves(gate_all, gate_rest, gate_out, swap_sem, local_sem.at[0], range(2))

    @pl.when(pl.program_id(0) == 0)
    def _():
        greet_all([other_of_pair()])
        for copy in first:
            copy.start()

    left = jnp.concatenate([x0[...], x1[...], x2[...], x3[...]], axis=1)
    squares = []
    for part in range(3):
        lanes = slice(part * local, (part + 1) * local)
        product = dot_of(left, matrix_ref[:, lanes], 1, 0)
        raw_ref[:, lanes] = product
        squares.append(product * product)
    square_ref[...] = sums_of(*squares[:2])
    inner_ref[...] = dot_of(low_ref[...], left, 1, 1).astype(BF)

    @pl.when(pl.program_id(0) == pl.num_programs(0) - 1)
    def _():
        wait_all(first)


def front_call(lefts, matrix, low, gate_all, gate_rest):
    rows, width = lefts[0].shape
    wide = matrix.shape[1]
    tile = row_tile(rows)
    cols = gate_all.shape[0]

    def whole(array):
        return pl.BlockSpec(array.shape, lambda m: (0, 0))

    return pl.pallas_call(
        front_kernel,
        out_shape=[
            jax.ShapeDtypeStruct((rows, wide), F32),
            jax.ShapeDtypeStruct((8, rows), F32),
            jax.ShapeDtypeStruct((48, rows), BF),
            jax.ShapeDtypeStruct(gate_all.shape, BF),
        ],
        grid=(rows // tile,),
        in_specs=[pl.BlockSpec((tile, width), lambda m: (m, 0))] * 4
        + [whole(matrix), whole(low), ANY_SPEC, ANY_SPEC],
        out_specs=[
            pl.BlockSpec((tile, wide), lambda m: (m, 0)),
            pl.BlockSpec((8, tile), lambda m: (0, m)),
            pl.BlockSpec((48, tile), lambda m: (0, m)),
            ANY_SPEC,
        ],
        scratch_shapes=[
            pltpu.SemaphoreType.DMA((2, cols - 1)),
            pltpu.SemaphoreType.DMA((1,)),
        ],
        compiler_params=talk_params(8),
        cost_estimate=cost_of(8 * rows * width * wide, 2**26),
        name="front",
    )(*lefts, matrix, low, gate_all, gate_rest)


def groups_kernel(row_ref, col_ref, rows_out, cols_out, local_sem, pair_sem, round_sem, deal_sem, row_sem):
    cols = col_ref.shape[0]
    col = lax.axis_index("col")
    places = [lax.rem(col + k, cols) for k in range(cols)]
    to = copy_to
    greet_all(row_and_col_peers() + [other_of_pair()])
    swap_rows = to(row_ref, rows_out.at[0, 1], pair_sem, 0, other_of_pair())
    swap_rows.start()
    dealt = [
        to(col_ref.at[places[k]], cols_out.at[0, 0, col], deal_sem, k - 1, {"col": places[k]})
        for k in range(1, cols)
    ]
    for copy in dealt:
        copy.start()
    keep_rows = pltpu.make_async_copy(row_ref, rows_out.at[0, 0], local_sem.at[0])
    keep_cols = pltpu.make_async_copy(col_ref.at[col], cols_out.at[0, 0, col], local_sem.at[1])
    keep_rows.start()
    keep_cols.start()
    for k in range(1, cols):
        came = lax.rem(col - k + cols, cols)
        to(col_ref.at[came], cols_out.at[0, 0, came], deal_sem, k - 1, {"col": places[k]}).wait_recv()
    keep_cols.wait()
    swap_cols = to(cols_out.at[0, 0], cols_out.at[0, 1], pair_sem, 1, other_of_pair())
    swap_cols.start()
    keep_rows.wait()
    swap_rows.wait_recv()
    rounds = [
        to(rows_out.at[0], rows_out.at[k], round_sem, k - 1, {"col": places[k]})
        for k in range(1, cols)
    ]
    for copy in rounds:
        copy.start()
    swap_cols.wait_recv()
    side = to(cols_out.at[0], cols_out.at[2], row_sem, 1, peer(2))
    core = to(cols_out.at[0], cols_out.at[1], row_sem, 0, peer(1))
    relay = to(cols_out.at[2], cols_out.at[3], row_sem, 2, peer(1))
    side.start()
    core.start()
    side.wait_recv()
    relay.start()
    core.wait()
    relay.wait()
    side.wait_send()
    for copy in rounds:
        copy.wait()
    for copy in dealt:
        copy.wait_send()
    swap_rows.wait_send()
    swap_cols.wait_send()


def groups_call(row_pack, col_pack):
    cols = col_pack.shape[0]
    return pl.pallas_call(
        groups_kernel,
        out_shape=[
            jax.ShapeDtypeStruct((cols, 2, *row_pack.shape), BF),
            jax.ShapeDtypeStruct((4, 2, *col_pack.shape), BF),
        ],
        in_specs=[ANY_SPEC] * 2,
        out_specs=[ANY_SPEC] * 2,
        scratch_shapes=[
            pltpu.SemaphoreType.DMA((2,)),
            pltpu.SemaphoreType.DMA((2, 2)),
            pltpu.SemaphoreType.DMA((2, cols - 1)),
            pltpu.SemaphoreType.DMA((2, cols - 1)),
            pltpu.SemaphoreType.DMA((2, 3)),
        ],
        compiler_params=talk_params(7),
        cost_estimate=cost_of(0, 2**26),
        name="groups",
    )(row_pack, col_pack)


def across(values, step):
    return lax.ppermute(values, "row", [(i, i ^ step) for i in range(4)])


def sum_row(values):
    values = values + across(values, 1)
    return values + across(values, 2)


def gather_col(values):
    return lax.all_gather(values, "col", axis=0, tiled=False)


def swap_pair(values):
    return lax.ppermute(values, "dp", [(0, 1), (1, 0)])


def round_col(values, cols):
    shift = lambda k: [(i, (i + k) % cols) for i in range(cols)]
    return [values] + [lax.ppermute(values, "col", shift(k)) for k in range(1, cols)]


def after(values, earlier):
    return lax.optimization_barrier((values, earlier))[0]


def group_shards(
    tokens,
    cotangent,
    qkv_weight,
    attn_weight,
    expand_weight,
    reduce_weight,
    headnorm_gain,
    post_gain,
    qkv_lowrank,
    qkv_uprank,
    attn_lowrank,
    attn_uprank,
    expand_lowrank,
    expand_uprank,
    reduce_lowrank,
    reduce_uprank,
    prefix_length,
    adapter_set,
):
    cols = lax.axis_size("col")
    pair = lax.axis_index("dp")
    me = lax.axis_index("row")
    col = lax.axis_index("col")
    rows, width = tokens.shape
    sub = qkv_weight.shape[2] // 4
    ff = expand_weight.shape[2]
    ff_sub = ff // 4
    ff_half = ff_sub // 2
    local = cols * sub
    ff_local = cols * ff_sub
    sequence = pair * cols + col
    mine = lax.dynamic_index_in_dim(adapter_set, sequence, 0, keepdims=False)
    prefix = lax.dynamic_slice_in_dim(prefix_length, sequence, 1)
    cols_sets = lax.dynamic_slice_in_dim(adapter_set, pair * cols, cols)

    row_pack = row_pack_of(
        mine.reshape(1),
        qkv_lowrank.transpose(0, 1, 3, 2),
        attn_uprank,
        expand_lowrank.transpose(0, 1, 3, 2),
        reduce_uprank,
    )
    col_pack = col_pack_of(
        jnp.concatenate([cols_sets, me.reshape(1)]),
        qkv_uprank,
        attn_lowrank.transpose(0, 2, 1),
        expand_uprank,
        reduce_lowrank.transpose(0, 2, 1),
    )

    place = jnp.stack([pair, col])

    qkv_own, attn_own = first_deal(qkv_weight, attn_weight)
    col_pack = after(col_pack, qkv_own)
    gate_own, qkv_rest, attn_rest, up_own, *others = second_deal(
        qkv_weight, attn_weight, expand_weight, tokens, after(row_pack, qkv_own)
    )
    token_parts = [tokens, *others[:3]]
    row_all = jnp.concatenate([row_pack, *others[3:]], axis=1)
    qkv_low = row_all[:48]
    attn_up = row_all[48:64]
    expand_low = row_all[64:96]
    reduce_up = row_all[96:112]
    qkv_all = gather_col(qkv_own)
    attn_all = gather_col(attn_own)
    gate_all = gather_col(gate_own)
    up_all = gather_col(up_own)
    reduce_own, gate_rest, up_rest, qkv_other, attn_other, col_all, gains = third_deal(
        expand_weight,
        after(reduce_weight, others[0]),
        qkv_all,
        qkv_rest,
        attn_all,
        attn_rest,
        col_pack,
        headnorm_gain,
    )
    reduce_all = gather_col(reduce_own)
    gains = gains.transpose(1, 0, 2).reshape(2, local)

    def own_columns(at, size):
        return col_all[:, :, at : at + size].transpose(1, 0, 2).reshape(16, cols * size)

    qkv_up = [own_columns(i * sub, sub) for i in range(3)]
    attn_low = own_columns(3 * sub, sub)
    expand_up = [own_columns(4 * sub + i * ff_sub, ff_sub) for i in range(2)]
    reduce_low = own_columns(4 * sub + 2 * ff_sub, ff_sub)

    qkv_up = jnp.concatenate(qkv_up)
    qkv_w = merge_qkv(place, qkv_all, qkv_other, qkv_low, qkv_up)
    attn_w = merge_out(place, [attn_all, attn_other], attn_low, attn_up)

    half = HEAD // 2
    freq = THETA ** (-2.0 * jnp.arange(half, dtype=F32) / HEAD)
    angle = jnp.arange(rows, dtype=jnp.int32).astype(F32)[:, None] * freq[None, :]
    cosine = jnp.concatenate([jnp.cos(angle)] * 2, axis=1)
    sine = jnp.sin(angle)
    sine = jnp.concatenate([-sine, sine], axis=1)

    raw, squares, qkv_inner, gate_part = front_call(
        token_parts, qkv_w, qkv_low, gate_all, gate_rest
    )
    scale = lax.rsqrt(sum_row(squares) / D + EPS)
    query, key, value = rotate_rows(raw, scale, gains, cosine, sine)
    limit = jnp.maximum(jnp.arange(rows, dtype=jnp.int32), prefix - 1)[None]
    mixed, log_total, branch, hidden, branch_stats, *hidden_parts, gate_other, up_other = branch_call(
        query,
        key,
        value,
        limit,
        attn_w,
        tokens,
        post_gain,
        (gate_all, gate_part, up_all, up_rest),
    )
    expand_w = [
        merge_expand(
            place, whole, other, expand_low[16 * i : 16 * i + 16], expand_up[i]
        )
        for i, (whole, other) in enumerate(((gate_all, gate_other), (up_all, up_other)))
    ]
    reduce_w = merge_out(place, [reduce_all], reduce_low, reduce_up)
    act, gate, upper, layer_out, expand_inner, reduce_inner, *result_parts = forward_call(
        hidden_parts, *expand_w, reduce_w, hidden, cotangent, post_gain, expand_low, reduce_low
    )
    d_hidden, d_reduce_inner, d_expand_inner, g_expand_up, *branch_parts = backward_call(
        result_parts,
        *expand_w,
        reduce_w,
        gate,
        upper,
        cotangent,
        branch,
        branch_stats,
        post_gain,
        reduce_up,
        jnp.concatenate(expand_up),
        expand_inner,
    )
    d_mixed, d_attn_inner = mixed_back(branch_parts, attn_w, attn_up)
    d_query, d_key, d_value, q_sums, k_sums = attend_back(
        prefix, query, d_mixed, mixed, log_total, key, value
    )
    attn_inner = sum_row(dot_of(attn_low, mixed, 1, 1)).astype(BF)
    reduce_inner = sum_row(reduce_inner).astype(BF)
    d_expand_inner = sum_row(d_expand_inner).astype(BF)
    g_reduce_up = ADAPTER_FACTOR * dot_of(reduce_inner, result_parts[0], 1, 0)
    g_reduce_low = dot_of(d_reduce_inner, act, 1, 0)
    g_expand_low = dot_of(d_expand_inner, hidden_parts[0], 1, 0)
    g_attn_up = ADAPTER_FACTOR * dot_of(attn_inner, branch_parts[0], 1, 0)
    g_attn_low = dot_of(d_attn_inner, mixed, 1, 0)
    input_grad, g_qkv_low, g_qkv_up = input_call(
        raw,
        d_query,
        d_key,
        d_value,
        qkv_w,
        d_hidden,
        scale,
        q_sums,
        k_sums,
        gains,
        cosine,
        sine,
        tokens,
        qkv_inner,
        qkv_up,
    )

    def by_col(grad):
        return grad.reshape(16, cols, -1).transpose(1, 0, 2)

    row_pack = jnp.concatenate([g_qkv_low, g_attn_up, g_expand_low, g_reduce_up], axis=0)
    col_pack = jnp.concatenate(
        [
            by_col(grad)
            for grad in (
                g_qkv_up[:16],
                g_qkv_up[16:32],
                g_qkv_up[32:],
                g_attn_low,
                g_expand_up[:16],
                g_expand_up[16:],
                g_reduce_low,
            )
        ],
        axis=2,
    )
    every_row, every_col = groups_call(row_pack.astype(BF), col_pack.astype(BF))
    place_of = jnp.arange(2 * cols, dtype=jnp.int32)
    row_place = (pair ^ (place_of % 2)) * cols + (col - place_of // 2 + cols) % cols
    col_place = (pair ^ (place_of // cols)) * cols + place_of % cols
    places = jnp.concatenate([row_place, col_place])
    chosen = places[:, None] == jnp.arange(2 * cols, dtype=jnp.int32)[None, :]
    ids = jnp.sum(jnp.where(chosen, adapter_set[None, :], 0), axis=1)
    ids = jnp.concatenate([ids, me.reshape(1)])
    qkv_low, qkv_up, attn_low, attn_up, expand_low, expand_up, reduce_low, reduce_up = finish_call(
        ids, every_row, every_col, sub, ff_sub
    )
    return (
        layer_out,
        input_grad,
        qkv_low.transpose(0, 1, 3, 2),
        qkv_up,
        attn_low.transpose(0, 2, 1),
        attn_up,
        expand_low.transpose(0, 1, 3, 2),
        expand_up,
        reduce_low.transpose(0, 2, 1),
        reduce_up,
    )


def shards(*arrays):
    whole = (
        lax.axis_size("dp") == 2
        and lax.axis_size("row") == 4
        and arrays[0].shape[0] == SEQUENCE_LENGTH
    )
    return group_shards(*arrays) if whole else general_shards(*arrays)


def solution(mesh):
    placed = (
        P(("dp", "col"), "row"),
        P(("dp", "col"), "row"),
        P(None, "row", "col"),
        P("col", "row"),
        P(None, "row", "col"),
        P("col", "row"),
        P(None, "col"),
        P(None, "row"),
        P(None, None, "row", None),
        P(None, None, None, "col"),
        P(None, "col", None),
        P(None, None, "row"),
        P(None, None, "row", None),
        P(None, None, None, "col"),
        P(None, "col", None),
        P(None, None, "row"),
        P(),
        P(),
    )
    return jax.shard_map(
        shards,
        mesh=mesh,
        in_specs=placed,
        out_specs=(
            P(("dp", "col"), "row"),
            P(("dp", "col"), "row"),
            P(None, None, "row", None),
            P(None, None, None, "col"),
            P(None, "col", None),
            P(None, None, "row"),
            P(None, None, "row", None),
            P(None, None, None, "col"),
            P(None, "col", None),
            P(None, None, "row"),
        ),
        check_vma=False,
    )
```

```python
import functools

import jax
import jax.numpy as jnp
from jax import lax
from jax.experimental import pallas as pl
from jax.experimental.pallas import tpu as pltpu
from jax.sharding import PartitionSpec as P

D = 2048
HEAD = 128
ADAPTER_RANK = 16
SETS = 8
SEQUENCE_LENGTH = 2048


EPS = 1e-06
THETA = 500000.0
ADAPTER_FACTOR = 0.5
NEG = -1e30


def via_col_row(input_rows, weight_matrix, adapt_mat, compute, seq_pick):
    gathered = lax.all_gather(input_rows, "col", axis=0, tiled=True)
    main, inner_value = compute(gathered, weight_matrix, adapt_mat, seq_pick, False)
    return (
        lax.psum_scatter(main, "row", scatter_dimension=0, tiled=True),
        lax.psum_scatter(inner_value, "row", scatter_dimension=0, tiled=True),
    )


def via_row_col(input_rows, weight_matrix, adapt_mat, compute, seq_pick):
    gathered = lax.all_gather(input_rows, "row", axis=0, tiled=True)
    main, inner_value = compute(gathered, weight_matrix, adapt_mat, seq_pick, False)
    return (
        lax.psum_scatter(main, "col", scatter_dimension=0, tiled=True),
        lax.psum_scatter(inner_value, "col", scatter_dimension=0, tiled=True),
    )


def row_total(values):
    return lax.psum(jnp.sum(values, axis=-1), "row")


def head_totals(first, second):
    return lax.psum((jnp.sum(first, axis=-1), jnp.sum(second, axis=-1)), "col")


def sum_col_tokens(values):
    return lax.psum(values.astype(jnp.bfloat16), ("dp", "col")).astype(jnp.float32)


def sum_row_tokens(values):
    return lax.psum(values.astype(jnp.bfloat16), ("dp", "row")).astype(jnp.float32)


def set_rows(group_sets, first_row, item_count):
    sequence = (first_row + jnp.arange(item_count, dtype=jnp.int32)) // SEQUENCE_LENGTH
    member = sequence[:, None] == jnp.arange(group_sets.shape[0], dtype=jnp.int32)[None, :]
    chosen = jnp.sum(jnp.where(member, group_sets[None, :], 0), axis=1)
    return (chosen[:, None] == jnp.arange(SETS, dtype=jnp.int32)[None, :]).astype(jnp.bfloat16)


def widen(inner_value, onehot, part_list):
    rows = inner_value.shape[0]
    spread = onehot[:, None, :, None] * inner_value.reshape(rows, part_list, 1, ADAPTER_RANK)
    return spread.reshape(rows, part_list, SETS * ADAPTER_RANK)


def adapter_in(gathered, pick, lowrank):
    part_list = lowrank.shape[0]
    width_in = lowrank.shape[2]
    item_count = pick.shape[0]
    chosen = jnp.einsum("sk,pkdr->sdpr", pick, lowrank, preferred_element_type=jnp.float32).astype(
        jnp.bfloat16
    )
    chosen = chosen.reshape(item_count, width_in, part_list * ADAPTER_RANK)
    product_value = jnp.einsum(
        "ehm,emx->ehx",
        gathered.reshape(item_count, SEQUENCE_LENGTH, width_in),
        chosen,
        preferred_element_type=jnp.float32,
    )
    return product_value.reshape(item_count * SEQUENCE_LENGTH, part_list * ADAPTER_RANK)


def adapter_back(gathered, pick, upward_rank):
    part_list = upward_rank.shape[0]
    width_out = upward_rank.shape[-1]
    item_count = pick.shape[0]
    chosen = jnp.einsum(
        "sk,pkre->sper", pick, upward_rank, preferred_element_type=jnp.float32
    ).astype(jnp.bfloat16)
    product_value = jnp.einsum(
        "slpe,sper->slpr",
        gathered.reshape(item_count, SEQUENCE_LENGTH, part_list, width_out),
        chosen,
        preferred_element_type=jnp.float32,
    )
    return ADAPTER_FACTOR * product_value.reshape(
        item_count * SEQUENCE_LENGTH, part_list * ADAPTER_RANK
    )


def adapter_out(wide_output, upward_rank):
    part_list = upward_rank.shape[0]
    flat_up = upward_rank.reshape(part_list, SETS * ADAPTER_RANK, upward_rank.shape[-1])
    return ADAPTER_FACTOR * jnp.einsum(
        "tpk,pke->tpe", wide_output, flat_up, preferred_element_type=jnp.float32
    )


def adapter_grad_in(wide_output, lowrank):
    part_list = lowrank.shape[0]
    width_in = lowrank.shape[2]
    flat_low = lowrank.transpose(0, 1, 3, 2).reshape(part_list, SETS * ADAPTER_RANK, width_in)
    return jnp.einsum("tpk,pkd->td", wide_output, flat_low, preferred_element_type=jnp.float32)


def up_grad(wide_output, gradient_list):
    part_list = gradient_list.shape[1]
    total_sum = ADAPTER_FACTOR * jnp.einsum(
        "jox,joq->oxq", wide_output, gradient_list, preferred_element_type=jnp.float32
    )
    return total_sum.reshape(part_list, SETS, ADAPTER_RANK, gradient_list.shape[2])


def low_grad(input_rows, wide_output):
    part_list = wide_output.shape[1]
    total_sum = jnp.einsum(
        "td,tpk->pkd", input_rows, wide_output, preferred_element_type=jnp.float32
    )
    return total_sum.reshape(part_list, SETS, ADAPTER_RANK, input_rows.shape[1]).transpose(
        0, 1, 3, 2
    )


def swiglu(gate, upper):
    return jax.nn.silu(gate) * upper


def norm_back(grad, values, scale, gain):
    weighted = gain * grad
    inner_sum = row_total(weighted * values)
    return scale[:, None] * weighted - values * (scale**3 * inner_sum / D)[:, None]


def qkv_forward(gathered, weight_matrix, low_flat, pick, per_row):
    input_rows = gathered[:, 0]
    main = jnp.einsum("td,pde->tpe", input_rows, weight_matrix, preferred_element_type=jnp.float32)
    lowrank = low_flat.reshape(3, SETS, low_flat.shape[1], ADAPTER_RANK)
    return (main, adapter_in(input_rows, pick, lowrank))


def expand_forward(gathered, weight_matrix, low_flat, pick, per_row):
    input_rows = gathered[:, 0]
    main = jnp.einsum("td,pdf->tpf", input_rows, weight_matrix, preferred_element_type=jnp.float32)
    lowrank = low_flat.reshape(2, SETS, low_flat.shape[1], ADAPTER_RANK)
    return (main, adapter_in(input_rows, pick, lowrank))


def single_forward(gathered, weight_matrix, low_four, pick, per_row):
    input_rows = gathered[:, 0]
    main = jnp.dot(input_rows, weight_matrix[0, 0], preferred_element_type=jnp.float32)
    return (main, adapter_in(input_rows, pick, low_four))


def single_backward(gathered, weight_matrix, up_flat, pick, per_row):
    main = jnp.einsum(
        "te,fe->tf", gathered[:, 0], weight_matrix, preferred_element_type=jnp.float32
    )
    upward_rank = up_flat.reshape(1, SETS, ADAPTER_RANK, up_flat.shape[1])
    return (main, adapter_back(gathered, pick, upward_rank))


def multi_backward(gathered, weight_matrix, up_flat, pick, per_row):
    part_list = weight_matrix.shape[0]
    main = jnp.einsum("tpf,pdf->td", gathered, weight_matrix, preferred_element_type=jnp.float32)
    upward_rank = up_flat.reshape(part_list, SETS, ADAPTER_RANK, up_flat.shape[2])
    return (main, adapter_back(gathered, pick, upward_rank))


def general_shards(
    tokens,
    cotangent,
    qkv_weight,
    attn_weight,
    expand_weight,
    reduce_weight,
    headnorm_gain,
    post_gain,
    qkv_lowrank,
    qkv_uprank,
    attn_lowrank,
    attn_uprank,
    expand_lowrank,
    expand_uprank,
    reduce_lowrank,
    reduce_uprank,
    prefix_length,
    adapter_set,
):
    rows_a = tokens.shape[0]
    group_rows = rows_a * lax.axis_size("col")
    rows_b = group_rows // lax.axis_size("row")
    group_seqs = group_rows // SEQUENCE_LENGTH
    group_first = lax.axis_index("dp") * group_seqs
    group_sets = lax.dynamic_slice_in_dim(adapter_set, group_first, group_seqs)
    group_prefix = lax.dynamic_slice_in_dim(prefix_length, group_first, group_seqs)
    seq_pick = (group_sets[:, None] == jnp.arange(SETS, dtype=jnp.int32)[None, :]).astype(
        jnp.bfloat16
    )
    pick_a = set_rows(group_sets, lax.axis_index("col") * rows_a, rows_a)
    pick_b = set_rows(group_sets, lax.axis_index("row") * rows_b, rows_b)
    width_row = qkv_weight.shape[1]
    width_col = qkv_weight.shape[2]
    ff_col = expand_weight.shape[2]
    qkv_low_flat = qkv_lowrank.reshape(3 * SETS, width_row, ADAPTER_RANK)
    projected, inner_value = via_col_row(
        tokens[:, None], qkv_weight, qkv_low_flat, qkv_forward, seq_pick
    )
    qkv_wide = widen(inner_value.astype(jnp.bfloat16), pick_b, 3)
    projected = projected + adapter_out(qkv_wide, qkv_uprank)
    queries = projected[:, 0]
    keys = projected[:, 1]
    values = projected[:, 2]
    query_sq, key_sq = head_totals(queries * queries, keys * keys)
    query_scale = lax.rsqrt(query_sq / D + EPS)
    key_scale = lax.rsqrt(key_sq / D + EPS)
    query_norm = queries * query_scale[:, None] * headnorm_gain[0]
    key_norm = keys * key_scale[:, None] * headnorm_gain[1]
    local_heads = queries.shape[1] // HEAD
    half = HEAD // 2
    freq = THETA ** (-2.0 * jnp.arange(half, dtype=jnp.float32) / HEAD)
    position = (jnp.arange(rows_b, dtype=jnp.int32) % SEQUENCE_LENGTH).astype(jnp.float32)
    angle = position[:, None] * freq[None, :]
    cosine = jnp.cos(angle)[:, None, :]
    sine = jnp.sin(angle)[:, None, :]

    def rotate(source):
        heads = source.reshape(rows_b, local_heads, HEAD)
        first = heads[..., :half]
        second = heads[..., half:]
        return jnp.concatenate(
            [first * cosine - second * sine, second * cosine + first * sine], axis=-1
        )

    def unrotate(gradient_list):
        first = gradient_list[..., :half]
        second = gradient_list[..., half:]
        return jnp.concatenate(
            [first * cosine + second * sine, second * cosine - first * sine], axis=-1
        ).reshape(rows_b, local_heads * HEAD)

    query_b = rotate(query_norm).astype(jnp.bfloat16)
    key_b = rotate(key_norm).astype(jnp.bfloat16)
    value_b = values.astype(jnp.bfloat16).reshape(rows_b, local_heads, HEAD)
    block = min(512, SEQUENCE_LENGTH)
    blocks = rows_b // block
    key_pos = jnp.arange(SEQUENCE_LENGTH, dtype=jnp.int32)
    local_first = lax.axis_index("row") * (rows_b // SEQUENCE_LENGTH)
    scale = HEAD ** (-0.5)

    def scores_of(index):
        start = index * block
        seq_start = start // SEQUENCE_LENGTH * SEQUENCE_LENGTH
        which = local_first + start // SEQUENCE_LENGTH
        prefix = jnp.sum(
            jnp.where(jnp.arange(group_seqs, dtype=jnp.int32) == which, group_prefix, 0)
        )
        rows = start - seq_start + jnp.arange(block, dtype=jnp.int32)
        allowed = (key_pos[None, :] <= rows[:, None]) | (key_pos[None, :] < prefix)
        query_blk = lax.dynamic_slice_in_dim(query_b, start, block, 0)
        raw = (
            jnp.einsum("qhd,khd->hqk", query_blk, key_b, preferred_element_type=jnp.float32) * scale
        )
        return (jnp.where(allowed[None], raw, NEG), start, seq_start)

    def attend_block(index):
        scores, start, seq_start = scores_of(index)
        top = jnp.max(scores, axis=-1, keepdims=True)
        powers = jnp.exp(scores - top)
        total_sum = jnp.sum(powers, axis=-1, keepdims=True)
        weights = (powers / total_sum).astype(jnp.bfloat16)
        output = jnp.einsum("hqk,khd->qhd", weights, value_b, preferred_element_type=jnp.float32)
        return (output, (top + jnp.log(total_sum))[..., 0])

    attended, logsum = lax.map(attend_block, jnp.arange(blocks, dtype=jnp.int32))
    mixed_b = attended.reshape(rows_b, local_heads * HEAD).astype(jnp.bfloat16)
    attn_weight_four = attn_weight.reshape(1, 1, width_col, width_row)
    attn_low_four = attn_lowrank.reshape(1, SETS, width_col, ADAPTER_RANK)
    branch, inner_value = via_row_col(
        mixed_b[:, None], attn_weight_four, attn_low_four, single_forward, seq_pick
    )
    attn_wide = widen(inner_value.astype(jnp.bfloat16), pick_a, 1)
    branch = branch + adapter_out(attn_wide, attn_uprank[None])[:, 0]
    branch_scale = lax.rsqrt(row_total(branch * branch) / D + EPS)
    hidden = tokens.astype(jnp.float32) + post_gain[0] * branch * branch_scale[:, None]
    hidden_b = hidden.astype(jnp.bfloat16)
    expand_low_flat = expand_lowrank.reshape(2 * SETS, width_row, ADAPTER_RANK)
    gate_up, inner_value = via_col_row(
        hidden_b[:, None], expand_weight, expand_low_flat, expand_forward, seq_pick
    )
    expand_wide = widen(inner_value.astype(jnp.bfloat16), pick_b, 2)
    gate_up = gate_up + adapter_out(expand_wide, expand_uprank)
    gate = gate_up[:, 0]
    upper = gate_up[:, 1]
    act_b = swiglu(gate, upper).astype(jnp.bfloat16)
    reduce_weight_four = reduce_weight.reshape(1, 1, ff_col, width_row)
    reduce_low_four = reduce_lowrank.reshape(1, SETS, ff_col, ADAPTER_RANK)
    result, inner_value = via_row_col(
        act_b[:, None], reduce_weight_four, reduce_low_four, single_forward, seq_pick
    )
    reduce_wide = widen(inner_value.astype(jnp.bfloat16), pick_a, 1)
    result = result + adapter_out(reduce_wide, reduce_uprank[None])[:, 0]
    result_scale = lax.rsqrt(row_total(result * result) / D + EPS)
    layer_out = (hidden + post_gain[1] * result * result_scale[:, None]).astype(jnp.bfloat16)
    incoming = cotangent.astype(jnp.float32)
    d_result = norm_back(incoming, result, result_scale, post_gain[1]).astype(jnp.bfloat16)
    grad_reduce_up = up_grad(reduce_wide, d_result[:, None])[0]
    grad_reduce_up = sum_col_tokens(grad_reduce_up)
    reduce_up_flat = reduce_uprank.reshape(SETS * ADAPTER_RANK, width_row)
    d_act, inner_value = via_col_row(
        d_result[:, None], reduce_weight, reduce_up_flat, single_backward, seq_pick
    )
    act_wide = widen(inner_value.astype(jnp.bfloat16), pick_b, 1)
    d_act = d_act + adapter_grad_in(act_wide, reduce_lowrank[None])
    grad_reduce_low = low_grad(act_b, act_wide)[0]
    grad_reduce_low = sum_row_tokens(grad_reduce_low)
    unused, pullback = jax.vjp(swiglu, gate, upper)
    d_gate, d_upper = pullback(d_act)
    d_gate_up = jnp.stack([d_gate, d_upper], axis=1).astype(jnp.bfloat16)
    grad_expand_up = up_grad(expand_wide, d_gate_up)
    grad_expand_up = sum_row_tokens(grad_expand_up)
    expand_up_flat = expand_uprank.reshape(2 * SETS, ADAPTER_RANK, ff_col)
    d_hidden_in, inner_value = via_row_col(
        d_gate_up, expand_weight, expand_up_flat, multi_backward, seq_pick
    )
    hidden_wide = widen(inner_value.astype(jnp.bfloat16), pick_a, 2)
    d_hidden = incoming + d_hidden_in + adapter_grad_in(hidden_wide, expand_lowrank)
    grad_expand_low = low_grad(hidden_b, hidden_wide)
    grad_expand_low = sum_col_tokens(grad_expand_low)
    d_branch = norm_back(d_hidden, branch, branch_scale, post_gain[0]).astype(jnp.bfloat16)
    grad_attn_up = up_grad(attn_wide, d_branch[:, None])[0]
    grad_attn_up = sum_col_tokens(grad_attn_up)
    attn_up_flat = attn_uprank.reshape(SETS * ADAPTER_RANK, width_row)
    d_mixed, inner_value = via_col_row(
        d_branch[:, None], attn_weight, attn_up_flat, single_backward, seq_pick
    )
    mixed_wide = widen(inner_value.astype(jnp.bfloat16), pick_b, 1)
    d_mixed = (d_mixed + adapter_grad_in(mixed_wide, attn_lowrank[None])).astype(jnp.bfloat16)
    grad_attn_low = low_grad(mixed_b, mixed_wide)[0]
    grad_attn_low = sum_row_tokens(grad_attn_low)
    d_mixed_heads = d_mixed.reshape(rows_b, local_heads, HEAD)

    def back_block(index, carry):
        d_query, d_key, d_value = carry
        scores, start, seq_start = scores_of(index)
        probs = jnp.exp(
            scores - lax.dynamic_index_in_dim(logsum, index, 0, keepdims=False)[..., None]
        )
        grad_blk = lax.dynamic_slice_in_dim(d_mixed_heads, start, block, 0)
        query_blk = lax.dynamic_slice_in_dim(query_b, start, block, 0)
        d_probs = jnp.einsum("qhd,khd->hqk", grad_blk, value_b, preferred_element_type=jnp.float32)
        delta = jnp.sum(probs * d_probs, axis=-1, keepdims=True)
        d_scores = (probs * (d_probs - delta)).astype(jnp.bfloat16)
        query_part = scale * jnp.einsum(
            "hqk,khd->qhd", d_scores, key_b, preferred_element_type=jnp.float32
        )
        key_part = scale * jnp.einsum(
            "hqk,qhd->khd", d_scores, query_blk, preferred_element_type=jnp.float32
        )
        value_part = jnp.einsum(
            "hqk,qhd->khd", probs.astype(jnp.bfloat16), grad_blk, preferred_element_type=jnp.float32
        )
        d_query = lax.dynamic_update_slice_in_dim(d_query, query_part, start, 0)
        d_key = d_key + key_part
        d_value = d_value + value_part
        return (d_query, d_key, d_value)

    zeros = jnp.zeros((rows_b, local_heads, HEAD), jnp.float32)
    d_query, d_key, d_value = lax.fori_loop(0, blocks, back_block, (zeros, zeros, zeros))
    query_weighted = headnorm_gain[0] * unrotate(d_query)
    key_weighted = headnorm_gain[1] * unrotate(d_key)
    query_sum, key_sum = head_totals(query_weighted * queries, key_weighted * keys)
    d_queries = (
        query_scale[:, None] * query_weighted - queries * (query_scale**3 * query_sum / D)[:, None]
    )
    d_keys = key_scale[:, None] * key_weighted - keys * (key_scale**3 * key_sum / D)[:, None]
    d_qkv = jnp.stack(
        [d_queries, d_keys, d_value.reshape(rows_b, local_heads * HEAD)], axis=1
    ).astype(jnp.bfloat16)
    grad_qkv_up = up_grad(qkv_wide, d_qkv)
    grad_qkv_up = sum_row_tokens(grad_qkv_up)
    qkv_up_flat = qkv_uprank.reshape(3 * SETS, ADAPTER_RANK, width_col)
    d_tokens_in, inner_value = via_row_col(d_qkv, qkv_weight, qkv_up_flat, multi_backward, seq_pick)
    tokens_wide = widen(inner_value.astype(jnp.bfloat16), pick_a, 3)
    input_grad = d_hidden + d_tokens_in + adapter_grad_in(tokens_wide, qkv_lowrank)
    grad_qkv_low = low_grad(tokens, tokens_wide)
    grad_qkv_low = sum_col_tokens(grad_qkv_low)
    return (
        layer_out,
        input_grad,
        grad_qkv_low,
        grad_qkv_up,
        grad_attn_low,
        grad_attn_up,
        grad_expand_low,
        grad_expand_up,
        grad_reduce_low,
        grad_reduce_up,
    )


LOG2E = 1.4426950408889634
Q_BLOCK = 512
K_BLOCK = 512
HEADS_AT_ONCE = 2
BF = jnp.bfloat16
F32 = jnp.float32


def dot_of(left, right, left_dim, right_dim, out=F32):
    return lax.dot_general(
        left, right, (((left_dim,), (right_dim,)), ((), ())), preferred_element_type=out
    )


def attend_rows(query, limit, key_of, value_of, blocks):
    rows = query.shape[0]
    key_pos = lax.broadcasted_iota(jnp.int32, (K_BLOCK, rows), 0)

    def body(index, carry):
        top, total, mixed = carry
        at = pl.multiple_of(index * K_BLOCK, K_BLOCK)
        scores = dot_of(key_of(at), query, 1, 1) * (HEAD**-0.5 * LOG2E)
        scores = jnp.where(key_pos <= limit - at, scores, NEG)
        top_now = jnp.maximum(top, jnp.max(scores, axis=0, keepdims=True))
        fade = jnp.exp2(top - top_now)
        powers = jnp.exp2(scores - top_now)
        total = fade * total + jnp.sum(powers, axis=0, keepdims=True)
        mixed = mixed * fade + dot_of(value_of(at), powers.astype(BF), 0, 0)
        return top_now, total, mixed

    top, total, mixed = lax.fori_loop(
        0,
        blocks,
        body,
        (
            jnp.full((1, rows), NEG, F32),
            jnp.zeros((1, rows), F32),
            jnp.zeros((HEAD, rows), F32),
        ),
    )
    return mixed / total, top + jnp.log2(total)


def in_parts(values, count):
    parts = []
    for _ in range(count):
        part = values.astype(BF)
        parts.append(part)
        values = values - part.astype(F32)
    return parts


def row_sums(values):
    return sums_of(values)[0:1]


def attend_back_kernel(
    prefix_ref,
    q_ref,
    grad_ref,
    out_ref,
    log_ref,
    k_ref,
    v_ref,
    dq_ref,
    dk_ref,
    dv_ref,
    q_sum_ref,
    k_sum_ref,
):
    rows = q_ref.shape[0]
    start = pl.program_id(1) * rows
    prefix = prefix_ref[0]
    blocks = lax.div(jnp.maximum(start + rows, prefix) + K_BLOCK - 1, K_BLOCK)

    @pl.when(pl.program_id(1) == 0)
    def _():
        dk_ref[...] = jnp.zeros_like(dk_ref)
        dv_ref[...] = jnp.zeros_like(dv_ref)

    limit = jnp.maximum(lax.broadcasted_iota(jnp.int32, (1, rows), 1) + start, prefix - 1)
    key_pos = lax.broadcasted_iota(jnp.int32, (K_BLOCK, rows), 0)
    heads = [slice(h * HEAD, (h + 1) * HEAD) for h in range(HEADS_AT_ONCE)]
    deltas = [
        row_sums(grad_ref[:, lanes].astype(F32) * out_ref[:, lanes].astype(F32)) for lanes in heads
    ]

    def body(index, carry):
        at = pl.multiple_of(index * K_BLOCK, K_BLOCK)
        span = pl.ds(at, K_BLOCK)
        seen = key_pos <= limit - at
        sums = []
        for h, lanes in enumerate(heads):
            query, grad, key = q_ref[:, lanes], grad_ref[:, lanes], k_ref[span, lanes]
            scores = dot_of(key, query, 1, 1) * (HEAD**-0.5 * LOG2E)
            probs = jnp.where(seen, jnp.exp2(scores - log_ref[h]), 0.0)
            d_probs = dot_of(v_ref[span, lanes], grad, 1, 1)
            d_scores = (probs * (d_probs - deltas[h])).astype(BF)
            dv_ref[span, lanes] += dot_of(probs.astype(BF), grad, 1, 0)
            dk_ref[span, lanes] += dot_of(d_scores, query, 1, 0)
            sums.append(carry[h] + dot_of(d_scores, key, 0, 0))
        return tuple(sums)

    d_queries = lax.fori_loop(0, blocks, body, (jnp.zeros((rows, HEAD), F32),) * len(heads))
    for h, lanes in enumerate(heads):
        d_query = d_queries[h] * HEAD**-0.5
        dq_ref[:, lanes] = d_query
        q_sum_ref[h] = row_sums(d_query * q_ref[:, lanes].astype(F32))

    @pl.when(pl.program_id(1) == pl.num_programs(1) - 1)
    def _():
        for h, lanes in enumerate(heads):
            d_key = dk_ref[:, lanes] * HEAD**-0.5
            dk_ref[:, lanes] = d_key
            k_sum_ref[h] = row_sums(d_key * k_ref[:, lanes].astype(F32))


def attend_back(prefix, query, grad, mixed, log_total, key, value):
    rows, length, heads = query.shape[0], key.shape[0], query.shape[1] // HEAD
    wide = HEADS_AT_ONCE * HEAD
    q_spec = pl.BlockSpec((Q_BLOCK, wide), lambda h, i, p: (i, h))
    k_spec = pl.BlockSpec((length, wide), lambda h, i, p: (0, h))
    row_spec = pl.BlockSpec((HEADS_AT_ONCE, 1, Q_BLOCK), lambda h, i, p: (h, 0, i))
    return pl.pallas_call(
        attend_back_kernel,
        out_shape=(
            jax.ShapeDtypeStruct(query.shape, F32),
            jax.ShapeDtypeStruct(key.shape, F32),
            jax.ShapeDtypeStruct(key.shape, F32),
            jax.ShapeDtypeStruct((heads, 1, rows), F32),
            jax.ShapeDtypeStruct((heads, 1, length), F32),
        ),
        grid_spec=pltpu.PrefetchScalarGridSpec(
            num_scalar_prefetch=1,
            grid=(heads // HEADS_AT_ONCE, rows // Q_BLOCK),
            in_specs=[q_spec, q_spec, q_spec, row_spec, k_spec, k_spec],
            out_specs=[
                q_spec,
                k_spec,
                k_spec,
                row_spec,
                pl.BlockSpec((HEADS_AT_ONCE, 1, length), lambda h, i, p: (h, 0, 0)),
            ],
        ),
        cost_estimate=pl.CostEstimate(
            flops=7 * rows * length * heads * HEAD,
            bytes_accessed=24 * rows * heads * HEAD,
            transcendentals=rows * length * heads,
        ),
        name="attend_back",
    )(prefix, query, grad, mixed, log_total, key, value)


def rotate_kernel(raw_ref, scale_ref, gain_ref, cos_ref, sin_ref, q_ref, k_ref, v_ref):
    width = q_ref.shape[1]
    cosine = cos_ref[...]
    sine = sin_ref[...]
    scales = scale_ref[...]
    for part, out in ((0, q_ref), (1, k_ref)):
        scale = column_of(scales, part)
        for at in range(0, width, HEAD):
            normed = raw_ref[:, part * width + at : part * width + at + HEAD] * scale
            normed = normed * gain_ref[part : part + 1, at : at + HEAD]
            turned = normed * cosine + pltpu.roll(normed, HEAD // 2, 1) * sine
            out[:, at : at + HEAD] = turned.astype(BF)
    v_ref[...] = raw_ref[:, 2 * width :].astype(BF)


def rotate_rows(raw, scales, gains, cosine, sine):
    rows, width = raw.shape[0], raw.shape[1] // 3
    step = min(512, rows)
    out_spec = pl.BlockSpec((step, width), lambda i: (i, 0))
    table = pl.BlockSpec((step, HEAD), lambda i: (i, 0))
    return pl.pallas_call(
        rotate_kernel,
        out_shape=(jax.ShapeDtypeStruct((rows, width), BF),) * 3,
        grid=(rows // step,),
        in_specs=[
            pl.BlockSpec((step, 3 * width), lambda i: (i, 0)),
            pl.BlockSpec((8, step), lambda i: (0, i)),
            pl.BlockSpec((2, width), lambda i: (0, 0)),
            table,
            table,
        ],
        out_specs=[out_spec] * 3,
        name="rotate_rows",
    )(raw, scales, gains, cosine, sine)


def row_pack_kernel(set_ref, qkv_ref, attn_ref, expand_ref, reduce_ref, out_ref):
    for part in range(3):
        out_ref[16 * part : 16 * part + 16, :] = qkv_ref[part, 0]
    out_ref[48:64, :] = attn_ref[0]
    for part in range(2):
        out_ref[64 + 16 * part : 80 + 16 * part, :] = expand_ref[part, 0]
    out_ref[96:112, :] = reduce_ref[0]


def row_pack_of(which, qkv_low, attn_up, expand_low, reduce_up):
    width = attn_up.shape[2]
    one = pl.BlockSpec((1, 16, width), lambda i, c: (c[0], 0, 0))

    def many(parts):
        return pl.BlockSpec((parts, 1, 16, width), lambda i, c: (0, c[0], 0, 0))

    return pl.pallas_call(
        row_pack_kernel,
        out_shape=jax.ShapeDtypeStruct((112, width), BF),
        grid_spec=pltpu.PrefetchScalarGridSpec(
            num_scalar_prefetch=1,
            grid=(1,),
            in_specs=[many(3), one, many(2), one],
            out_specs=pl.BlockSpec((112, width), lambda i, c: (0, 0)),
        ),
        name="row_pack",
    )(which, qkv_low, attn_up, expand_low, reduce_up)


def col_pack_kernel(set_ref, qkv_ref, attn_ref, expand_ref, reduce_ref, out_ref):
    sub, ff_sub = qkv_ref.shape[3], expand_ref.shape[3]
    for part in range(3):
        out_ref[0, :, part * sub : (part + 1) * sub] = qkv_ref[part, 0]
    at = 4 * sub
    out_ref[0, :, 3 * sub : at] = attn_ref[0]
    for part in range(2):
        out_ref[0, :, at : at + ff_sub] = expand_ref[part, 0]
        at += ff_sub
    out_ref[0, :, at:] = reduce_ref[0]


def col_pack_of(which, qkv_up, attn_low, expand_up, reduce_low):
    cols = which.shape[0] - 1
    sub, ff_sub = qkv_up.shape[3] // 4, expand_up.shape[3] // 4

    def many(parts, size):
        return pl.BlockSpec((parts, 1, 16, size), lambda i, c: (0, c[i], 0, c[cols]))

    def one(size):
        return pl.BlockSpec((1, 16, size), lambda i, c: (c[i], 0, c[cols]))

    total = 4 * sub + 3 * ff_sub
    return pl.pallas_call(
        col_pack_kernel,
        out_shape=jax.ShapeDtypeStruct((cols, 16, total), BF),
        grid_spec=pltpu.PrefetchScalarGridSpec(
            num_scalar_prefetch=1,
            grid=(cols,),
            in_specs=[many(3, sub), one(sub), many(2, ff_sub), one(ff_sub)],
            out_specs=pl.BlockSpec((1, 16, total), lambda i, c: (i, 0, 0)),
        ),
        name="col_pack",
    )(which, qkv_up, attn_low, expand_up, reduce_low)


def finish_kernel(ids_ref, rows_ref, cols_ref, *outs):
    qkv_low, qkv_up, attn_low, attn_up, expand_low, expand_up, reduce_low, reduce_up = outs
    cols = cols_ref.shape[2]
    groups = 2 * cols
    step = pl.program_id(0)
    me = ids_ref[2 * groups]
    sub = qkv_up.shape[3] // 4
    ff_sub = expand_up.shape[3] // 4

    @pl.when(step == 0)
    def _():
        for out in outs:
            out[...] = jnp.zeros_like(out)

    here = ids_ref[step]
    term = rows_ref[step // 2, lax.rem(step, 2)].astype(F32)
    for part in range(3):
        qkv_low[part, here] += term[16 * part : 16 * part + 16]
    attn_up[here] += term[48:64]
    for part in range(2):
        expand_low[part, here] += term[64 + 16 * part : 80 + 16 * part]
    reduce_up[here] += term[96:112]
    here = ids_ref[groups + step]
    for row in range(4):
        term = cols_ref[me ^ row, step // cols, lax.rem(step, cols)].astype(F32)
        near = slice(row * sub, (row + 1) * sub)
        wide = slice(row * ff_sub, (row + 1) * ff_sub)
        for part in range(3):
            qkv_up[part, here, :, near] += term[:, part * sub : (part + 1) * sub]
        attn_low[here, :, near] += term[:, 3 * sub : 4 * sub]
        for part in range(2):
            at = 4 * sub + part * ff_sub
            expand_up[part, here, :, wide] += term[:, at : at + ff_sub]
        reduce_low[here, :, wide] += term[:, 4 * sub + 2 * ff_sub :]


def finish_call(ids, rows, cols, sub, ff_sub):
    width = rows.shape[3]
    shapes = [
        (3, width),
        (3, 4 * sub),
        (0, 4 * sub),
        (0, width),
        (2, width),
        (2, 4 * ff_sub),
        (0, 4 * ff_sub),
        (0, width),
    ]
    out_shape, out_specs = [], []
    for parts, size in shapes:
        if parts:
            out_shape.append(jax.ShapeDtypeStruct((parts, SETS, 16, size), F32))
            out_specs.append(pl.BlockSpec((parts, SETS, 16, size), lambda k, c: (0, 0, 0, 0)))
        else:
            out_shape.append(jax.ShapeDtypeStruct((SETS, 16, size), F32))
            out_specs.append(pl.BlockSpec((SETS, 16, size), lambda k, c: (0, 0, 0)))

    def whole(array):
        return pl.BlockSpec(array.shape, lambda k, c: (0,) * array.ndim)

    return pl.pallas_call(
        finish_kernel,
        out_shape=out_shape,
        grid_spec=pltpu.PrefetchScalarGridSpec(
            num_scalar_prefetch=1,
            grid=(2 * cols.shape[2],),
            in_specs=[whole(rows), whole(cols)],
            out_specs=out_specs,
        ),
        name="finish",
    )(ids, rows, cols)


def cost_of(flops, bytes_accessed):
    return pl.CostEstimate(flops=int(flops), bytes_accessed=int(bytes_accessed), transcendentals=0)


def row_tile(rows):
    return min(512, rows)


def merge_rows_kernel(pair_ref, own_ref, other_ref, low_ref, up_ref, out_ref):
    def put(piece):
        for block in range(4):
            base = piece[0, block].astype(F32)
            extra = dot_of(low_ref[block, 0], up_ref[...], 0, 0)
            out_ref[block, 0] = (base + ADAPTER_FACTOR * extra).astype(BF)

    mine = pl.program_id(0) == pair_ref[0]
    pl.when(mine)(functools.partial(put, own_ref))
    pl.when(jnp.logical_not(mine))(functools.partial(put, other_ref))


def merge_qkv_kernel(pair_ref, own_ref, other_ref, low_ref, up_ref, out_ref):
    cols, sub = own_ref.shape[0], own_ref.shape[4]

    def put(piece, back):
        for block in range(4):
            extra = dot_of(low_ref[block, 0], up_ref[...], 0, 0)
            for index in range(cols):
                at = lax.rem(index - back + cols, cols)
                lanes = slice(index * sub, (index + 1) * sub)
                base = piece[at, block, 0].astype(F32)
                out_ref[block, 0, :, lanes] = (base + ADAPTER_FACTOR * extra[:, lanes]).astype(BF)

    mine = pl.program_id(0) == pair_ref[0]
    pl.when(mine)(functools.partial(put, own_ref, 0))
    pl.when(jnp.logical_not(mine))(functools.partial(put, other_ref, pair_ref[1]))


def merge_columns_kernel(pair_ref, *refs):
    *pieces, low_ref, up_ref, out_ref = refs
    width = out_ref.shape[1] // 4

    def put(piece):
        for block in range(4):
            span = slice(block * width, (block + 1) * width)
            extra = dot_of(low_ref[0], up_ref[:, span], 0, 0)
            out_ref[:, span] = (piece[0, block].astype(F32) + ADAPTER_FACTOR * extra).astype(BF)

    if len(pieces) == 1:
        put(pieces[0])
        return
    mine = pl.program_id(0) == pair_ref[0]
    pl.when(mine)(functools.partial(put, pieces[0]))
    pl.when(jnp.logical_not(mine))(functools.partial(put, pieces[1]))


def merge_qkv(pair, own, other, low, up):
    cols, _, parts, cut, sub = own.shape

    def piece(half):
        def place(h, p, pair_ref):
            mine = h == half(pair_ref[0])
            return (0, 0, jnp.where(mine, p, jnp.where(h == 0, 0, parts - 1)), 0, 0)

        return pl.BlockSpec((cols, 4, 1, cut, sub), place)

    whole = pl.pallas_call(
        merge_qkv_kernel,
        out_shape=jax.ShapeDtypeStruct((4, 2, cut, parts * cols * sub), BF),
        grid_spec=pltpu.PrefetchScalarGridSpec(
            num_scalar_prefetch=1,
            grid=(2, parts),
            in_specs=[
                piece(lambda one: one),
                piece(lambda one: 1 - one),
                pl.BlockSpec((4, 1, 16, cut), lambda h, p, one: (0, h, p, 0)),
                pl.BlockSpec((16, cols * sub), lambda h, p, one: (p, 0)),
            ],
            out_specs=pl.BlockSpec((4, 1, cut, cols * sub), lambda h, p, one: (0, h, 0, p)),
        ),
        cost_estimate=cost_of(0, 8 * own.size),
        name="merge_qkv",
    )(pair, own, other, low.reshape(16 * parts, 4, 2, cut).transpose(1, 2, 0, 3), up)
    return whole.reshape(8 * cut, parts * cols * sub)


def half_specs(block, cols):
    def piece(half, relative):
        def place(h, c, pair_ref):
            at = jnp.where(h == half(pair_ref[0]), c, jnp.where(h == 0, 0, cols - 1))
            if relative:
                at = lax.rem(at - pair_ref[1] + cols, cols)
            return (at,) + (0,) * (len(block) - 1)

        return pl.BlockSpec(block, place)

    return [piece(lambda one: one, False), piece(lambda one: 1 - one, True)]


def merge_expand(pair, own, other, low, up):
    cols, _, width, cut = own.shape
    whole = pl.pallas_call(
        merge_rows_kernel,
        out_shape=jax.ShapeDtypeStruct((4, 1, width, 2 * cols * cut), BF),
        grid_spec=pltpu.PrefetchScalarGridSpec(
            num_scalar_prefetch=1,
            grid=(2, cols),
            in_specs=half_specs((1, 4, width, cut), cols)
            + [
                pl.BlockSpec((4, 1, 16, width), lambda h, c, one: (0, 0, 0, 0)),
                pl.BlockSpec((16, cut), lambda h, c, one: (0, 2 * c + h)),
            ],
            out_specs=pl.BlockSpec((4, 1, width, cut), lambda h, c, one: (0, 0, 0, 2 * c + h)),
        ),
        cost_estimate=cost_of(0, 8 * own.size),
        name="merge_expand",
    )(pair, own, other, low.reshape(16, 4, 1, width).transpose(1, 2, 0, 3), up)
    return whole.reshape(4 * width, 2 * cols * cut)


def merge_out(pair, pieces, low, up):
    cols, _, rows, width = pieces[0].shape
    takes = len(pieces)
    block = (1, 4, rows, width)
    specs = half_specs(block, cols)
    if takes == 1:
        specs = [pl.BlockSpec(block, lambda h, c, one: (c, 0, 0, 0))]
    return pl.pallas_call(
        merge_columns_kernel,
        out_shape=jax.ShapeDtypeStruct((takes * cols * rows, 4 * width), BF),
        grid_spec=pltpu.PrefetchScalarGridSpec(
            num_scalar_prefetch=1,
            grid=(takes, cols),
            in_specs=specs
            + [
                pl.BlockSpec((1, 16, rows), lambda h, c, one: (takes * c + h, 0, 0)),
                pl.BlockSpec((16, 4 * width), lambda h, c, one: (0, 0)),
            ],
            out_specs=pl.BlockSpec((rows, 4 * width), lambda h, c, one: (takes * c + h, 0)),
        ),
        cost_estimate=cost_of(0, 4 * takes * pieces[0].size),
        name="merge_out",
    )(pair, *pieces, low.reshape(16, takes * cols, rows).transpose(1, 0, 2), up)


def mixed_back_kernel(x0, x1, x2, x3, matrix_ref, up_ref, out_ref, inner_ref):
    left = jnp.concatenate([x0[...], x1[...], x2[...], x3[...]], axis=1)
    out_ref[...] = dot_of(left, matrix_ref[...], 1, 1).astype(BF)
    inner_ref[...] = (ADAPTER_FACTOR * dot_of(up_ref[...], left, 1, 1)).astype(BF)


def mixed_back(lefts, matrix, up):
    rows, width = lefts[0].shape
    local = matrix.shape[0]
    tile = row_tile(rows)

    def whole(array):
        return pl.BlockSpec(array.shape, lambda m: (0, 0))

    return pl.pallas_call(
        mixed_back_kernel,
        out_shape=[
            jax.ShapeDtypeStruct((rows, local), BF),
            jax.ShapeDtypeStruct((16, rows), BF),
        ],
        grid=(rows // tile,),
        in_specs=[pl.BlockSpec((tile, width), lambda m: (m, 0))] * 4 + [whole(matrix), whole(up)],
        out_specs=[
            pl.BlockSpec((tile, local), lambda m: (m, 0)),
            pl.BlockSpec((16, tile), lambda m: (0, m)),
        ],
        cost_estimate=cost_of(8 * rows * width * local, 8 * width * (rows + local)),
        name="mixed_back",
    )(*lefts, matrix, up)


BLOCK = 256
RING = 5


def peer(step):
    return {"row": lax.axis_index("row") ^ step}


def send(source, target, sems, index, step):
    return pltpu.make_async_remote_copy(
        src_ref=source,
        dst_ref=target,
        send_sem=sems.at[0, index],
        recv_sem=sems.at[1, index],
        device_id=peer(step),
        device_id_type=pl.DeviceIdType.MESH,
    )


def greet():
    barrier = pltpu.get_barrier_semaphore()
    for step in (1, 2, 3):
        pl.semaphore_signal(
            barrier, inc=1, device_id=peer(step), device_id_type=pl.DeviceIdType.MESH
        )
    pl.semaphore_wait(barrier, 3)


def exchange_scratch(count, width, gathers):
    sem = pltpu.SemaphoreType.DMA((2, count))
    shapes = [
        pltpu.VMEM((2, 2, BLOCK, width), BF),
        pltpu.VMEM((count, 2, BLOCK, width), BF),
        pltpu.VMEM((2, BLOCK, width), F32),
        pltpu.VMEM((2, BLOCK, width), BF),
        pltpu.VMEM((count, BLOCK, width), BF),
        pltpu.VMEM((RING, BLOCK, width), F32),
        sem,
        sem,
    ]
    if gathers:
        shapes += [
            pltpu.VMEM((count, 8, BLOCK), F32),
            pltpu.VMEM((3, count, 8, BLOCK), F32),
        ] + [sem] * 6
    return shapes


def run_blocks(
    count, bufs, compute, stats, finish, own_ref=None, arrived=None, extra=None, own_rows=None
):
    pair_out, pair_in, far, side_out, side_in, near, pair_sem, side_sem, *rest = bufs
    gathers = own_ref is not None
    if gathers:
        stat_own, stat_in, stat_1, stat_2, stat_3, core_sem, far_sem, relay_sem = rest
        stat_sems = (stat_1, stat_2, stat_3)

    def rows_of(c):
        return pl.ds(pl.multiple_of(c * BLOCK, BLOCK), BLOCK)

    def to_core(c):
        return send(pair_out.at[lax.rem(c, 2)], pair_in.at[c], pair_sem, c, 1)

    def to_side(c):
        return send(side_out.at[lax.rem(c, 2)], side_in.at[c], side_sem, c, 2)

    def to_stat(c, step):
        return send(stat_own.at[c], stat_in.at[step - 1, c], stat_sems[step - 1], c, step)

    def gather_core(c):
        return send(own_ref.at[rows_of(c)], arrived[0].at[rows_of(c)], core_sem, c, 1)

    def gather_side(c):
        return send(own_ref.at[rows_of(c)], arrived[1].at[rows_of(c)], far_sem, c, 2)

    def relay(c):
        return send(arrived[1].at[rows_of(c)], arrived[2].at[rows_of(c)], relay_sem, c, 1)

    def stage(c, body):
        pl.when(jnp.logical_and(c >= 0, c < count))(functools.partial(body, c))

    def multiply(c):
        @pl.when(c >= 2)
        def _():
            to_core(c - 2).wait_send()

        slot = lax.rem(c, 2)

        def put(block, value):
            if block == 0:
                near[lax.rem(c, RING)] = value
            elif block == 2:
                far[slot] = value
            else:
                pair_out[slot, block // 2] = value.astype(BF)
            if block == 3:
                to_core(c).start()

        compute(c, put)

    def sum_core(c):
        @pl.when(c >= 2)
        def _():
            to_side(c - 2).wait_send()

        to_core(c).wait_recv()
        slot = lax.rem(c, 2)
        side_out[slot] = (far[slot] + pair_in[c, 1].astype(F32)).astype(BF)
        to_side(c).start()
        at = lax.rem(c, RING)
        near[at] = near[at] + pair_in[c, 0].astype(F32)
        if extra is not None:
            extra[0](c)

    def sum_side(c):
        if extra is not None:
            extra[1](c)
        to_side(c).wait_recv()
        at = lax.rem(c, RING)
        total = near[at] + side_in[c].astype(F32)
        if not gathers:
            finish(c, rows_of(c), total)
            return
        near[at] = total
        stat_own[c] = stats(c, rows_of(c), total)
        for step in (1, 2, 3):
            to_stat(c, step).start()

    def normalise(c):
        total = stat_own[c]
        for step in (1, 2, 3):
            to_stat(c, step).wait_recv()
            total = total + stat_in[step - 1, c]
        own_ref[rows_of(c), :] = finish(c, rows_of(c), near[lax.rem(c, RING)], total)
        gather_side(c).start()
        gather_core(c).start()
        if own_rows is not None:
            own_rows(c).start()

    def pass_on(c):
        gather_side(c).wait_recv()
        relay(c).start()

    def body(t, carry):
        stage(t - 1, sum_core)
        stage(t, multiply)
        stage(t - 2, sum_side)
        if gathers:
            stage(t - 3, normalise)
            stage(t - 4, pass_on)
        return carry

    lax.fori_loop(0, count + (4 if gathers else 2), body, 0)

    def close(c, carry):
        if gathers:
            for step in (1, 2, 3):
                to_stat(c, step).wait_send()
            gather_core(c).wait()
            gather_side(c).wait_send()
            relay(c).wait()
        return carry

    if gathers:
        lax.fori_loop(0, count, close, 0)
    for c in range(max(count - 2, 0), count):
        to_core(c).wait_send()
        to_side(c).wait_send()


def sums_of(*values):
    out = None
    for index, value in enumerate(values):
        pick = lax.broadcasted_iota(jnp.int32, (8, value.shape[1]), 0) == index
        pick = pick.astype(F32).astype(BF)
        for part in in_parts(value, 2):
            term = dot_of(pick, part, 1, 1)
            out = term if out is None else out + term
    return out


def column_of(stats, index):
    parts = jnp.concatenate(in_parts(stats, 3), axis=0)
    pick = lax.rem(lax.broadcasted_iota(jnp.int32, (parts.shape[0], HEAD), 0), 8) == index
    return dot_of(parts, pick.astype(F32).astype(BF), 0, 0)[:, :1]


def branch_kernel(
    q_ref,
    k_ref,
    v_ref,
    limit_ref,
    matrix_ref,
    tokens_ref,
    gain_ref,
    gate_all,
    gate_part,
    upper_all,
    upper_rest,
    mixed_ref,
    log_ref,
    branch_ref,
    hidden_ref,
    stat_ref,
    own_ref,
    *rest,
):
    arrived, halves, rest = rest[:3], rest[3:5], rest[5:]
    swap_sems, local_sem, *bufs = rest
    width = own_ref.shape[1]
    count = own_ref.shape[0] // BLOCK
    greet_all([peer(step) for step in (1, 2, 3)] + [other_of_pair()])
    later = range(2, gate_all.shape[0])
    swaps = exchange_halves(
        gate_all, None, halves[0], swap_sems.at[0], local_sem.at[0], later
    )
    swaps += exchange_halves(upper_all, upper_rest, halves[1], swap_sems.at[1], local_sem.at[1])
    for copy in swaps:
        copy.start()

    heads = log_ref.shape[0]

    def attend(group):
        rows = span_of(group, Q_BLOCK)
        reach = jnp.maximum((group + 1) * Q_BLOCK, SEQUENCE_LENGTH // 2)

        def head(h, carry):
            lanes = span_of(h, HEAD)
            mixed, logs = attend_rows(
                q_ref[rows, lanes],
                limit_ref[:, rows],
                lambda at: k_ref[pl.ds(at, K_BLOCK), lanes],
                lambda at: v_ref[pl.ds(at, K_BLOCK), lanes],
                reach // K_BLOCK,
            )
            mixed_ref[rows, lanes] = mixed.T.astype(BF)
            log_ref[h, :, rows] = logs
            return carry

        lax.fori_loop(0, heads, head, 0)

    def compute(c, put):
        ratio = Q_BLOCK // BLOCK
        pl.when(lax.rem(c, ratio) == 0)(lambda: attend(c // ratio))
        left = mixed_ref[pl.ds(pl.multiple_of(c * BLOCK, BLOCK), BLOCK), :]
        for block in (1, 3, 2, 0):
            put(block, dot_of(left, matrix_ref[:, block * width : (block + 1) * width], 1, 0))

    def stats(c, rows, branch):
        branch_ref[rows, :] = branch
        return sums_of(branch * branch)

    def finish(c, rows, branch, total):
        stat_ref[c] = total
        scale = lax.rsqrt(column_of(total, 0) / D + EPS)
        hidden = tokens_ref[rows, :].astype(F32) + gain_ref[0:1, :] * branch * scale
        hidden_ref[rows, :] = hidden
        return hidden.astype(BF)

    run_blocks(count, bufs, compute, stats, finish, own_ref, arrived)
    wait_all(swaps)


VMEM_SPEC = pl.BlockSpec(memory_space=pltpu.VMEM)
ANY_SPEC = pl.BlockSpec(memory_space=pl.ANY)


def talk_params(number):
    return pltpu.CompilerParams(
        collective_id=number, has_side_effects=True, vmem_limit_bytes=63 * 2**20
    )


def branch_call(query, key, value, limit, matrix, tokens, gain, halves):
    rows, width = tokens.shape
    local = query.shape[1]
    count = rows // BLOCK
    cols = halves[0].shape[0]
    part = jax.ShapeDtypeStruct((rows, width), BF)
    whole = jax.ShapeDtypeStruct((rows, width), F32)
    half = jax.ShapeDtypeStruct(halves[0].shape, BF)
    return pl.pallas_call(
        branch_kernel,
        out_shape=[
            jax.ShapeDtypeStruct((rows, local), BF),
            jax.ShapeDtypeStruct((local // HEAD, 1, rows), F32),
            whole,
            whole,
            jax.ShapeDtypeStruct((count, 8, BLOCK), F32),
        ]
        + [part] * 4
        + [half] * 2,
        in_specs=[VMEM_SPEC] * 7 + [ANY_SPEC] * 4,
        out_specs=[VMEM_SPEC] * 6 + [ANY_SPEC] * 5,
        scratch_shapes=[
            pltpu.SemaphoreType.DMA((2, 2, cols - 1)),
            pltpu.SemaphoreType.DMA((2,)),
        ]
        + exchange_scratch(count, width, True),
        input_output_aliases={8: 9},
        compiler_params=talk_params(0),
        cost_estimate=cost_of(8 * rows * width * matrix.shape[0], 2**27),
        name="branch",
    )(query, key, value, limit, matrix, tokens, gain, *halves)


def rows_out(buffer, outer, sems, index):
    def copy(c):
        rows = span_of(c, BLOCK)
        return pltpu.make_async_copy(buffer.at[rows], outer.at[rows], sems.at[index, c])

    return copy


def wait_rows(count, *copies):
    def body(c, carry):
        for copy in copies:
            copy(c).wait()
        return carry

    lax.fori_loop(0, count, body, 0)


def load_lefts(lefts, buffer, sems, count):
    width = buffer.shape[2] // 4

    def copies(c):
        slot = lax.rem(c, 2)
        rows = pl.ds(pl.multiple_of(c * BLOCK, BLOCK), BLOCK)
        return [
            pltpu.make_async_copy(
                left.at[rows], buffer.at[slot, :, index * width : (index + 1) * width], sems.at[slot, index]
            )
            for index, left in enumerate(lefts)
        ]

    def start(c):
        @pl.when(c < count)
        def _():
            for copy in copies(c):
                copy.start()

    def wait(c):
        for copy in copies(c):
            copy.wait()

    return start, wait


def move_rows(outer, buffer, sems, index, inward):
    def copy(c):
        slot = lax.rem(c, 2)
        rows = pl.ds(pl.multiple_of(c * BLOCK, BLOCK), BLOCK)
        ends = (outer.at[rows], buffer.at[slot])
        if not inward:
            ends = ends[::-1]
        return pltpu.make_async_copy(*ends, sems.at[index, slot])

    return copy


def forward_kernel(
    x0,
    x1,
    x2,
    x3,
    gate_hbm,
    upper_hbm,
    reduce_hbm,
    hidden_hbm,
    cot_hbm,
    gain_ref,
    expand_low_ref,
    reduce_low_ref,
    act_out,
    gate_out,
    upper_out,
    layer_out,
    expand_inner_ref,
    reduce_inner_ref,
    own_out,
    *rest,
):
    arrived, rest = rest[:3], rest[3:]
    gate_w, upper_w, reduce_w, lefts, act_buf, gate_buf, upper_buf, *rest = rest
    hidden_ref, cot_ref, layer_ref, own_ref, w_sem, x_sem, o_sem, r_sem, *bufs = rest
    width = own_ref.shape[1]
    count = own_ref.shape[0] // BLOCK
    ff = gate_w.shape[1]
    tile = min(1024, ff)
    loads = [
        pltpu.make_async_copy(source, target, w_sem.at[index])
        for index, (source, target) in enumerate(
            (
                (gate_hbm, gate_w),
                (upper_hbm, upper_w),
                (reduce_hbm, reduce_w),
                (cot_hbm, cot_ref),
                (hidden_hbm, hidden_ref),
            )
        )
    ]
    start_left, wait_left = load_lefts((x0, x1, x2, x3), lefts, x_sem, count)
    start_left(0)
    for load in loads:
        load.start()
    layer_rows = rows_out(layer_ref, layer_out, r_sem, 0)
    own_rows = rows_out(own_ref, own_out, r_sem, 1)
    greet()
    outs = [
        move_rows(outer, buffer, o_sem, index, False)
        for index, (outer, buffer) in enumerate(
            ((act_out, act_buf), (gate_out, gate_buf), (upper_out, upper_buf))
        )
    ]

    def compute(c, put):
        slot = lax.rem(c, 2)
        wait_left(c)
        start_left(c + 1)

        @pl.when(c == 0)
        def _():
            loads[0].wait()
            loads[1].wait()

        @pl.when(c >= 2)
        def _():
            for out in outs:
                out(c - 2).wait()

        def tiles(n, carry):
            at = pl.ds(pl.multiple_of(n * tile, tile), tile)
            left = lefts[slot]
            gate = dot_of(left, gate_w[:, at], 1, 0)
            upper = dot_of(left, upper_w[:, at], 1, 0)
            act_buf[slot, :, at] = (gate * jax.nn.sigmoid(gate) * upper).astype(BF)
            gate_buf[slot, :, at] = gate.astype(BF)
            upper_buf[slot, :, at] = upper.astype(BF)
            return carry

        lax.fori_loop(0, ff // tile, tiles, 0)
        for out in outs:
            out(c).start()

        @pl.when(c == 0)
        def _():
            loads[2].wait()

        for block in (1, 3, 2, 0):
            span = slice(block * width, (block + 1) * width)
            put(block, dot_of(act_buf[slot], reduce_w[:, span], 1, 0))
        rows = span_of(c, BLOCK)
        expand_inner_ref[:, rows] = dot_of(expand_low_ref[...], lefts[slot], 1, 1).astype(BF)
        reduce_inner_ref[:, rows] = dot_of(reduce_low_ref[...], act_buf[slot], 1, 1)

    def stats(c, rows, result):
        @pl.when(c == 0)
        def _():
            loads[3].wait()
            loads[4].wait()

        weighted = gain_ref[1:2, :] * cot_ref[rows, :].astype(F32)
        return sums_of(result * result, weighted * result)

    def finish(c, rows, result, total):
        scale = lax.rsqrt(column_of(total, 0) / D + EPS)
        gain = gain_ref[1:2, :]
        layer_ref[rows, :] = (hidden_ref[rows, :] + gain * result * scale).astype(BF)
        layer_rows(c).start()
        weighted = gain * cot_ref[rows, :].astype(F32)
        inner = column_of(total, 1)
        return (scale * weighted - result * (scale * scale * scale * inner / D)).astype(BF)

    run_blocks(count, bufs, compute, stats, finish, own_ref, arrived, own_rows=own_rows)
    wait_rows(count, layer_rows, own_rows)
    for c in range(max(count - 2, 0), count):
        for out in outs:
            out(c).wait()


def forward_call(lefts, gate_w, upper_w, reduce_w, hidden, cotangent, gain, low, reduce_low):
    rows, width = hidden.shape
    count = rows // BLOCK
    ff = gate_w.shape[1]
    part = jax.ShapeDtypeStruct((rows, width), BF)
    wide = jax.ShapeDtypeStruct((rows, ff), BF)
    return pl.pallas_call(
        forward_kernel,
        out_shape=[wide] * 3
        + [
            part,
            jax.ShapeDtypeStruct((32, rows), BF),
            jax.ShapeDtypeStruct((16, rows), F32),
        ]
        + [part] * 4,
        in_specs=[ANY_SPEC] * 9 + [VMEM_SPEC] * 3,
        out_specs=[ANY_SPEC] * 4 + [VMEM_SPEC] * 2 + [ANY_SPEC] * 4,
        scratch_shapes=[
            pltpu.VMEM(gate_w.shape, BF),
            pltpu.VMEM(upper_w.shape, BF),
            pltpu.VMEM(reduce_w.shape, BF),
            pltpu.VMEM((2, BLOCK, 4 * width), BF),
            pltpu.VMEM((2, BLOCK, ff), BF),
            pltpu.VMEM((2, BLOCK, ff), BF),
            pltpu.VMEM((2, BLOCK, ff), BF),
            pltpu.VMEM((rows, width), F32),
            pltpu.VMEM((rows, width), BF),
            pltpu.VMEM((rows, width), BF),
            pltpu.VMEM((rows, width), BF),
            pltpu.SemaphoreType.DMA((5,)),
            pltpu.SemaphoreType.DMA((2, 4)),
            pltpu.SemaphoreType.DMA((3, 2)),
            pltpu.SemaphoreType.DMA((2, count)),
        ]
        + exchange_scratch(count, width, True),
        compiler_params=talk_params(1),
        cost_estimate=cost_of(24 * rows * width * ff, 2**27),
        name="forward",
    )(*lefts, gate_w, upper_w, reduce_w, hidden, cotangent, gain, low, reduce_low)


def backward_kernel(
    x0,
    x1,
    x2,
    x3,
    gate_hbm,
    upper_hbm,
    reduce_hbm,
    gate_in,
    upper_in,
    cot_hbm,
    branch_hbm,
    stat_ref,
    gain_ref,
    reduce_up_ref,
    expand_up_ref,
    expand_inner_ref,
    d_hidden_out,
    reduce_inner_ref,
    d_inner_ref,
    up_grad_ref,
    own_out,
    *rest,
):
    arrived, rest = rest[:3], rest[3:]
    gate_w, upper_w, reduce_w, lefts, gate_buf, upper_buf, d_gate_buf, d_upper_buf, *rest = rest
    branch_ref, cot_ref, d_hidden_ref, own_ref, w_sem, x_sem, i_sem, r_sem, *bufs = rest
    width = own_ref.shape[1]
    count = own_ref.shape[0] // BLOCK
    ff = gate_w.shape[1]
    up_grad_ref[...] = jnp.zeros_like(up_grad_ref)
    tile = min(1024, ff)
    loads = [
        pltpu.make_async_copy(source, target, w_sem.at[index])
        for index, (source, target) in enumerate(
            (
                (reduce_hbm, reduce_w),
                (gate_hbm, gate_w),
                (upper_hbm, upper_w),
                (cot_hbm, cot_ref),
                (branch_hbm, branch_ref),
            )
        )
    ]
    start_left, wait_left = load_lefts((x0, x1, x2, x3), lefts, x_sem, count)
    ins = [
        move_rows(outer, buffer, i_sem, index, True)
        for index, (outer, buffer) in enumerate(((gate_in, gate_buf), (upper_in, upper_buf)))
    ]
    start_left(0)
    for one in ins:
        one(0).start()
    for load in loads:
        load.start()
    hidden_rows = rows_out(d_hidden_ref, d_hidden_out, r_sem, 0)
    own_rows = rows_out(own_ref, own_out, r_sem, 1)
    greet()

    def compute(c, put):
        slot = lax.rem(c, 2)
        wait_left(c)
        start_left(c + 1)
        for one in ins:
            one(c).wait()

        @pl.when(c + 1 < count)
        def _():
            for one in ins:
                one(c + 1).start()

        @pl.when(c == 0)
        def _():
            loads[0].wait()

        def tiles(n, carry):
            at = pl.ds(pl.multiple_of(n * tile, tile), tile)
            d_act = dot_of(lefts[slot], reduce_w[at, :], 1, 1)
            gate = gate_buf[slot, :, at].astype(F32)
            sigma = jax.nn.sigmoid(gate)
            d_gate = d_act * upper_buf[slot, :, at].astype(F32) * (sigma * (1 + gate * (1 - sigma)))
            d_gate_buf[:, at] = d_gate.astype(BF)
            d_upper_buf[:, at] = (d_act * (gate * sigma)).astype(BF)
            return carry

        lax.fori_loop(0, ff // tile, tiles, 0)
        @pl.when(c == 0)
        def _():
            loads[1].wait()
            loads[2].wait()

        for block in (1, 3, 2, 0):
            span = slice(block * width, (block + 1) * width)
            put(
                block,
                dot_of(d_gate_buf[...], gate_w[span, :], 1, 1)
                + dot_of(d_upper_buf[...], upper_w[span, :], 1, 1),
            )
        rows = span_of(c, BLOCK)
        inner = dot_of(reduce_up_ref[...], lefts[slot], 1, 1)
        reduce_inner_ref[:, rows] = (ADAPTER_FACTOR * inner).astype(BF)
        for part, grad in enumerate((d_gate_buf, d_upper_buf)):
            own = slice(16 * part, 16 * part + 16)
            d_inner_ref[own, rows] = ADAPTER_FACTOR * dot_of(expand_up_ref[own, :], grad[...], 1, 1)
            up_grad_ref[own, :] += ADAPTER_FACTOR * dot_of(
                expand_inner_ref[own, rows], grad[...], 1, 0
            )

    def stats(c, rows, total):
        @pl.when(c == 0)
        def _():
            loads[3].wait()
            loads[4].wait()

        d_hidden = cot_ref[rows, :].astype(F32) + total
        d_hidden_ref[rows, :] = d_hidden
        hidden_rows(c).start()
        return sums_of(gain_ref[0:1, :] * d_hidden * branch_ref[rows, :])

    def finish(c, rows, total, sums):
        scale = lax.rsqrt(column_of(stat_ref[c], 0) / D + EPS)
        weighted = gain_ref[0:1, :] * d_hidden_ref[rows, :]
        inner = column_of(sums, 0)
        back = scale * scale * scale * inner / D
        return (scale * weighted - branch_ref[rows, :] * back).astype(BF)

    run_blocks(count, bufs, compute, stats, finish, own_ref, arrived, own_rows=own_rows)
    wait_rows(count, hidden_rows, own_rows)


def backward_call(
    lefts, gate_w, upper_w, reduce_w, gate, upper, cotangent, branch, stats, gain, *adapters
):
    rows, width = branch.shape
    count = rows // BLOCK
    ff = gate_w.shape[1]
    part = jax.ShapeDtypeStruct((rows, width), BF)
    return pl.pallas_call(
        backward_kernel,
        out_shape=[
            jax.ShapeDtypeStruct((rows, width), F32),
            jax.ShapeDtypeStruct((16, rows), BF),
            jax.ShapeDtypeStruct((32, rows), F32),
            jax.ShapeDtypeStruct((32, ff), F32),
        ]
        + [part] * 4,
        in_specs=[ANY_SPEC] * 11 + [VMEM_SPEC] * 5,
        out_specs=[ANY_SPEC] + [VMEM_SPEC] * 3 + [ANY_SPEC] * 4,
        scratch_shapes=[
            pltpu.VMEM(gate_w.shape, BF),
            pltpu.VMEM(upper_w.shape, BF),
            pltpu.VMEM(reduce_w.shape, BF),
            pltpu.VMEM((2, BLOCK, 4 * width), BF),
            pltpu.VMEM((2, BLOCK, ff), BF),
            pltpu.VMEM((2, BLOCK, ff), BF),
            pltpu.VMEM((BLOCK, ff), BF),
            pltpu.VMEM((BLOCK, ff), BF),
            pltpu.VMEM((rows, width), F32),
            pltpu.VMEM((rows, width), BF),
            pltpu.VMEM((rows, width), F32),
            pltpu.VMEM((rows, width), BF),
            pltpu.SemaphoreType.DMA((5,)),
            pltpu.SemaphoreType.DMA((2, 4)),
            pltpu.SemaphoreType.DMA((2, 2)),
            pltpu.SemaphoreType.DMA((2, count)),
        ]
        + exchange_scratch(count, width, True),
        compiler_params=talk_params(2),
        cost_estimate=cost_of(24 * rows * width * ff, 2**27),
        name="backward",
    )(
        *lefts, gate_w, upper_w, reduce_w, gate, upper, cotangent, branch, stats, gain, *adapters
    )


def input_kernel(
    raw_hbm,
    dq_hbm,
    dk_hbm,
    dv_hbm,
    act_hbm,
    mixed_hbm,
    branch_hbm,
    hidden_hbm,
    result_hbm,
    matrix_hbm,
    d_hidden_hbm,
    tokens_hbm,
    scale_ref,
    q_sum_ref,
    k_sum_ref,
    gain_ref,
    cos_ref,
    sin_ref,
    inner_ref,
    up_ref,
    part_ref,
    d_inner_ref,
    expand_grad_ref,
    out_hbm,
    rows_out_hbm,
    cols_out_hbm,
    raw_buf,
    dq_buf,
    dk_buf,
    dv_buf,
    act_buf,
    mixed_buf,
    branch_buf,
    hidden_buf,
    result_buf,
    matrix_ref,
    d_hidden_ref,
    tokens_ref,
    out_ref,
    left_ref,
    inner_out,
    inner_in,
    inner_mid,
    inner_far,
    sum_own,
    sum_in,
    columns,
    up_all,
    part_in,
    part_mid,
    part_far,
    in_sem,
    core_sem,
    far_sem,
    sum_sem,
    part_sem,
    load_sem,
    r_sem,
    row_grad_ref,
    attn_grad_ref,
    reduce_grad_ref,
    row_pack,
    col_pack,
    *bufs,
):
    group_sems, bufs = bufs[:5], bufs[5:]
    width = out_ref.shape[1]
    local = dq_buf.shape[2]
    count = out_ref.shape[0] // BLOCK
    ins = [
        move_rows(outer, buffer, in_sem, index, True)
        for index, (outer, buffer) in enumerate(
            (
                (raw_hbm, raw_buf),
                (dq_hbm, dq_buf),
                (dk_hbm, dk_buf),
                (dv_hbm, dv_buf),
                (act_hbm, act_buf),
                (mixed_hbm, mixed_buf),
                (branch_hbm, branch_buf),
                (hidden_hbm, hidden_buf),
                (result_hbm, result_buf),
            )
        )
    ]
    for one in ins:
        one(0).start()
    loads = [
        pltpu.make_async_copy(source, target, load_sem.at[index])
        for index, (source, target) in enumerate(
            ((matrix_hbm, matrix_ref), (d_hidden_hbm, d_hidden_ref), (tokens_hbm, tokens_ref))
        )
    ]
    for load in loads:
        load.start()
    out_rows = rows_out(out_ref, out_hbm, r_sem, 0)
    for grad in (row_grad_ref, attn_grad_ref, reduce_grad_ref):
        grad[...] = jnp.zeros_like(grad)
    up_all[...] = jnp.zeros_like(up_all)
    sum_own[...] = jnp.zeros_like(sum_own)
    for row, part in enumerate((q_sum_ref, k_sum_ref)):
        total = part[0]
        for h in range(1, part.shape[0]):
            total = total + part[h]
        sum_own[row : row + 1, :] = total
    greet_all(row_and_col_peers() + [other_of_pair()])
    exchanges = [send(sum_own, sum_in.at[step - 1], sum_sem, step - 1, step) for step in (1, 2, 3)]
    for copy in exchanges:
        copy.start()
    part_core = send(part_ref, part_in, part_sem, 0, 1)
    part_side = send(part_mid, part_far, part_sem, 1, 2)
    part_core.start()
    part_core.wait()
    part_mid[...] = (part_ref[...].astype(F32) + part_in[...].astype(F32)).astype(BF)
    part_side.start()
    for copy in exchanges:
        copy.wait()
    total = sum_own[...] + sum_in[0] + sum_in[1] + sum_in[2]
    scales = scale_ref[...]
    backs = scales * scales * total / D
    for part in range(2):
        columns[part] = jnp.broadcast_to(column_of(scales, part), columns.shape[1:])
        columns[2 + part] = jnp.broadcast_to(column_of(backs, part), columns.shape[1:])

    def inner_core(c):
        return send(inner_out.at[lax.rem(c, 2)], inner_in.at[c], core_sem, c, 1)

    def inner_side(c):
        return send(inner_mid.at[lax.rem(c, 2)], inner_far.at[c], far_sem, c, 2)

    def after_core(c):
        @pl.when(c >= 2)
        def _():
            inner_side(c - 2).wait_send()

        inner_core(c).wait_recv()
        slot = lax.rem(c, 2)
        total = inner_out[slot].astype(F32) + inner_in[c].astype(F32)
        inner_mid[slot] = total.astype(BF)
        inner_side(c).start()

    def after_side(c):
        inner_side(c).wait_recv()
        total = inner_mid[lax.rem(c, 2)].astype(F32) + inner_far[c].astype(F32)
        row_grad_ref[:48, :] += dot_of(total.astype(BF), tokens_ref[span_of(c, BLOCK), :], 1, 0)

    def compute(c, put):
        slot = lax.rem(c, 2)
        for one in ins:
            one(c).wait()

        @pl.when(c + 1 < count)
        def _():
            for one in ins:
                one(c + 1).start()

        @pl.when(c >= 2)
        def _():
            inner_core(c - 2).wait_send()

        rows = span_of(c, BLOCK)
        cosine = cos_ref[rows, :]
        sine = sin_ref[rows, :]
        for part, grad in ((0, dq_buf), (1, dk_buf)):
            scale = columns[part, rows, :]
            back = columns[2 + part, rows, :]
            for at in range(0, local, HEAD):
                turned = grad[slot, :, at : at + HEAD]
                turned = turned * cosine - pltpu.roll(turned, HEAD // 2, 1) * sine
                turned = turned * gain_ref[part : part + 1, at : at + HEAD] * scale
                lane = part * local + at
                left_ref[:, lane : lane + HEAD] = (
                    turned - raw_buf[slot, :, lane : lane + HEAD] * back
                ).astype(BF)
        left_ref[:, 2 * local :] = dv_buf[slot].astype(BF)
        left = left_ref[...]
        inner_out[slot] = (ADAPTER_FACTOR * dot_of(up_ref[...], left, 1, 1)).astype(BF)
        inner_core(c).start()
        up_all[...] += dot_of(inner_ref[:, rows], left, 1, 0)

        @pl.when(c == 0)
        def _():
            for load in loads:
                load.wait()
            part_side.wait()

        for block in (1, 3, 2, 0):
            put(block, dot_of(left, matrix_ref[block * width : (block + 1) * width, :], 1, 1))
        whole = part_mid[:, rows].astype(F32) + part_far[:, rows].astype(F32)
        whole = whole.astype(BF)
        for at, size, first, other, factor in (
            (48, 16, 0, branch_buf, ADAPTER_FACTOR),
            (64, 32, 32, hidden_buf, 1.0),
            (96, 16, 16, result_buf, ADAPTER_FACTOR),
        ):
            term = dot_of(whole[first : first + size], other[slot], 1, 0)
            row_grad_ref[at : at + size, :] += factor * term
        attn_grad_ref[...] += dot_of(d_inner_ref[:16, rows], mixed_buf[slot], 1, 0)
        reduce_grad_ref[...] += dot_of(d_inner_ref[16:, rows], act_buf[slot], 1, 0)

    def finish(c, rows, total):
        out_ref[rows, :] = d_hidden_ref[rows, :] + total
        out_rows(c).start()

    run_blocks(count, bufs, compute, None, finish, extra=(after_core, after_side))
    row_pack[...] = row_grad_ref[...].astype(BF)
    cols = col_pack.shape[0]
    pieces = [
        (up_all, 16 * part, part * local, local, ADAPTER_FACTOR) for part in range(3)
    ]
    ff = reduce_grad_ref.shape[1]
    pieces += [
        (attn_grad_ref, 0, 0, local, 1.0),
        (expand_grad_ref, 0, 0, ff, 1.0),
        (expand_grad_ref, 16, 0, ff, 1.0),
        (reduce_grad_ref, 0, 0, ff, 1.0),
    ]
    lane = 0
    for ref, row, at, size, factor in pieces:
        size = size // cols
        for index in range(cols):
            piece = ref[row : row + 16, at + index * size : at + (index + 1) * size]
            col_pack[index, :, lane : lane + size] = (factor * piece).astype(BF)
        lane += size
    exchange_groups(row_pack, col_pack, rows_out_hbm, cols_out_hbm, group_sems)
    wait_rows(count, out_rows)
    for c in range(max(count - 2, 0), count):
        inner_core(c).wait_send()
        inner_side(c).wait_send()


def input_call(
    raw, d_query, d_key, d_value, act, mixed, branch, hidden, result, matrix, d_hidden, *others
):
    rows, width = d_hidden.shape
    local = d_query.shape[1]
    ff = act.shape[1]
    cols = lax.axis_size("col")
    lanes = (4 * local + 3 * ff) // cols
    count = rows // BLOCK
    grad = pltpu.VMEM((2, BLOCK, local), F32)
    part = pltpu.VMEM((2, BLOCK, width), BF)
    inner = pltpu.VMEM((2, 48, BLOCK), BF)
    arrived = pltpu.VMEM((count, 48, BLOCK), BF)
    total = pltpu.VMEM((64, rows), BF)
    sem = pltpu.SemaphoreType.DMA((2, count))
    return pl.pallas_call(
        input_kernel,
        out_shape=[
            jax.ShapeDtypeStruct((rows, width), F32),
            jax.ShapeDtypeStruct((cols, 2, 112, width), BF),
            jax.ShapeDtypeStruct((4, 2, cols, 16, lanes), BF),
        ],
        in_specs=[ANY_SPEC] * 12 + [VMEM_SPEC] * 11,
        out_specs=[ANY_SPEC] * 3,
        scratch_shapes=[
            pltpu.VMEM((2, BLOCK, 3 * local), F32),
            grad,
            grad,
            grad,
            pltpu.VMEM((2, BLOCK, ff), BF),
            pltpu.VMEM((2, BLOCK, local), BF),
            part,
            part,
            part,
            pltpu.VMEM(matrix.shape, BF),
            pltpu.VMEM((rows, width), F32),
            pltpu.VMEM((rows, width), BF),
            pltpu.VMEM((rows, width), F32),
            pltpu.VMEM((BLOCK, 3 * local), BF),
            inner,
            arrived,
            inner,
            arrived,
            pltpu.VMEM((8, rows), F32),
            pltpu.VMEM((3, 8, rows), F32),
            pltpu.VMEM((4, rows, HEAD), F32),
            pltpu.VMEM((48, 3 * local), F32),
            total,
            total,
            total,
            pltpu.SemaphoreType.DMA((9, 2)),
            sem,
            sem,
            pltpu.SemaphoreType.DMA((2, 3)),
            pltpu.SemaphoreType.DMA((2, 2)),
            pltpu.SemaphoreType.DMA((3,)),
            pltpu.SemaphoreType.DMA((1, count)),
            pltpu.VMEM((112, width), F32),
            pltpu.VMEM((16, local), F32),
            pltpu.VMEM((16, ff), F32),
            pltpu.VMEM((112, width), BF),
            pltpu.VMEM((cols, 16, lanes), BF),
            pltpu.SemaphoreType.DMA((2,)),
            pltpu.SemaphoreType.DMA((2, 2)),
            pltpu.SemaphoreType.DMA((2, cols - 1)),
            pltpu.SemaphoreType.DMA((2, cols - 1)),
            pltpu.SemaphoreType.DMA((2, 2, 3)),
        ]
        + exchange_scratch(count, width, False),
        compiler_params=talk_params(3),
        cost_estimate=cost_of(24 * rows * width * local, 2**26),
        name="input_grad",
    )(raw, d_query, d_key, d_value, act, mixed, branch, hidden, result, matrix, d_hidden, *others)


def deal(items, outs, sems):
    me = lax.axis_index("row")
    copies = []
    for index, (view, out) in enumerate(zip(items, outs)):
        mine = [pltpu.make_async_copy(view(me), out.at[0], sems.at[0, index, 0])]
        for step in (1, 2, 3):
            mine.append(
                pltpu.make_async_remote_copy(
                    src_ref=view(me ^ step),
                    dst_ref=out.at[step],
                    send_sem=sems.at[0, index, step],
                    recv_sem=sems.at[1, index, step],
                    device_id=peer(step),
                    device_id_type=pl.DeviceIdType.MESH,
                )
            )
        copies.append(mine)
    return copies


def start_all(copies):
    for step in (2, 3, 1, 0):
        copies[step].start()


def wait_all(copies):
    for copy in copies:
        copy.wait()


def span_of(at, size):
    return pl.ds(pl.multiple_of(at * size, size), size)


def qkv_view(ref, half):
    _, rows, columns = ref.shape
    return lambda row: ref.at[:, span_of(half, rows // 2), span_of(row, columns // 4)]


def attn_view(ref, half):
    cut = ref.shape[0] // 8
    return lambda row: ref.at[span_of(2 * row + half, cut)]


def expand_view(ref, part, half):
    cut = ref.shape[2] // 8
    return lambda row: ref.at[part, :, span_of(2 * row + half, cut)]


def reduce_view(ref):
    cut = ref.shape[0] // 4
    return lambda row: ref.at[span_of(row, cut)]


def like_views(shapes):
    return [jax.ShapeDtypeStruct((4, *shape), BF) for shape in shapes]


def first_deal_kernel(qkv_ref, attn_ref, qkv_out, attn_out, sems):
    half = lax.axis_index("dp")
    greet()
    copies = deal([qkv_view(qkv_ref, half), attn_view(attn_ref, half)], [qkv_out, attn_out], sems)
    for one in copies:
        start_all(one)
    for one in copies:
        wait_all(one)


def first_deal(qkv_weight, attn_weight):
    parts, rows, columns = qkv_weight.shape
    return pl.pallas_call(
        first_deal_kernel,
        out_shape=like_views(
            [(parts, rows // 2, columns // 4), (attn_weight.shape[0] // 8, attn_weight.shape[1])]
        ),
        in_specs=[ANY_SPEC] * 2,
        out_specs=[ANY_SPEC] * 2,
        scratch_shapes=[pltpu.SemaphoreType.DMA((2, 2, 4))],
        compiler_params=talk_params(4),
        cost_estimate=cost_of(0, 2**26),
        name="first_deal",
    )(qkv_weight, attn_weight)


def second_deal_kernel(qkv_ref, attn_ref, expand_ref, tokens_ref, pack_ref, *rest):
    *outs, t1, t2, t3, p1, p2, p3, sems, token_sem, pack_sem = rest
    half = lax.axis_index("dp")
    greet()
    gate, rest_qkv, rest_attn, upper = deal(
        [
            expand_view(expand_ref, 0, half),
            qkv_view(qkv_ref, 1 - half),
            attn_view(attn_ref, 1 - half),
            expand_view(expand_ref, 1, half),
        ],
        outs,
        sems,
    )
    gathers = []
    for source, targets, one_sem in ((pack_ref, (p1, p2, p3), pack_sem), (tokens_ref, (t1, t2, t3), token_sem)):
        gathers.append(
            (
                send(source, targets[1], one_sem, 1, 2),
                send(source, targets[0], one_sem, 0, 1),
                send(targets[1], targets[2], one_sem, 2, 1),
            )
        )
    start_all(gate)
    start_all(rest_qkv)
    start_all(rest_attn)
    for side, core, _ in gathers:
        side.start()
        core.start()
    start_all(upper)
    for side, core, relay in gathers:
        side.wait_recv()
        relay.start()
    for one in (gate, rest_qkv, rest_attn, upper):
        wait_all(one)
    for side, core, relay in gathers:
        side.wait_send()
        core.wait()
        relay.wait()


def second_deal(qkv_weight, attn_weight, expand_weight, tokens, pack):
    parts, rows, columns = qkv_weight.shape
    cut = expand_weight.shape[2] // 8
    wide = (expand_weight.shape[1], cut)
    sem = pltpu.SemaphoreType.DMA((2, 3))
    return pl.pallas_call(
        second_deal_kernel,
        out_shape=like_views(
            [
                wide,
                (parts, rows // 2, columns // 4),
                (attn_weight.shape[0] // 8, attn_weight.shape[1]),
                wide,
            ]
        )
        + [jax.ShapeDtypeStruct(tokens.shape, BF)] * 3
        + [jax.ShapeDtypeStruct(pack.shape, BF)] * 3,
        in_specs=[ANY_SPEC] * 5,
        out_specs=[ANY_SPEC] * 10,
        scratch_shapes=[pltpu.SemaphoreType.DMA((2, 4, 4)), sem, sem],
        compiler_params=talk_params(5),
        cost_estimate=cost_of(0, 2**27),
        name="second_deal",
    )(qkv_weight, attn_weight, expand_weight, tokens, pack)


def greet_all(peers):
    barrier = pltpu.get_barrier_semaphore()
    for device in peers:
        pl.semaphore_signal(barrier, inc=1, device_id=device, device_id_type=pl.DeviceIdType.MESH)
    pl.semaphore_wait(barrier, len(peers))


def copy_to(source, target, sems, index, device):
    return pltpu.make_async_remote_copy(
        src_ref=source,
        dst_ref=target,
        send_sem=sems.at[0, index],
        recv_sem=sems.at[1, index],
        device_id=device,
        device_id_type=pl.DeviceIdType.MESH,
    )


def other_of_pair():
    return {"dp": 1 - lax.axis_index("dp")}


def exchange_halves(whole, rest, out, sems, local_sem, steps=None):
    cols = whole.shape[0]
    col = lax.axis_index("col")
    copies = []
    for k in range(cols) if steps is None else steps:
        if k == 0:
            copies.append(pltpu.make_async_copy(rest, out.at[0], local_sem))
            continue
        place = lax.rem(col + k, cols)
        copies.append(copy_to(whole.at[place], out.at[k], sems, k - 1, other_of_pair()))
    return copies


def send_round(view, out, sems, local_sem):
    cols = out.shape[0]
    col = lax.axis_index("col")
    local = pltpu.make_async_copy(view(col), out.at[col], local_sem)
    sends = []
    arrivals = []
    for k in range(1, cols):
        place = lax.rem(col + k, cols)
        came = lax.rem(col - k + cols, cols)
        sends.append(copy_to(view(place), out.at[col], sems, k - 1, {"col": place}))
        arrivals.append(copy_to(view(place), out.at[came], sems, k - 1, {"col": place}))

    def wait():
        local.wait()
        for one in arrivals:
            one.wait_recv()
        for one in sends:
            one.wait_send()

    return [local, *sends], wait


def row_and_col_peers():
    cols = lax.axis_size("col")
    col = lax.axis_index("col")
    return [peer(step) for step in (1, 2, 3)] + [
        {"col": lax.rem(col + k, cols)} for k in range(1, cols)
    ]


def third_deal_kernel(
    expand_ref, reduce_ref, qkv_all, qkv_rest, attn_all, attn_rest, pack_ref, gain_ref, *rest
):
    *outs, qkv_out, attn_out, pack_out, gain_out = rest[:7]
    deal_sem, qkv_sem, attn_sem, pack_sem, gain_sem, local_sem = rest[7:]
    other = 1 - lax.axis_index("dp")
    me = lax.axis_index("row")
    greet_all(row_and_col_peers() + [other_of_pair()])
    sub = gain_out.shape[2]
    swaps = exchange_halves(qkv_all, qkv_rest, qkv_out, qkv_sem, local_sem.at[0])
    swaps += exchange_halves(attn_all, attn_rest, attn_out, attn_sem, local_sem.at[1])
    packs, wait_packs = send_round(lambda place: pack_ref.at[place], pack_out, pack_sem, local_sem.at[2])
    gains, wait_gains = send_round(
        lambda place: gain_ref.at[:, span_of(me, sub)], gain_out, gain_sem, local_sem.at[3]
    )
    for copy in packs + gains + swaps:
        copy.start()
    copies = deal(
        [
            reduce_view(reduce_ref),
            expand_view(expand_ref, 0, other),
            expand_view(expand_ref, 1, other),
        ],
        outs,
        deal_sem,
    )
    for one in copies:
        start_all(one)
    wait_packs()
    wait_gains()
    for one in copies:
        wait_all(one)
    wait_all(swaps)


def third_deal(expand_weight, reduce_weight, qkv_all, qkv_rest, attn_all, attn_rest, pack, gain):
    wide = (expand_weight.shape[1], expand_weight.shape[2] // 8)
    cols = qkv_all.shape[0]
    round_sem = pltpu.SemaphoreType.DMA((2, cols - 1))
    return pl.pallas_call(
        third_deal_kernel,
        out_shape=like_views([(reduce_weight.shape[0] // 4, reduce_weight.shape[1]), wide, wide])
        + [
            jax.ShapeDtypeStruct(qkv_all.shape, BF),
            jax.ShapeDtypeStruct(attn_all.shape, BF),
            jax.ShapeDtypeStruct(pack.shape, BF),
            jax.ShapeDtypeStruct((cols, gain.shape[0], gain.shape[1] // 4), F32),
        ],
        in_specs=[ANY_SPEC] * 8,
        out_specs=[ANY_SPEC] * 7,
        scratch_shapes=[
            pltpu.SemaphoreType.DMA((2, 3, 4)),
            round_sem,
            round_sem,
            round_sem,
            round_sem,
            pltpu.SemaphoreType.DMA((4,)),
        ],
        compiler_params=talk_params(6),
        cost_estimate=cost_of(0, 2**27),
        name="third_deal",
    )(expand_weight, reduce_weight, qkv_all, qkv_rest, attn_all, attn_rest, pack, gain)


def front_kernel(
    x0,
    x1,
    x2,
    x3,
    matrix_ref,
    low_ref,
    gate_all,
    gate_rest,
    raw_ref,
    square_ref,
    inner_ref,
    gate_out,
    swap_sem,
    local_sem,
):
    local = raw_ref.shape[1] // 3
    first = exchange_halves(gate_all, gate_rest, gate_out, swap_sem, local_sem.at[0], range(2))

    @pl.when(pl.program_id(0) == 0)
    def _():
        greet_all([other_of_pair()])
        for copy in first:
            copy.start()

    left = jnp.concatenate([x0[...], x1[...], x2[...], x3[...]], axis=1)
    squares = []
    for part in range(3):
        lanes = slice(part * local, (part + 1) * local)
        product = dot_of(left, matrix_ref[:, lanes], 1, 0)
        raw_ref[:, lanes] = product
        squares.append(product * product)
    square_ref[...] = sums_of(*squares[:2])
    inner_ref[...] = dot_of(low_ref[...], left, 1, 1).astype(BF)

    @pl.when(pl.program_id(0) == pl.num_programs(0) - 1)
    def _():
        wait_all(first)


def front_call(lefts, matrix, low, gate_all, gate_rest):
    rows, width = lefts[0].shape
    wide = matrix.shape[1]
    tile = row_tile(rows)
    cols = gate_all.shape[0]

    def whole(array):
        return pl.BlockSpec(array.shape, lambda m: (0, 0))

    return pl.pallas_call(
        front_kernel,
        out_shape=[
            jax.ShapeDtypeStruct((rows, wide), F32),
            jax.ShapeDtypeStruct((8, rows), F32),
            jax.ShapeDtypeStruct((48, rows), BF),
            jax.ShapeDtypeStruct(gate_all.shape, BF),
        ],
        grid=(rows // tile,),
        in_specs=[pl.BlockSpec((tile, width), lambda m: (m, 0))] * 4
        + [whole(matrix), whole(low), ANY_SPEC, ANY_SPEC],
        out_specs=[
            pl.BlockSpec((tile, wide), lambda m: (m, 0)),
            pl.BlockSpec((8, tile), lambda m: (0, m)),
            pl.BlockSpec((48, tile), lambda m: (0, m)),
            ANY_SPEC,
        ],
        scratch_shapes=[
            pltpu.SemaphoreType.DMA((2, cols - 1)),
            pltpu.SemaphoreType.DMA((1,)),
        ],
        compiler_params=talk_params(8),
        cost_estimate=cost_of(8 * rows * width * wide, 2**26),
        name="front",
    )(*lefts, matrix, low, gate_all, gate_rest)


def exchange_groups(row_ref, col_ref, rows_out, cols_out, sems):
    local_sem, pair_sem, round_sem, deal_sem, row_sem = sems
    cols = col_ref.shape[0]
    col = lax.axis_index("col")
    places = [lax.rem(col + k, cols) for k in range(cols)]
    to = copy_to
    swap_rows = to(row_ref, rows_out.at[0, 1], pair_sem, 0, other_of_pair())
    swap_rows.start()
    dealt = [
        to(col_ref.at[places[k]], cols_out.at[0, 0, col], deal_sem, k - 1, {"col": places[k]})
        for k in range(1, cols)
    ]
    for copy in dealt:
        copy.start()
    keep_rows = pltpu.make_async_copy(row_ref, rows_out.at[0, 0], local_sem.at[0])
    keep_cols = pltpu.make_async_copy(col_ref.at[col], cols_out.at[0, 0, col], local_sem.at[1])
    keep_rows.start()
    keep_cols.start()
    for k in range(1, cols):
        came = lax.rem(col - k + cols, cols)
        to(col_ref.at[came], cols_out.at[0, 0, came], deal_sem, k - 1, {"col": places[k]}).wait_recv()
    keep_cols.wait()
    swap_cols = to(cols_out.at[0, 0], cols_out.at[0, 1], pair_sem, 1, other_of_pair())
    swap_cols.start()

    def spread(which):
        side = to(cols_out.at[0, which], cols_out.at[2, which], row_sem.at[which], 1, peer(2))
        core = to(cols_out.at[0, which], cols_out.at[1, which], row_sem.at[which], 0, peer(1))
        relay = to(cols_out.at[2, which], cols_out.at[3, which], row_sem.at[which], 2, peer(1))
        side.start()
        core.start()
        return side, core, relay

    spreads = [spread(0)]
    keep_rows.wait()
    swap_rows.wait_recv()
    rounds = [
        to(rows_out.at[0], rows_out.at[k], round_sem, k - 1, {"col": places[k]})
        for k in range(1, cols)
    ]
    for copy in rounds:
        copy.start()
    swap_cols.wait_recv()
    spreads.append(spread(1))
    for side, core, relay in spreads:
        side.wait_recv()
        relay.start()
    for side, core, relay in spreads:
        core.wait()
        relay.wait()
        side.wait_send()
    for copy in rounds:
        copy.wait()
    for copy in dealt:
        copy.wait_send()
    swap_rows.wait_send()
    swap_cols.wait_send()


def across(values, step):
    return lax.ppermute(values, "row", [(i, i ^ step) for i in range(4)])


def sum_row(values):
    values = values + across(values, 1)
    return values + across(values, 2)


def gather_col(values):
    return lax.all_gather(values, "col", axis=0, tiled=False)


def swap_pair(values):
    return lax.ppermute(values, "dp", [(0, 1), (1, 0)])


def round_col(values, cols):
    shift = lambda k: [(i, (i + k) % cols) for i in range(cols)]
    return [values] + [lax.ppermute(values, "col", shift(k)) for k in range(1, cols)]


def after(values, earlier):
    return lax.optimization_barrier((values, earlier))[0]


def group_shards(
    tokens,
    cotangent,
    qkv_weight,
    attn_weight,
    expand_weight,
    reduce_weight,
    headnorm_gain,
    post_gain,
    qkv_lowrank,
    qkv_uprank,
    attn_lowrank,
    attn_uprank,
    expand_lowrank,
    expand_uprank,
    reduce_lowrank,
    reduce_uprank,
    prefix_length,
    adapter_set,
):
    cols = lax.axis_size("col")
    pair = lax.axis_index("dp")
    me = lax.axis_index("row")
    col = lax.axis_index("col")
    rows, width = tokens.shape
    sub = qkv_weight.shape[2] // 4
    ff = expand_weight.shape[2]
    ff_sub = ff // 4
    ff_half = ff_sub // 2
    local = cols * sub
    ff_local = cols * ff_sub
    sequence = pair * cols + col
    mine = lax.dynamic_index_in_dim(adapter_set, sequence, 0, keepdims=False)
    prefix = lax.dynamic_slice_in_dim(prefix_length, sequence, 1)
    cols_sets = lax.dynamic_slice_in_dim(adapter_set, pair * cols, cols)

    row_pack = row_pack_of(
        mine.reshape(1),
        qkv_lowrank.transpose(0, 1, 3, 2),
        attn_uprank,
        expand_lowrank.transpose(0, 1, 3, 2),
        reduce_uprank,
    )
    col_pack = col_pack_of(
        jnp.concatenate([cols_sets, me.reshape(1)]),
        qkv_uprank,
        attn_lowrank.transpose(0, 2, 1),
        expand_uprank,
        reduce_lowrank.transpose(0, 2, 1),
    )

    place = jnp.stack([pair, col])

    qkv_own, attn_own = first_deal(qkv_weight, attn_weight)
    col_pack = after(col_pack, qkv_own)
    gate_own, qkv_rest, attn_rest, up_own, *others = second_deal(
        qkv_weight, attn_weight, expand_weight, tokens, after(row_pack, qkv_own)
    )
    token_parts = [tokens, *others[:3]]
    row_all = jnp.concatenate([row_pack, *others[3:]], axis=1)
    qkv_low = row_all[:48]
    attn_up = row_all[48:64]
    expand_low = row_all[64:96]
    reduce_up = row_all[96:112]
    qkv_all = gather_col(qkv_own)
    attn_all = gather_col(attn_own)
    gate_all = gather_col(gate_own)
    up_all = gather_col(up_own)
    reduce_own, gate_rest, up_rest, qkv_other, attn_other, col_all, gains = third_deal(
        expand_weight,
        after(reduce_weight, others[0]),
        qkv_all,
        qkv_rest,
        attn_all,
        attn_rest,
        col_pack,
        headnorm_gain,
    )
    reduce_all = gather_col(reduce_own)
    gains = gains.transpose(1, 0, 2).reshape(2, local)

    def own_columns(at, size):
        return col_all[:, :, at : at + size].transpose(1, 0, 2).reshape(16, cols * size)

    qkv_up = [own_columns(i * sub, sub) for i in range(3)]
    attn_low = own_columns(3 * sub, sub)
    expand_up = [own_columns(4 * sub + i * ff_sub, ff_sub) for i in range(2)]
    reduce_low = own_columns(4 * sub + 2 * ff_sub, ff_sub)

    diagonal_up = jnp.concatenate(
        [
            jnp.pad(up, ((0, 0), (i * local, (2 - i) * local))) for i, up in enumerate(qkv_up)
        ]
    )
    qkv_up = jnp.concatenate(qkv_up)
    qkv_w = merge_qkv(place, qkv_all, qkv_other, qkv_low, qkv_up)
    attn_w = merge_out(place, [attn_all, attn_other], attn_low, attn_up)

    half = HEAD // 2
    freq = THETA ** (-2.0 * jnp.arange(half, dtype=F32) / HEAD)
    angle = jnp.arange(rows, dtype=jnp.int32).astype(F32)[:, None] * freq[None, :]
    cosine = jnp.concatenate([jnp.cos(angle)] * 2, axis=1)
    sine = jnp.sin(angle)
    sine = jnp.concatenate([-sine, sine], axis=1)

    raw, squares, qkv_inner, gate_part = front_call(
        token_parts, qkv_w, qkv_low, gate_all, gate_rest
    )
    scale = lax.rsqrt(sum_row(squares) / D + EPS)
    query, key, value = rotate_rows(raw, scale, gains, cosine, sine)
    limit = jnp.maximum(jnp.arange(rows, dtype=jnp.int32), prefix - 1)[None]
    mixed, log_total, branch, hidden, branch_stats, *hidden_parts, gate_other, up_other = branch_call(
        query,
        key,
        value,
        limit,
        attn_w,
        tokens,
        post_gain,
        (gate_all, gate_part, up_all, up_rest),
    )
    expand_w = [
        merge_expand(
            place, whole, other, expand_low[16 * i : 16 * i + 16], expand_up[i]
        )
        for i, (whole, other) in enumerate(((gate_all, gate_other), (up_all, up_other)))
    ]
    reduce_w = merge_out(place, [reduce_all], reduce_low, reduce_up)
    act, gate, upper, layer_out, expand_inner, reduce_inner, *result_parts = forward_call(
        hidden_parts, *expand_w, reduce_w, hidden, cotangent, post_gain, expand_low, reduce_low
    )
    d_hidden, d_reduce_inner, d_expand_inner, g_expand_up, *branch_parts = backward_call(
        result_parts,
        *expand_w,
        reduce_w,
        gate,
        upper,
        cotangent,
        branch,
        branch_stats,
        post_gain,
        reduce_up,
        jnp.concatenate(expand_up),
        expand_inner,
    )
    d_mixed, d_attn_inner = mixed_back(branch_parts, attn_w, attn_up)
    d_query, d_key, d_value, q_sums, k_sums = attend_back(
        prefix, query, d_mixed, mixed, log_total, key, value
    )
    partials = jnp.concatenate(
        [dot_of(attn_low, mixed, 1, 1), reduce_inner, d_expand_inner]
    ).astype(BF)
    input_grad, every_row, every_col = input_call(
        raw,
        d_query,
        d_key,
        d_value,
        act,
        mixed,
        branch_parts[0],
        hidden_parts[0],
        result_parts[0],
        qkv_w,
        d_hidden,
        tokens,
        scale,
        q_sums,
        k_sums,
        gains,
        cosine,
        sine,
        qkv_inner,
        diagonal_up,
        partials,
        jnp.concatenate([d_attn_inner, d_reduce_inner]),
        g_expand_up,
    )

    place_of = jnp.arange(2 * cols, dtype=jnp.int32)
    row_place = (pair ^ (place_of % 2)) * cols + (col - place_of // 2 + cols) % cols
    col_place = (pair ^ (place_of // cols)) * cols + place_of % cols
    places = jnp.concatenate([row_place, col_place])
    chosen = places[:, None] == jnp.arange(2 * cols, dtype=jnp.int32)[None, :]
    ids = jnp.sum(jnp.where(chosen, adapter_set[None, :], 0), axis=1)
    ids = jnp.concatenate([ids, me.reshape(1)])
    qkv_low, qkv_up, attn_low, attn_up, expand_low, expand_up, reduce_low, reduce_up = finish_call(
        ids, every_row, every_col, sub, ff_sub
    )
    return (
        layer_out,
        input_grad,
        qkv_low.transpose(0, 1, 3, 2),
        qkv_up,
        attn_low.transpose(0, 2, 1),
        attn_up,
        expand_low.transpose(0, 1, 3, 2),
        expand_up,
        reduce_low.transpose(0, 2, 1),
        reduce_up,
    )


def shards(*arrays):
    whole = (
        lax.axis_size("dp") == 2
        and lax.axis_size("row") == 4
        and arrays[0].shape[0] == SEQUENCE_LENGTH
    )
    return group_shards(*arrays) if whole else general_shards(*arrays)


def solution(mesh):
    placed = (
        P(("dp", "col"), "row"),
        P(("dp", "col"), "row"),
        P(None, "row", "col"),
        P("col", "row"),
        P(None, "row", "col"),
        P("col", "row"),
        P(None, "col"),
        P(None, "row"),
        P(None, None, "row", None),
        P(None, None, None, "col"),
        P(None, "col", None),
        P(None, None, "row"),
        P(None, None, "row", None),
        P(None, None, None, "col"),
        P(None, "col", None),
        P(None, None, "row"),
        P(),
        P(),
    )
    return jax.shard_map(
        shards,
        mesh=mesh,
        in_specs=placed,
        out_specs=(
            P(("dp", "col"), "row"),
            P(("dp", "col"), "row"),
            P(None, None, "row", None),
            P(None, None, None, "col"),
            P(None, "col", None),
            P(None, None, "row"),
            P(None, None, "row", None),
            P(None, None, None, "col"),
            P(None, "col", None),
            P(None, None, "row"),
        ),
        check_vma=False,
    )
```

```python
import functools

import jax
import jax.numpy as jnp
from jax import lax
from jax.experimental import pallas as pl
from jax.experimental.pallas import tpu as pltpu
from jax.sharding import PartitionSpec as P

D = 2048
HEAD = 128
ADAPTER_RANK = 16
SETS = 8
SEQUENCE_LENGTH = 2048


EPS = 1e-06
THETA = 500000.0
ADAPTER_FACTOR = 0.5
NEG = -1e30


def via_col_row(input_rows, weight_matrix, adapt_mat, compute, seq_pick):
    gathered = lax.all_gather(input_rows, "col", axis=0, tiled=True)
    main, inner_value = compute(gathered, weight_matrix, adapt_mat, seq_pick, False)
    return (
        lax.psum_scatter(main, "row", scatter_dimension=0, tiled=True),
        lax.psum_scatter(inner_value, "row", scatter_dimension=0, tiled=True),
    )


def via_row_col(input_rows, weight_matrix, adapt_mat, compute, seq_pick):
    gathered = lax.all_gather(input_rows, "row", axis=0, tiled=True)
    main, inner_value = compute(gathered, weight_matrix, adapt_mat, seq_pick, False)
    return (
        lax.psum_scatter(main, "col", scatter_dimension=0, tiled=True),
        lax.psum_scatter(inner_value, "col", scatter_dimension=0, tiled=True),
    )


def row_total(values):
    return lax.psum(jnp.sum(values, axis=-1), "row")


def head_totals(first, second):
    return lax.psum((jnp.sum(first, axis=-1), jnp.sum(second, axis=-1)), "col")


def sum_col_tokens(values):
    return lax.psum(values.astype(jnp.bfloat16), ("dp", "col")).astype(jnp.float32)


def sum_row_tokens(values):
    return lax.psum(values.astype(jnp.bfloat16), ("dp", "row")).astype(jnp.float32)


def set_rows(group_sets, first_row, item_count):
    sequence = (first_row + jnp.arange(item_count, dtype=jnp.int32)) // SEQUENCE_LENGTH
    member = sequence[:, None] == jnp.arange(group_sets.shape[0], dtype=jnp.int32)[None, :]
    chosen = jnp.sum(jnp.where(member, group_sets[None, :], 0), axis=1)
    return (chosen[:, None] == jnp.arange(SETS, dtype=jnp.int32)[None, :]).astype(jnp.bfloat16)


def widen(inner_value, onehot, part_list):
    rows = inner_value.shape[0]
    spread = onehot[:, None, :, None] * inner_value.reshape(rows, part_list, 1, ADAPTER_RANK)
    return spread.reshape(rows, part_list, SETS * ADAPTER_RANK)


def adapter_in(gathered, pick, lowrank):
    part_list = lowrank.shape[0]
    width_in = lowrank.shape[2]
    item_count = pick.shape[0]
    chosen = jnp.einsum("sk,pkdr->sdpr", pick, lowrank, preferred_element_type=jnp.float32).astype(
        jnp.bfloat16
    )
    chosen = chosen.reshape(item_count, width_in, part_list * ADAPTER_RANK)
    product_value = jnp.einsum(
        "ehm,emx->ehx",
        gathered.reshape(item_count, SEQUENCE_LENGTH, width_in),
        chosen,
        preferred_element_type=jnp.float32,
    )
    return product_value.reshape(item_count * SEQUENCE_LENGTH, part_list * ADAPTER_RANK)


def adapter_back(gathered, pick, upward_rank):
    part_list = upward_rank.shape[0]
    width_out = upward_rank.shape[-1]
    item_count = pick.shape[0]
    chosen = jnp.einsum(
        "sk,pkre->sper", pick, upward_rank, preferred_element_type=jnp.float32
    ).astype(jnp.bfloat16)
    product_value = jnp.einsum(
        "slpe,sper->slpr",
        gathered.reshape(item_count, SEQUENCE_LENGTH, part_list, width_out),
        chosen,
        preferred_element_type=jnp.float32,
    )
    return ADAPTER_FACTOR * product_value.reshape(
        item_count * SEQUENCE_LENGTH, part_list * ADAPTER_RANK
    )


def adapter_out(wide_output, upward_rank):
    part_list = upward_rank.shape[0]
    flat_up = upward_rank.reshape(part_list, SETS * ADAPTER_RANK, upward_rank.shape[-1])
    return ADAPTER_FACTOR * jnp.einsum(
        "tpk,pke->tpe", wide_output, flat_up, preferred_element_type=jnp.float32
    )


def adapter_grad_in(wide_output, lowrank):
    part_list = lowrank.shape[0]
    width_in = lowrank.shape[2]
    flat_low = lowrank.transpose(0, 1, 3, 2).reshape(part_list, SETS * ADAPTER_RANK, width_in)
    return jnp.einsum("tpk,pkd->td", wide_output, flat_low, preferred_element_type=jnp.float32)


def up_grad(wide_output, gradient_list):
    part_list = gradient_list.shape[1]
    total_sum = ADAPTER_FACTOR * jnp.einsum(
        "jox,joq->oxq", wide_output, gradient_list, preferred_element_type=jnp.float32
    )
    return total_sum.reshape(part_list, SETS, ADAPTER_RANK, gradient_list.shape[2])


def low_grad(input_rows, wide_output):
    part_list = wide_output.shape[1]
    total_sum = jnp.einsum(
        "td,tpk->pkd", input_rows, wide_output, preferred_element_type=jnp.float32
    )
    return total_sum.reshape(part_list, SETS, ADAPTER_RANK, input_rows.shape[1]).transpose(
        0, 1, 3, 2
    )


def swiglu(gate, upper):
    return jax.nn.silu(gate) * upper


def norm_back(grad, values, scale, gain):
    weighted = gain * grad
    inner_sum = row_total(weighted * values)
    return scale[:, None] * weighted - values * (scale**3 * inner_sum / D)[:, None]


def qkv_forward(gathered, weight_matrix, low_flat, pick, per_row):
    input_rows = gathered[:, 0]
    main = jnp.einsum("td,pde->tpe", input_rows, weight_matrix, preferred_element_type=jnp.float32)
    lowrank = low_flat.reshape(3, SETS, low_flat.shape[1], ADAPTER_RANK)
    return (main, adapter_in(input_rows, pick, lowrank))


def expand_forward(gathered, weight_matrix, low_flat, pick, per_row):
    input_rows = gathered[:, 0]
    main = jnp.einsum("td,pdf->tpf", input_rows, weight_matrix, preferred_element_type=jnp.float32)
    lowrank = low_flat.reshape(2, SETS, low_flat.shape[1], ADAPTER_RANK)
    return (main, adapter_in(input_rows, pick, lowrank))


def single_forward(gathered, weight_matrix, low_four, pick, per_row):
    input_rows = gathered[:, 0]
    main = jnp.dot(input_rows, weight_matrix[0, 0], preferred_element_type=jnp.float32)
    return (main, adapter_in(input_rows, pick, low_four))


def single_backward(gathered, weight_matrix, up_flat, pick, per_row):
    main = jnp.einsum(
        "te,fe->tf", gathered[:, 0], weight_matrix, preferred_element_type=jnp.float32
    )
    upward_rank = up_flat.reshape(1, SETS, ADAPTER_RANK, up_flat.shape[1])
    return (main, adapter_back(gathered, pick, upward_rank))


def multi_backward(gathered, weight_matrix, up_flat, pick, per_row):
    part_list = weight_matrix.shape[0]
    main = jnp.einsum("tpf,pdf->td", gathered, weight_matrix, preferred_element_type=jnp.float32)
    upward_rank = up_flat.reshape(part_list, SETS, ADAPTER_RANK, up_flat.shape[2])
    return (main, adapter_back(gathered, pick, upward_rank))


def general_shards(
    tokens,
    cotangent,
    qkv_weight,
    attn_weight,
    expand_weight,
    reduce_weight,
    headnorm_gain,
    post_gain,
    qkv_lowrank,
    qkv_uprank,
    attn_lowrank,
    attn_uprank,
    expand_lowrank,
    expand_uprank,
    reduce_lowrank,
    reduce_uprank,
    prefix_length,
    adapter_set,
):
    rows_a = tokens.shape[0]
    group_rows = rows_a * lax.axis_size("col")
    rows_b = group_rows // lax.axis_size("row")
    group_seqs = group_rows // SEQUENCE_LENGTH
    group_first = lax.axis_index("dp") * group_seqs
    group_sets = lax.dynamic_slice_in_dim(adapter_set, group_first, group_seqs)
    group_prefix = lax.dynamic_slice_in_dim(prefix_length, group_first, group_seqs)
    seq_pick = (group_sets[:, None] == jnp.arange(SETS, dtype=jnp.int32)[None, :]).astype(
        jnp.bfloat16
    )
    pick_a = set_rows(group_sets, lax.axis_index("col") * rows_a, rows_a)
    pick_b = set_rows(group_sets, lax.axis_index("row") * rows_b, rows_b)
    width_row = qkv_weight.shape[1]
    width_col = qkv_weight.shape[2]
    ff_col = expand_weight.shape[2]
    qkv_low_flat = qkv_lowrank.reshape(3 * SETS, width_row, ADAPTER_RANK)
    projected, inner_value = via_col_row(
        tokens[:, None], qkv_weight, qkv_low_flat, qkv_forward, seq_pick
    )
    qkv_wide = widen(inner_value.astype(jnp.bfloat16), pick_b, 3)
    projected = projected + adapter_out(qkv_wide, qkv_uprank)
    queries = projected[:, 0]
    keys = projected[:, 1]
    values = projected[:, 2]
    query_sq, key_sq = head_totals(queries * queries, keys * keys)
    query_scale = lax.rsqrt(query_sq / D + EPS)
    key_scale = lax.rsqrt(key_sq / D + EPS)
    query_norm = queries * query_scale[:, None] * headnorm_gain[0]
    key_norm = keys * key_scale[:, None] * headnorm_gain[1]
    local_heads = queries.shape[1] // HEAD
    half = HEAD // 2
    freq = THETA ** (-2.0 * jnp.arange(half, dtype=jnp.float32) / HEAD)
    position = (jnp.arange(rows_b, dtype=jnp.int32) % SEQUENCE_LENGTH).astype(jnp.float32)
    angle = position[:, None] * freq[None, :]
    cosine = jnp.cos(angle)[:, None, :]
    sine = jnp.sin(angle)[:, None, :]

    def rotate(source):
        heads = source.reshape(rows_b, local_heads, HEAD)
        first = heads[..., :half]
        second = heads[..., half:]
        return jnp.concatenate(
            [first * cosine - second * sine, second * cosine + first * sine], axis=-1
        )

    def unrotate(gradient_list):
        first = gradient_list[..., :half]
        second = gradient_list[..., half:]
        return jnp.concatenate(
            [first * cosine + second * sine, second * cosine - first * sine], axis=-1
        ).reshape(rows_b, local_heads * HEAD)

    query_b = rotate(query_norm).astype(jnp.bfloat16)
    key_b = rotate(key_norm).astype(jnp.bfloat16)
    value_b = values.astype(jnp.bfloat16).reshape(rows_b, local_heads, HEAD)
    block = min(512, SEQUENCE_LENGTH)
    blocks = rows_b // block
    key_pos = jnp.arange(SEQUENCE_LENGTH, dtype=jnp.int32)
    local_first = lax.axis_index("row") * (rows_b // SEQUENCE_LENGTH)
    scale = HEAD ** (-0.5)

    def scores_of(index):
        start = index * block
        seq_start = start // SEQUENCE_LENGTH * SEQUENCE_LENGTH
        which = local_first + start // SEQUENCE_LENGTH
        prefix = jnp.sum(
            jnp.where(jnp.arange(group_seqs, dtype=jnp.int32) == which, group_prefix, 0)
        )
        rows = start - seq_start + jnp.arange(block, dtype=jnp.int32)
        allowed = (key_pos[None, :] <= rows[:, None]) | (key_pos[None, :] < prefix)
        query_blk = lax.dynamic_slice_in_dim(query_b, start, block, 0)
        raw = (
            jnp.einsum("qhd,khd->hqk", query_blk, key_b, preferred_element_type=jnp.float32) * scale
        )
        return (jnp.where(allowed[None], raw, NEG), start, seq_start)

    def attend_block(index):
        scores, start, seq_start = scores_of(index)
        top = jnp.max(scores, axis=-1, keepdims=True)
        powers = jnp.exp(scores - top)
        total_sum = jnp.sum(powers, axis=-1, keepdims=True)
        weights = (powers / total_sum).astype(jnp.bfloat16)
        output = jnp.einsum("hqk,khd->qhd", weights, value_b, preferred_element_type=jnp.float32)
        return (output, (top + jnp.log(total_sum))[..., 0])

    attended, logsum = lax.map(attend_block, jnp.arange(blocks, dtype=jnp.int32))
    mixed_b = attended.reshape(rows_b, local_heads * HEAD).astype(jnp.bfloat16)
    attn_weight_four = attn_weight.reshape(1, 1, width_col, width_row)
    attn_low_four = attn_lowrank.reshape(1, SETS, width_col, ADAPTER_RANK)
    branch, inner_value = via_row_col(
        mixed_b[:, None], attn_weight_four, attn_low_four, single_forward, seq_pick
    )
    attn_wide = widen(inner_value.astype(jnp.bfloat16), pick_a, 1)
    branch = branch + adapter_out(attn_wide, attn_uprank[None])[:, 0]
    branch_scale = lax.rsqrt(row_total(branch * branch) / D + EPS)
    hidden = tokens.astype(jnp.float32) + post_gain[0] * branch * branch_scale[:, None]
    hidden_b = hidden.astype(jnp.bfloat16)
    expand_low_flat = expand_lowrank.reshape(2 * SETS, width_row, ADAPTER_RANK)
    gate_up, inner_value = via_col_row(
        hidden_b[:, None], expand_weight, expand_low_flat, expand_forward, seq_pick
    )
    expand_wide = widen(inner_value.astype(jnp.bfloat16), pick_b, 2)
    gate_up = gate_up + adapter_out(expand_wide, expand_uprank)
    gate = gate_up[:, 0]
    upper = gate_up[:, 1]
    act_b = swiglu(gate, upper).astype(jnp.bfloat16)
    reduce_weight_four = reduce_weight.reshape(1, 1, ff_col, width_row)
    reduce_low_four = reduce_lowrank.reshape(1, SETS, ff_col, ADAPTER_RANK)
    result, inner_value = via_row_col(
        act_b[:, None], reduce_weight_four, reduce_low_four, single_forward, seq_pick
    )
    reduce_wide = widen(inner_value.astype(jnp.bfloat16), pick_a, 1)
    result = result + adapter_out(reduce_wide, reduce_uprank[None])[:, 0]
    result_scale = lax.rsqrt(row_total(result * result) / D + EPS)
    layer_out = (hidden + post_gain[1] * result * result_scale[:, None]).astype(jnp.bfloat16)
    incoming = cotangent.astype(jnp.float32)
    d_result = norm_back(incoming, result, result_scale, post_gain[1]).astype(jnp.bfloat16)
    grad_reduce_up = up_grad(reduce_wide, d_result[:, None])[0]
    grad_reduce_up = sum_col_tokens(grad_reduce_up)
    reduce_up_flat = reduce_uprank.reshape(SETS * ADAPTER_RANK, width_row)
    d_act, inner_value = via_col_row(
        d_result[:, None], reduce_weight, reduce_up_flat, single_backward, seq_pick
    )
    act_wide = widen(inner_value.astype(jnp.bfloat16), pick_b, 1)
    d_act = d_act + adapter_grad_in(act_wide, reduce_lowrank[None])
    grad_reduce_low = low_grad(act_b, act_wide)[0]
    grad_reduce_low = sum_row_tokens(grad_reduce_low)
    unused, pullback = jax.vjp(swiglu, gate, upper)
    d_gate, d_upper = pullback(d_act)
    d_gate_up = jnp.stack([d_gate, d_upper], axis=1).astype(jnp.bfloat16)
    grad_expand_up = up_grad(expand_wide, d_gate_up)
    grad_expand_up = sum_row_tokens(grad_expand_up)
    expand_up_flat = expand_uprank.reshape(2 * SETS, ADAPTER_RANK, ff_col)
    d_hidden_in, inner_value = via_row_col(
        d_gate_up, expand_weight, expand_up_flat, multi_backward, seq_pick
    )
    hidden_wide = widen(inner_value.astype(jnp.bfloat16), pick_a, 2)
    d_hidden = incoming + d_hidden_in + adapter_grad_in(hidden_wide, expand_lowrank)
    grad_expand_low = low_grad(hidden_b, hidden_wide)
    grad_expand_low = sum_col_tokens(grad_expand_low)
    d_branch = norm_back(d_hidden, branch, branch_scale, post_gain[0]).astype(jnp.bfloat16)
    grad_attn_up = up_grad(attn_wide, d_branch[:, None])[0]
    grad_attn_up = sum_col_tokens(grad_attn_up)
    attn_up_flat = attn_uprank.reshape(SETS * ADAPTER_RANK, width_row)
    d_mixed, inner_value = via_col_row(
        d_branch[:, None], attn_weight, attn_up_flat, single_backward, seq_pick
    )
    mixed_wide = widen(inner_value.astype(jnp.bfloat16), pick_b, 1)
    d_mixed = (d_mixed + adapter_grad_in(mixed_wide, attn_lowrank[None])).astype(jnp.bfloat16)
    grad_attn_low = low_grad(mixed_b, mixed_wide)[0]
    grad_attn_low = sum_row_tokens(grad_attn_low)
    d_mixed_heads = d_mixed.reshape(rows_b, local_heads, HEAD)

    def back_block(index, carry):
        d_query, d_key, d_value = carry
        scores, start, seq_start = scores_of(index)
        probs = jnp.exp(
            scores - lax.dynamic_index_in_dim(logsum, index, 0, keepdims=False)[..., None]
        )
        grad_blk = lax.dynamic_slice_in_dim(d_mixed_heads, start, block, 0)
        query_blk = lax.dynamic_slice_in_dim(query_b, start, block, 0)
        d_probs = jnp.einsum("qhd,khd->hqk", grad_blk, value_b, preferred_element_type=jnp.float32)
        delta = jnp.sum(probs * d_probs, axis=-1, keepdims=True)
        d_scores = (probs * (d_probs - delta)).astype(jnp.bfloat16)
        query_part = scale * jnp.einsum(
            "hqk,khd->qhd", d_scores, key_b, preferred_element_type=jnp.float32
        )
        key_part = scale * jnp.einsum(
            "hqk,qhd->khd", d_scores, query_blk, preferred_element_type=jnp.float32
        )
        value_part = jnp.einsum(
            "hqk,qhd->khd", probs.astype(jnp.bfloat16), grad_blk, preferred_element_type=jnp.float32
        )
        d_query = lax.dynamic_update_slice_in_dim(d_query, query_part, start, 0)
        d_key = d_key + key_part
        d_value = d_value + value_part
        return (d_query, d_key, d_value)

    zeros = jnp.zeros((rows_b, local_heads, HEAD), jnp.float32)
    d_query, d_key, d_value = lax.fori_loop(0, blocks, back_block, (zeros, zeros, zeros))
    query_weighted = headnorm_gain[0] * unrotate(d_query)
    key_weighted = headnorm_gain[1] * unrotate(d_key)
    query_sum, key_sum = head_totals(query_weighted * queries, key_weighted * keys)
    d_queries = (
        query_scale[:, None] * query_weighted - queries * (query_scale**3 * query_sum / D)[:, None]
    )
    d_keys = key_scale[:, None] * key_weighted - keys * (key_scale**3 * key_sum / D)[:, None]
    d_qkv = jnp.stack(
        [d_queries, d_keys, d_value.reshape(rows_b, local_heads * HEAD)], axis=1
    ).astype(jnp.bfloat16)
    grad_qkv_up = up_grad(qkv_wide, d_qkv)
    grad_qkv_up = sum_row_tokens(grad_qkv_up)
    qkv_up_flat = qkv_uprank.reshape(3 * SETS, ADAPTER_RANK, width_col)
    d_tokens_in, inner_value = via_row_col(d_qkv, qkv_weight, qkv_up_flat, multi_backward, seq_pick)
    tokens_wide = widen(inner_value.astype(jnp.bfloat16), pick_a, 3)
    input_grad = d_hidden + d_tokens_in + adapter_grad_in(tokens_wide, qkv_lowrank)
    grad_qkv_low = low_grad(tokens, tokens_wide)
    grad_qkv_low = sum_col_tokens(grad_qkv_low)
    return (
        layer_out,
        input_grad,
        grad_qkv_low,
        grad_qkv_up,
        grad_attn_low,
        grad_attn_up,
        grad_expand_low,
        grad_expand_up,
        grad_reduce_low,
        grad_reduce_up,
    )


LOG2E = 1.4426950408889634
Q_BLOCK = 512
K_BLOCK = 512
BF = jnp.bfloat16
F32 = jnp.float32
VMEM_SPEC = pl.BlockSpec(memory_space=pltpu.VMEM)
ANY_SPEC = pl.BlockSpec(memory_space=pl.ANY)


def dot_of(left, right, left_dim, right_dim, out=F32):
    return lax.dot_general(
        left, right, (((left_dim,), (right_dim,)), ((), ())), preferred_element_type=out
    )


def attend_rows(query, limit, key_of, value_of, blocks):
    rows = query.shape[0]
    key_pos = lax.broadcasted_iota(jnp.int32, (K_BLOCK, rows), 0)

    def body(index, carry):
        top, total, mixed = carry
        at = pl.multiple_of(index * K_BLOCK, K_BLOCK)
        scores = dot_of(key_of(at), query, 1, 1) * (HEAD**-0.5 * LOG2E)
        scores = jnp.where(key_pos <= limit - at, scores, NEG)
        top_now = jnp.maximum(top, jnp.max(scores, axis=0, keepdims=True))
        fade = jnp.exp2(top - top_now)
        powers = jnp.exp2(scores - top_now)
        total = fade * total + jnp.sum(powers, axis=0, keepdims=True)
        mixed = mixed * fade + dot_of(value_of(at), powers.astype(BF), 0, 0)
        return top_now, total, mixed

    top, total, mixed = lax.fori_loop(
        0,
        blocks,
        body,
        (
            jnp.full((1, rows), NEG, F32),
            jnp.zeros((1, rows), F32),
            jnp.zeros((HEAD, rows), F32),
        ),
    )
    return mixed / total, top + jnp.log2(total)


def in_parts(values, count):
    parts = []
    for _ in range(count):
        part = values.astype(BF)
        parts.append(part)
        values = values - part.astype(F32)
    return parts


def row_sums(values):
    return sums_of(values)[0:1]


def attend_back_kernel(
    q_ref,
    x0,
    x1,
    x2,
    x3,
    matrix_ref,
    up_ref,
    out_ref,
    probs_hbm,
    k_ref,
    v_ref,
    dq_ref,
    dk_ref,
    dv_ref,
    q_sum_ref,
    k_sum_ref,
    inner_ref,
    grad_ref,
    probs_ref,
    sems,
):
    rows, local = q_ref.shape
    group = pl.program_id(0)
    heads = [slice(at, at + HEAD) for at in range(0, local, HEAD)]
    blocks = jnp.maximum((group + 1) * rows, SEQUENCE_LENGTH // 2) // K_BLOCK

    def fetch(index):
        slot = lax.rem(index, 2)
        return [
            pltpu.make_async_copy(
                probs_hbm.at[h, group, index], probs_ref.at[slot, h], sems.at[slot, h]
            )
            for h in range(len(heads))
        ]

    for copy in fetch(0):
        copy.start()
    left = jnp.concatenate([x0[...], x1[...], x2[...], x3[...]], axis=1)
    grad_ref[...] = dot_of(left, matrix_ref[...], 1, 1).astype(BF)
    inner_ref[...] = (ADAPTER_FACTOR * dot_of(up_ref[...], left, 1, 1)).astype(BF)

    @pl.when(group == 0)
    def _():
        dk_ref[...] = jnp.zeros_like(dk_ref)
        dv_ref[...] = jnp.zeros_like(dv_ref)

    deltas = [
        row_sums(grad_ref[:, lanes].astype(F32) * out_ref[:, lanes].astype(F32)) for lanes in heads
    ]

    def body(index, carry):
        at = pl.multiple_of(index * K_BLOCK, K_BLOCK)
        span = pl.ds(at, K_BLOCK)
        slot = lax.rem(index, 2)
        for copy in fetch(index):
            copy.wait()

        @pl.when(index + 1 < blocks)
        def _():
            for copy in fetch(index + 1):
                copy.start()

        sums = []
        for h, lanes in enumerate(heads):
            query, grad, key = q_ref[:, lanes], grad_ref[:, lanes], k_ref[span, lanes]
            probs = probs_ref[slot, h]
            d_probs = dot_of(v_ref[span, lanes], grad, 1, 1)
            d_scores = (probs.astype(F32) * (d_probs - deltas[h])).astype(BF)
            dv_ref[span, lanes] += dot_of(probs, grad, 1, 0)
            dk_ref[span, lanes] += dot_of(d_scores, query, 1, 0)
            sums.append(carry[h] + dot_of(d_scores, key, 0, 0))
        return tuple(sums)

    d_queries = lax.fori_loop(0, blocks, body, (jnp.zeros((rows, HEAD), F32),) * len(heads))
    for h, lanes in enumerate(heads):
        d_query = d_queries[h] * HEAD**-0.5
        dq_ref[:, lanes] = d_query
        q_sum_ref[h] = row_sums(d_query * q_ref[:, lanes].astype(F32))

    @pl.when(group == pl.num_programs(0) - 1)
    def _():
        for h, lanes in enumerate(heads):
            d_key = dk_ref[:, lanes] * HEAD**-0.5
            dk_ref[:, lanes] = d_key
            k_sum_ref[h] = row_sums(d_key * k_ref[:, lanes].astype(F32))


def attend_back(query, lefts, matrix, up, mixed, probs, key, value):
    rows, length, local = query.shape[0], key.shape[0], query.shape[1]
    heads = local // HEAD
    q_spec = pl.BlockSpec((Q_BLOCK, local), lambda i: (i, 0))
    x_spec = pl.BlockSpec((Q_BLOCK, lefts[0].shape[1]), lambda i: (i, 0))

    def whole(array):
        return pl.BlockSpec(array.shape, lambda i: (0,) * array.ndim)

    return pl.pallas_call(
        attend_back_kernel,
        out_shape=(
            jax.ShapeDtypeStruct(query.shape, F32),
            jax.ShapeDtypeStruct(key.shape, F32),
            jax.ShapeDtypeStruct(key.shape, F32),
            jax.ShapeDtypeStruct((heads, 1, rows), F32),
            jax.ShapeDtypeStruct((heads, 1, length), F32),
            jax.ShapeDtypeStruct((16, rows), BF),
        ),
        grid=(rows // Q_BLOCK,),
        in_specs=[q_spec]
        + [x_spec] * 4
        + [whole(matrix), whole(up), q_spec, ANY_SPEC, whole(key), whole(value)],
        out_specs=[
            q_spec,
            whole(key),
            whole(value),
            pl.BlockSpec((heads, 1, Q_BLOCK), lambda i: (0, 0, i)),
            pl.BlockSpec((heads, 1, length), lambda i: (0, 0, 0)),
            pl.BlockSpec((16, Q_BLOCK), lambda i: (0, i)),
        ],
        scratch_shapes=[
            pltpu.VMEM((Q_BLOCK, local), BF),
            pltpu.VMEM((2, heads, K_BLOCK, Q_BLOCK), BF),
            pltpu.SemaphoreType.DMA((2, heads)),
        ],
        cost_estimate=pl.CostEstimate(
            flops=7 * rows * length * heads * HEAD,
            bytes_accessed=24 * rows * heads * HEAD,
            transcendentals=0,
        ),
        name="attend_back",
    )(query, *lefts, matrix, up, mixed, probs, key, value)


def rotate_kernel(raw_ref, scale_ref, gain_ref, cos_ref, sin_ref, q_ref, k_ref, v_ref):
    width = q_ref.shape[1]
    cosine = cos_ref[...]
    sine = sin_ref[...]
    scales = scale_ref[...]
    for part, out in ((0, q_ref), (1, k_ref)):
        scale = column_of(scales, part)
        for at in range(0, width, HEAD):
            normed = raw_ref[:, part * width + at : part * width + at + HEAD] * scale
            normed = normed * gain_ref[part : part + 1, at : at + HEAD]
            turned = normed * cosine + pltpu.roll(normed, HEAD // 2, 1) * sine
            out[:, at : at + HEAD] = turned.astype(BF)
    v_ref[...] = raw_ref[:, 2 * width :].astype(BF)


def rotate_rows(raw, scales, gains, cosine, sine):
    rows, width = raw.shape[0], raw.shape[1] // 3
    step = min(512, rows)
    out_spec = pl.BlockSpec((step, width), lambda i: (i, 0))
    table = pl.BlockSpec((step, HEAD), lambda i: (i, 0))
    return pl.pallas_call(
        rotate_kernel,
        out_shape=(jax.ShapeDtypeStruct((rows, width), BF),) * 3,
        grid=(rows // step,),
        in_specs=[
            pl.BlockSpec((step, 3 * width), lambda i: (i, 0)),
            pl.BlockSpec((8, step), lambda i: (0, i)),
            pl.BlockSpec((2, width), lambda i: (0, 0)),
            table,
            table,
        ],
        out_specs=[out_spec] * 3,
        name="rotate_rows",
    )(raw, scales, gains, cosine, sine)


def row_pack_kernel(set_ref, qkv_ref, attn_ref, expand_ref, reduce_ref, out_ref):
    for part in range(3):
        out_ref[16 * part : 16 * part + 16, :] = qkv_ref[part, 0]
    out_ref[48:64, :] = attn_ref[0]
    for part in range(2):
        out_ref[64 + 16 * part : 80 + 16 * part, :] = expand_ref[part, 0]
    out_ref[96:112, :] = reduce_ref[0]


def row_pack_of(which, qkv_low, attn_up, expand_low, reduce_up):
    width = attn_up.shape[2]
    one = pl.BlockSpec((1, 16, width), lambda i, c: (c[0], 0, 0))

    def many(parts):
        return pl.BlockSpec((parts, 1, 16, width), lambda i, c: (0, c[0], 0, 0))

    return pl.pallas_call(
        row_pack_kernel,
        out_shape=jax.ShapeDtypeStruct((112, width), BF),
        grid_spec=pltpu.PrefetchScalarGridSpec(
            num_scalar_prefetch=1,
            grid=(1,),
            in_specs=[many(3), one, many(2), one],
            out_specs=pl.BlockSpec((112, width), lambda i, c: (0, 0)),
        ),
        name="row_pack",
    )(which, qkv_low, attn_up, expand_low, reduce_up)


def col_pack_kernel(set_ref, qkv_ref, attn_ref, expand_ref, reduce_ref, out_ref):
    sub, ff_sub = qkv_ref.shape[3], expand_ref.shape[3]
    for part in range(3):
        out_ref[0, :, part * sub : (part + 1) * sub] = qkv_ref[part, 0]
    at = 4 * sub
    out_ref[0, :, 3 * sub : at] = attn_ref[0]
    for part in range(2):
        out_ref[0, :, at : at + ff_sub] = expand_ref[part, 0]
        at += ff_sub
    out_ref[0, :, at:] = reduce_ref[0]


def col_pack_of(which, qkv_up, attn_low, expand_up, reduce_low):
    cols = which.shape[0] - 1
    sub, ff_sub = qkv_up.shape[3] // 4, expand_up.shape[3] // 4

    def many(parts, size):
        return pl.BlockSpec((parts, 1, 16, size), lambda i, c: (0, c[i], 0, c[cols]))

    def one(size):
        return pl.BlockSpec((1, 16, size), lambda i, c: (c[i], 0, c[cols]))

    total = 4 * sub + 3 * ff_sub
    return pl.pallas_call(
        col_pack_kernel,
        out_shape=jax.ShapeDtypeStruct((cols, 16, total), BF),
        grid_spec=pltpu.PrefetchScalarGridSpec(
            num_scalar_prefetch=1,
            grid=(cols,),
            in_specs=[many(3, sub), one(sub), many(2, ff_sub), one(ff_sub)],
            out_specs=pl.BlockSpec((1, 16, total), lambda i, c: (i, 0, 0)),
        ),
        name="col_pack",
    )(which, qkv_up, attn_low, expand_up, reduce_low)


def finish_kernel(ids_ref, rows_ref, cols_ref, *outs):
    qkv_low, qkv_up, attn_low, attn_up, expand_low, expand_up, reduce_low, reduce_up = outs
    cols = cols_ref.shape[2]
    groups = 2 * cols
    step = pl.program_id(0)
    me = ids_ref[2 * groups]
    sub = qkv_up.shape[3] // 4
    ff_sub = expand_up.shape[3] // 4

    @pl.when(step == 0)
    def _():
        for out in outs:
            out[...] = jnp.zeros_like(out)

    here = ids_ref[step]
    term = rows_ref[step // 2, lax.rem(step, 2)].astype(F32)
    for part in range(3):
        qkv_low[part, here] += term[16 * part : 16 * part + 16]
    attn_up[here] += term[48:64]
    for part in range(2):
        expand_low[part, here] += term[64 + 16 * part : 80 + 16 * part]
    reduce_up[here] += term[96:112]
    here = ids_ref[groups + step]
    for row in range(4):
        term = cols_ref[me ^ row, step // cols, lax.rem(step, cols)].astype(F32)
        near = slice(row * sub, (row + 1) * sub)
        wide = slice(row * ff_sub, (row + 1) * ff_sub)
        for part in range(3):
            qkv_up[part, here, :, near] += term[:, part * sub : (part + 1) * sub]
        attn_low[here, :, near] += term[:, 3 * sub : 4 * sub]
        for part in range(2):
            at = 4 * sub + part * ff_sub
            expand_up[part, here, :, wide] += term[:, at : at + ff_sub]
        reduce_low[here, :, wide] += term[:, 4 * sub + 2 * ff_sub :]


def finish_call(ids, rows, cols, sub, ff_sub):
    width = rows.shape[3]
    shapes = [
        (3, width),
        (3, 4 * sub),
        (0, 4 * sub),
        (0, width),
        (2, width),
        (2, 4 * ff_sub),
        (0, 4 * ff_sub),
        (0, width),
    ]
    out_shape, out_specs = [], []
    for parts, size in shapes:
        if parts:
            out_shape.append(jax.ShapeDtypeStruct((parts, SETS, 16, size), F32))
            out_specs.append(pl.BlockSpec((parts, SETS, 16, size), lambda k, c: (0, 0, 0, 0)))
        else:
            out_shape.append(jax.ShapeDtypeStruct((SETS, 16, size), F32))
            out_specs.append(pl.BlockSpec((SETS, 16, size), lambda k, c: (0, 0, 0)))

    def whole(array):
        return pl.BlockSpec(array.shape, lambda k, c: (0,) * array.ndim)

    return pl.pallas_call(
        finish_kernel,
        out_shape=out_shape,
        grid_spec=pltpu.PrefetchScalarGridSpec(
            num_scalar_prefetch=1,
            grid=(2 * cols.shape[2],),
            in_specs=[whole(rows), whole(cols)],
            out_specs=out_specs,
        ),
        name="finish",
    )(ids, rows, cols)


def cost_of(flops, bytes_accessed):
    return pl.CostEstimate(flops=int(flops), bytes_accessed=int(bytes_accessed), transcendentals=0)


def row_tile(rows):
    return min(512, rows)


def merge_rows_kernel(pair_ref, own_ref, other_ref, low_ref, up_ref, out_ref):
    def put(piece):
        for block in range(4):
            base = piece[0, block].astype(F32)
            extra = dot_of(low_ref[block, 0], up_ref[...], 0, 0)
            out_ref[block, 0] = (base + ADAPTER_FACTOR * extra).astype(BF)

    mine = pl.program_id(0) == pair_ref[0]
    pl.when(mine)(functools.partial(put, own_ref))
    pl.when(jnp.logical_not(mine))(functools.partial(put, other_ref))


def merge_qkv_kernel(pair_ref, own_ref, other_ref, low_ref, up_ref, out_ref):
    cols, sub = own_ref.shape[0], own_ref.shape[4]

    def put(piece, back):
        for block in range(4):
            extra = dot_of(low_ref[block, 0], up_ref[...], 0, 0)
            for index in range(cols):
                at = lax.rem(index - back + cols, cols)
                lanes = slice(index * sub, (index + 1) * sub)
                base = piece[at, block, 0].astype(F32)
                out_ref[block, 0, :, lanes] = (base + ADAPTER_FACTOR * extra[:, lanes]).astype(BF)

    mine = pl.program_id(0) == pair_ref[0]
    pl.when(mine)(functools.partial(put, own_ref, 0))
    pl.when(jnp.logical_not(mine))(functools.partial(put, other_ref, pair_ref[1]))


def merge_columns_kernel(pair_ref, *refs):
    *pieces, low_ref, up_ref, out_ref = refs
    width = out_ref.shape[1] // 4

    def put(piece):
        for block in range(4):
            span = slice(block * width, (block + 1) * width)
            extra = dot_of(low_ref[0], up_ref[:, span], 0, 0)
            out_ref[:, span] = (piece[0, block].astype(F32) + ADAPTER_FACTOR * extra).astype(BF)

    if len(pieces) == 1:
        put(pieces[0])
        return
    mine = pl.program_id(0) == pair_ref[0]
    pl.when(mine)(functools.partial(put, pieces[0]))
    pl.when(jnp.logical_not(mine))(functools.partial(put, pieces[1]))


def merge_qkv(pair, own, other, low, up):
    cols, _, parts, cut, sub = own.shape

    def piece(half):
        def place(h, p, pair_ref):
            mine = h == half(pair_ref[0])
            return (0, 0, jnp.where(mine, p, jnp.where(h == 0, 0, parts - 1)), 0, 0)

        return pl.BlockSpec((cols, 4, 1, cut, sub), place)

    whole = pl.pallas_call(
        merge_qkv_kernel,
        out_shape=jax.ShapeDtypeStruct((4, 2, cut, parts * cols * sub), BF),
        grid_spec=pltpu.PrefetchScalarGridSpec(
            num_scalar_prefetch=1,
            grid=(2, parts),
            in_specs=[
                piece(lambda one: one),
                piece(lambda one: 1 - one),
                pl.BlockSpec((4, 1, 16, cut), lambda h, p, one: (0, h, p, 0)),
                pl.BlockSpec((16, cols * sub), lambda h, p, one: (p, 0)),
            ],
            out_specs=pl.BlockSpec((4, 1, cut, cols * sub), lambda h, p, one: (0, h, 0, p)),
        ),
        cost_estimate=cost_of(0, 8 * own.size),
        name="merge_qkv",
    )(pair, own, other, low.reshape(16 * parts, 4, 2, cut).transpose(1, 2, 0, 3), up)
    return whole.reshape(8 * cut, parts * cols * sub)


def half_specs(block, cols):
    def piece(half, relative):
        def place(h, c, pair_ref):
            at = jnp.where(h == half(pair_ref[0]), c, jnp.where(h == 0, 0, cols - 1))
            if relative:
                at = lax.rem(at - pair_ref[1] + cols, cols)
            return (at,) + (0,) * (len(block) - 1)

        return pl.BlockSpec(block, place)

    return [piece(lambda one: one, False), piece(lambda one: 1 - one, True)]


def merge_expand(pair, own, other, low, up):
    cols, _, width, cut = own.shape
    whole = pl.pallas_call(
        merge_rows_kernel,
        out_shape=jax.ShapeDtypeStruct((4, 1, width, 2 * cols * cut), BF),
        grid_spec=pltpu.PrefetchScalarGridSpec(
            num_scalar_prefetch=1,
            grid=(2, cols),
            in_specs=half_specs((1, 4, width, cut), cols)
            + [
                pl.BlockSpec((4, 1, 16, width), lambda h, c, one: (0, 0, 0, 0)),
                pl.BlockSpec((16, cut), lambda h, c, one: (0, 2 * c + h)),
            ],
            out_specs=pl.BlockSpec((4, 1, width, cut), lambda h, c, one: (0, 0, 0, 2 * c + h)),
        ),
        cost_estimate=cost_of(0, 8 * own.size),
        name="merge_expand",
    )(pair, own, other, low.reshape(16, 4, 1, width).transpose(1, 2, 0, 3), up)
    return whole.reshape(4 * width, 2 * cols * cut)


def merge_out(pair, pieces, low, up):
    cols, _, rows, width = pieces[0].shape
    takes = len(pieces)
    block = (1, 4, rows, width)
    specs = half_specs(block, cols)
    if takes == 1:
        specs = [pl.BlockSpec(block, lambda h, c, one: (c, 0, 0, 0))]
    return pl.pallas_call(
        merge_columns_kernel,
        out_shape=jax.ShapeDtypeStruct((takes * cols * rows, 4 * width), BF),
        grid_spec=pltpu.PrefetchScalarGridSpec(
            num_scalar_prefetch=1,
            grid=(takes, cols),
            in_specs=specs
            + [
                pl.BlockSpec((1, 16, rows), lambda h, c, one: (takes * c + h, 0, 0)),
                pl.BlockSpec((16, 4 * width), lambda h, c, one: (0, 0)),
            ],
            out_specs=pl.BlockSpec((rows, 4 * width), lambda h, c, one: (takes * c + h, 0)),
        ),
        cost_estimate=cost_of(0, 4 * takes * pieces[0].size),
        name="merge_out",
    )(pair, *pieces, low.reshape(16, takes * cols, rows).transpose(1, 0, 2), up)


BLOCK = 256
RING = 5


def peer(step):
    return {"row": lax.axis_index("row") ^ step}


def send(source, target, sems, index, step):
    return pltpu.make_async_remote_copy(
        src_ref=source,
        dst_ref=target,
        send_sem=sems.at[0, index],
        recv_sem=sems.at[1, index],
        device_id=peer(step),
        device_id_type=pl.DeviceIdType.MESH,
    )


def greet():
    barrier = pltpu.get_barrier_semaphore()
    for step in (1, 2, 3):
        pl.semaphore_signal(
            barrier, inc=1, device_id=peer(step), device_id_type=pl.DeviceIdType.MESH
        )
    pl.semaphore_wait(barrier, 3)


def exchange_scratch(count, width, gathers):
    sem = pltpu.SemaphoreType.DMA((2, count))
    shapes = [
        pltpu.VMEM((2, 2, BLOCK, width), BF),
        pltpu.VMEM((count, 2, BLOCK, width), BF),
        pltpu.VMEM((2, BLOCK, width), F32),
        pltpu.VMEM((2, BLOCK, width), BF),
        pltpu.VMEM((count, BLOCK, width), BF),
        pltpu.VMEM((RING, BLOCK, width), F32),
        sem,
        sem,
    ]
    if gathers:
        shapes += [
            pltpu.VMEM((count, 8, BLOCK), F32),
            pltpu.VMEM((3, count, 8, BLOCK), F32),
        ] + [sem] * 6
    return shapes


def run_blocks(
    count,
    bufs,
    compute,
    stats,
    finish,
    own_ref=None,
    arrived=None,
    extra=None,
    own_rows=None,
    idle=None,
):
    pair_out, pair_in, far, side_out, side_in, near, pair_sem, side_sem, *rest = bufs
    gathers = own_ref is not None
    if gathers:
        stat_own, stat_in, stat_1, stat_2, stat_3, core_sem, far_sem, relay_sem = rest
        stat_sems = (stat_1, stat_2, stat_3)

    def rows_of(c):
        return pl.ds(pl.multiple_of(c * BLOCK, BLOCK), BLOCK)

    def to_core(c):
        return send(pair_out.at[lax.rem(c, 2)], pair_in.at[c], pair_sem, c, 1)

    def to_side(c):
        return send(side_out.at[lax.rem(c, 2)], side_in.at[c], side_sem, c, 2)

    def to_stat(c, step):
        return send(stat_own.at[c], stat_in.at[step - 1, c], stat_sems[step - 1], c, step)

    def gather_core(c):
        return send(own_ref.at[rows_of(c)], arrived[0].at[rows_of(c)], core_sem, c, 1)

    def gather_side(c):
        return send(own_ref.at[rows_of(c)], arrived[1].at[rows_of(c)], far_sem, c, 2)

    def relay(c):
        return send(arrived[1].at[rows_of(c)], arrived[2].at[rows_of(c)], relay_sem, c, 1)

    def stage(c, body):
        pl.when(jnp.logical_and(c >= 0, c < count))(functools.partial(body, c))

    def multiply(c):
        @pl.when(c >= 2)
        def _():
            to_core(c - 2).wait_send()

        slot = lax.rem(c, 2)

        def put(block, value):
            if block == 0:
                near[lax.rem(c, RING)] = value
            elif block == 2:
                far[slot] = value
            else:
                pair_out[slot, block // 2] = value.astype(BF)
            if block == 3:
                to_core(c).start()

        compute(c, put)

    def sum_core(c):
        @pl.when(c >= 2)
        def _():
            to_side(c - 2).wait_send()

        to_core(c).wait_recv()
        slot = lax.rem(c, 2)
        side_out[slot] = (far[slot] + pair_in[c, 1].astype(F32)).astype(BF)
        to_side(c).start()
        at = lax.rem(c, RING)
        near[at] = near[at] + pair_in[c, 0].astype(F32)
        if extra is not None:
            extra[0](c)

    def sum_side(c):
        if extra is not None:
            extra[1](c)
        to_side(c).wait_recv()
        at = lax.rem(c, RING)
        total = near[at] + side_in[c].astype(F32)
        if not gathers:
            finish(c, rows_of(c), total)
            return
        near[at] = total
        stat_own[c] = stats(c, rows_of(c), total)
        for step in (1, 2, 3):
            to_stat(c, step).start()

    def normalise(c):
        total = stat_own[c]
        for step in (1, 2, 3):
            to_stat(c, step).wait_recv()
            total = total + stat_in[step - 1, c]
        own_ref[rows_of(c), :] = finish(c, rows_of(c), near[lax.rem(c, RING)], total)
        gather_side(c).start()
        gather_core(c).start()
        if own_rows is not None:
            own_rows(c).start()

    def pass_on(c):
        gather_side(c).wait_recv()
        relay(c).start()

    def body(t, carry):
        stage(t - 1, sum_core)
        stage(t, multiply)
        stage(t - 2, sum_side)
        if gathers:
            stage(t - 3, normalise)
            stage(t - 4, pass_on)
        if idle is not None:
            pl.when(t >= 1)(lambda: idle(t - 1))
        return carry

    lax.fori_loop(0, count + (4 if gathers else 2), body, 0)

    def close(c, carry):
        if gathers:
            for step in (1, 2, 3):
                to_stat(c, step).wait_send()
            gather_core(c).wait()
            gather_side(c).wait_send()
            relay(c).wait()
        return carry

    if gathers:
        lax.fori_loop(0, count, close, 0)
    for c in range(max(count - 2, 0), count):
        to_core(c).wait_send()
        to_side(c).wait_send()


def sums_of(*values):
    out = None
    for index, value in enumerate(values):
        pick = lax.broadcasted_iota(jnp.int32, (8, value.shape[1]), 0) == index
        pick = pick.astype(F32).astype(BF)
        for part in in_parts(value, 2):
            term = dot_of(pick, part, 1, 1)
            out = term if out is None else out + term
    return out


def column_of(stats, index):
    parts = jnp.concatenate(in_parts(stats, 3), axis=0)
    pick = lax.rem(lax.broadcasted_iota(jnp.int32, (parts.shape[0], HEAD), 0), 8) == index
    return dot_of(parts, pick.astype(F32).astype(BF), 0, 0)[:, :1]


def branch_kernel(
    q_ref,
    k_ref,
    v_ref,
    limit_ref,
    matrix_ref,
    tokens_ref,
    gain_ref,
    gate_all,
    gate_other,
    upper_all,
    upper_other,
    mixed_ref,
    branch_ref,
    hidden_ref,
    stat_ref,
    own_ref,
    *rest,
):
    arrived, halves, probs_hbm, rest = rest[:3], rest[3:5], rest[5], rest[6:]
    swap_sems, stage, stage_sem, log_ref, *bufs = rest
    width = own_ref.shape[1]
    count = own_ref.shape[0] // BLOCK
    greet_all([peer(step) for step in (1, 2, 3)] + [other_of_pair()])
    cols = gate_all.shape[0]
    swaps = exchange_halves(gate_all, halves[0], swap_sems.at[0], range(2, cols))
    swaps += exchange_halves(upper_all, halves[1], swap_sems.at[1], range(1, cols))
    for copy in swaps:
        copy.start()

    heads = mixed_ref.shape[1] // HEAD
    key_pos = lax.broadcasted_iota(jnp.int32, (K_BLOCK, Q_BLOCK), 0)

    def blocks_of(group):
        return jnp.maximum((group + 1) * Q_BLOCK, SEQUENCE_LENGTH // 2) // K_BLOCK

    def attend(group):
        rows = span_of(group, Q_BLOCK)

        def head(h, carry):
            lanes = span_of(h, HEAD)
            mixed, logs = attend_rows(
                q_ref[rows, lanes],
                limit_ref[:, rows],
                lambda at: k_ref[pl.ds(at, K_BLOCK), lanes],
                lambda at: v_ref[pl.ds(at, K_BLOCK), lanes],
                blocks_of(group),
            )
            mixed_ref[rows, lanes] = mixed.T.astype(BF)
            log_ref[h, :, rows] = logs
            return carry

        lax.fori_loop(0, heads, head, 0)

    ratio = Q_BLOCK // BLOCK
    share = heads // ratio

    def keep_some(turn):
        group = turn // ratio
        rows = span_of(group, Q_BLOCK)
        blocks = blocks_of(group)
        first = lax.rem(turn, ratio) * share

        def head(h, carry):
            lanes = span_of(h, HEAD)

            def out(index):
                slot = lax.rem(index, 2)
                return pltpu.make_async_copy(
                    stage.at[slot], probs_hbm.at[h, group, index], stage_sem.at[slot]
                )

            def keep(index, carry):
                @pl.when(index >= 2)
                def _():
                    out(index - 2).wait()

                at = pl.multiple_of(index * K_BLOCK, K_BLOCK)
                scores = dot_of(k_ref[pl.ds(at, K_BLOCK), lanes], q_ref[rows, lanes], 1, 1)
                powers = jnp.exp2(scores * (HEAD**-0.5 * LOG2E) - log_ref[h, :, rows])
                seen = key_pos <= limit_ref[:, rows] - at
                stage[lax.rem(index, 2)] = jnp.where(seen, powers, 0.0).astype(BF)
                out(index).start()
                return carry

            lax.fori_loop(0, blocks, keep, 0)
            out(blocks - 2).wait()
            out(blocks - 1).wait()
            return carry

        lax.fori_loop(first, first + share, head, 0)

    def idle(turn):
        pl.when(turn < count)(lambda: keep_some(turn))

    def compute(c, put):
        pl.when(lax.rem(c, ratio) == 0)(lambda: attend(c // ratio))
        left = mixed_ref[pl.ds(pl.multiple_of(c * BLOCK, BLOCK), BLOCK), :]
        for block in (1, 3, 2, 0):
            put(block, dot_of(left, matrix_ref[:, block * width : (block + 1) * width], 1, 0))

    def stats(c, rows, branch):
        branch_ref[rows, :] = branch
        return sums_of(branch * branch)

    def finish(c, rows, branch, total):
        stat_ref[c] = total
        scale = lax.rsqrt(column_of(total, 0) / D + EPS)
        hidden = tokens_ref[rows, :].astype(F32) + gain_ref[0:1, :] * branch * scale
        hidden_ref[rows, :] = hidden
        return hidden.astype(BF)

    run_blocks(count, bufs, compute, stats, finish, own_ref, arrived, idle=idle)
    wait_all(swaps)


def talk_params(number):
    return pltpu.CompilerParams(
        collective_id=number, has_side_effects=True, vmem_limit_bytes=63 * 2**20
    )


def branch_call(query, key, value, limit, matrix, tokens, gain, halves):
    rows, width = tokens.shape
    local = query.shape[1]
    count = rows // BLOCK
    cols = halves[0].shape[0]
    part = jax.ShapeDtypeStruct((rows, width), BF)
    whole = jax.ShapeDtypeStruct((rows, width), F32)
    half = jax.ShapeDtypeStruct(halves[0].shape, BF)
    return pl.pallas_call(
        branch_kernel,
        out_shape=[
            jax.ShapeDtypeStruct((rows, local), BF),
            whole,
            whole,
            jax.ShapeDtypeStruct((count, 8, BLOCK), F32),
        ]
        + [part] * 4
        + [half] * 2
        + [
            jax.ShapeDtypeStruct(
                (local // HEAD, rows // Q_BLOCK, rows // K_BLOCK, K_BLOCK, Q_BLOCK), BF
            )
        ],
        in_specs=[VMEM_SPEC] * 7 + [ANY_SPEC] * 4,
        out_specs=[VMEM_SPEC] * 5 + [ANY_SPEC] * 6,
        scratch_shapes=[
            pltpu.SemaphoreType.DMA((2, 2, cols - 1)),
            pltpu.VMEM((2, K_BLOCK, Q_BLOCK), BF),
            pltpu.SemaphoreType.DMA((2,)),
            pltpu.VMEM((local // HEAD, 1, rows), F32),
        ]
        + exchange_scratch(count, width, True),
        input_output_aliases={8: 8, 10: 9},
        compiler_params=talk_params(0),
        cost_estimate=cost_of(8 * rows * width * matrix.shape[0], 2**27),
        name="branch",
    )(query, key, value, limit, matrix, tokens, gain, *halves)


def rows_out(buffer, outer, sems, index):
    def copy(c):
        rows = span_of(c, BLOCK)
        return pltpu.make_async_copy(buffer.at[rows], outer.at[rows], sems.at[index, c])

    return copy


def wait_rows(count, *copies):
    def body(c, carry):
        for copy in copies:
            copy(c).wait()
        return carry

    lax.fori_loop(0, count, body, 0)


def load_lefts(lefts, buffer, sems, count):
    width = buffer.shape[2] // 4

    def copies(c):
        slot = lax.rem(c, 2)
        rows = pl.ds(pl.multiple_of(c * BLOCK, BLOCK), BLOCK)
        return [
            pltpu.make_async_copy(
                left.at[rows], buffer.at[slot, :, index * width : (index + 1) * width], sems.at[slot, index]
            )
            for index, left in enumerate(lefts)
        ]

    def start(c):
        @pl.when(c < count)
        def _():
            for copy in copies(c):
                copy.start()

    def wait(c):
        for copy in copies(c):
            copy.wait()

    return start, wait


def move_rows(outer, buffer, sems, index, inward):
    def copy(c):
        slot = lax.rem(c, 2)
        rows = pl.ds(pl.multiple_of(c * BLOCK, BLOCK), BLOCK)
        ends = (outer.at[rows], buffer.at[slot])
        if not inward:
            ends = ends[::-1]
        return pltpu.make_async_copy(*ends, sems.at[index, slot])

    return copy


def forward_kernel(
    x0,
    x1,
    x2,
    x3,
    gate_hbm,
    upper_hbm,
    reduce_hbm,
    hidden_hbm,
    cot_hbm,
    gain_ref,
    expand_low_ref,
    reduce_low_ref,
    act_out,
    gate_out,
    upper_out,
    layer_out,
    expand_inner_ref,
    reduce_inner_ref,
    own_out,
    *rest,
):
    arrived, rest = rest[:3], rest[3:]
    gate_w, upper_w, reduce_w, lefts, act_buf, gate_buf, upper_buf, *rest = rest
    hidden_ref, cot_ref, layer_ref, own_ref, w_sem, x_sem, o_sem, r_sem, *bufs = rest
    width = own_ref.shape[1]
    count = own_ref.shape[0] // BLOCK
    ff = gate_w.shape[1]
    tile = ff // 2
    loads = [
        pltpu.make_async_copy(source, target, w_sem.at[index])
        for index, (source, target) in enumerate(
            (
                (gate_hbm.at[:, :tile], gate_w.at[:, :tile]),
                (upper_hbm.at[:, :tile], upper_w.at[:, :tile]),
                (reduce_hbm, reduce_w),
                (cot_hbm, cot_ref),
                (hidden_hbm, hidden_ref),
                (gate_hbm.at[:, tile:], gate_w.at[:, tile:]),
                (upper_hbm.at[:, tile:], upper_w.at[:, tile:]),
            )
        )
    ]
    start_left, wait_left = load_lefts((x0, x1, x2, x3), lefts, x_sem, count)
    start_left(0)
    for index in (0, 1, 5, 6, 2, 3, 4):
        loads[index].start()
    layer_rows = rows_out(layer_ref, layer_out, r_sem, 0)
    own_rows = rows_out(own_ref, own_out, r_sem, 1)
    greet()
    outs = [
        move_rows(outer, buffer, o_sem, index, False)
        for index, (outer, buffer) in enumerate(
            ((act_out, act_buf), (gate_out, gate_buf), (upper_out, upper_buf))
        )
    ]

    def compute(c, put):
        slot = lax.rem(c, 2)
        wait_left(c)
        start_left(c + 1)

        @pl.when(c == 0)
        def _():
            loads[0].wait()
            loads[1].wait()

        @pl.when(c >= 2)
        def _():
            for out in outs:
                out(c - 2).wait()

        def tiles(n, carry):
            @pl.when(jnp.logical_and(c == 0, n == 1))
            def _():
                loads[5].wait()
                loads[6].wait()

            at = pl.ds(pl.multiple_of(n * tile, tile), tile)
            left = lefts[slot]
            gate = dot_of(left, gate_w[:, at], 1, 0)
            upper = dot_of(left, upper_w[:, at], 1, 0)
            act_buf[slot, :, at] = (gate * jax.nn.sigmoid(gate) * upper).astype(BF)
            gate_buf[slot, :, at] = gate.astype(BF)
            upper_buf[slot, :, at] = upper.astype(BF)
            return carry

        lax.fori_loop(0, ff // tile, tiles, 0)
        for out in outs:
            out(c).start()

        @pl.when(c == 0)
        def _():
            loads[2].wait()

        for block in (1, 3, 2, 0):
            span = slice(block * width, (block + 1) * width)
            put(block, dot_of(act_buf[slot], reduce_w[:, span], 1, 0))
        rows = span_of(c, BLOCK)
        expand_inner_ref[:, rows] = dot_of(expand_low_ref[...], lefts[slot], 1, 1).astype(BF)
        reduce_inner_ref[:, rows] = dot_of(reduce_low_ref[...], act_buf[slot], 1, 1)

    def stats(c, rows, result):
        @pl.when(c == 0)
        def _():
            loads[3].wait()
            loads[4].wait()

        weighted = gain_ref[1:2, :] * cot_ref[rows, :].astype(F32)
        return sums_of(result * result, weighted * result)

    def finish(c, rows, result, total):
        scale = lax.rsqrt(column_of(total, 0) / D + EPS)
        gain = gain_ref[1:2, :]
        layer_ref[rows, :] = (hidden_ref[rows, :] + gain * result * scale).astype(BF)
        layer_rows(c).start()
        weighted = gain * cot_ref[rows, :].astype(F32)
        inner = column_of(total, 1)
        return (scale * weighted - result * (scale * scale * scale * inner / D)).astype(BF)

    run_blocks(count, bufs, compute, stats, finish, own_ref, arrived, own_rows=own_rows)
    wait_rows(count, layer_rows, own_rows)
    for c in range(max(count - 2, 0), count):
        for out in outs:
            out(c).wait()


def forward_call(lefts, gate_w, upper_w, reduce_w, hidden, cotangent, gain, low, reduce_low):
    rows, width = hidden.shape
    count = rows // BLOCK
    ff = gate_w.shape[1]
    part = jax.ShapeDtypeStruct((rows, width), BF)
    wide = jax.ShapeDtypeStruct((rows, ff), BF)
    return pl.pallas_call(
        forward_kernel,
        out_shape=[wide] * 3
        + [
            part,
            jax.ShapeDtypeStruct((32, rows), BF),
            jax.ShapeDtypeStruct((16, rows), F32),
        ]
        + [part] * 4,
        in_specs=[ANY_SPEC] * 9 + [VMEM_SPEC] * 3,
        out_specs=[ANY_SPEC] * 4 + [VMEM_SPEC] * 2 + [ANY_SPEC] * 4,
        scratch_shapes=[
            pltpu.VMEM(gate_w.shape, BF),
            pltpu.VMEM(upper_w.shape, BF),
            pltpu.VMEM(reduce_w.shape, BF),
            pltpu.VMEM((2, BLOCK, 4 * width), BF),
            pltpu.VMEM((2, BLOCK, ff), BF),
            pltpu.VMEM((2, BLOCK, ff), BF),
            pltpu.VMEM((2, BLOCK, ff), BF),
            pltpu.VMEM((rows, width), F32),
            pltpu.VMEM((rows, width), BF),
            pltpu.VMEM((rows, width), BF),
            pltpu.VMEM((rows, width), BF),
            pltpu.SemaphoreType.DMA((7,)),
            pltpu.SemaphoreType.DMA((2, 4)),
            pltpu.SemaphoreType.DMA((3, 2)),
            pltpu.SemaphoreType.DMA((2, count)),
        ]
        + exchange_scratch(count, width, True),
        compiler_params=talk_params(1),
        cost_estimate=cost_of(24 * rows * width * ff, 2**27),
        name="forward",
    )(*lefts, gate_w, upper_w, reduce_w, hidden, cotangent, gain, low, reduce_low)


def backward_kernel(
    x0,
    x1,
    x2,
    x3,
    gate_hbm,
    upper_hbm,
    reduce_hbm,
    gate_in,
    upper_in,
    cot_hbm,
    branch_hbm,
    stat_ref,
    gain_ref,
    reduce_up_ref,
    expand_up_ref,
    expand_inner_ref,
    d_hidden_out,
    reduce_inner_ref,
    d_inner_ref,
    up_grad_ref,
    own_out,
    *rest,
):
    arrived, rest = rest[:3], rest[3:]
    gate_w, upper_w, reduce_w, lefts, gate_buf, upper_buf, d_gate_buf, d_upper_buf, *rest = rest
    branch_ref, cot_ref, d_hidden_ref, own_ref, w_sem, x_sem, i_sem, r_sem, *bufs = rest
    width = own_ref.shape[1]
    count = own_ref.shape[0] // BLOCK
    ff = gate_w.shape[1]
    up_grad_ref[...] = jnp.zeros_like(up_grad_ref)
    tile = ff // 2
    loads = [
        pltpu.make_async_copy(source, target, w_sem.at[index])
        for index, (source, target) in enumerate(
            (
                (reduce_hbm.at[:tile], reduce_w.at[:tile]),
                (gate_hbm, gate_w),
                (upper_hbm, upper_w),
                (cot_hbm, cot_ref),
                (branch_hbm, branch_ref),
                (reduce_hbm.at[tile:], reduce_w.at[tile:]),
            )
        )
    ]
    start_left, wait_left = load_lefts((x0, x1, x2, x3), lefts, x_sem, count)
    ins = [
        move_rows(outer, buffer, i_sem, index, True)
        for index, (outer, buffer) in enumerate(((gate_in, gate_buf), (upper_in, upper_buf)))
    ]
    start_left(0)
    for one in ins:
        one(0).start()
    for index in (0, 5, 1, 2, 3, 4):
        loads[index].start()
    hidden_rows = rows_out(d_hidden_ref, d_hidden_out, r_sem, 0)
    own_rows = rows_out(own_ref, own_out, r_sem, 1)
    greet()

    def compute(c, put):
        slot = lax.rem(c, 2)
        wait_left(c)
        start_left(c + 1)
        for one in ins:
            one(c).wait()

        @pl.when(c + 1 < count)
        def _():
            for one in ins:
                one(c + 1).start()

        @pl.when(c == 0)
        def _():
            loads[0].wait()

        def tiles(n, carry):
            @pl.when(jnp.logical_and(c == 0, n == 1))
            def _():
                loads[5].wait()

            at = pl.ds(pl.multiple_of(n * tile, tile), tile)
            d_act = dot_of(lefts[slot], reduce_w[at, :], 1, 1)
            gate = gate_buf[slot, :, at].astype(F32)
            sigma = jax.nn.sigmoid(gate)
            d_gate = d_act * upper_buf[slot, :, at].astype(F32) * (sigma * (1 + gate * (1 - sigma)))
            d_gate_buf[:, at] = d_gate.astype(BF)
            d_upper_buf[:, at] = (d_act * (gate * sigma)).astype(BF)
            return carry

        lax.fori_loop(0, ff // tile, tiles, 0)
        @pl.when(c == 0)
        def _():
            loads[1].wait()
            loads[2].wait()

        for block in (1, 3, 2, 0):
            span = slice(block * width, (block + 1) * width)
            put(
                block,
                dot_of(d_gate_buf[...], gate_w[span, :], 1, 1)
                + dot_of(d_upper_buf[...], upper_w[span, :], 1, 1),
            )
        rows = span_of(c, BLOCK)
        inner = dot_of(reduce_up_ref[...], lefts[slot], 1, 1)
        reduce_inner_ref[:, rows] = (ADAPTER_FACTOR * inner).astype(BF)
        for part, grad in enumerate((d_gate_buf, d_upper_buf)):
            own = slice(16 * part, 16 * part + 16)
            d_inner_ref[own, rows] = ADAPTER_FACTOR * dot_of(expand_up_ref[own, :], grad[...], 1, 1)
            up_grad_ref[own, :] += ADAPTER_FACTOR * dot_of(
                expand_inner_ref[own, rows], grad[...], 1, 0
            )

    def stats(c, rows, total):
        @pl.when(c == 0)
        def _():
            loads[3].wait()
            loads[4].wait()

        d_hidden = cot_ref[rows, :].astype(F32) + total
        d_hidden_ref[rows, :] = d_hidden
        hidden_rows(c).start()
        return sums_of(gain_ref[0:1, :] * d_hidden * branch_ref[rows, :])

    def finish(c, rows, total, sums):
        scale = lax.rsqrt(column_of(stat_ref[c], 0) / D + EPS)
        weighted = gain_ref[0:1, :] * d_hidden_ref[rows, :]
        inner = column_of(sums, 0)
        back = scale * scale * scale * inner / D
        return (scale * weighted - branch_ref[rows, :] * back).astype(BF)

    run_blocks(count, bufs, compute, stats, finish, own_ref, arrived, own_rows=own_rows)
    wait_rows(count, hidden_rows, own_rows)


def backward_call(
    lefts, gate_w, upper_w, reduce_w, gate, upper, cotangent, branch, stats, gain, *adapters
):
    rows, width = branch.shape
    count = rows // BLOCK
    ff = gate_w.shape[1]
    part = jax.ShapeDtypeStruct((rows, width), BF)
    return pl.pallas_call(
        backward_kernel,
        out_shape=[
            jax.ShapeDtypeStruct((rows, width), F32),
            jax.ShapeDtypeStruct((16, rows), BF),
            jax.ShapeDtypeStruct((32, rows), F32),
            jax.ShapeDtypeStruct((32, ff), F32),
        ]
        + [part] * 4,
        in_specs=[ANY_SPEC] * 11 + [VMEM_SPEC] * 5,
        out_specs=[ANY_SPEC] + [VMEM_SPEC] * 3 + [ANY_SPEC] * 4,
        scratch_shapes=[
            pltpu.VMEM(gate_w.shape, BF),
            pltpu.VMEM(upper_w.shape, BF),
            pltpu.VMEM(reduce_w.shape, BF),
            pltpu.VMEM((2, BLOCK, 4 * width), BF),
            pltpu.VMEM((2, BLOCK, ff), BF),
            pltpu.VMEM((2, BLOCK, ff), BF),
            pltpu.VMEM((BLOCK, ff), BF),
            pltpu.VMEM((BLOCK, ff), BF),
            pltpu.VMEM((rows, width), F32),
            pltpu.VMEM((rows, width), BF),
            pltpu.VMEM((rows, width), F32),
            pltpu.VMEM((rows, width), BF),
            pltpu.SemaphoreType.DMA((6,)),
            pltpu.SemaphoreType.DMA((2, 4)),
            pltpu.SemaphoreType.DMA((2, 2)),
            pltpu.SemaphoreType.DMA((2, count)),
        ]
        + exchange_scratch(count, width, True),
        compiler_params=talk_params(2),
        cost_estimate=cost_of(24 * rows * width * ff, 2**27),
        name="backward",
    )(
        *lefts, gate_w, upper_w, reduce_w, gate, upper, cotangent, branch, stats, gain, *adapters
    )


def input_kernel(
    raw_hbm,
    dq_hbm,
    dk_hbm,
    dv_hbm,
    act_hbm,
    mixed_hbm,
    branch_hbm,
    hidden_hbm,
    result_hbm,
    matrix_hbm,
    d_hidden_hbm,
    tokens_hbm,
    scale_ref,
    q_sum_ref,
    k_sum_ref,
    gain_ref,
    cos_ref,
    sin_ref,
    inner_ref,
    up_ref,
    part_ref,
    d_inner_ref,
    expand_grad_ref,
    out_hbm,
    rows_out_hbm,
    cols_out_hbm,
    raw_buf,
    dq_buf,
    dk_buf,
    dv_buf,
    act_buf,
    mixed_buf,
    branch_buf,
    hidden_buf,
    result_buf,
    matrix_ref,
    d_hidden_ref,
    tokens_ref,
    out_ref,
    left_ref,
    inner_out,
    inner_in,
    inner_mid,
    inner_far,
    sum_own,
    sum_in,
    columns,
    up_all,
    part_in,
    part_mid,
    part_far,
    in_sem,
    core_sem,
    far_sem,
    sum_sem,
    part_sem,
    load_sem,
    r_sem,
    row_grad_ref,
    attn_grad_ref,
    reduce_grad_ref,
    row_pack,
    col_pack,
    *bufs,
):
    group_sems, bufs = bufs[:5], bufs[5:]
    width = out_ref.shape[1]
    local = dq_buf.shape[2]
    count = out_ref.shape[0] // BLOCK
    ins = [
        move_rows(outer, buffer, in_sem, index, True)
        for index, (outer, buffer) in enumerate(
            (
                (raw_hbm, raw_buf),
                (dq_hbm, dq_buf),
                (dk_hbm, dk_buf),
                (dv_hbm, dv_buf),
                (act_hbm, act_buf),
                (mixed_hbm, mixed_buf),
                (branch_hbm, branch_buf),
                (hidden_hbm, hidden_buf),
                (result_hbm, result_buf),
            )
        )
    ]
    for one in ins:
        one(0).start()
    loads = [
        pltpu.make_async_copy(source, target, load_sem.at[index])
        for index, (source, target) in enumerate(
            ((matrix_hbm, matrix_ref), (d_hidden_hbm, d_hidden_ref), (tokens_hbm, tokens_ref))
        )
    ]
    for load in loads:
        load.start()
    out_rows = rows_out(out_ref, out_hbm, r_sem, 0)
    for grad in (row_grad_ref, attn_grad_ref, reduce_grad_ref):
        grad[...] = jnp.zeros_like(grad)
    up_all[...] = jnp.zeros_like(up_all)
    sum_own[...] = jnp.zeros_like(sum_own)
    for row, part in enumerate((q_sum_ref, k_sum_ref)):
        total = part[0]
        for h in range(1, part.shape[0]):
            total = total + part[h]
        sum_own[row : row + 1, :] = total
    greet_all(row_and_col_peers() + [other_of_pair()])
    exchanges = [send(sum_own, sum_in.at[step - 1], sum_sem, step - 1, step) for step in (1, 2, 3)]
    for copy in exchanges:
        copy.start()
    part_core = send(part_ref, part_in, part_sem, 0, 1)
    part_side = send(part_mid, part_far, part_sem, 1, 2)
    part_core.start()
    part_core.wait()
    part_mid[...] = (part_ref[...].astype(F32) + part_in[...].astype(F32)).astype(BF)
    part_side.start()
    for copy in exchanges:
        copy.wait()
    total = sum_own[...] + sum_in[0] + sum_in[1] + sum_in[2]
    scales = scale_ref[...]
    backs = scales * scales * total / D
    for part in range(2):
        columns[part] = jnp.broadcast_to(column_of(scales, part), columns.shape[1:])
        columns[2 + part] = jnp.broadcast_to(column_of(backs, part), columns.shape[1:])

    def inner_core(c):
        return send(inner_out.at[lax.rem(c, 2)], inner_in.at[c], core_sem, c, 1)

    def inner_side(c):
        return send(inner_mid.at[lax.rem(c, 2)], inner_far.at[c], far_sem, c, 2)

    def after_core(c):
        @pl.when(c >= 2)
        def _():
            inner_side(c - 2).wait_send()

        inner_core(c).wait_recv()
        slot = lax.rem(c, 2)
        total = inner_out[slot].astype(F32) + inner_in[c].astype(F32)
        inner_mid[slot] = total.astype(BF)
        inner_side(c).start()

    def after_side(c):
        inner_side(c).wait_recv()
        total = inner_mid[lax.rem(c, 2)].astype(F32) + inner_far[c].astype(F32)
        row_grad_ref[:48, :] += dot_of(total.astype(BF), tokens_ref[span_of(c, BLOCK), :], 1, 0)

    def compute(c, put):
        slot = lax.rem(c, 2)
        for one in ins:
            one(c).wait()

        @pl.when(c + 1 < count)
        def _():
            for one in ins:
                one(c + 1).start()

        @pl.when(c >= 2)
        def _():
            inner_core(c - 2).wait_send()

        rows = span_of(c, BLOCK)
        cosine = cos_ref[rows, :]
        sine = sin_ref[rows, :]
        for part, grad in ((0, dq_buf), (1, dk_buf)):
            scale = columns[part, rows, :]
            back = columns[2 + part, rows, :]
            for at in range(0, local, HEAD):
                turned = grad[slot, :, at : at + HEAD]
                turned = turned * cosine - pltpu.roll(turned, HEAD // 2, 1) * sine
                turned = turned * gain_ref[part : part + 1, at : at + HEAD] * scale
                lane = part * local + at
                left_ref[:, lane : lane + HEAD] = (
                    turned - raw_buf[slot, :, lane : lane + HEAD] * back
                ).astype(BF)
        left_ref[:, 2 * local :] = dv_buf[slot].astype(BF)
        left = left_ref[...]
        inner_out[slot] = (ADAPTER_FACTOR * dot_of(up_ref[...], left, 1, 1)).astype(BF)
        inner_core(c).start()
        up_all[...] += dot_of(inner_ref[:, rows], left, 1, 0)

        @pl.when(c == 0)
        def _():
            for load in loads:
                load.wait()
            part_side.wait()

        for block in (1, 3, 2, 0):
            put(block, dot_of(left, matrix_ref[block * width : (block + 1) * width, :], 1, 1))
        whole = part_mid[:, rows].astype(F32) + part_far[:, rows].astype(F32)
        whole = whole.astype(BF)
        for at, size, first, other, factor in (
            (48, 16, 0, branch_buf, ADAPTER_FACTOR),
            (64, 32, 32, hidden_buf, 1.0),
            (96, 16, 16, result_buf, ADAPTER_FACTOR),
        ):
            term = dot_of(whole[first : first + size], other[slot], 1, 0)
            row_grad_ref[at : at + size, :] += factor * term
        attn_grad_ref[...] += dot_of(d_inner_ref[:16, rows], mixed_buf[slot], 1, 0)
        reduce_grad_ref[...] += dot_of(d_inner_ref[16:, rows], act_buf[slot], 1, 0)

    def finish(c, rows, total):
        out_ref[rows, :] = d_hidden_ref[rows, :] + total
        out_rows(c).start()

    run_blocks(count, bufs, compute, None, finish, extra=(after_core, after_side))
    row_pack[...] = row_grad_ref[...].astype(BF)
    cols = col_pack.shape[0]
    pieces = [
        (up_all, 16 * part, part * local, local, ADAPTER_FACTOR) for part in range(3)
    ]
    ff = reduce_grad_ref.shape[1]
    pieces += [
        (attn_grad_ref, 0, 0, local, 1.0),
        (expand_grad_ref, 0, 0, ff, 1.0),
        (expand_grad_ref, 16, 0, ff, 1.0),
        (reduce_grad_ref, 0, 0, ff, 1.0),
    ]
    lane = 0
    for ref, row, at, size, factor in pieces:
        size = size // cols
        for index in range(cols):
            piece = ref[row : row + 16, at + index * size : at + (index + 1) * size]
            col_pack[index, :, lane : lane + size] = (factor * piece).astype(BF)
        lane += size
    exchange_groups(row_pack, col_pack, rows_out_hbm, cols_out_hbm, group_sems)
    wait_rows(count, out_rows)
    for c in range(max(count - 2, 0), count):
        inner_core(c).wait_send()
        inner_side(c).wait_send()


def input_call(
    raw, d_query, d_key, d_value, act, mixed, branch, hidden, result, matrix, d_hidden, *others
):
    rows, width = d_hidden.shape
    local = d_query.shape[1]
    ff = act.shape[1]
    cols = lax.axis_size("col")
    lanes = (4 * local + 3 * ff) // cols
    count = rows // BLOCK
    grad = pltpu.VMEM((2, BLOCK, local), F32)
    part = pltpu.VMEM((2, BLOCK, width), BF)
    inner = pltpu.VMEM((2, 48, BLOCK), BF)
    arrived = pltpu.VMEM((count, 48, BLOCK), BF)
    total = pltpu.VMEM((64, rows), BF)
    sem = pltpu.SemaphoreType.DMA((2, count))
    return pl.pallas_call(
        input_kernel,
        out_shape=[
            jax.ShapeDtypeStruct((rows, width), F32),
            jax.ShapeDtypeStruct((cols, 2, 112, width), BF),
            jax.ShapeDtypeStruct((4, 2, cols, 16, lanes), BF),
        ],
        in_specs=[ANY_SPEC] * 12 + [VMEM_SPEC] * 11,
        out_specs=[ANY_SPEC] * 3,
        scratch_shapes=[
            pltpu.VMEM((2, BLOCK, 3 * local), F32),
            grad,
            grad,
            grad,
            pltpu.VMEM((2, BLOCK, ff), BF),
            pltpu.VMEM((2, BLOCK, local), BF),
            part,
            part,
            part,
            pltpu.VMEM(matrix.shape, BF),
            pltpu.VMEM((rows, width), F32),
            pltpu.VMEM((rows, width), BF),
            pltpu.VMEM((rows, width), F32),
            pltpu.VMEM((BLOCK, 3 * local), BF),
            inner,
            arrived,
            inner,
            arrived,
            pltpu.VMEM((8, rows), F32),
            pltpu.VMEM((3, 8, rows), F32),
            pltpu.VMEM((4, rows, HEAD), F32),
            pltpu.VMEM((48, 3 * local), F32),
            total,
            total,
            total,
            pltpu.SemaphoreType.DMA((9, 2)),
            sem,
            sem,
            pltpu.SemaphoreType.DMA((2, 3)),
            pltpu.SemaphoreType.DMA((2, 2)),
            pltpu.SemaphoreType.DMA((3,)),
            pltpu.SemaphoreType.DMA((1, count)),
            pltpu.VMEM((112, width), F32),
            pltpu.VMEM((16, local), F32),
            pltpu.VMEM((16, ff), F32),
            pltpu.VMEM((112, width), BF),
            pltpu.VMEM((cols, 16, lanes), BF),
            pltpu.SemaphoreType.DMA((2,)),
            pltpu.SemaphoreType.DMA((2, 2)),
            pltpu.SemaphoreType.DMA((2, cols - 1)),
            pltpu.SemaphoreType.DMA((2, cols - 1)),
            pltpu.SemaphoreType.DMA((2, 2, 3)),
        ]
        + exchange_scratch(count, width, False),
        compiler_params=talk_params(3),
        cost_estimate=cost_of(24 * rows * width * local, 2**26),
        name="input_grad",
    )(raw, d_query, d_key, d_value, act, mixed, branch, hidden, result, matrix, d_hidden, *others)


def deal(items, outs, sems):
    me = lax.axis_index("row")
    copies = []
    for index, (view, out) in enumerate(zip(items, outs)):
        mine = [pltpu.make_async_copy(view(me), out.at[0], sems.at[0, index, 0])]
        for step in (1, 2, 3):
            mine.append(
                pltpu.make_async_remote_copy(
                    src_ref=view(me ^ step),
                    dst_ref=out.at[step],
                    send_sem=sems.at[0, index, step],
                    recv_sem=sems.at[1, index, step],
                    device_id=peer(step),
                    device_id_type=pl.DeviceIdType.MESH,
                )
            )
        copies.append(mine)
    return copies


def start_all(copies):
    for step in (2, 3, 1, 0):
        copies[step].start()


def wait_all(copies):
    for copy in copies:
        copy.wait()


def span_of(at, size):
    return pl.ds(pl.multiple_of(at * size, size), size)


def qkv_view(ref, half):
    _, rows, columns = ref.shape
    return lambda row: ref.at[:, span_of(half, rows // 2), span_of(row, columns // 4)]


def attn_view(ref, half):
    cut = ref.shape[0] // 8
    return lambda row: ref.at[span_of(2 * row + half, cut)]


def expand_view(ref, part, half):
    cut = ref.shape[2] // 8
    return lambda row: ref.at[part, :, span_of(2 * row + half, cut)]


def reduce_view(ref):
    cut = ref.shape[0] // 4
    return lambda row: ref.at[span_of(row, cut)]


def like_views(shapes):
    return [jax.ShapeDtypeStruct((4, *shape), BF) for shape in shapes]


def attn_deal_kernel(attn_ref, attn_out, sems):
    greet()
    (copies,) = deal([attn_view(attn_ref, lax.axis_index("dp"))], [attn_out], sems)
    start_all(copies)
    wait_all(copies)


def attn_deal(attn_weight):
    return pl.pallas_call(
        attn_deal_kernel,
        out_shape=like_views([(attn_weight.shape[0] // 8, attn_weight.shape[1])])[0],
        in_specs=[ANY_SPEC],
        out_specs=ANY_SPEC,
        scratch_shapes=[pltpu.SemaphoreType.DMA((2, 1, 4))],
        compiler_params=talk_params(4),
        cost_estimate=cost_of(0, 2**25),
        name="attn_deal",
    )(attn_weight)


def first_deal_kernel(qkv_ref, expand_ref, qkv_out, gate_out, sems):
    half = lax.axis_index("dp")
    greet()
    copies = deal([qkv_view(qkv_ref, half), expand_view(expand_ref, 0, half)], [qkv_out, gate_out], sems)
    for one in copies:
        start_all(one)
    for one in copies:
        wait_all(one)


def first_deal(qkv_weight, expand_weight):
    parts, rows, columns = qkv_weight.shape
    return pl.pallas_call(
        first_deal_kernel,
        out_shape=like_views(
            [
                (parts, rows // 2, columns // 4),
                (expand_weight.shape[1], expand_weight.shape[2] // 8),
            ]
        ),
        in_specs=[ANY_SPEC] * 2,
        out_specs=[ANY_SPEC] * 2,
        scratch_shapes=[pltpu.SemaphoreType.DMA((2, 2, 4))],
        compiler_params=talk_params(9),
        cost_estimate=cost_of(0, 2**26),
        name="first_deal",
    )(qkv_weight, expand_weight)


def second_deal_kernel(qkv_ref, attn_ref, expand_ref, tokens_ref, pack_ref, *rest):
    qkv_other, attn_other, upper_out, t1, t2, t3, p1, p2, p3, sems, token_sem, pack_sem = rest
    half = lax.axis_index("dp")
    greet()
    rest_qkv, rest_attn, upper = deal(
        [
            qkv_view(qkv_ref, 1 - half),
            attn_view(attn_ref, 1 - half),
            expand_view(expand_ref, 1, half),
        ],
        [qkv_other.at[0], attn_other.at[0], upper_out],
        sems,
    )
    gathers = []
    for source, targets, one_sem in ((pack_ref, (p1, p2, p3), pack_sem), (tokens_ref, (t1, t2, t3), token_sem)):
        gathers.append(
            (
                send(source, targets[1], one_sem, 1, 2),
                send(source, targets[0], one_sem, 0, 1),
                send(targets[1], targets[2], one_sem, 2, 1),
            )
        )
    start_all(rest_qkv)
    start_all(rest_attn)
    for side, core, _ in gathers:
        side.start()
        core.start()
    start_all(upper)
    for side, core, relay in gathers:
        side.wait_recv()
        relay.start()
    for one in (rest_qkv, rest_attn, upper):
        wait_all(one)
    for side, core, relay in gathers:
        side.wait_send()
        core.wait()
        relay.wait()


def second_deal(qkv_weight, attn_weight, expand_weight, tokens, pack, cols):
    parts, rows, columns = qkv_weight.shape
    cut = expand_weight.shape[2] // 8
    wide = (expand_weight.shape[1], cut)
    sem = pltpu.SemaphoreType.DMA((2, 3))
    return pl.pallas_call(
        second_deal_kernel,
        out_shape=[
            jax.ShapeDtypeStruct((cols, 4, parts, rows // 2, columns // 4), BF),
            jax.ShapeDtypeStruct((cols, 4, attn_weight.shape[0] // 8, attn_weight.shape[1]), BF),
            jax.ShapeDtypeStruct((4, *wide), BF),
        ]
        + [jax.ShapeDtypeStruct(tokens.shape, BF)] * 3
        + [jax.ShapeDtypeStruct(pack.shape, BF)] * 3,
        in_specs=[ANY_SPEC] * 5,
        out_specs=[ANY_SPEC] * 9,
        scratch_shapes=[pltpu.SemaphoreType.DMA((2, 3, 4)), sem, sem],
        compiler_params=talk_params(5),
        cost_estimate=cost_of(0, 2**27),
        name="second_deal",
    )(qkv_weight, attn_weight, expand_weight, tokens, pack)


def greet_all(peers):
    barrier = pltpu.get_barrier_semaphore()
    for device in peers:
        pl.semaphore_signal(barrier, inc=1, device_id=device, device_id_type=pl.DeviceIdType.MESH)
    pl.semaphore_wait(barrier, len(peers))


def copy_to(source, target, sems, index, device):
    return pltpu.make_async_remote_copy(
        src_ref=source,
        dst_ref=target,
        send_sem=sems.at[0, index],
        recv_sem=sems.at[1, index],
        device_id=device,
        device_id_type=pl.DeviceIdType.MESH,
    )


def other_of_pair():
    return {"dp": 1 - lax.axis_index("dp")}


def exchange_halves(whole, out, sems, steps):
    cols = whole.shape[0]
    col = lax.axis_index("col")
    copies = []
    for k in steps:
        place = lax.rem(col + k, cols)
        copies.append(copy_to(whole.at[place], out.at[k], sems, k - 1, other_of_pair()))
    return copies


def send_round(view, out, sems, local_sem):
    cols = out.shape[0]
    col = lax.axis_index("col")
    local = pltpu.make_async_copy(view(col), out.at[col], local_sem)
    sends = []
    arrivals = []
    for k in range(1, cols):
        place = lax.rem(col + k, cols)
        came = lax.rem(col - k + cols, cols)
        sends.append(copy_to(view(place), out.at[col], sems, k - 1, {"col": place}))
        arrivals.append(copy_to(view(place), out.at[came], sems, k - 1, {"col": place}))

    def wait():
        local.wait()
        for one in arrivals:
            one.wait_recv()
        for one in sends:
            one.wait_send()

    return [local, *sends], wait


def row_and_col_peers():
    cols = lax.axis_size("col")
    col = lax.axis_index("col")
    return [peer(step) for step in (1, 2, 3)] + [
        {"col": lax.rem(col + k, cols)} for k in range(1, cols)
    ]


def third_deal_kernel(
    expand_ref, reduce_ref, qkv_all, qkv_other, attn_all, attn_other, pack_ref, gain_ref, *rest
):
    reduce_out, gate_out, upper_out, qkv_out, attn_out, pack_out, gain_out = rest[:7]
    deal_sem, qkv_sem, attn_sem, pack_sem, gain_sem, local_sem = rest[7:]
    other = 1 - lax.axis_index("dp")
    me = lax.axis_index("row")
    greet_all(row_and_col_peers() + [other_of_pair()])
    sub = gain_out.shape[2]
    steps = range(1, qkv_all.shape[0])
    swaps = exchange_halves(qkv_all, qkv_out, qkv_sem, steps)
    swaps += exchange_halves(attn_all, attn_out, attn_sem, steps)
    packs, wait_packs = send_round(lambda place: pack_ref.at[place], pack_out, pack_sem, local_sem.at[2])
    gains, wait_gains = send_round(
        lambda place: gain_ref.at[:, span_of(me, sub)], gain_out, gain_sem, local_sem.at[3]
    )
    for copy in packs + gains + swaps:
        copy.start()
    copies = deal(
        [
            reduce_view(reduce_ref),
            expand_view(expand_ref, 0, other),
            expand_view(expand_ref, 1, other),
        ],
        [reduce_out, gate_out.at[0], upper_out.at[0]],
        deal_sem,
    )
    for one in copies:
        start_all(one)
    wait_packs()
    wait_gains()
    for one in copies:
        wait_all(one)
    wait_all(swaps)


def third_deal(expand_weight, reduce_weight, qkv_all, qkv_other, attn_all, attn_other, pack, gain):
    wide = (expand_weight.shape[1], expand_weight.shape[2] // 8)
    cols = qkv_all.shape[0]
    round_sem = pltpu.SemaphoreType.DMA((2, cols - 1))
    return pl.pallas_call(
        third_deal_kernel,
        out_shape=like_views([(reduce_weight.shape[0] // 4, reduce_weight.shape[1])])
        + [jax.ShapeDtypeStruct((cols, 4, *wide), BF)] * 2
        + [
            jax.ShapeDtypeStruct(qkv_all.shape, BF),
            jax.ShapeDtypeStruct(attn_all.shape, BF),
            jax.ShapeDtypeStruct(pack.shape, BF),
            jax.ShapeDtypeStruct((cols, gain.shape[0], gain.shape[1] // 4), F32),
        ],
        in_specs=[ANY_SPEC] * 8,
        out_specs=[ANY_SPEC] * 7,
        scratch_shapes=[
            pltpu.SemaphoreType.DMA((2, 3, 4)),
            round_sem,
            round_sem,
            round_sem,
            round_sem,
            pltpu.SemaphoreType.DMA((4,)),
        ],
        input_output_aliases={3: 3, 5: 4},
        compiler_params=talk_params(6),
        cost_estimate=cost_of(0, 2**27),
        name="third_deal",
    )(expand_weight, reduce_weight, qkv_all, qkv_other, attn_all, attn_other, pack, gain)


def front_kernel(
    x0,
    x1,
    x2,
    x3,
    matrix_ref,
    low_ref,
    gate_all,
    gate_other,
    raw_ref,
    square_ref,
    inner_ref,
    gate_out,
    swap_sem,
):
    local = raw_ref.shape[1] // 3
    first = exchange_halves(gate_all, gate_out, swap_sem, range(1, 2))

    @pl.when(pl.program_id(0) == 0)
    def _():
        greet_all([other_of_pair()])
        for copy in first:
            copy.start()

    left = jnp.concatenate([x0[...], x1[...], x2[...], x3[...]], axis=1)
    squares = []
    for part in range(3):
        lanes = slice(part * local, (part + 1) * local)
        product = dot_of(left, matrix_ref[:, lanes], 1, 0)
        raw_ref[:, lanes] = product
        squares.append(product * product)
    square_ref[...] = sums_of(*squares[:2])
    inner_ref[...] = dot_of(low_ref[...], left, 1, 1).astype(BF)

    @pl.when(pl.program_id(0) == pl.num_programs(0) - 1)
    def _():
        wait_all(first)


def front_call(lefts, matrix, low, gate_all, gate_other):
    rows, width = lefts[0].shape
    wide = matrix.shape[1]
    tile = row_tile(rows)
    cols = gate_all.shape[0]

    def whole(array):
        return pl.BlockSpec(array.shape, lambda m: (0, 0))

    return pl.pallas_call(
        front_kernel,
        out_shape=[
            jax.ShapeDtypeStruct((rows, wide), F32),
            jax.ShapeDtypeStruct((8, rows), F32),
            jax.ShapeDtypeStruct((48, rows), BF),
            jax.ShapeDtypeStruct(gate_all.shape, BF),
        ],
        grid=(rows // tile,),
        in_specs=[pl.BlockSpec((tile, width), lambda m: (m, 0))] * 4
        + [whole(matrix), whole(low), ANY_SPEC, ANY_SPEC],
        out_specs=[
            pl.BlockSpec((tile, wide), lambda m: (m, 0)),
            pl.BlockSpec((8, tile), lambda m: (0, m)),
            pl.BlockSpec((48, tile), lambda m: (0, m)),
            ANY_SPEC,
        ],
        scratch_shapes=[
            pltpu.SemaphoreType.DMA((2, cols - 1)),
        ],
        input_output_aliases={7: 3},
        compiler_params=talk_params(8),
        cost_estimate=cost_of(8 * rows * width * wide, 2**26),
        name="front",
    )(*lefts, matrix, low, gate_all, gate_other)


def exchange_groups(row_ref, col_ref, rows_out, cols_out, sems):
    local_sem, pair_sem, round_sem, deal_sem, row_sem = sems
    cols = col_ref.shape[0]
    col = lax.axis_index("col")
    places = [lax.rem(col + k, cols) for k in range(cols)]
    to = copy_to
    swap_rows = to(row_ref, rows_out.at[0, 1], pair_sem, 0, other_of_pair())
    swap_rows.start()
    dealt = [
        to(col_ref.at[places[k]], cols_out.at[0, 0, col], deal_sem, k - 1, {"col": places[k]})
        for k in range(1, cols)
    ]
    for copy in dealt:
        copy.start()
    keep_rows = pltpu.make_async_copy(row_ref, rows_out.at[0, 0], local_sem.at[0])
    keep_cols = pltpu.make_async_copy(col_ref.at[col], cols_out.at[0, 0, col], local_sem.at[1])
    keep_rows.start()
    keep_cols.start()
    for k in range(1, cols):
        came = lax.rem(col - k + cols, cols)
        to(col_ref.at[came], cols_out.at[0, 0, came], deal_sem, k - 1, {"col": places[k]}).wait_recv()
    keep_cols.wait()
    swap_cols = to(cols_out.at[0, 0], cols_out.at[0, 1], pair_sem, 1, other_of_pair())
    swap_cols.start()

    def spread(which):
        side = to(cols_out.at[0, which], cols_out.at[2, which], row_sem.at[which], 1, peer(2))
        core = to(cols_out.at[0, which], cols_out.at[1, which], row_sem.at[which], 0, peer(1))
        relay = to(cols_out.at[2, which], cols_out.at[3, which], row_sem.at[which], 2, peer(1))
        side.start()
        core.start()
        return side, core, relay

    spreads = [spread(0)]
    keep_rows.wait()
    swap_rows.wait_recv()
    rounds = [
        to(rows_out.at[0], rows_out.at[k], round_sem, k - 1, {"col": places[k]})
        for k in range(1, cols)
    ]
    for copy in rounds:
        copy.start()
    swap_cols.wait_recv()
    spreads.append(spread(1))
    for side, core, relay in spreads:
        side.wait_recv()
        relay.start()
    for side, core, relay in spreads:
        core.wait()
        relay.wait()
        side.wait_send()
    for copy in rounds:
        copy.wait()
    for copy in dealt:
        copy.wait_send()
    swap_rows.wait_send()
    swap_cols.wait_send()


def across(values, step):
    return lax.ppermute(values, "row", [(i, i ^ step) for i in range(4)])


def sum_row(values):
    values = values + across(values, 1)
    return values + across(values, 2)


def gather_col(values):
    return lax.all_gather(values, "col", axis=0, tiled=False)


def swap_pair(values):
    return lax.ppermute(values, "dp", [(0, 1), (1, 0)])


def round_col(values, cols):
    shift = lambda k: [(i, (i + k) % cols) for i in range(cols)]
    return [values] + [lax.ppermute(values, "col", shift(k)) for k in range(1, cols)]


def after(values, earlier):
    return lax.optimization_barrier((values, earlier))[0]


def group_shards(
    tokens,
    cotangent,
    qkv_weight,
    attn_weight,
    expand_weight,
    reduce_weight,
    headnorm_gain,
    post_gain,
    qkv_lowrank,
    qkv_uprank,
    attn_lowrank,
    attn_uprank,
    expand_lowrank,
    expand_uprank,
    reduce_lowrank,
    reduce_uprank,
    prefix_length,
    adapter_set,
):
    cols = lax.axis_size("col")
    pair = lax.axis_index("dp")
    me = lax.axis_index("row")
    col = lax.axis_index("col")
    rows, width = tokens.shape
    sub = qkv_weight.shape[2] // 4
    ff = expand_weight.shape[2]
    ff_sub = ff // 4
    ff_half = ff_sub // 2
    local = cols * sub
    ff_local = cols * ff_sub
    sequence = pair * cols + col
    mine = lax.dynamic_index_in_dim(adapter_set, sequence, 0, keepdims=False)
    prefix = lax.dynamic_slice_in_dim(prefix_length, sequence, 1)
    cols_sets = lax.dynamic_slice_in_dim(adapter_set, pair * cols, cols)

    attn_own = attn_deal(attn_weight)
    qkv_own, gate_own = first_deal(after(qkv_weight, attn_own), expand_weight)
    row_pack = row_pack_of(
        after(mine.reshape(1), qkv_own),
        qkv_lowrank.transpose(0, 1, 3, 2),
        attn_uprank,
        expand_lowrank.transpose(0, 1, 3, 2),
        reduce_uprank,
    )
    col_pack = col_pack_of(
        jnp.concatenate([cols_sets, me.reshape(1)]),
        qkv_uprank,
        attn_lowrank.transpose(0, 2, 1),
        expand_uprank,
        reduce_lowrank.transpose(0, 2, 1),
    )

    place = jnp.stack([pair, col])

    col_pack = after(col_pack, qkv_own)
    qkv_other, attn_other, up_own, *others = second_deal(
        qkv_weight, attn_weight, expand_weight, tokens, row_pack, cols
    )
    token_parts = [tokens, *others[:3]]
    row_all = jnp.concatenate([row_pack, *others[3:]], axis=1)
    qkv_low = row_all[:48]
    attn_up = row_all[48:64]
    expand_low = row_all[64:96]
    reduce_up = row_all[96:112]
    qkv_all = gather_col(qkv_own)
    attn_all = gather_col(attn_own)
    gate_all = gather_col(after(gate_own, row_pack))
    up_all = gather_col(up_own)
    reduce_own, gate_other, up_other, qkv_other, attn_other, col_all, gains = third_deal(
        expand_weight,
        after(reduce_weight, others[0]),
        qkv_all,
        qkv_other,
        attn_all,
        attn_other,
        col_pack,
        headnorm_gain,
    )
    reduce_all = gather_col(reduce_own)
    gains = gains.transpose(1, 0, 2).reshape(2, local)

    def own_columns(at, size):
        return col_all[:, :, at : at + size].transpose(1, 0, 2).reshape(16, cols * size)

    qkv_up = [own_columns(i * sub, sub) for i in range(3)]
    attn_low = own_columns(3 * sub, sub)
    expand_up = [own_columns(4 * sub + i * ff_sub, ff_sub) for i in range(2)]
    reduce_low = own_columns(4 * sub + 2 * ff_sub, ff_sub)

    diagonal_up = jnp.concatenate(
        [
            jnp.pad(up, ((0, 0), (i * local, (2 - i) * local))) for i, up in enumerate(qkv_up)
        ]
    )
    qkv_up = jnp.concatenate(qkv_up)
    qkv_w = merge_qkv(place, qkv_all, qkv_other, qkv_low, qkv_up)
    attn_w = merge_out(place, [attn_all, attn_other], attn_low, attn_up)

    half = HEAD // 2
    freq = THETA ** (-2.0 * jnp.arange(half, dtype=F32) / HEAD)
    angle = jnp.arange(rows, dtype=jnp.int32).astype(F32)[:, None] * freq[None, :]
    cosine = jnp.concatenate([jnp.cos(angle)] * 2, axis=1)
    sine = jnp.sin(angle)
    sine = jnp.concatenate([-sine, sine], axis=1)

    raw, squares, qkv_inner, gate_other = front_call(
        token_parts, qkv_w, qkv_low, gate_all, gate_other
    )
    scale = lax.rsqrt(sum_row(squares) / D + EPS)
    query, key, value = rotate_rows(raw, scale, gains, cosine, sine)
    limit = jnp.maximum(jnp.arange(rows, dtype=jnp.int32), prefix - 1)[None]
    mixed, branch, hidden, branch_stats, *hidden_parts, gate_other, up_other, probs = branch_call(
        query,
        key,
        value,
        limit,
        attn_w,
        tokens,
        post_gain,
        (gate_all, gate_other, up_all, up_other),
    )
    expand_w = [
        merge_expand(
            place, whole, other, expand_low[16 * i : 16 * i + 16], expand_up[i]
        )
        for i, (whole, other) in enumerate(((gate_all, gate_other), (up_all, up_other)))
    ]
    reduce_w = merge_out(place, [reduce_all], reduce_low, reduce_up)
    act, gate, upper, layer_out, expand_inner, reduce_inner, *result_parts = forward_call(
        hidden_parts, *expand_w, reduce_w, hidden, cotangent, post_gain, expand_low, reduce_low
    )
    d_hidden, d_reduce_inner, d_expand_inner, g_expand_up, *branch_parts = backward_call(
        result_parts,
        *expand_w,
        reduce_w,
        gate,
        upper,
        cotangent,
        branch,
        branch_stats,
        post_gain,
        reduce_up,
        jnp.concatenate(expand_up),
        expand_inner,
    )
    d_query, d_key, d_value, q_sums, k_sums, d_attn_inner = attend_back(
        query, branch_parts, attn_w, attn_up, mixed, probs, key, value
    )
    partials = jnp.concatenate(
        [dot_of(attn_low, mixed, 1, 1), reduce_inner, d_expand_inner]
    ).astype(BF)
    input_grad, every_row, every_col = input_call(
        raw,
        d_query,
        d_key,
        d_value,
        act,
        mixed,
        branch_parts[0],
        hidden_parts[0],
        result_parts[0],
        qkv_w,
        d_hidden,
        tokens,
        scale,
        q_sums,
        k_sums,
        gains,
        cosine,
        sine,
        qkv_inner,
        diagonal_up,
        partials,
        jnp.concatenate([d_attn_inner, d_reduce_inner]),
        g_expand_up,
    )

    place_of = jnp.arange(2 * cols, dtype=jnp.int32)
    row_place = (pair ^ (place_of % 2)) * cols + (col - place_of // 2 + cols) % cols
    col_place = (pair ^ (place_of // cols)) * cols + place_of % cols
    places = jnp.concatenate([row_place, col_place])
    chosen = places[:, None] == jnp.arange(2 * cols, dtype=jnp.int32)[None, :]
    ids = jnp.sum(jnp.where(chosen, adapter_set[None, :], 0), axis=1)
    ids = jnp.concatenate([ids, me.reshape(1)])
    qkv_low, qkv_up, attn_low, attn_up, expand_low, expand_up, reduce_low, reduce_up = finish_call(
        ids, every_row, every_col, sub, ff_sub
    )
    return (
        layer_out,
        input_grad,
        qkv_low.transpose(0, 1, 3, 2),
        qkv_up,
        attn_low.transpose(0, 2, 1),
        attn_up,
        expand_low.transpose(0, 1, 3, 2),
        expand_up,
        reduce_low.transpose(0, 2, 1),
        reduce_up,
    )


def shards(*arrays):
    whole = (
        lax.axis_size("dp") == 2
        and lax.axis_size("row") == 4
        and arrays[0].shape[0] == SEQUENCE_LENGTH
    )
    return group_shards(*arrays) if whole else general_shards(*arrays)


def solution(mesh):
    placed = (
        P(("dp", "col"), "row"),
        P(("dp", "col"), "row"),
        P(None, "row", "col"),
        P("col", "row"),
        P(None, "row", "col"),
        P("col", "row"),
        P(None, "col"),
        P(None, "row"),
        P(None, None, "row", None),
        P(None, None, None, "col"),
        P(None, "col", None),
        P(None, None, "row"),
        P(None, None, "row", None),
        P(None, None, None, "col"),
        P(None, "col", None),
        P(None, None, "row"),
        P(),
        P(),
    )
    return jax.shard_map(
        shards,
        mesh=mesh,
        in_specs=placed,
        out_specs=(
            P(("dp", "col"), "row"),
            P(("dp", "col"), "row"),
            P(None, None, "row", None),
            P(None, None, None, "col"),
            P(None, "col", None),
            P(None, None, "row"),
            P(None, None, "row", None),
            P(None, None, None, "col"),
            P(None, "col", None),
            P(None, None, "row"),
        ),
        check_vma=False,
    )
```

```python
import functools

import jax
import jax.numpy as jnp
from jax import lax
from jax.experimental import pallas as pl
from jax.experimental.pallas import tpu as pltpu
from jax.sharding import PartitionSpec as P

D = 2048
HEAD = 128
ADAPTER_RANK = 16
SETS = 8
SEQUENCE_LENGTH = 2048


EPS = 1e-06
THETA = 500000.0
ADAPTER_FACTOR = 0.5
NEG = -1e30


def via_col_row(input_rows, weight_matrix, adapt_mat, compute, seq_pick):
    gathered = lax.all_gather(input_rows, "col", axis=0, tiled=True)
    main, inner_value = compute(gathered, weight_matrix, adapt_mat, seq_pick, False)
    return (
        lax.psum_scatter(main, "row", scatter_dimension=0, tiled=True),
        lax.psum_scatter(inner_value, "row", scatter_dimension=0, tiled=True),
    )


def via_row_col(input_rows, weight_matrix, adapt_mat, compute, seq_pick):
    gathered = lax.all_gather(input_rows, "row", axis=0, tiled=True)
    main, inner_value = compute(gathered, weight_matrix, adapt_mat, seq_pick, False)
    return (
        lax.psum_scatter(main, "col", scatter_dimension=0, tiled=True),
        lax.psum_scatter(inner_value, "col", scatter_dimension=0, tiled=True),
    )


def row_total(values):
    return lax.psum(jnp.sum(values, axis=-1), "row")


def head_totals(first, second):
    return lax.psum((jnp.sum(first, axis=-1), jnp.sum(second, axis=-1)), "col")


def sum_col_tokens(values):
    return lax.psum(values.astype(jnp.bfloat16), ("dp", "col")).astype(jnp.float32)


def sum_row_tokens(values):
    return lax.psum(values.astype(jnp.bfloat16), ("dp", "row")).astype(jnp.float32)


def set_rows(group_sets, first_row, item_count):
    sequence = (first_row + jnp.arange(item_count, dtype=jnp.int32)) // SEQUENCE_LENGTH
    member = sequence[:, None] == jnp.arange(group_sets.shape[0], dtype=jnp.int32)[None, :]
    chosen = jnp.sum(jnp.where(member, group_sets[None, :], 0), axis=1)
    return (chosen[:, None] == jnp.arange(SETS, dtype=jnp.int32)[None, :]).astype(jnp.bfloat16)


def widen(inner_value, onehot, part_list):
    rows = inner_value.shape[0]
    spread = onehot[:, None, :, None] * inner_value.reshape(rows, part_list, 1, ADAPTER_RANK)
    return spread.reshape(rows, part_list, SETS * ADAPTER_RANK)


def adapter_in(gathered, pick, lowrank):
    part_list = lowrank.shape[0]
    width_in = lowrank.shape[2]
    item_count = pick.shape[0]
    chosen = jnp.einsum("sk,pkdr->sdpr", pick, lowrank, preferred_element_type=jnp.float32).astype(
        jnp.bfloat16
    )
    chosen = chosen.reshape(item_count, width_in, part_list * ADAPTER_RANK)
    product_value = jnp.einsum(
        "ehm,emx->ehx",
        gathered.reshape(item_count, SEQUENCE_LENGTH, width_in),
        chosen,
        preferred_element_type=jnp.float32,
    )
    return product_value.reshape(item_count * SEQUENCE_LENGTH, part_list * ADAPTER_RANK)


def adapter_back(gathered, pick, upward_rank):
    part_list = upward_rank.shape[0]
    width_out = upward_rank.shape[-1]
    item_count = pick.shape[0]
    chosen = jnp.einsum(
        "sk,pkre->sper", pick, upward_rank, preferred_element_type=jnp.float32
    ).astype(jnp.bfloat16)
    product_value = jnp.einsum(
        "slpe,sper->slpr",
        gathered.reshape(item_count, SEQUENCE_LENGTH, part_list, width_out),
        chosen,
        preferred_element_type=jnp.float32,
    )
    return ADAPTER_FACTOR * product_value.reshape(
        item_count * SEQUENCE_LENGTH, part_list * ADAPTER_RANK
    )


def adapter_out(wide_output, upward_rank):
    part_list = upward_rank.shape[0]
    flat_up = upward_rank.reshape(part_list, SETS * ADAPTER_RANK, upward_rank.shape[-1])
    return ADAPTER_FACTOR * jnp.einsum(
        "tpk,pke->tpe", wide_output, flat_up, preferred_element_type=jnp.float32
    )


def adapter_grad_in(wide_output, lowrank):
    part_list = lowrank.shape[0]
    width_in = lowrank.shape[2]
    flat_low = lowrank.transpose(0, 1, 3, 2).reshape(part_list, SETS * ADAPTER_RANK, width_in)
    return jnp.einsum("tpk,pkd->td", wide_output, flat_low, preferred_element_type=jnp.float32)


def up_grad(wide_output, gradient_list):
    part_list = gradient_list.shape[1]
    total_sum = ADAPTER_FACTOR * jnp.einsum(
        "jox,joq->oxq", wide_output, gradient_list, preferred_element_type=jnp.float32
    )
    return total_sum.reshape(part_list, SETS, ADAPTER_RANK, gradient_list.shape[2])


def low_grad(input_rows, wide_output):
    part_list = wide_output.shape[1]
    total_sum = jnp.einsum(
        "td,tpk->pkd", input_rows, wide_output, preferred_element_type=jnp.float32
    )
    return total_sum.reshape(part_list, SETS, ADAPTER_RANK, input_rows.shape[1]).transpose(
        0, 1, 3, 2
    )


def swiglu(gate, upper):
    return jax.nn.silu(gate) * upper


def norm_back(grad, values, scale, gain):
    weighted = gain * grad
    inner_sum = row_total(weighted * values)
    return scale[:, None] * weighted - values * (scale**3 * inner_sum / D)[:, None]


def qkv_forward(gathered, weight_matrix, low_flat, pick, per_row):
    input_rows = gathered[:, 0]
    main = jnp.einsum("td,pde->tpe", input_rows, weight_matrix, preferred_element_type=jnp.float32)
    lowrank = low_flat.reshape(3, SETS, low_flat.shape[1], ADAPTER_RANK)
    return (main, adapter_in(input_rows, pick, lowrank))


def expand_forward(gathered, weight_matrix, low_flat, pick, per_row):
    input_rows = gathered[:, 0]
    main = jnp.einsum("td,pdf->tpf", input_rows, weight_matrix, preferred_element_type=jnp.float32)
    lowrank = low_flat.reshape(2, SETS, low_flat.shape[1], ADAPTER_RANK)
    return (main, adapter_in(input_rows, pick, lowrank))


def single_forward(gathered, weight_matrix, low_four, pick, per_row):
    input_rows = gathered[:, 0]
    main = jnp.dot(input_rows, weight_matrix[0, 0], preferred_element_type=jnp.float32)
    return (main, adapter_in(input_rows, pick, low_four))


def single_backward(gathered, weight_matrix, up_flat, pick, per_row):
    main = jnp.einsum(
        "te,fe->tf", gathered[:, 0], weight_matrix, preferred_element_type=jnp.float32
    )
    upward_rank = up_flat.reshape(1, SETS, ADAPTER_RANK, up_flat.shape[1])
    return (main, adapter_back(gathered, pick, upward_rank))


def multi_backward(gathered, weight_matrix, up_flat, pick, per_row):
    part_list = weight_matrix.shape[0]
    main = jnp.einsum("tpf,pdf->td", gathered, weight_matrix, preferred_element_type=jnp.float32)
    upward_rank = up_flat.reshape(part_list, SETS, ADAPTER_RANK, up_flat.shape[2])
    return (main, adapter_back(gathered, pick, upward_rank))


def general_shards(
    tokens,
    cotangent,
    qkv_weight,
    attn_weight,
    expand_weight,
    reduce_weight,
    headnorm_gain,
    post_gain,
    qkv_lowrank,
    qkv_uprank,
    attn_lowrank,
    attn_uprank,
    expand_lowrank,
    expand_uprank,
    reduce_lowrank,
    reduce_uprank,
    prefix_length,
    adapter_set,
):
    rows_a = tokens.shape[0]
    group_rows = rows_a * lax.axis_size("col")
    rows_b = group_rows // lax.axis_size("row")
    group_seqs = group_rows // SEQUENCE_LENGTH
    group_first = lax.axis_index("dp") * group_seqs
    group_sets = lax.dynamic_slice_in_dim(adapter_set, group_first, group_seqs)
    group_prefix = lax.dynamic_slice_in_dim(prefix_length, group_first, group_seqs)
    seq_pick = (group_sets[:, None] == jnp.arange(SETS, dtype=jnp.int32)[None, :]).astype(
        jnp.bfloat16
    )
    pick_a = set_rows(group_sets, lax.axis_index("col") * rows_a, rows_a)
    pick_b = set_rows(group_sets, lax.axis_index("row") * rows_b, rows_b)
    width_row = qkv_weight.shape[1]
    width_col = qkv_weight.shape[2]
    ff_col = expand_weight.shape[2]
    qkv_low_flat = qkv_lowrank.reshape(3 * SETS, width_row, ADAPTER_RANK)
    projected, inner_value = via_col_row(
        tokens[:, None], qkv_weight, qkv_low_flat, qkv_forward, seq_pick
    )
    qkv_wide = widen(inner_value.astype(jnp.bfloat16), pick_b, 3)
    projected = projected + adapter_out(qkv_wide, qkv_uprank)
    queries = projected[:, 0]
    keys = projected[:, 1]
    values = projected[:, 2]
    query_sq, key_sq = head_totals(queries * queries, keys * keys)
    query_scale = lax.rsqrt(query_sq / D + EPS)
    key_scale = lax.rsqrt(key_sq / D + EPS)
    query_norm = queries * query_scale[:, None] * headnorm_gain[0]
    key_norm = keys * key_scale[:, None] * headnorm_gain[1]
    local_heads = queries.shape[1] // HEAD
    half = HEAD // 2
    freq = THETA ** (-2.0 * jnp.arange(half, dtype=jnp.float32) / HEAD)
    position = (jnp.arange(rows_b, dtype=jnp.int32) % SEQUENCE_LENGTH).astype(jnp.float32)
    angle = position[:, None] * freq[None, :]
    cosine = jnp.cos(angle)[:, None, :]
    sine = jnp.sin(angle)[:, None, :]

    def rotate(source):
        heads = source.reshape(rows_b, local_heads, HEAD)
        first = heads[..., :half]
        second = heads[..., half:]
        return jnp.concatenate(
            [first * cosine - second * sine, second * cosine + first * sine], axis=-1
        )

    def unrotate(gradient_list):
        first = gradient_list[..., :half]
        second = gradient_list[..., half:]
        return jnp.concatenate(
            [first * cosine + second * sine, second * cosine - first * sine], axis=-1
        ).reshape(rows_b, local_heads * HEAD)

    query_b = rotate(query_norm).astype(jnp.bfloat16)
    key_b = rotate(key_norm).astype(jnp.bfloat16)
    value_b = values.astype(jnp.bfloat16).reshape(rows_b, local_heads, HEAD)
    block = min(512, SEQUENCE_LENGTH)
    blocks = rows_b // block
    key_pos = jnp.arange(SEQUENCE_LENGTH, dtype=jnp.int32)
    local_first = lax.axis_index("row") * (rows_b // SEQUENCE_LENGTH)
    scale = HEAD ** (-0.5)

    def scores_of(index):
        start = index * block
        seq_start = start // SEQUENCE_LENGTH * SEQUENCE_LENGTH
        which = local_first + start // SEQUENCE_LENGTH
        prefix = jnp.sum(
            jnp.where(jnp.arange(group_seqs, dtype=jnp.int32) == which, group_prefix, 0)
        )
        rows = start - seq_start + jnp.arange(block, dtype=jnp.int32)
        allowed = (key_pos[None, :] <= rows[:, None]) | (key_pos[None, :] < prefix)
        query_blk = lax.dynamic_slice_in_dim(query_b, start, block, 0)
        raw = (
            jnp.einsum("qhd,khd->hqk", query_blk, key_b, preferred_element_type=jnp.float32) * scale
        )
        return (jnp.where(allowed[None], raw, NEG), start, seq_start)

    def attend_block(index):
        scores, start, seq_start = scores_of(index)
        top = jnp.max(scores, axis=-1, keepdims=True)
        powers = jnp.exp(scores - top)
        total_sum = jnp.sum(powers, axis=-1, keepdims=True)
        weights = (powers / total_sum).astype(jnp.bfloat16)
        output = jnp.einsum("hqk,khd->qhd", weights, value_b, preferred_element_type=jnp.float32)
        return (output, (top + jnp.log(total_sum))[..., 0])

    attended, logsum = lax.map(attend_block, jnp.arange(blocks, dtype=jnp.int32))
    mixed_b = attended.reshape(rows_b, local_heads * HEAD).astype(jnp.bfloat16)
    attn_weight_four = attn_weight.reshape(1, 1, width_col, width_row)
    attn_low_four = attn_lowrank.reshape(1, SETS, width_col, ADAPTER_RANK)
    branch, inner_value = via_row_col(
        mixed_b[:, None], attn_weight_four, attn_low_four, single_forward, seq_pick
    )
    attn_wide = widen(inner_value.astype(jnp.bfloat16), pick_a, 1)
    branch = branch + adapter_out(attn_wide, attn_uprank[None])[:, 0]
    branch_scale = lax.rsqrt(row_total(branch * branch) / D + EPS)
    hidden = tokens.astype(jnp.float32) + post_gain[0] * branch * branch_scale[:, None]
    hidden_b = hidden.astype(jnp.bfloat16)
    expand_low_flat = expand_lowrank.reshape(2 * SETS, width_row, ADAPTER_RANK)
    gate_up, inner_value = via_col_row(
        hidden_b[:, None], expand_weight, expand_low_flat, expand_forward, seq_pick
    )
    expand_wide = widen(inner_value.astype(jnp.bfloat16), pick_b, 2)
    gate_up = gate_up + adapter_out(expand_wide, expand_uprank)
    gate = gate_up[:, 0]
    upper = gate_up[:, 1]
    act_b = swiglu(gate, upper).astype(jnp.bfloat16)
    reduce_weight_four = reduce_weight.reshape(1, 1, ff_col, width_row)
    reduce_low_four = reduce_lowrank.reshape(1, SETS, ff_col, ADAPTER_RANK)
    result, inner_value = via_row_col(
        act_b[:, None], reduce_weight_four, reduce_low_four, single_forward, seq_pick
    )
    reduce_wide = widen(inner_value.astype(jnp.bfloat16), pick_a, 1)
    result = result + adapter_out(reduce_wide, reduce_uprank[None])[:, 0]
    result_scale = lax.rsqrt(row_total(result * result) / D + EPS)
    layer_out = (hidden + post_gain[1] * result * result_scale[:, None]).astype(jnp.bfloat16)
    incoming = cotangent.astype(jnp.float32)
    d_result = norm_back(incoming, result, result_scale, post_gain[1]).astype(jnp.bfloat16)
    grad_reduce_up = up_grad(reduce_wide, d_result[:, None])[0]
    grad_reduce_up = sum_col_tokens(grad_reduce_up)
    reduce_up_flat = reduce_uprank.reshape(SETS * ADAPTER_RANK, width_row)
    d_act, inner_value = via_col_row(
        d_result[:, None], reduce_weight, reduce_up_flat, single_backward, seq_pick
    )
    act_wide = widen(inner_value.astype(jnp.bfloat16), pick_b, 1)
    d_act = d_act + adapter_grad_in(act_wide, reduce_lowrank[None])
    grad_reduce_low = low_grad(act_b, act_wide)[0]
    grad_reduce_low = sum_row_tokens(grad_reduce_low)
    unused, pullback = jax.vjp(swiglu, gate, upper)
    d_gate, d_upper = pullback(d_act)
    d_gate_up = jnp.stack([d_gate, d_upper], axis=1).astype(jnp.bfloat16)
    grad_expand_up = up_grad(expand_wide, d_gate_up)
    grad_expand_up = sum_row_tokens(grad_expand_up)
    expand_up_flat = expand_uprank.reshape(2 * SETS, ADAPTER_RANK, ff_col)
    d_hidden_in, inner_value = via_row_col(
        d_gate_up, expand_weight, expand_up_flat, multi_backward, seq_pick
    )
    hidden_wide = widen(inner_value.astype(jnp.bfloat16), pick_a, 2)
    d_hidden = incoming + d_hidden_in + adapter_grad_in(hidden_wide, expand_lowrank)
    grad_expand_low = low_grad(hidden_b, hidden_wide)
    grad_expand_low = sum_col_tokens(grad_expand_low)
    d_branch = norm_back(d_hidden, branch, branch_scale, post_gain[0]).astype(jnp.bfloat16)
    grad_attn_up = up_grad(attn_wide, d_branch[:, None])[0]
    grad_attn_up = sum_col_tokens(grad_attn_up)
    attn_up_flat = attn_uprank.reshape(SETS * ADAPTER_RANK, width_row)
    d_mixed, inner_value = via_col_row(
        d_branch[:, None], attn_weight, attn_up_flat, single_backward, seq_pick
    )
    mixed_wide = widen(inner_value.astype(jnp.bfloat16), pick_b, 1)
    d_mixed = (d_mixed + adapter_grad_in(mixed_wide, attn_lowrank[None])).astype(jnp.bfloat16)
    grad_attn_low = low_grad(mixed_b, mixed_wide)[0]
    grad_attn_low = sum_row_tokens(grad_attn_low)
    d_mixed_heads = d_mixed.reshape(rows_b, local_heads, HEAD)

    def back_block(index, carry):
        d_query, d_key, d_value = carry
        scores, start, seq_start = scores_of(index)
        probs = jnp.exp(
            scores - lax.dynamic_index_in_dim(logsum, index, 0, keepdims=False)[..., None]
        )
        grad_blk = lax.dynamic_slice_in_dim(d_mixed_heads, start, block, 0)
        query_blk = lax.dynamic_slice_in_dim(query_b, start, block, 0)
        d_probs = jnp.einsum("qhd,khd->hqk", grad_blk, value_b, preferred_element_type=jnp.float32)
        delta = jnp.sum(probs * d_probs, axis=-1, keepdims=True)
        d_scores = (probs * (d_probs - delta)).astype(jnp.bfloat16)
        query_part = scale * jnp.einsum(
            "hqk,khd->qhd", d_scores, key_b, preferred_element_type=jnp.float32
        )
        key_part = scale * jnp.einsum(
            "hqk,qhd->khd", d_scores, query_blk, preferred_element_type=jnp.float32
        )
        value_part = jnp.einsum(
            "hqk,qhd->khd", probs.astype(jnp.bfloat16), grad_blk, preferred_element_type=jnp.float32
        )
        d_query = lax.dynamic_update_slice_in_dim(d_query, query_part, start, 0)
        d_key = d_key + key_part
        d_value = d_value + value_part
        return (d_query, d_key, d_value)

    zeros = jnp.zeros((rows_b, local_heads, HEAD), jnp.float32)
    d_query, d_key, d_value = lax.fori_loop(0, blocks, back_block, (zeros, zeros, zeros))
    query_weighted = headnorm_gain[0] * unrotate(d_query)
    key_weighted = headnorm_gain[1] * unrotate(d_key)
    query_sum, key_sum = head_totals(query_weighted * queries, key_weighted * keys)
    d_queries = (
        query_scale[:, None] * query_weighted - queries * (query_scale**3 * query_sum / D)[:, None]
    )
    d_keys = key_scale[:, None] * key_weighted - keys * (key_scale**3 * key_sum / D)[:, None]
    d_qkv = jnp.stack(
        [d_queries, d_keys, d_value.reshape(rows_b, local_heads * HEAD)], axis=1
    ).astype(jnp.bfloat16)
    grad_qkv_up = up_grad(qkv_wide, d_qkv)
    grad_qkv_up = sum_row_tokens(grad_qkv_up)
    qkv_up_flat = qkv_uprank.reshape(3 * SETS, ADAPTER_RANK, width_col)
    d_tokens_in, inner_value = via_row_col(d_qkv, qkv_weight, qkv_up_flat, multi_backward, seq_pick)
    tokens_wide = widen(inner_value.astype(jnp.bfloat16), pick_a, 3)
    input_grad = d_hidden + d_tokens_in + adapter_grad_in(tokens_wide, qkv_lowrank)
    grad_qkv_low = low_grad(tokens, tokens_wide)
    grad_qkv_low = sum_col_tokens(grad_qkv_low)
    return (
        layer_out,
        input_grad,
        grad_qkv_low,
        grad_qkv_up,
        grad_attn_low,
        grad_attn_up,
        grad_expand_low,
        grad_expand_up,
        grad_reduce_low,
        grad_reduce_up,
    )


LOG2E = 1.4426950408889634
Q_BLOCK = 512
K_BLOCK = 512
BF = jnp.bfloat16
F32 = jnp.float32
VMEM_SPEC = pl.BlockSpec(memory_space=pltpu.VMEM)
ANY_SPEC = pl.BlockSpec(memory_space=pl.ANY)


def dot_of(left, right, left_dim, right_dim, out=F32):
    return lax.dot_general(
        left, right, (((left_dim,), (right_dim,)), ((), ())), preferred_element_type=out
    )


def attend_rows(query, limit, key_of, value_of, blocks):
    rows = query.shape[0]
    key_pos = lax.broadcasted_iota(jnp.int32, (K_BLOCK, rows), 0)

    def body(index, carry):
        top, total, mixed = carry
        at = pl.multiple_of(index * K_BLOCK, K_BLOCK)
        scores = dot_of(key_of(at), query, 1, 1) * (HEAD**-0.5 * LOG2E)
        scores = jnp.where(key_pos <= limit - at, scores, NEG)
        top_now = jnp.maximum(top, jnp.max(scores, axis=0, keepdims=True))
        fade = jnp.exp2(top - top_now)
        powers = jnp.exp2(scores - top_now)
        total = fade * total + jnp.sum(powers, axis=0, keepdims=True)
        mixed = mixed * fade + dot_of(value_of(at), powers.astype(BF), 0, 0)
        return top_now, total, mixed

    top, total, mixed = lax.fori_loop(
        0,
        blocks,
        body,
        (
            jnp.full((1, rows), NEG, F32),
            jnp.zeros((1, rows), F32),
            jnp.zeros((HEAD, rows), F32),
        ),
    )
    return mixed / total, top + jnp.log2(total)


def in_parts(values, count):
    parts = []
    for _ in range(count):
        part = values.astype(BF)
        parts.append(part)
        values = values - part.astype(F32)
    return parts


def row_sums(values):
    return sums_of(values)[0:1]


def attend_back_kernel(
    q_ref,
    x0,
    x1,
    x2,
    x3,
    matrix_ref,
    up_ref,
    out_ref,
    probs_hbm,
    k_ref,
    v_ref,
    dq_ref,
    dk_ref,
    dv_ref,
    q_sum_ref,
    k_sum_ref,
    inner_ref,
    grad_ref,
    probs_ref,
    sems,
):
    rows, local = q_ref.shape
    group = pl.program_id(0)
    heads = [slice(at, at + HEAD) for at in range(0, local, HEAD)]
    blocks = jnp.maximum((group + 1) * rows, SEQUENCE_LENGTH // 2) // K_BLOCK

    def fetch(index):
        slot = lax.rem(index, 2)
        return [
            pltpu.make_async_copy(
                probs_hbm.at[h, group, index], probs_ref.at[slot, h], sems.at[slot, h]
            )
            for h in range(len(heads))
        ]

    for copy in fetch(0):
        copy.start()
    left = jnp.concatenate([x0[...], x1[...], x2[...], x3[...]], axis=1)
    grad_ref[...] = dot_of(left, matrix_ref[...], 1, 1).astype(BF)
    inner_ref[...] = (ADAPTER_FACTOR * dot_of(up_ref[...], left, 1, 1)).astype(BF)

    @pl.when(group == 0)
    def _():
        dk_ref[...] = jnp.zeros_like(dk_ref)
        dv_ref[...] = jnp.zeros_like(dv_ref)

    deltas = [
        row_sums(grad_ref[:, lanes].astype(F32) * out_ref[:, lanes].astype(F32)) for lanes in heads
    ]

    def body(index, carry):
        at = pl.multiple_of(index * K_BLOCK, K_BLOCK)
        span = pl.ds(at, K_BLOCK)
        slot = lax.rem(index, 2)
        for copy in fetch(index):
            copy.wait()

        @pl.when(index + 1 < blocks)
        def _():
            for copy in fetch(index + 1):
                copy.start()

        sums = []
        for h, lanes in enumerate(heads):
            query, grad, key = q_ref[:, lanes], grad_ref[:, lanes], k_ref[span, lanes]
            probs = probs_ref[slot, h]
            d_probs = dot_of(v_ref[span, lanes], grad, 1, 1)
            d_scores = (probs.astype(F32) * (d_probs - deltas[h])).astype(BF)
            dv_ref[span, lanes] += dot_of(probs, grad, 1, 0)
            dk_ref[span, lanes] += dot_of(d_scores, query, 1, 0)
            sums.append(carry[h] + dot_of(d_scores, key, 0, 0))
        return tuple(sums)

    d_queries = lax.fori_loop(0, blocks, body, (jnp.zeros((rows, HEAD), F32),) * len(heads))
    for h, lanes in enumerate(heads):
        d_query = d_queries[h] * HEAD**-0.5
        dq_ref[:, lanes] = d_query
        q_sum_ref[h] = row_sums(d_query * q_ref[:, lanes].astype(F32))

    @pl.when(group == pl.num_programs(0) - 1)
    def _():
        for h, lanes in enumerate(heads):
            d_key = dk_ref[:, lanes] * HEAD**-0.5
            dk_ref[:, lanes] = d_key
            k_sum_ref[h] = row_sums(d_key * k_ref[:, lanes].astype(F32))


def attend_back(query, lefts, matrix, up, mixed, probs, key, value):
    rows, length, local = query.shape[0], key.shape[0], query.shape[1]
    heads = local // HEAD
    q_spec = pl.BlockSpec((Q_BLOCK, local), lambda i: (i, 0))
    x_spec = pl.BlockSpec((Q_BLOCK, lefts[0].shape[1]), lambda i: (i, 0))

    def whole(array):
        return pl.BlockSpec(array.shape, lambda i: (0,) * array.ndim)

    return pl.pallas_call(
        attend_back_kernel,
        out_shape=(
            jax.ShapeDtypeStruct(query.shape, F32),
            jax.ShapeDtypeStruct(key.shape, F32),
            jax.ShapeDtypeStruct(key.shape, F32),
            jax.ShapeDtypeStruct((heads, 1, rows), F32),
            jax.ShapeDtypeStruct((heads, 1, length), F32),
            jax.ShapeDtypeStruct((16, rows), BF),
        ),
        grid=(rows // Q_BLOCK,),
        in_specs=[q_spec]
        + [x_spec] * 4
        + [whole(matrix), whole(up), q_spec, ANY_SPEC, whole(key), whole(value)],
        out_specs=[
            q_spec,
            whole(key),
            whole(value),
            pl.BlockSpec((heads, 1, Q_BLOCK), lambda i: (0, 0, i)),
            pl.BlockSpec((heads, 1, length), lambda i: (0, 0, 0)),
            pl.BlockSpec((16, Q_BLOCK), lambda i: (0, i)),
        ],
        scratch_shapes=[
            pltpu.VMEM((Q_BLOCK, local), BF),
            pltpu.VMEM((2, heads, K_BLOCK, Q_BLOCK), BF),
            pltpu.SemaphoreType.DMA((2, heads)),
        ],
        cost_estimate=pl.CostEstimate(
            flops=7 * rows * length * heads * HEAD,
            bytes_accessed=24 * rows * heads * HEAD,
            transcendentals=0,
        ),
        name="attend_back",
    )(query, *lefts, matrix, up, mixed, probs, key, value)


def rotate_kernel(raw_ref, scale_ref, gain_ref, cos_ref, sin_ref, q_ref, k_ref, v_ref):
    width = q_ref.shape[1]
    cosine = cos_ref[...]
    sine = sin_ref[...]
    scales = scale_ref[...]
    for part, out in ((0, q_ref), (1, k_ref)):
        scale = column_of(scales, part)
        for at in range(0, width, HEAD):
            normed = raw_ref[:, part * width + at : part * width + at + HEAD] * scale
            normed = normed * gain_ref[part : part + 1, at : at + HEAD]
            turned = normed * cosine + pltpu.roll(normed, HEAD // 2, 1) * sine
            out[:, at : at + HEAD] = turned.astype(BF)
    v_ref[...] = raw_ref[:, 2 * width :].astype(BF)


def rotate_rows(raw, scales, gains, cosine, sine):
    rows, width = raw.shape[0], raw.shape[1] // 3
    step = min(512, rows)
    out_spec = pl.BlockSpec((step, width), lambda i: (i, 0))
    table = pl.BlockSpec((step, HEAD), lambda i: (i, 0))
    return pl.pallas_call(
        rotate_kernel,
        out_shape=(jax.ShapeDtypeStruct((rows, width), BF),) * 3,
        grid=(rows // step,),
        in_specs=[
            pl.BlockSpec((step, 3 * width), lambda i: (i, 0)),
            pl.BlockSpec((8, step), lambda i: (0, i)),
            pl.BlockSpec((2, width), lambda i: (0, 0)),
            table,
            table,
        ],
        out_specs=[out_spec] * 3,
        name="rotate_rows",
    )(raw, scales, gains, cosine, sine)


def row_pack_kernel(set_ref, qkv_ref, attn_ref, expand_ref, reduce_ref, out_ref):
    for part in range(3):
        out_ref[16 * part : 16 * part + 16, :] = qkv_ref[part, 0]
    out_ref[48:64, :] = attn_ref[0]
    for part in range(2):
        out_ref[64 + 16 * part : 80 + 16 * part, :] = expand_ref[part, 0]
    out_ref[96:112, :] = reduce_ref[0]


def row_pack_of(which, qkv_low, attn_up, expand_low, reduce_up):
    width = attn_up.shape[2]
    one = pl.BlockSpec((1, 16, width), lambda i, c: (c[0], 0, 0))

    def many(parts):
        return pl.BlockSpec((parts, 1, 16, width), lambda i, c: (0, c[0], 0, 0))

    return pl.pallas_call(
        row_pack_kernel,
        out_shape=jax.ShapeDtypeStruct((112, width), BF),
        grid_spec=pltpu.PrefetchScalarGridSpec(
            num_scalar_prefetch=1,
            grid=(1,),
            in_specs=[many(3), one, many(2), one],
            out_specs=pl.BlockSpec((112, width), lambda i, c: (0, 0)),
        ),
        name="row_pack",
    )(which, qkv_low, attn_up, expand_low, reduce_up)


def col_pack_kernel(set_ref, qkv_ref, attn_ref, expand_ref, reduce_ref, out_ref):
    sub, ff_sub = qkv_ref.shape[3], expand_ref.shape[3]
    for part in range(3):
        out_ref[0, :, part * sub : (part + 1) * sub] = qkv_ref[part, 0]
    at = 4 * sub
    out_ref[0, :, 3 * sub : at] = attn_ref[0]
    for part in range(2):
        out_ref[0, :, at : at + ff_sub] = expand_ref[part, 0]
        at += ff_sub
    out_ref[0, :, at:] = reduce_ref[0]


def col_pack_of(which, qkv_up, attn_low, expand_up, reduce_low):
    cols = which.shape[0] - 1
    sub, ff_sub = qkv_up.shape[3] // 4, expand_up.shape[3] // 4

    def many(parts, size):
        return pl.BlockSpec((parts, 1, 16, size), lambda i, c: (0, c[i], 0, c[cols]))

    def one(size):
        return pl.BlockSpec((1, 16, size), lambda i, c: (c[i], 0, c[cols]))

    total = 4 * sub + 3 * ff_sub
    return pl.pallas_call(
        col_pack_kernel,
        out_shape=jax.ShapeDtypeStruct((cols, 16, total), BF),
        grid_spec=pltpu.PrefetchScalarGridSpec(
            num_scalar_prefetch=1,
            grid=(cols,),
            in_specs=[many(3, sub), one(sub), many(2, ff_sub), one(ff_sub)],
            out_specs=pl.BlockSpec((1, 16, total), lambda i, c: (i, 0, 0)),
        ),
        name="col_pack",
    )(which, qkv_up, attn_low, expand_up, reduce_low)


def finish_kernel(ids_ref, rows_ref, cols_ref, *outs):
    qkv_low, qkv_up, attn_low, attn_up, expand_low, expand_up, reduce_low, reduce_up = outs
    cols = cols_ref.shape[2]
    groups = 2 * cols
    step = pl.program_id(0)
    me = ids_ref[2 * groups]
    sub = qkv_up.shape[3] // 4
    ff_sub = expand_up.shape[3] // 4

    @pl.when(step == 0)
    def _():
        for out in outs:
            out[...] = jnp.zeros_like(out)

    here = ids_ref[step]
    term = rows_ref[step // 2, lax.rem(step, 2)].astype(F32)
    for part in range(3):
        qkv_low[part, here] += term[16 * part : 16 * part + 16]
    attn_up[here] += term[48:64]
    for part in range(2):
        expand_low[part, here] += term[64 + 16 * part : 80 + 16 * part]
    reduce_up[here] += term[96:112]
    here = ids_ref[groups + step]
    for row in range(4):
        term = cols_ref[me ^ row, step // cols, lax.rem(step, cols)].astype(F32)
        near = slice(row * sub, (row + 1) * sub)
        wide = slice(row * ff_sub, (row + 1) * ff_sub)
        for part in range(3):
            qkv_up[part, here, :, near] += term[:, part * sub : (part + 1) * sub]
        attn_low[here, :, near] += term[:, 3 * sub : 4 * sub]
        for part in range(2):
            at = 4 * sub + part * ff_sub
            expand_up[part, here, :, wide] += term[:, at : at + ff_sub]
        reduce_low[here, :, wide] += term[:, 4 * sub + 2 * ff_sub :]


def finish_call(ids, rows, cols, sub, ff_sub):
    width = rows.shape[3]
    shapes = [
        (3, width),
        (3, 4 * sub),
        (0, 4 * sub),
        (0, width),
        (2, width),
        (2, 4 * ff_sub),
        (0, 4 * ff_sub),
        (0, width),
    ]
    out_shape, out_specs = [], []
    for parts, size in shapes:
        if parts:
            out_shape.append(jax.ShapeDtypeStruct((parts, SETS, 16, size), F32))
            out_specs.append(pl.BlockSpec((parts, SETS, 16, size), lambda k, c: (0, 0, 0, 0)))
        else:
            out_shape.append(jax.ShapeDtypeStruct((SETS, 16, size), F32))
            out_specs.append(pl.BlockSpec((SETS, 16, size), lambda k, c: (0, 0, 0)))

    def whole(array):
        return pl.BlockSpec(array.shape, lambda k, c: (0,) * array.ndim)

    return pl.pallas_call(
        finish_kernel,
        out_shape=out_shape,
        grid_spec=pltpu.PrefetchScalarGridSpec(
            num_scalar_prefetch=1,
            grid=(2 * cols.shape[2],),
            in_specs=[whole(rows), whole(cols)],
            out_specs=out_specs,
        ),
        name="finish",
    )(ids, rows, cols)


def cost_of(flops, bytes_accessed):
    return pl.CostEstimate(flops=int(flops), bytes_accessed=int(bytes_accessed), transcendentals=0)


def row_tile(rows):
    return min(512, rows)


def merge_rows_kernel(pair_ref, own_ref, other_ref, low_ref, up_ref, out_ref):
    def put(piece):
        for block in range(4):
            base = piece[0, block].astype(F32)
            extra = dot_of(low_ref[block, 0], up_ref[...], 0, 0)
            out_ref[block, 0] = (base + ADAPTER_FACTOR * extra).astype(BF)

    mine = pl.program_id(0) == pair_ref[0]
    pl.when(mine)(functools.partial(put, own_ref))
    pl.when(jnp.logical_not(mine))(functools.partial(put, other_ref))


def merge_qkv_kernel(pair_ref, own_ref, other_ref, low_ref, up_ref, out_ref):
    cols, sub = own_ref.shape[0], own_ref.shape[4]

    def put(piece, back):
        for block in range(4):
            extra = dot_of(low_ref[block, 0], up_ref[...], 0, 0)
            for index in range(cols):
                at = lax.rem(index - back + cols, cols)
                lanes = slice(index * sub, (index + 1) * sub)
                base = piece[at, block, 0].astype(F32)
                out_ref[block, 0, :, lanes] = (base + ADAPTER_FACTOR * extra[:, lanes]).astype(BF)

    mine = pl.program_id(0) == pair_ref[0]
    pl.when(mine)(functools.partial(put, own_ref, 0))
    pl.when(jnp.logical_not(mine))(functools.partial(put, other_ref, pair_ref[1]))


def merge_columns_kernel(pair_ref, *refs):
    *pieces, low_ref, up_ref, out_ref = refs
    width = out_ref.shape[1] // 4

    def put(piece):
        for block in range(4):
            span = slice(block * width, (block + 1) * width)
            extra = dot_of(low_ref[0], up_ref[:, span], 0, 0)
            out_ref[:, span] = (piece[0, block].astype(F32) + ADAPTER_FACTOR * extra).astype(BF)

    if len(pieces) == 1:
        put(pieces[0])
        return
    mine = pl.program_id(0) == pair_ref[0]
    pl.when(mine)(functools.partial(put, pieces[0]))
    pl.when(jnp.logical_not(mine))(functools.partial(put, pieces[1]))


def merge_qkv(pair, own, other, low, up):
    cols, _, parts, cut, sub = own.shape

    def piece(half):
        def place(h, p, pair_ref):
            mine = h == half(pair_ref[0])
            return (0, 0, jnp.where(mine, p, jnp.where(h == 0, 0, parts - 1)), 0, 0)

        return pl.BlockSpec((cols, 4, 1, cut, sub), place)

    whole = pl.pallas_call(
        merge_qkv_kernel,
        out_shape=jax.ShapeDtypeStruct((4, 2, cut, parts * cols * sub), BF),
        grid_spec=pltpu.PrefetchScalarGridSpec(
            num_scalar_prefetch=1,
            grid=(2, parts),
            in_specs=[
                piece(lambda one: one),
                piece(lambda one: 1 - one),
                pl.BlockSpec((4, 1, 16, cut), lambda h, p, one: (0, h, p, 0)),
                pl.BlockSpec((16, cols * sub), lambda h, p, one: (p, 0)),
            ],
            out_specs=pl.BlockSpec((4, 1, cut, cols * sub), lambda h, p, one: (0, h, 0, p)),
        ),
        cost_estimate=cost_of(0, 8 * own.size),
        name="merge_qkv",
    )(pair, own, other, low.reshape(16 * parts, 4, 2, cut).transpose(1, 2, 0, 3), up)
    return whole.reshape(8 * cut, parts * cols * sub)


def half_specs(block, cols):
    def piece(half, relative):
        def place(h, c, pair_ref):
            at = jnp.where(h == half(pair_ref[0]), c, jnp.where(h == 0, 0, cols - 1))
            if relative:
                at = lax.rem(at - pair_ref[1] + cols, cols)
            return (at,) + (0,) * (len(block) - 1)

        return pl.BlockSpec(block, place)

    return [piece(lambda one: one, False), piece(lambda one: 1 - one, True)]


def merge_expand(pair, own, other, low, up):
    cols, _, width, cut = own.shape
    whole = pl.pallas_call(
        merge_rows_kernel,
        out_shape=jax.ShapeDtypeStruct((4, 1, width, 2 * cols * cut), BF),
        grid_spec=pltpu.PrefetchScalarGridSpec(
            num_scalar_prefetch=1,
            grid=(2, cols),
            in_specs=half_specs((1, 4, width, cut), cols)
            + [
                pl.BlockSpec((4, 1, 16, width), lambda h, c, one: (0, 0, 0, 0)),
                pl.BlockSpec((16, cut), lambda h, c, one: (0, 2 * c + h)),
            ],
            out_specs=pl.BlockSpec((4, 1, width, cut), lambda h, c, one: (0, 0, 0, 2 * c + h)),
        ),
        cost_estimate=cost_of(0, 8 * own.size),
        name="merge_expand",
    )(pair, own, other, low.reshape(16, 4, 1, width).transpose(1, 2, 0, 3), up)
    return whole.reshape(4 * width, 2 * cols * cut)


def merge_out(pair, pieces, low, up):
    cols, _, rows, width = pieces[0].shape
    takes = len(pieces)
    block = (1, 4, rows, width)
    specs = half_specs(block, cols)
    if takes == 1:
        specs = [pl.BlockSpec(block, lambda h, c, one: (c, 0, 0, 0))]
    return pl.pallas_call(
        merge_columns_kernel,
        out_shape=jax.ShapeDtypeStruct((takes * cols * rows, 4 * width), BF),
        grid_spec=pltpu.PrefetchScalarGridSpec(
            num_scalar_prefetch=1,
            grid=(takes, cols),
            in_specs=specs
            + [
                pl.BlockSpec((1, 16, rows), lambda h, c, one: (takes * c + h, 0, 0)),
                pl.BlockSpec((16, 4 * width), lambda h, c, one: (0, 0)),
            ],
            out_specs=pl.BlockSpec((rows, 4 * width), lambda h, c, one: (takes * c + h, 0)),
        ),
        cost_estimate=cost_of(0, 4 * takes * pieces[0].size),
        name="merge_out",
    )(pair, *pieces, low.reshape(16, takes * cols, rows).transpose(1, 0, 2), up)


BLOCK = 256
RING = 5


def peer(step):
    return {"row": lax.axis_index("row") ^ step}


def send(source, target, sems, index, step):
    return pltpu.make_async_remote_copy(
        src_ref=source,
        dst_ref=target,
        send_sem=sems.at[0, index],
        recv_sem=sems.at[1, index],
        device_id=peer(step),
        device_id_type=pl.DeviceIdType.MESH,
    )


def greet():
    barrier = pltpu.get_barrier_semaphore()
    for step in (1, 2, 3):
        pl.semaphore_signal(
            barrier, inc=1, device_id=peer(step), device_id_type=pl.DeviceIdType.MESH
        )
    pl.semaphore_wait(barrier, 3)


def exchange_scratch(count, width, gathers):
    sem = pltpu.SemaphoreType.DMA((2, count))
    shapes = [
        pltpu.VMEM((2, 2, BLOCK, width), BF),
        pltpu.VMEM((count, 2, BLOCK, width), BF),
        pltpu.VMEM((2, BLOCK, width), F32),
        pltpu.VMEM((2, BLOCK, width), BF),
        pltpu.VMEM((count, BLOCK, width), BF),
        pltpu.VMEM((RING, BLOCK, width), F32),
        sem,
        sem,
    ]
    if gathers:
        shapes += [
            pltpu.VMEM((count, 8, BLOCK), F32),
            pltpu.VMEM((3, count, 8, BLOCK), F32),
        ] + [sem] * 6
    return shapes


def run_blocks(
    count,
    bufs,
    compute,
    stats,
    finish,
    own_ref=None,
    arrived=None,
    extra=None,
    own_rows=None,
    idle=None,
):
    pair_out, pair_in, far, side_out, side_in, near, pair_sem, side_sem, *rest = bufs
    gathers = own_ref is not None
    if gathers:
        stat_own, stat_in, stat_1, stat_2, stat_3, core_sem, far_sem, relay_sem = rest
        stat_sems = (stat_1, stat_2, stat_3)

    def rows_of(c):
        return pl.ds(pl.multiple_of(c * BLOCK, BLOCK), BLOCK)

    def to_core(c):
        return send(pair_out.at[lax.rem(c, 2)], pair_in.at[c], pair_sem, c, 1)

    def to_side(c):
        return send(side_out.at[lax.rem(c, 2)], side_in.at[c], side_sem, c, 2)

    def to_stat(c, step):
        return send(stat_own.at[c], stat_in.at[step - 1, c], stat_sems[step - 1], c, step)

    def gather_core(c):
        return send(own_ref.at[rows_of(c)], arrived[0].at[rows_of(c)], core_sem, c, 1)

    def gather_side(c):
        return send(own_ref.at[rows_of(c)], arrived[1].at[rows_of(c)], far_sem, c, 2)

    def relay(c):
        return send(arrived[1].at[rows_of(c)], arrived[2].at[rows_of(c)], relay_sem, c, 1)

    def stage(c, body):
        pl.when(jnp.logical_and(c >= 0, c < count))(functools.partial(body, c))

    def multiply(c):
        @pl.when(c >= 2)
        def _():
            to_core(c - 2).wait_send()

        slot = lax.rem(c, 2)

        def put(block, value):
            if block == 0:
                near[lax.rem(c, RING)] = value
            elif block == 2:
                far[slot] = value
            else:
                pair_out[slot, block // 2] = value.astype(BF)
            if block == 3:
                to_core(c).start()

        compute(c, put)

    def sum_core(c):
        @pl.when(c >= 2)
        def _():
            to_side(c - 2).wait_send()

        to_core(c).wait_recv()
        slot = lax.rem(c, 2)
        side_out[slot] = (far[slot] + pair_in[c, 1].astype(F32)).astype(BF)
        to_side(c).start()
        at = lax.rem(c, RING)
        near[at] = near[at] + pair_in[c, 0].astype(F32)
        if extra is not None:
            extra[0](c)

    def sum_side(c):
        if extra is not None:
            extra[1](c)
        to_side(c).wait_recv()
        at = lax.rem(c, RING)
        total = near[at] + side_in[c].astype(F32)
        if not gathers:
            finish(c, rows_of(c), total)
            return
        near[at] = total
        stat_own[c] = stats(c, rows_of(c), total)
        for step in (1, 2, 3):
            to_stat(c, step).start()

    def normalise(c):
        total = stat_own[c]
        for step in (1, 2, 3):
            to_stat(c, step).wait_recv()
            total = total + stat_in[step - 1, c]
        own_ref[rows_of(c), :] = finish(c, rows_of(c), near[lax.rem(c, RING)], total)
        gather_side(c).start()
        gather_core(c).start()
        if own_rows is not None:
            own_rows(c).start()

    def pass_on(c):
        gather_side(c).wait_recv()
        relay(c).start()

    def body(t, carry):
        stage(t - 1, sum_core)
        stage(t, multiply)
        stage(t - 2, sum_side)
        if gathers:
            stage(t - 3, normalise)
            stage(t - 4, pass_on)
        if idle is not None:
            pl.when(t >= 2)(lambda: idle(t - 2))
        return carry

    lax.fori_loop(0, count + (4 if gathers else 2), body, 0)

    def close(c, carry):
        if gathers:
            for step in (1, 2, 3):
                to_stat(c, step).wait_send()
            gather_core(c).wait()
            gather_side(c).wait_send()
            relay(c).wait()
        return carry

    if gathers:
        lax.fori_loop(0, count, close, 0)
    for c in range(max(count - 2, 0), count):
        to_core(c).wait_send()
        to_side(c).wait_send()


def sums_of(*values):
    out = None
    for index, value in enumerate(values):
        pick = lax.broadcasted_iota(jnp.int32, (8, value.shape[1]), 0) == index
        pick = pick.astype(F32).astype(BF)
        for part in in_parts(value, 2):
            term = dot_of(pick, part, 1, 1)
            out = term if out is None else out + term
    return out


def column_of(stats, index):
    parts = jnp.concatenate(in_parts(stats, 3), axis=0)
    pick = lax.rem(lax.broadcasted_iota(jnp.int32, (parts.shape[0], HEAD), 0), 8) == index
    return dot_of(parts, pick.astype(F32).astype(BF), 0, 0)[:, :1]


def branch_kernel(
    q_ref,
    k_ref,
    v_ref,
    limit_ref,
    matrix_ref,
    tokens_ref,
    gain_ref,
    gate_all,
    gate_other,
    upper_all,
    upper_other,
    mixed_ref,
    branch_ref,
    hidden_ref,
    stat_ref,
    own_ref,
    *rest,
):
    arrived, halves, probs_hbm, rest = rest[:3], rest[3:5], rest[5], rest[6:]
    swap_sems, stage, stage_sem, log_ref, *bufs = rest
    width = own_ref.shape[1]
    count = own_ref.shape[0] // BLOCK
    greet_all([peer(step) for step in (1, 2, 3)] + [other_of_pair()])
    cols = gate_all.shape[0]
    swaps = exchange_halves(gate_all, halves[0], swap_sems.at[0], range(2, cols))
    swaps += exchange_halves(upper_all, halves[1], swap_sems.at[1], range(1, cols))
    for copy in swaps:
        copy.start()

    heads = mixed_ref.shape[1] // HEAD
    key_pos = lax.broadcasted_iota(jnp.int32, (K_BLOCK, Q_BLOCK), 0)

    def blocks_of(group):
        return jnp.maximum((group + 1) * Q_BLOCK, SEQUENCE_LENGTH // 2) // K_BLOCK

    def attend(group):
        rows = span_of(group, Q_BLOCK)

        def head(h, carry):
            lanes = span_of(h, HEAD)
            mixed, logs = attend_rows(
                q_ref[rows, lanes],
                limit_ref[:, rows],
                lambda at: k_ref[pl.ds(at, K_BLOCK), lanes],
                lambda at: v_ref[pl.ds(at, K_BLOCK), lanes],
                blocks_of(group),
            )
            mixed_ref[rows, lanes] = mixed.T.astype(BF)
            log_ref[h, :, rows] = logs
            return carry

        lax.fori_loop(0, heads, head, 0)

    ratio = Q_BLOCK // BLOCK
    share = heads // ratio

    def keep_some(turn):
        group = turn // ratio
        rows = span_of(group, Q_BLOCK)
        blocks = blocks_of(group)
        first = lax.rem(turn, ratio) * share

        def head(h, carry):
            lanes = span_of(h, HEAD)

            def out(index):
                slot = lax.rem(index, 2)
                return pltpu.make_async_copy(
                    stage.at[slot], probs_hbm.at[h, group, index], stage_sem.at[slot]
                )

            def keep(index, carry):
                @pl.when(index >= 2)
                def _():
                    out(index - 2).wait()

                at = pl.multiple_of(index * K_BLOCK, K_BLOCK)
                scores = dot_of(k_ref[pl.ds(at, K_BLOCK), lanes], q_ref[rows, lanes], 1, 1)
                powers = jnp.exp2(scores * (HEAD**-0.5 * LOG2E) - log_ref[h, :, rows])
                seen = key_pos <= limit_ref[:, rows] - at
                stage[lax.rem(index, 2)] = jnp.where(seen, powers, 0.0).astype(BF)
                out(index).start()
                return carry

            lax.fori_loop(0, blocks, keep, 0)
            out(blocks - 2).wait()
            out(blocks - 1).wait()
            return carry

        lax.fori_loop(first, first + share, head, 0)

    def idle(turn):
        pl.when(turn < count)(lambda: keep_some(turn))

    def compute(c, put):
        pl.when(lax.rem(c, ratio) == 0)(lambda: attend(c // ratio))
        left = mixed_ref[pl.ds(pl.multiple_of(c * BLOCK, BLOCK), BLOCK), :]
        for block in (1, 3, 2, 0):
            put(block, dot_of(left, matrix_ref[:, block * width : (block + 1) * width], 1, 0))

    def stats(c, rows, branch):
        branch_ref[rows, :] = branch
        return sums_of(branch * branch)

    def finish(c, rows, branch, total):
        stat_ref[c] = total
        scale = lax.rsqrt(column_of(total, 0) / D + EPS)
        hidden = tokens_ref[rows, :].astype(F32) + gain_ref[0:1, :] * branch * scale
        hidden_ref[rows, :] = hidden
        return hidden.astype(BF)

    run_blocks(count, bufs, compute, stats, finish, own_ref, arrived, idle=idle)
    wait_all(swaps)


def talk_params(number):
    return pltpu.CompilerParams(
        collective_id=number, has_side_effects=True, vmem_limit_bytes=63 * 2**20
    )


def branch_call(query, key, value, limit, matrix, tokens, gain, halves):
    rows, width = tokens.shape
    local = query.shape[1]
    count = rows // BLOCK
    cols = halves[0].shape[0]
    part = jax.ShapeDtypeStruct((rows, width), BF)
    whole = jax.ShapeDtypeStruct((rows, width), F32)
    half = jax.ShapeDtypeStruct(halves[0].shape, BF)
    return pl.pallas_call(
        branch_kernel,
        out_shape=[
            jax.ShapeDtypeStruct((rows, local), BF),
            whole,
            whole,
            jax.ShapeDtypeStruct((count, 8, BLOCK), F32),
        ]
        + [part] * 4
        + [half] * 2
        + [
            jax.ShapeDtypeStruct(
                (local // HEAD, rows // Q_BLOCK, rows // K_BLOCK, K_BLOCK, Q_BLOCK), BF
            )
        ],
        in_specs=[VMEM_SPEC] * 7 + [ANY_SPEC] * 4,
        out_specs=[VMEM_SPEC] * 5 + [ANY_SPEC] * 6,
        scratch_shapes=[
            pltpu.SemaphoreType.DMA((2, 2, cols - 1)),
            pltpu.VMEM((2, K_BLOCK, Q_BLOCK), BF),
            pltpu.SemaphoreType.DMA((2,)),
            pltpu.VMEM((local // HEAD, 1, rows), F32),
        ]
        + exchange_scratch(count, width, True),
        input_output_aliases={8: 8, 10: 9},
        compiler_params=talk_params(0),
        cost_estimate=cost_of(8 * rows * width * matrix.shape[0], 2**27),
        name="branch",
    )(query, key, value, limit, matrix, tokens, gain, *halves)


def rows_out(buffer, outer, sems, index):
    def copy(c):
        rows = span_of(c, BLOCK)
        return pltpu.make_async_copy(buffer.at[rows], outer.at[rows], sems.at[index, c])

    return copy


def wait_rows(count, *copies):
    def body(c, carry):
        for copy in copies:
            copy(c).wait()
        return carry

    lax.fori_loop(0, count, body, 0)


def load_lefts(lefts, buffer, sems, count):
    width = buffer.shape[2] // 4

    def copies(c):
        slot = lax.rem(c, 2)
        rows = pl.ds(pl.multiple_of(c * BLOCK, BLOCK), BLOCK)
        return [
            pltpu.make_async_copy(
                left.at[rows], buffer.at[slot, :, index * width : (index + 1) * width], sems.at[slot, index]
            )
            for index, left in enumerate(lefts)
        ]

    def start(c):
        @pl.when(c < count)
        def _():
            for copy in copies(c):
                copy.start()

    def wait(c):
        for copy in copies(c):
            copy.wait()

    return start, wait


def move_rows(outer, buffer, sems, index, inward):
    def copy(c):
        slot = lax.rem(c, 2)
        rows = pl.ds(pl.multiple_of(c * BLOCK, BLOCK), BLOCK)
        ends = (outer.at[rows], buffer.at[slot])
        if not inward:
            ends = ends[::-1]
        return pltpu.make_async_copy(*ends, sems.at[index, slot])

    return copy


def forward_kernel(
    x0,
    x1,
    x2,
    x3,
    gate_hbm,
    upper_hbm,
    reduce_hbm,
    hidden_hbm,
    cot_hbm,
    gain_ref,
    expand_low_ref,
    reduce_low_ref,
    act_out,
    gate_out,
    upper_out,
    layer_out,
    expand_inner_ref,
    reduce_inner_ref,
    own_out,
    *rest,
):
    arrived, rest = rest[:3], rest[3:]
    gate_w, upper_w, reduce_w, lefts, act_buf, gate_buf, upper_buf, *rest = rest
    hidden_ref, cot_ref, layer_ref, own_ref, w_sem, x_sem, o_sem, r_sem, *bufs = rest
    width = own_ref.shape[1]
    count = own_ref.shape[0] // BLOCK
    ff = gate_w.shape[1]
    tile = ff // 2
    loads = [
        pltpu.make_async_copy(source, target, w_sem.at[index])
        for index, (source, target) in enumerate(
            (
                (gate_hbm.at[:, :tile], gate_w.at[:, :tile]),
                (upper_hbm.at[:, :tile], upper_w.at[:, :tile]),
                (reduce_hbm, reduce_w),
                (cot_hbm, cot_ref),
                (hidden_hbm, hidden_ref),
                (gate_hbm.at[:, tile:], gate_w.at[:, tile:]),
                (upper_hbm.at[:, tile:], upper_w.at[:, tile:]),
            )
        )
    ]
    start_left, wait_left = load_lefts((x0, x1, x2, x3), lefts, x_sem, count)
    start_left(0)
    for index in (0, 1, 5, 6, 2, 3, 4):
        loads[index].start()
    layer_rows = rows_out(layer_ref, layer_out, r_sem, 0)
    own_rows = rows_out(own_ref, own_out, r_sem, 1)
    greet()
    outs = [
        move_rows(outer, buffer, o_sem, index, False)
        for index, (outer, buffer) in enumerate(
            ((act_out, act_buf), (gate_out, gate_buf), (upper_out, upper_buf))
        )
    ]

    def compute(c, put):
        slot = lax.rem(c, 2)
        wait_left(c)
        start_left(c + 1)

        @pl.when(c == 0)
        def _():
            loads[0].wait()
            loads[1].wait()

        @pl.when(c >= 2)
        def _():
            for out in outs:
                out(c - 2).wait()

        def tiles(n, carry):
            @pl.when(jnp.logical_and(c == 0, n == 1))
            def _():
                loads[5].wait()
                loads[6].wait()

            at = pl.ds(pl.multiple_of(n * tile, tile), tile)
            left = lefts[slot]
            gate = dot_of(left, gate_w[:, at], 1, 0)
            upper = dot_of(left, upper_w[:, at], 1, 0)
            act_buf[slot, :, at] = (gate * jax.nn.sigmoid(gate) * upper).astype(BF)
            gate_buf[slot, :, at] = gate.astype(BF)
            upper_buf[slot, :, at] = upper.astype(BF)
            return carry

        lax.fori_loop(0, ff // tile, tiles, 0)
        for out in outs:
            out(c).start()

        @pl.when(c == 0)
        def _():
            loads[2].wait()

        for block in (1, 3, 2, 0):
            span = slice(block * width, (block + 1) * width)
            put(block, dot_of(act_buf[slot], reduce_w[:, span], 1, 0))
        rows = span_of(c, BLOCK)
        expand_inner_ref[:, rows] = dot_of(expand_low_ref[...], lefts[slot], 1, 1).astype(BF)
        reduce_inner_ref[:, rows] = dot_of(reduce_low_ref[...], act_buf[slot], 1, 1)

    def stats(c, rows, result):
        @pl.when(c == 0)
        def _():
            loads[3].wait()
            loads[4].wait()

        weighted = gain_ref[1:2, :] * cot_ref[rows, :].astype(F32)
        return sums_of(result * result, weighted * result)

    def finish(c, rows, result, total):
        scale = lax.rsqrt(column_of(total, 0) / D + EPS)
        gain = gain_ref[1:2, :]
        layer_ref[rows, :] = (hidden_ref[rows, :] + gain * result * scale).astype(BF)
        layer_rows(c).start()
        weighted = gain * cot_ref[rows, :].astype(F32)
        inner = column_of(total, 1)
        return (scale * weighted - result * (scale * scale * scale * inner / D)).astype(BF)

    run_blocks(count, bufs, compute, stats, finish, own_ref, arrived, own_rows=own_rows)
    wait_rows(count, layer_rows, own_rows)
    for c in range(max(count - 2, 0), count):
        for out in outs:
            out(c).wait()


def forward_call(lefts, gate_w, upper_w, reduce_w, hidden, cotangent, gain, low, reduce_low):
    rows, width = hidden.shape
    count = rows // BLOCK
    ff = gate_w.shape[1]
    part = jax.ShapeDtypeStruct((rows, width), BF)
    wide = jax.ShapeDtypeStruct((rows, ff), BF)
    return pl.pallas_call(
        forward_kernel,
        out_shape=[wide] * 3
        + [
            part,
            jax.ShapeDtypeStruct((32, rows), BF),
            jax.ShapeDtypeStruct((16, rows), F32),
        ]
        + [part] * 4,
        in_specs=[ANY_SPEC] * 9 + [VMEM_SPEC] * 3,
        out_specs=[ANY_SPEC] * 4 + [VMEM_SPEC] * 2 + [ANY_SPEC] * 4,
        scratch_shapes=[
            pltpu.VMEM(gate_w.shape, BF),
            pltpu.VMEM(upper_w.shape, BF),
            pltpu.VMEM(reduce_w.shape, BF),
            pltpu.VMEM((2, BLOCK, 4 * width), BF),
            pltpu.VMEM((2, BLOCK, ff), BF),
            pltpu.VMEM((2, BLOCK, ff), BF),
            pltpu.VMEM((2, BLOCK, ff), BF),
            pltpu.VMEM((rows, width), F32),
            pltpu.VMEM((rows, width), BF),
            pltpu.VMEM((rows, width), BF),
            pltpu.VMEM((rows, width), BF),
            pltpu.SemaphoreType.DMA((7,)),
            pltpu.SemaphoreType.DMA((2, 4)),
            pltpu.SemaphoreType.DMA((3, 2)),
            pltpu.SemaphoreType.DMA((2, count)),
        ]
        + exchange_scratch(count, width, True),
        compiler_params=talk_params(1),
        cost_estimate=cost_of(24 * rows * width * ff, 2**27),
        name="forward",
    )(*lefts, gate_w, upper_w, reduce_w, hidden, cotangent, gain, low, reduce_low)


def backward_kernel(
    x0,
    x1,
    x2,
    x3,
    gate_hbm,
    upper_hbm,
    reduce_hbm,
    gate_in,
    upper_in,
    cot_hbm,
    branch_hbm,
    stat_ref,
    gain_ref,
    reduce_up_ref,
    expand_up_ref,
    expand_inner_ref,
    d_hidden_out,
    reduce_inner_ref,
    d_inner_ref,
    up_grad_ref,
    own_out,
    *rest,
):
    arrived, rest = rest[:3], rest[3:]
    gate_w, upper_w, reduce_w, lefts, gate_buf, upper_buf, d_gate_buf, d_upper_buf, *rest = rest
    branch_ref, cot_ref, d_hidden_ref, own_ref, w_sem, x_sem, i_sem, r_sem, *bufs = rest
    width = own_ref.shape[1]
    count = own_ref.shape[0] // BLOCK
    ff = gate_w.shape[1]
    up_grad_ref[...] = jnp.zeros_like(up_grad_ref)
    tile = ff // 2
    loads = [
        pltpu.make_async_copy(source, target, w_sem.at[index])
        for index, (source, target) in enumerate(
            (
                (reduce_hbm.at[:tile], reduce_w.at[:tile]),
                (gate_hbm, gate_w),
                (upper_hbm, upper_w),
                (cot_hbm, cot_ref),
                (branch_hbm, branch_ref),
                (reduce_hbm.at[tile:], reduce_w.at[tile:]),
            )
        )
    ]
    start_left, wait_left = load_lefts((x0, x1, x2, x3), lefts, x_sem, count)
    ins = [
        move_rows(outer, buffer, i_sem, index, True)
        for index, (outer, buffer) in enumerate(((gate_in, gate_buf), (upper_in, upper_buf)))
    ]
    start_left(0)
    for one in ins:
        one(0).start()
    for index in (0, 5, 1, 2, 3, 4):
        loads[index].start()
    hidden_rows = rows_out(d_hidden_ref, d_hidden_out, r_sem, 0)
    own_rows = rows_out(own_ref, own_out, r_sem, 1)
    greet()

    def compute(c, put):
        slot = lax.rem(c, 2)
        wait_left(c)
        start_left(c + 1)
        for one in ins:
            one(c).wait()

        @pl.when(c + 1 < count)
        def _():
            for one in ins:
                one(c + 1).start()

        @pl.when(c == 0)
        def _():
            loads[0].wait()

        def tiles(n, carry):
            @pl.when(jnp.logical_and(c == 0, n == 1))
            def _():
                loads[5].wait()

            at = pl.ds(pl.multiple_of(n * tile, tile), tile)
            d_act = dot_of(lefts[slot], reduce_w[at, :], 1, 1)
            gate = gate_buf[slot, :, at].astype(F32)
            sigma = jax.nn.sigmoid(gate)
            d_gate = d_act * upper_buf[slot, :, at].astype(F32) * (sigma * (1 + gate * (1 - sigma)))
            d_gate_buf[:, at] = d_gate.astype(BF)
            d_upper_buf[:, at] = (d_act * (gate * sigma)).astype(BF)
            return carry

        lax.fori_loop(0, ff // tile, tiles, 0)
        @pl.when(c == 0)
        def _():
            loads[1].wait()
            loads[2].wait()

        for block in (1, 3, 2, 0):
            span = slice(block * width, (block + 1) * width)
            put(
                block,
                dot_of(d_gate_buf[...], gate_w[span, :], 1, 1)
                + dot_of(d_upper_buf[...], upper_w[span, :], 1, 1),
            )
        rows = span_of(c, BLOCK)
        inner = dot_of(reduce_up_ref[...], lefts[slot], 1, 1)
        reduce_inner_ref[:, rows] = (ADAPTER_FACTOR * inner).astype(BF)
        for part, grad in enumerate((d_gate_buf, d_upper_buf)):
            own = slice(16 * part, 16 * part + 16)
            d_inner_ref[own, rows] = ADAPTER_FACTOR * dot_of(expand_up_ref[own, :], grad[...], 1, 1)
            up_grad_ref[own, :] += ADAPTER_FACTOR * dot_of(
                expand_inner_ref[own, rows], grad[...], 1, 0
            )

    def stats(c, rows, total):
        @pl.when(c == 0)
        def _():
            loads[3].wait()
            loads[4].wait()

        d_hidden = cot_ref[rows, :].astype(F32) + total
        d_hidden_ref[rows, :] = d_hidden
        hidden_rows(c).start()
        return sums_of(gain_ref[0:1, :] * d_hidden * branch_ref[rows, :])

    def finish(c, rows, total, sums):
        scale = lax.rsqrt(column_of(stat_ref[c], 0) / D + EPS)
        weighted = gain_ref[0:1, :] * d_hidden_ref[rows, :]
        inner = column_of(sums, 0)
        back = scale * scale * scale * inner / D
        return (scale * weighted - branch_ref[rows, :] * back).astype(BF)

    run_blocks(count, bufs, compute, stats, finish, own_ref, arrived, own_rows=own_rows)
    wait_rows(count, hidden_rows, own_rows)


def backward_call(
    lefts, gate_w, upper_w, reduce_w, gate, upper, cotangent, branch, stats, gain, *adapters
):
    rows, width = branch.shape
    count = rows // BLOCK
    ff = gate_w.shape[1]
    part = jax.ShapeDtypeStruct((rows, width), BF)
    return pl.pallas_call(
        backward_kernel,
        out_shape=[
            jax.ShapeDtypeStruct((rows, width), F32),
            jax.ShapeDtypeStruct((16, rows), BF),
            jax.ShapeDtypeStruct((32, rows), F32),
            jax.ShapeDtypeStruct((32, ff), F32),
        ]
        + [part] * 4,
        in_specs=[ANY_SPEC] * 11 + [VMEM_SPEC] * 5,
        out_specs=[ANY_SPEC] + [VMEM_SPEC] * 3 + [ANY_SPEC] * 4,
        scratch_shapes=[
            pltpu.VMEM(gate_w.shape, BF),
            pltpu.VMEM(upper_w.shape, BF),
            pltpu.VMEM(reduce_w.shape, BF),
            pltpu.VMEM((2, BLOCK, 4 * width), BF),
            pltpu.VMEM((2, BLOCK, ff), BF),
            pltpu.VMEM((2, BLOCK, ff), BF),
            pltpu.VMEM((BLOCK, ff), BF),
            pltpu.VMEM((BLOCK, ff), BF),
            pltpu.VMEM((rows, width), F32),
            pltpu.VMEM((rows, width), BF),
            pltpu.VMEM((rows, width), F32),
            pltpu.VMEM((rows, width), BF),
            pltpu.SemaphoreType.DMA((6,)),
            pltpu.SemaphoreType.DMA((2, 4)),
            pltpu.SemaphoreType.DMA((2, 2)),
            pltpu.SemaphoreType.DMA((2, count)),
        ]
        + exchange_scratch(count, width, True),
        compiler_params=talk_params(2),
        cost_estimate=cost_of(24 * rows * width * ff, 2**27),
        name="backward",
    )(
        *lefts, gate_w, upper_w, reduce_w, gate, upper, cotangent, branch, stats, gain, *adapters
    )


def input_kernel(
    raw_hbm,
    dq_hbm,
    dk_hbm,
    dv_hbm,
    act_hbm,
    mixed_hbm,
    branch_hbm,
    hidden_hbm,
    result_hbm,
    matrix_hbm,
    d_hidden_hbm,
    tokens_hbm,
    scale_ref,
    q_sum_ref,
    k_sum_ref,
    gain_ref,
    cos_ref,
    sin_ref,
    inner_ref,
    up_ref,
    part_ref,
    d_inner_ref,
    expand_grad_ref,
    out_hbm,
    rows_out_hbm,
    cols_out_hbm,
    raw_buf,
    dq_buf,
    dk_buf,
    dv_buf,
    act_buf,
    mixed_buf,
    branch_buf,
    hidden_buf,
    result_buf,
    matrix_ref,
    d_hidden_ref,
    tokens_ref,
    out_ref,
    left_ref,
    inner_out,
    inner_in,
    inner_mid,
    inner_far,
    sum_own,
    sum_in,
    columns,
    up_all,
    part_in,
    part_mid,
    part_far,
    in_sem,
    core_sem,
    far_sem,
    sum_sem,
    part_sem,
    load_sem,
    r_sem,
    row_grad_ref,
    attn_grad_ref,
    reduce_grad_ref,
    row_pack,
    col_pack,
    *bufs,
):
    group_sems, bufs = bufs[:5], bufs[5:]
    width = out_ref.shape[1]
    local = dq_buf.shape[2]
    count = out_ref.shape[0] // BLOCK
    ins = [
        move_rows(outer, buffer, in_sem, index, True)
        for index, (outer, buffer) in enumerate(
            (
                (raw_hbm, raw_buf),
                (dq_hbm, dq_buf),
                (dk_hbm, dk_buf),
                (dv_hbm, dv_buf),
                (act_hbm, act_buf),
                (mixed_hbm, mixed_buf),
                (branch_hbm, branch_buf),
                (hidden_hbm, hidden_buf),
                (result_hbm, result_buf),
            )
        )
    ]
    for one in ins:
        one(0).start()
    loads = [
        pltpu.make_async_copy(source, target, load_sem.at[index])
        for index, (source, target) in enumerate(
            ((matrix_hbm, matrix_ref), (d_hidden_hbm, d_hidden_ref), (tokens_hbm, tokens_ref))
        )
    ]
    for load in loads:
        load.start()
    out_rows = rows_out(out_ref, out_hbm, r_sem, 0)
    for grad in (row_grad_ref, attn_grad_ref, reduce_grad_ref):
        grad[...] = jnp.zeros_like(grad)
    up_all[...] = jnp.zeros_like(up_all)
    sum_own[...] = jnp.zeros_like(sum_own)
    for row, part in enumerate((q_sum_ref, k_sum_ref)):
        total = part[0]
        for h in range(1, part.shape[0]):
            total = total + part[h]
        sum_own[row : row + 1, :] = total
    greet_all(row_and_col_peers() + [other_of_pair()])
    exchanges = [send(sum_own, sum_in.at[step - 1], sum_sem, step - 1, step) for step in (1, 2, 3)]
    for copy in exchanges:
        copy.start()
    part_core = send(part_ref, part_in, part_sem, 0, 1)
    part_side = send(part_mid, part_far, part_sem, 1, 2)
    part_core.start()
    part_core.wait()
    part_mid[...] = (part_ref[...].astype(F32) + part_in[...].astype(F32)).astype(BF)
    part_side.start()
    for copy in exchanges:
        copy.wait()
    total = sum_own[...] + sum_in[0] + sum_in[1] + sum_in[2]
    scales = scale_ref[...]
    backs = scales * scales * total / D
    for part in range(2):
        columns[part] = jnp.broadcast_to(column_of(scales, part), columns.shape[1:])
        columns[2 + part] = jnp.broadcast_to(column_of(backs, part), columns.shape[1:])

    def inner_core(c):
        return send(inner_out.at[lax.rem(c, 2)], inner_in.at[c], core_sem, c, 1)

    def inner_side(c):
        return send(inner_mid.at[lax.rem(c, 2)], inner_far.at[c], far_sem, c, 2)

    def after_core(c):
        @pl.when(c >= 2)
        def _():
            inner_side(c - 2).wait_send()

        inner_core(c).wait_recv()
        slot = lax.rem(c, 2)
        total = inner_out[slot].astype(F32) + inner_in[c].astype(F32)
        inner_mid[slot] = total.astype(BF)
        inner_side(c).start()

    def after_side(c):
        inner_side(c).wait_recv()
        total = inner_mid[lax.rem(c, 2)].astype(F32) + inner_far[c].astype(F32)
        row_grad_ref[:48, :] += dot_of(total.astype(BF), tokens_ref[span_of(c, BLOCK), :], 1, 0)

    def compute(c, put):
        slot = lax.rem(c, 2)
        for one in ins:
            one(c).wait()

        @pl.when(c + 1 < count)
        def _():
            for one in ins:
                one(c + 1).start()

        @pl.when(c >= 2)
        def _():
            inner_core(c - 2).wait_send()

        rows = span_of(c, BLOCK)
        cosine = cos_ref[rows, :]
        sine = sin_ref[rows, :]
        for part, grad in ((0, dq_buf), (1, dk_buf)):
            scale = columns[part, rows, :]
            back = columns[2 + part, rows, :]
            for at in range(0, local, HEAD):
                turned = grad[slot, :, at : at + HEAD]
                turned = turned * cosine - pltpu.roll(turned, HEAD // 2, 1) * sine
                turned = turned * gain_ref[part : part + 1, at : at + HEAD] * scale
                lane = part * local + at
                left_ref[:, lane : lane + HEAD] = (
                    turned - raw_buf[slot, :, lane : lane + HEAD] * back
                ).astype(BF)
        left_ref[:, 2 * local :] = dv_buf[slot].astype(BF)
        left = left_ref[...]
        inner_out[slot] = (ADAPTER_FACTOR * dot_of(up_ref[...], left, 1, 1)).astype(BF)
        inner_core(c).start()
        up_all[...] += dot_of(inner_ref[:, rows], left, 1, 0)

        @pl.when(c == 0)
        def _():
            for load in loads:
                load.wait()
            part_side.wait()

        for block in (1, 3, 2, 0):
            put(block, dot_of(left, matrix_ref[block * width : (block + 1) * width, :], 1, 1))
        whole = part_mid[:, rows].astype(F32) + part_far[:, rows].astype(F32)
        whole = whole.astype(BF)
        for at, size, first, other, factor in (
            (48, 16, 0, branch_buf, ADAPTER_FACTOR),
            (64, 32, 32, hidden_buf, 1.0),
            (96, 16, 16, result_buf, ADAPTER_FACTOR),
        ):
            term = dot_of(whole[first : first + size], other[slot], 1, 0)
            row_grad_ref[at : at + size, :] += factor * term
        attn_grad_ref[...] += dot_of(d_inner_ref[:16, rows], mixed_buf[slot], 1, 0)
        reduce_grad_ref[...] += dot_of(d_inner_ref[16:, rows], act_buf[slot], 1, 0)

    def finish(c, rows, total):
        out_ref[rows, :] = d_hidden_ref[rows, :] + total
        out_rows(c).start()

    run_blocks(count, bufs, compute, None, finish, extra=(after_core, after_side))
    row_pack[...] = row_grad_ref[...].astype(BF)
    cols = col_pack.shape[0]
    pieces = [
        (up_all, 16 * part, part * local, local, ADAPTER_FACTOR) for part in range(3)
    ]
    ff = reduce_grad_ref.shape[1]
    pieces += [
        (attn_grad_ref, 0, 0, local, 1.0),
        (expand_grad_ref, 0, 0, ff, 1.0),
        (expand_grad_ref, 16, 0, ff, 1.0),
        (reduce_grad_ref, 0, 0, ff, 1.0),
    ]
    lane = 0
    for ref, row, at, size, factor in pieces:
        size = size // cols
        for index in range(cols):
            piece = ref[row : row + 16, at + index * size : at + (index + 1) * size]
            col_pack[index, :, lane : lane + size] = (factor * piece).astype(BF)
        lane += size
    exchange_groups(row_pack, col_pack, rows_out_hbm, cols_out_hbm, group_sems)
    wait_rows(count, out_rows)
    for c in range(max(count - 2, 0), count):
        inner_core(c).wait_send()
        inner_side(c).wait_send()


def input_call(
    raw, d_query, d_key, d_value, act, mixed, branch, hidden, result, matrix, d_hidden, *others
):
    rows, width = d_hidden.shape
    local = d_query.shape[1]
    ff = act.shape[1]
    cols = lax.axis_size("col")
    lanes = (4 * local + 3 * ff) // cols
    count = rows // BLOCK
    grad = pltpu.VMEM((2, BLOCK, local), F32)
    part = pltpu.VMEM((2, BLOCK, width), BF)
    inner = pltpu.VMEM((2, 48, BLOCK), BF)
    arrived = pltpu.VMEM((count, 48, BLOCK), BF)
    total = pltpu.VMEM((64, rows), BF)
    sem = pltpu.SemaphoreType.DMA((2, count))
    return pl.pallas_call(
        input_kernel,
        out_shape=[
            jax.ShapeDtypeStruct((rows, width), F32),
            jax.ShapeDtypeStruct((cols, 2, 112, width), BF),
            jax.ShapeDtypeStruct((4, 2, cols, 16, lanes), BF),
        ],
        in_specs=[ANY_SPEC] * 12 + [VMEM_SPEC] * 11,
        out_specs=[ANY_SPEC] * 3,
        scratch_shapes=[
            pltpu.VMEM((2, BLOCK, 3 * local), F32),
            grad,
            grad,
            grad,
            pltpu.VMEM((2, BLOCK, ff), BF),
            pltpu.VMEM((2, BLOCK, local), BF),
            part,
            part,
            part,
            pltpu.VMEM(matrix.shape, BF),
            pltpu.VMEM((rows, width), F32),
            pltpu.VMEM((rows, width), BF),
            pltpu.VMEM((rows, width), F32),
            pltpu.VMEM((BLOCK, 3 * local), BF),
            inner,
            arrived,
            inner,
            arrived,
            pltpu.VMEM((8, rows), F32),
            pltpu.VMEM((3, 8, rows), F32),
            pltpu.VMEM((4, rows, HEAD), F32),
            pltpu.VMEM((48, 3 * local), F32),
            total,
            total,
            total,
            pltpu.SemaphoreType.DMA((9, 2)),
            sem,
            sem,
            pltpu.SemaphoreType.DMA((2, 3)),
            pltpu.SemaphoreType.DMA((2, 2)),
            pltpu.SemaphoreType.DMA((3,)),
            pltpu.SemaphoreType.DMA((1, count)),
            pltpu.VMEM((112, width), F32),
            pltpu.VMEM((16, local), F32),
            pltpu.VMEM((16, ff), F32),
            pltpu.VMEM((112, width), BF),
            pltpu.VMEM((cols, 16, lanes), BF),
            pltpu.SemaphoreType.DMA((2,)),
            pltpu.SemaphoreType.DMA((2, 2)),
            pltpu.SemaphoreType.DMA((2, cols - 1)),
            pltpu.SemaphoreType.DMA((2, cols - 1)),
            pltpu.SemaphoreType.DMA((2, 2, 3)),
        ]
        + exchange_scratch(count, width, False),
        compiler_params=talk_params(3),
        cost_estimate=cost_of(24 * rows * width * local, 2**26),
        name="input_grad",
    )(raw, d_query, d_key, d_value, act, mixed, branch, hidden, result, matrix, d_hidden, *others)


def deal(items, outs, sems):
    me = lax.axis_index("row")
    copies = []
    for index, (view, out) in enumerate(zip(items, outs)):
        mine = [pltpu.make_async_copy(view(me), out.at[0], sems.at[0, index, 0])]
        for step in (1, 2, 3):
            mine.append(
                pltpu.make_async_remote_copy(
                    src_ref=view(me ^ step),
                    dst_ref=out.at[step],
                    send_sem=sems.at[0, index, step],
                    recv_sem=sems.at[1, index, step],
                    device_id=peer(step),
                    device_id_type=pl.DeviceIdType.MESH,
                )
            )
        copies.append(mine)
    return copies


def start_all(copies):
    for step in (2, 3, 1, 0):
        copies[step].start()


def wait_all(copies):
    for copy in copies:
        copy.wait()


def span_of(at, size):
    return pl.ds(pl.multiple_of(at * size, size), size)


def qkv_view(ref, half):
    _, rows, columns = ref.shape
    return lambda row: ref.at[:, span_of(half, rows // 2), span_of(row, columns // 4)]


def attn_view(ref, half):
    cut = ref.shape[0] // 8
    return lambda row: ref.at[span_of(2 * row + half, cut)]


def expand_view(ref, part, half):
    cut = ref.shape[2] // 8
    return lambda row: ref.at[part, :, span_of(2 * row + half, cut)]


def reduce_view(ref):
    cut = ref.shape[0] // 4
    return lambda row: ref.at[span_of(row, cut)]


def like_views(shapes):
    return [jax.ShapeDtypeStruct((4, *shape), BF) for shape in shapes]


def attn_deal_kernel(attn_ref, attn_out, sems):
    greet()
    (copies,) = deal([attn_view(attn_ref, lax.axis_index("dp"))], [attn_out], sems)
    start_all(copies)
    wait_all(copies)


def attn_deal(attn_weight):
    return pl.pallas_call(
        attn_deal_kernel,
        out_shape=like_views([(attn_weight.shape[0] // 8, attn_weight.shape[1])])[0],
        in_specs=[ANY_SPEC],
        out_specs=ANY_SPEC,
        scratch_shapes=[pltpu.SemaphoreType.DMA((2, 1, 4))],
        compiler_params=talk_params(4),
        cost_estimate=cost_of(0, 2**25),
        name="attn_deal",
    )(attn_weight)


def first_deal_kernel(qkv_ref, expand_ref, qkv_out, gate_out, sems):
    half = lax.axis_index("dp")
    greet()
    copies = deal([qkv_view(qkv_ref, half), expand_view(expand_ref, 0, half)], [qkv_out, gate_out], sems)
    for one in copies:
        start_all(one)
    for one in copies:
        wait_all(one)


def first_deal(qkv_weight, expand_weight):
    parts, rows, columns = qkv_weight.shape
    return pl.pallas_call(
        first_deal_kernel,
        out_shape=like_views(
            [
                (parts, rows // 2, columns // 4),
                (expand_weight.shape[1], expand_weight.shape[2] // 8),
            ]
        ),
        in_specs=[ANY_SPEC] * 2,
        out_specs=[ANY_SPEC] * 2,
        scratch_shapes=[pltpu.SemaphoreType.DMA((2, 2, 4))],
        compiler_params=talk_params(9),
        cost_estimate=cost_of(0, 2**26),
        name="first_deal",
    )(qkv_weight, expand_weight)


def second_deal_kernel(qkv_ref, attn_ref, expand_ref, tokens_ref, pack_ref, *rest):
    qkv_other, attn_other, upper_out, t1, t2, t3, p1, p2, p3, sems, token_sem, pack_sem = rest
    half = lax.axis_index("dp")
    greet()
    rest_qkv, rest_attn, upper = deal(
        [
            qkv_view(qkv_ref, 1 - half),
            attn_view(attn_ref, 1 - half),
            expand_view(expand_ref, 1, half),
        ],
        [qkv_other.at[0], attn_other.at[0], upper_out],
        sems,
    )
    gathers = []
    for source, targets, one_sem in ((pack_ref, (p1, p2, p3), pack_sem), (tokens_ref, (t1, t2, t3), token_sem)):
        gathers.append(
            (
                send(source, targets[1], one_sem, 1, 2),
                send(source, targets[0], one_sem, 0, 1),
                send(targets[1], targets[2], one_sem, 2, 1),
            )
        )
    start_all(rest_qkv)
    start_all(rest_attn)
    for side, core, _ in gathers:
        side.start()
        core.start()
    start_all(upper)
    for side, core, relay in gathers:
        side.wait_recv()
        relay.start()
    for one in (rest_qkv, rest_attn, upper):
        wait_all(one)
    for side, core, relay in gathers:
        side.wait_send()
        core.wait()
        relay.wait()


def second_deal(qkv_weight, attn_weight, expand_weight, tokens, pack, cols):
    parts, rows, columns = qkv_weight.shape
    cut = expand_weight.shape[2] // 8
    wide = (expand_weight.shape[1], cut)
    sem = pltpu.SemaphoreType.DMA((2, 3))
    return pl.pallas_call(
        second_deal_kernel,
        out_shape=[
            jax.ShapeDtypeStruct((cols, 4, parts, rows // 2, columns // 4), BF),
            jax.ShapeDtypeStruct((cols, 4, attn_weight.shape[0] // 8, attn_weight.shape[1]), BF),
            jax.ShapeDtypeStruct((4, *wide), BF),
        ]
        + [jax.ShapeDtypeStruct(tokens.shape, BF)] * 3
        + [jax.ShapeDtypeStruct(pack.shape, BF)] * 3,
        in_specs=[ANY_SPEC] * 5,
        out_specs=[ANY_SPEC] * 9,
        scratch_shapes=[pltpu.SemaphoreType.DMA((2, 3, 4)), sem, sem],
        compiler_params=talk_params(5),
        cost_estimate=cost_of(0, 2**27),
        name="second_deal",
    )(qkv_weight, attn_weight, expand_weight, tokens, pack)


def greet_all(peers):
    barrier = pltpu.get_barrier_semaphore()
    for device in peers:
        pl.semaphore_signal(barrier, inc=1, device_id=device, device_id_type=pl.DeviceIdType.MESH)
    pl.semaphore_wait(barrier, len(peers))


def copy_to(source, target, sems, index, device):
    return pltpu.make_async_remote_copy(
        src_ref=source,
        dst_ref=target,
        send_sem=sems.at[0, index],
        recv_sem=sems.at[1, index],
        device_id=device,
        device_id_type=pl.DeviceIdType.MESH,
    )


def other_of_pair():
    return {"dp": 1 - lax.axis_index("dp")}


def exchange_halves(whole, out, sems, steps):
    cols = whole.shape[0]
    col = lax.axis_index("col")
    copies = []
    for k in steps:
        place = lax.rem(col + k, cols)
        copies.append(copy_to(whole.at[place], out.at[k], sems, k - 1, other_of_pair()))
    return copies


def send_round(view, out, sems, local_sem):
    cols = out.shape[0]
    col = lax.axis_index("col")
    local = pltpu.make_async_copy(view(col), out.at[col], local_sem)
    sends = []
    arrivals = []
    for k in range(1, cols):
        place = lax.rem(col + k, cols)
        came = lax.rem(col - k + cols, cols)
        sends.append(copy_to(view(place), out.at[col], sems, k - 1, {"col": place}))
        arrivals.append(copy_to(view(place), out.at[came], sems, k - 1, {"col": place}))

    def wait():
        local.wait()
        for one in arrivals:
            one.wait_recv()
        for one in sends:
            one.wait_send()

    return [local, *sends], wait


def row_and_col_peers():
    cols = lax.axis_size("col")
    col = lax.axis_index("col")
    return [peer(step) for step in (1, 2, 3)] + [
        {"col": lax.rem(col + k, cols)} for k in range(1, cols)
    ]


def third_deal_kernel(
    expand_ref, reduce_ref, qkv_all, qkv_other, attn_all, attn_other, pack_ref, gain_ref, *rest
):
    reduce_out, gate_out, upper_out, qkv_out, attn_out, pack_out, gain_out = rest[:7]
    deal_sem, qkv_sem, attn_sem, pack_sem, gain_sem, local_sem = rest[7:]
    other = 1 - lax.axis_index("dp")
    me = lax.axis_index("row")
    greet_all(row_and_col_peers() + [other_of_pair()])
    sub = gain_out.shape[2]
    steps = range(1, qkv_all.shape[0])
    swaps = exchange_halves(qkv_all, qkv_out, qkv_sem, steps)
    swaps += exchange_halves(attn_all, attn_out, attn_sem, steps)
    packs, wait_packs = send_round(lambda place: pack_ref.at[place], pack_out, pack_sem, local_sem.at[2])
    gains, wait_gains = send_round(
        lambda place: gain_ref.at[:, span_of(me, sub)], gain_out, gain_sem, local_sem.at[3]
    )
    for copy in packs + gains + swaps:
        copy.start()
    copies = deal(
        [
            reduce_view(reduce_ref),
            expand_view(expand_ref, 0, other),
            expand_view(expand_ref, 1, other),
        ],
        [reduce_out, gate_out.at[0], upper_out.at[0]],
        deal_sem,
    )
    for one in copies:
        start_all(one)
    wait_packs()
    wait_gains()
    for one in copies:
        wait_all(one)
    wait_all(swaps)


def third_deal(expand_weight, reduce_weight, qkv_all, qkv_other, attn_all, attn_other, pack, gain):
    wide = (expand_weight.shape[1], expand_weight.shape[2] // 8)
    cols = qkv_all.shape[0]
    round_sem = pltpu.SemaphoreType.DMA((2, cols - 1))
    return pl.pallas_call(
        third_deal_kernel,
        out_shape=like_views([(reduce_weight.shape[0] // 4, reduce_weight.shape[1])])
        + [jax.ShapeDtypeStruct((cols, 4, *wide), BF)] * 2
        + [
            jax.ShapeDtypeStruct(qkv_all.shape, BF),
            jax.ShapeDtypeStruct(attn_all.shape, BF),
            jax.ShapeDtypeStruct(pack.shape, BF),
            jax.ShapeDtypeStruct((cols, gain.shape[0], gain.shape[1] // 4), F32),
        ],
        in_specs=[ANY_SPEC] * 8,
        out_specs=[ANY_SPEC] * 7,
        scratch_shapes=[
            pltpu.SemaphoreType.DMA((2, 3, 4)),
            round_sem,
            round_sem,
            round_sem,
            round_sem,
            pltpu.SemaphoreType.DMA((4,)),
        ],
        input_output_aliases={3: 3, 5: 4},
        compiler_params=talk_params(6),
        cost_estimate=cost_of(0, 2**27),
        name="third_deal",
    )(expand_weight, reduce_weight, qkv_all, qkv_other, attn_all, attn_other, pack, gain)


def front_kernel(
    x0,
    x1,
    x2,
    x3,
    matrix_ref,
    low_ref,
    gate_all,
    gate_other,
    raw_ref,
    square_ref,
    inner_ref,
    gate_out,
    swap_sem,
):
    local = raw_ref.shape[1] // 3
    first = exchange_halves(gate_all, gate_out, swap_sem, range(1, 2))

    @pl.when(pl.program_id(0) == 0)
    def _():
        greet_all([other_of_pair()])
        for copy in first:
            copy.start()

    left = jnp.concatenate([x0[...], x1[...], x2[...], x3[...]], axis=1)
    squares = []
    for part in range(3):
        lanes = slice(part * local, (part + 1) * local)
        product = dot_of(left, matrix_ref[:, lanes], 1, 0)
        raw_ref[:, lanes] = product
        squares.append(product * product)
    square_ref[...] = sums_of(*squares[:2])
    inner_ref[...] = dot_of(low_ref[...], left, 1, 1).astype(BF)

    @pl.when(pl.program_id(0) == pl.num_programs(0) - 1)
    def _():
        wait_all(first)


def front_call(lefts, matrix, low, gate_all, gate_other):
    rows, width = lefts[0].shape
    wide = matrix.shape[1]
    tile = row_tile(rows)
    cols = gate_all.shape[0]

    def whole(array):
        return pl.BlockSpec(array.shape, lambda m: (0, 0))

    return pl.pallas_call(
        front_kernel,
        out_shape=[
            jax.ShapeDtypeStruct((rows, wide), F32),
            jax.ShapeDtypeStruct((8, rows), F32),
            jax.ShapeDtypeStruct((48, rows), BF),
            jax.ShapeDtypeStruct(gate_all.shape, BF),
        ],
        grid=(rows // tile,),
        in_specs=[pl.BlockSpec((tile, width), lambda m: (m, 0))] * 4
        + [whole(matrix), whole(low), ANY_SPEC, ANY_SPEC],
        out_specs=[
            pl.BlockSpec((tile, wide), lambda m: (m, 0)),
            pl.BlockSpec((8, tile), lambda m: (0, m)),
            pl.BlockSpec((48, tile), lambda m: (0, m)),
            ANY_SPEC,
        ],
        scratch_shapes=[
            pltpu.SemaphoreType.DMA((2, cols - 1)),
        ],
        input_output_aliases={7: 3},
        compiler_params=talk_params(8),
        cost_estimate=cost_of(8 * rows * width * wide, 2**26),
        name="front",
    )(*lefts, matrix, low, gate_all, gate_other)


def exchange_groups(row_ref, col_ref, rows_out, cols_out, sems):
    local_sem, pair_sem, round_sem, deal_sem, row_sem = sems
    cols = col_ref.shape[0]
    col = lax.axis_index("col")
    places = [lax.rem(col + k, cols) for k in range(cols)]
    to = copy_to
    swap_rows = to(row_ref, rows_out.at[0, 1], pair_sem, 0, other_of_pair())
    swap_rows.start()
    dealt = [
        to(col_ref.at[places[k]], cols_out.at[0, 0, col], deal_sem, k - 1, {"col": places[k]})
        for k in range(1, cols)
    ]
    for copy in dealt:
        copy.start()
    keep_rows = pltpu.make_async_copy(row_ref, rows_out.at[0, 0], local_sem.at[0])
    keep_cols = pltpu.make_async_copy(col_ref.at[col], cols_out.at[0, 0, col], local_sem.at[1])
    keep_rows.start()
    keep_cols.start()
    for k in range(1, cols):
        came = lax.rem(col - k + cols, cols)
        to(col_ref.at[came], cols_out.at[0, 0, came], deal_sem, k - 1, {"col": places[k]}).wait_recv()
    keep_cols.wait()
    swap_cols = to(cols_out.at[0, 0], cols_out.at[0, 1], pair_sem, 1, other_of_pair())
    swap_cols.start()

    def spread(which):
        side = to(cols_out.at[0, which], cols_out.at[2, which], row_sem.at[which], 1, peer(2))
        core = to(cols_out.at[0, which], cols_out.at[1, which], row_sem.at[which], 0, peer(1))
        relay = to(cols_out.at[2, which], cols_out.at[3, which], row_sem.at[which], 2, peer(1))
        side.start()
        core.start()
        return side, core, relay

    spreads = [spread(0)]
    keep_rows.wait()
    swap_rows.wait_recv()
    rounds = [
        to(rows_out.at[0], rows_out.at[k], round_sem, k - 1, {"col": places[k]})
        for k in range(1, cols)
    ]
    for copy in rounds:
        copy.start()
    swap_cols.wait_recv()
    spreads.append(spread(1))
    for side, core, relay in spreads:
        side.wait_recv()
        relay.start()
    for side, core, relay in spreads:
        core.wait()
        relay.wait()
        side.wait_send()
    for copy in rounds:
        copy.wait()
    for copy in dealt:
        copy.wait_send()
    swap_rows.wait_send()
    swap_cols.wait_send()


def across(values, step):
    return lax.ppermute(values, "row", [(i, i ^ step) for i in range(4)])


def sum_row(values):
    values = values + across(values, 1)
    return values + across(values, 2)


def gather_col(values):
    return lax.all_gather(values, "col", axis=0, tiled=False)


def swap_pair(values):
    return lax.ppermute(values, "dp", [(0, 1), (1, 0)])


def round_col(values, cols):
    shift = lambda k: [(i, (i + k) % cols) for i in range(cols)]
    return [values] + [lax.ppermute(values, "col", shift(k)) for k in range(1, cols)]


def after(values, earlier):
    return lax.optimization_barrier((values, earlier))[0]


def group_shards(
    tokens,
    cotangent,
    qkv_weight,
    attn_weight,
    expand_weight,
    reduce_weight,
    headnorm_gain,
    post_gain,
    qkv_lowrank,
    qkv_uprank,
    attn_lowrank,
    attn_uprank,
    expand_lowrank,
    expand_uprank,
    reduce_lowrank,
    reduce_uprank,
    prefix_length,
    adapter_set,
):
    cols = lax.axis_size("col")
    pair = lax.axis_index("dp")
    me = lax.axis_index("row")
    col = lax.axis_index("col")
    rows, width = tokens.shape
    sub = qkv_weight.shape[2] // 4
    ff = expand_weight.shape[2]
    ff_sub = ff // 4
    ff_half = ff_sub // 2
    local = cols * sub
    ff_local = cols * ff_sub
    sequence = pair * cols + col
    mine = lax.dynamic_index_in_dim(adapter_set, sequence, 0, keepdims=False)
    prefix = lax.dynamic_slice_in_dim(prefix_length, sequence, 1)
    cols_sets = lax.dynamic_slice_in_dim(adapter_set, pair * cols, cols)

    attn_own = attn_deal(attn_weight)
    qkv_own, gate_own = first_deal(after(qkv_weight, attn_own), expand_weight)
    row_pack = row_pack_of(
        after(mine.reshape(1), qkv_own),
        qkv_lowrank.transpose(0, 1, 3, 2),
        attn_uprank,
        expand_lowrank.transpose(0, 1, 3, 2),
        reduce_uprank,
    )
    col_pack = col_pack_of(
        jnp.concatenate([cols_sets, me.reshape(1)]),
        qkv_uprank,
        attn_lowrank.transpose(0, 2, 1),
        expand_uprank,
        reduce_lowrank.transpose(0, 2, 1),
    )

    place = jnp.stack([pair, col])

    col_pack = after(col_pack, qkv_own)
    qkv_other, attn_other, up_own, *others = second_deal(
        qkv_weight, attn_weight, expand_weight, tokens, row_pack, cols
    )
    token_parts = [tokens, *others[:3]]
    row_all = jnp.concatenate([row_pack, *others[3:]], axis=1)
    qkv_low = row_all[:48]
    attn_up = row_all[48:64]
    expand_low = row_all[64:96]
    reduce_up = row_all[96:112]
    qkv_all = gather_col(qkv_own)
    attn_all = gather_col(attn_own)
    gate_all = gather_col(after(gate_own, row_pack))
    up_all = gather_col(up_own)
    reduce_own, gate_other, up_other, qkv_other, attn_other, col_all, gains = third_deal(
        expand_weight,
        after(reduce_weight, others[0]),
        qkv_all,
        qkv_other,
        attn_all,
        attn_other,
        col_pack,
        headnorm_gain,
    )
    reduce_all = gather_col(reduce_own)
    gains = gains.transpose(1, 0, 2).reshape(2, local)

    def own_columns(at, size):
        return col_all[:, :, at : at + size].transpose(1, 0, 2).reshape(16, cols * size)

    qkv_up = [own_columns(i * sub, sub) for i in range(3)]
    attn_low = own_columns(3 * sub, sub)
    expand_up = [own_columns(4 * sub + i * ff_sub, ff_sub) for i in range(2)]
    reduce_low = own_columns(4 * sub + 2 * ff_sub, ff_sub)

    diagonal_up = jnp.concatenate(
        [
            jnp.pad(up, ((0, 0), (i * local, (2 - i) * local))) for i, up in enumerate(qkv_up)
        ]
    )
    qkv_up = jnp.concatenate(qkv_up)
    qkv_w = merge_qkv(place, qkv_all, qkv_other, qkv_low, qkv_up)
    attn_w = merge_out(place, [attn_all, attn_other], attn_low, attn_up)

    half = HEAD // 2
    freq = THETA ** (-2.0 * jnp.arange(half, dtype=F32) / HEAD)
    angle = jnp.arange(rows, dtype=jnp.int32).astype(F32)[:, None] * freq[None, :]
    cosine = jnp.concatenate([jnp.cos(angle)] * 2, axis=1)
    sine = jnp.sin(angle)
    sine = jnp.concatenate([-sine, sine], axis=1)

    raw, squares, qkv_inner, gate_other = front_call(
        token_parts, qkv_w, qkv_low, gate_all, gate_other
    )
    scale = lax.rsqrt(sum_row(squares) / D + EPS)
    query, key, value = rotate_rows(raw, scale, gains, cosine, sine)
    limit = jnp.maximum(jnp.arange(rows, dtype=jnp.int32), prefix - 1)[None]
    mixed, branch, hidden, branch_stats, *hidden_parts, gate_other, up_other, probs = branch_call(
        query,
        key,
        value,
        limit,
        attn_w,
        tokens,
        post_gain,
        (gate_all, gate_other, up_all, up_other),
    )
    expand_w = [
        merge_expand(
            place, whole, other, expand_low[16 * i : 16 * i + 16], expand_up[i]
        )
        for i, (whole, other) in enumerate(((gate_all, gate_other), (up_all, up_other)))
    ]
    reduce_w = merge_out(place, [reduce_all], reduce_low, reduce_up)
    act, gate, upper, layer_out, expand_inner, reduce_inner, *result_parts = forward_call(
        hidden_parts, *expand_w, reduce_w, hidden, cotangent, post_gain, expand_low, reduce_low
    )
    d_hidden, d_reduce_inner, d_expand_inner, g_expand_up, *branch_parts = backward_call(
        result_parts,
        *expand_w,
        reduce_w,
        gate,
        upper,
        cotangent,
        branch,
        branch_stats,
        post_gain,
        reduce_up,
        jnp.concatenate(expand_up),
        expand_inner,
    )
    d_query, d_key, d_value, q_sums, k_sums, d_attn_inner = attend_back(
        query, branch_parts, attn_w, attn_up, mixed, probs, key, value
    )
    partials = jnp.concatenate(
        [dot_of(attn_low, mixed, 1, 1), reduce_inner, d_expand_inner]
    ).astype(BF)
    input_grad, every_row, every_col = input_call(
        raw,
        d_query,
        d_key,
        d_value,
        act,
        mixed,
        branch_parts[0],
        hidden_parts[0],
        result_parts[0],
        qkv_w,
        d_hidden,
        tokens,
        scale,
        q_sums,
        k_sums,
        gains,
        cosine,
        sine,
        qkv_inner,
        diagonal_up,
        partials,
        jnp.concatenate([d_attn_inner, d_reduce_inner]),
        g_expand_up,
    )

    place_of = jnp.arange(2 * cols, dtype=jnp.int32)
    row_place = (pair ^ (place_of % 2)) * cols + (col - place_of // 2 + cols) % cols
    col_place = (pair ^ (place_of // cols)) * cols + place_of % cols
    places = jnp.concatenate([row_place, col_place])
    chosen = places[:, None] == jnp.arange(2 * cols, dtype=jnp.int32)[None, :]
    ids = jnp.sum(jnp.where(chosen, adapter_set[None, :], 0), axis=1)
    ids = jnp.concatenate([ids, me.reshape(1)])
    qkv_low, qkv_up, attn_low, attn_up, expand_low, expand_up, reduce_low, reduce_up = finish_call(
        ids, every_row, every_col, sub, ff_sub
    )
    return (
        layer_out,
        input_grad,
        qkv_low.transpose(0, 1, 3, 2),
        qkv_up,
        attn_low.transpose(0, 2, 1),
        attn_up,
        expand_low.transpose(0, 1, 3, 2),
        expand_up,
        reduce_low.transpose(0, 2, 1),
        reduce_up,
    )


def shards(*arrays):
    whole = (
        lax.axis_size("dp") == 2
        and lax.axis_size("row") == 4
        and arrays[0].shape[0] == SEQUENCE_LENGTH
    )
    return group_shards(*arrays) if whole else general_shards(*arrays)


def solution(mesh):
    placed = (
        P(("dp", "col"), "row"),
        P(("dp", "col"), "row"),
        P(None, "row", "col"),
        P("col", "row"),
        P(None, "row", "col"),
        P("col", "row"),
        P(None, "col"),
        P(None, "row"),
        P(None, None, "row", None),
        P(None, None, None, "col"),
        P(None, "col", None),
        P(None, None, "row"),
        P(None, None, "row", None),
        P(None, None, None, "col"),
        P(None, "col", None),
        P(None, None, "row"),
        P(),
        P(),
    )
    return jax.shard_map(
        shards,
        mesh=mesh,
        in_specs=placed,
        out_specs=(
            P(("dp", "col"), "row"),
            P(("dp", "col"), "row"),
            P(None, None, "row", None),
            P(None, None, None, "col"),
            P(None, "col", None),
            P(None, None, "row"),
            P(None, None, "row", None),
            P(None, None, None, "col"),
            P(None, "col", None),
            P(None, None, "row"),
        ),
        check_vma=False,
    )
```
